32 devices in a mesh: ctx: 8 (over z, y), wt: 4 (over x, core).
Axes of the slice: x: 2, y: 2, z: 4, core: 2. Of those that a mesh axis runs over, the one named last changes fastest.
Arguments:
- hidden: bfloat16 [4, 4096, 768], P('wt', 'ctx'), may hold values from -6 to 6
- teacher: bfloat16 [4, 4096, 768], P('wt', 'ctx'), may hold values from -40 to 40
- lengths: int32 [4, 6], replicated, may hold values from 1 to 2048, 3584 in all within a row
- deal: int32 [4, 4096], P('wt'), may hold values from 0 to 4095, as said below
- w_in: bfloat16 [768, 1536], P('wt'), may hold values from -2 to 2
- b_in: bfloat16 [3, 384], P(None, 'wt'), may hold values from -3 to 3
- dw_kernel: bfloat16 [9, 768], P(None, 'wt'), may hold values from -3 to 3
- pw_weight: bfloat16 [768, 384], P('wt'), may hold values from -0.21875 to 0.21875
- pw_bias: bfloat16 [384], P('wt'), may hold values from -3 to 3
- kern_weight: bfloat16 [384, 54], P('wt'), may hold values from -0.3125 to 0.3125
- kern_bias: bfloat16 [54], replicated, may hold values from -3 to 3
- out_weight: bfloat16 [768, 768], P('wt'), may hold values from -0.625 to 0.625
- out_bias: bfloat16 [768], P('wt'), may hold values from -3 to 3
- norm1_gain: bfloat16 [768], P('wt'), may hold values from 0.5 to 1.5
- norm1_bias: bfloat16 [768], P('wt'), may hold values from -3 to 3
- ffn_in: bfloat16 [2, 384, 1536], P(None, 'wt'), may hold values from -0.3125 to 0.3125
- ffn_in_bias: bfloat16 [3072], P('wt'), may hold values from -3 to 3
- ffn_out: bfloat16 [2, 1536, 384], P(None, 'wt'), may hold values from -0.21875 to 0.21875
- ffn_out_bias: bfloat16 [768], P('wt'), may hold values from -3 to 3
- norm2_gain: bfloat16 [768], P('wt'), may hold values from 0.5 to 1.5
- norm2_bias: bfloat16 [768], P('wt'), may hold values from -3 to 3
Outputs:
- output: bfloat16 [4, 4096, 768], P('wt', 'ctx')
- teacher_loss: float32 [], replicated
- grad_hidden: float32 [4, 4096, 768], P('wt', 'ctx')
- grad_w_in: float32 [768, 1536], P('wt')
- grad_b_in: float32 [3, 384], P(None, 'wt')
- grad_dw_kernel: float32 [9, 768], P(None, 'wt')
- grad_pw_weight: float32 [768, 384], P('wt')
- grad_pw_bias: float32 [384], P('wt')
- grad_kern_weight: float32 [384, 54], P('wt')
- grad_kern_bias: float32 [54], replicated
- grad_out_weight: float32 [768, 768], P('wt')
- grad_out_bias: float32 [768], P('wt')
- grad_norm1_gain: float32 [768], P('wt')
- grad_norm1_bias: float32 [768], P('wt')
- grad_ffn_in: float32 [2, 384, 1536], P(None, 'wt')
- grad_ffn_in_bias: float32 [3072], P('wt')
- grad_ffn_out: float32 [2, 1536, 384], P(None, 'wt')
- grad_ffn_out_bias: float32 [768], P('wt')
- grad_norm2_gain: float32 [768], P('wt')
- grad_norm2_bias: float32 [768], P('wt')
The draws below stay inside these ranges and needn't reach their ends.
Inputs may be any that keep to these rules, and one draw needn't show every extreme that they name: Each row of 6 lengths sums to 3584, and its largest is 2048. `deal`: each row is a permutation of the 4096 slots; rows i * 512 to (i + 1) * 512 - 1 hold, from every aligned block of 512 slots, exactly the 64 slots whose offset in the block lies in [i * 64, (i + 1) * 64), in any order.
All inputs are finite; a program needn't handle non-finite values.
Results may differ from the reference program's by a relative error of at most 0.022.
Values may be sent and summed in bfloat16 or wider, within the bound.
A program may use at most 384 MiB of HBM per device.

```python
import math
import jax
import jax.numpy as jnp
import numpy as np
from jax import lax

D = 768
H = 6
HD = 64
FF = 3072
NG = 2
KW = 9
TOK_DEV = 512
SEQS = 6
A = 384
GROUPS = 4
GROUP_TOK = 4096
PIECE = 64
VALID = 3584
MAXLEN = 2048


def draw_teacher(key, part):
    shape = (GROUPS, GROUP_TOK, D)
    base = jax.random.normal(key, shape, jnp.float32)
    reach = math.log(3.0)
    rise = jnp.exp(reach * jnp.arange(GROUP_TOK, dtype=jnp.float32) / GROUP_TOK)
    tilt = jnp.exp(0.4 * jnp.arange(GROUPS, dtype=jnp.float32) / GROUPS)
    return (base * rise[None, :, None] * tilt[:, None, None]).astype(jnp.bfloat16)


def draw_deal(key, part):
    owners = GROUP_TOK // TOK_DEV
    device = jnp.arange(owners, dtype=jnp.int32)[:, None]
    column = jnp.arange(TOK_DEV, dtype=jnp.int32)[None, :]
    base = column // PIECE * TOK_DEV + device * PIECE + column % PIECE
    streams = jax.random.split(jax.random.fold_in(key, 17), GROUPS * owners)
    orders = jax.vmap(lambda stream: jax.random.permutation(stream, TOK_DEV))(streams)
    orders = orders.astype(jnp.int32).reshape(GROUPS, owners, TOK_DEV)
    tiled = jnp.broadcast_to(base[None], (GROUPS, owners, TOK_DEV))
    return jnp.take_along_axis(tiled, orders, axis=2).reshape(GROUPS, GROUP_TOK).astype(jnp.int32)


def draw_w_in(key, part):
    shape = (D, 4 * A)
    base = jnp.clip(jax.random.normal(jax.random.fold_in(key, 29), shape, jnp.float32), -6.0, 6.0)
    column = jnp.arange(4 * A, dtype=jnp.int32)
    factor = jnp.where(column >= 3 * A, 2.0, 1.0).astype(jnp.float32)
    deviation = (D * 2 / 5) ** (-0.5)
    return (base * factor[None, :] * deviation).astype(jnp.bfloat16)


def block_scale(stream_key, shape, cuts, smallest, largest):
    factor_of = 1.0
    for axis_at, shards_of in cuts:
        steps = jax.random.uniform(jax.random.fold_in(jax.random.fold_in(stream_key, 6), axis_at), (shards_of,), jnp.float32, smallest / len(cuts), largest / len(cuts))
        factor_of = factor_of * jnp.repeat(jnp.exp(steps), shape[axis_at] // shards_of).reshape((-1,) + (1,) * (len(shape) - 1 - axis_at))
    return factor_of


def split_up(number_of, total, most, lean):
    portions = [(1 << 20) // math.isqrt(standing ** lean) + 1 for standing in range(2, number_of + 1)]
    rest, counts = total - most - (number_of - 1), [1] * (number_of - 1)
    while rest > 0:
        candidates = [i for i in range(number_of - 1) if counts[i] < most]
        whole, budget = sum([portions[i] for i in candidates]), rest
        for i in candidates:
            addition = min(most - counts[i], max(1, budget * portions[i] // whole), rest)
            counts[i] = counts[i] + addition
            rest = rest - addition
    return np.array([most] + counts)


def ragged(own_key, amount, total, limit, lean):
    if amount == 2:
        one = jax.random.randint(own_key, (), max(1, total - limit), min(limit, total - 1) + 1)
        return jnp.stack([one, total - one])
    sizes = jnp.asarray(split_up(amount, total, limit, lean), jnp.int32)
    couples = (amount - 1) // 2
    source_of, receiver = sizes[1:1 + 2 * couples:2], sizes[2:2 + 2 * couples:2]
    room = jnp.minimum(source_of - 1, limit - receiver)
    shifted = jax.random.randint(jax.random.fold_in(own_key, 1), (couples,), 0, 1 << 20) % (room + 1)
    sizes = sizes.at[1:1 + 2 * couples:2].set(source_of - shifted).at[2:2 + 2 * couples:2].set(receiver + shifted)
    return sizes[jax.random.permutation(jax.random.fold_in(own_key, 2), amount)]


def scatter_about(stream_key, extent, scale, most, pieces=(), kind=jnp.bfloat16):
    loudness = block_scale(stream_key, extent, pieces, -0.22, 0.18) if pieces else 1.0
    values = jax.random.normal(stream_key, extent, jnp.float32) * scale * loudness
    return jnp.minimum(jnp.maximum(values, -most), most).astype(kind)


def setup_inputs(seed: int = 0) -> dict:
    key_of = jax.random.split(jax.random.key(seed), 22)
    return {
        "hidden": scatter_about(key_of[0], (GROUPS, GROUP_TOK, D), 1.0, 6.0, ((0, 4), (1, 8))),
        "teacher": draw_teacher(jax.random.fold_in(key_of[21], 71), 0),
        "lengths": jax.vmap(lambda own: ragged(own, SEQS, VALID, MAXLEN, 2))(jax.random.split(key_of[2], GROUPS)).reshape((GROUPS, SEQS)).astype(jnp.int32),
        "deal": draw_deal(jax.random.fold_in(key_of[21], 71), 0),
        "w_in": draw_w_in(jax.random.fold_in(key_of[21], 71), 0),
        "b_in": scatter_about(key_of[5], (3, A), 0.5, 3.0, ((1, 4),)),
        "dw_kernel": scatter_about(key_of[6], (KW, D), (KW // 2) ** -0.5, 3.0, ((1, 4),)),
        "pw_weight": scatter_about(key_of[7], (D, A), D ** -0.5, 0.21875, ((0, 4),)),
        "pw_bias": scatter_about(key_of[8], (A,), 0.5, 3.0, ((0, 4),)),
        "kern_weight": scatter_about(key_of[9], (A, H * KW), A ** -0.5, 0.3125, ((0, 4),)),
        "kern_bias": scatter_about(key_of[10], (H * KW,), 0.5, 3.0),
        "out_weight": scatter_about(key_of[11], (D, D), (D // 8) ** -0.5, 0.625, ((0, 4),)),
        "out_bias": scatter_about(key_of[12], (D,), 0.5, 3.0, ((0, 4),)),
        "norm1_gain": jnp.clip(1.0 + 0.1 * jax.random.normal(key_of[13], (D,), jnp.float32), 0.5, 1.5).astype(jnp.bfloat16),
        "norm1_bias": scatter_about(key_of[14], (D,), 0.5, 3.0, ((0, 4),)),
        "ffn_in": scatter_about(key_of[15], (NG, D // NG, FF // NG), (D // NG) ** -0.5, 0.3125, ((1, 4),)),
        "ffn_in_bias": scatter_about(key_of[16], (FF,), 0.5, 3.0, ((0, 4),)),
        "ffn_out": scatter_about(key_of[17], (NG, FF // NG, D // NG), (FF // 4) ** -0.5, 0.21875, ((1, 4),)),
        "ffn_out_bias": scatter_about(key_of[18], (D,), 0.5, 3.0, ((0, 4),)),
        "norm2_gain": jnp.clip(1.0 + 0.1 * jax.random.normal(key_of[19], (D,), jnp.float32), 0.5, 1.5).astype(jnp.bfloat16),
        "norm2_bias": scatter_about(key_of[20], (D,), 0.5, 3.0, ((0, 4),)),
    }


@jax.custom_vjp
def low(v):
    return lax.optimization_barrier(v.astype(jnp.bfloat16)).astype(jnp.float32)

@jax.custom_vjp
def low_back(v):
    return v

def low_keep(v):
    return (low(v), None)

def low_pass(kept, grad):
    return (grad,)

def back_keep(v):
    return (v, None)

def back_low(kept, grad):
    return (low(grad),)
low.defvjp(low_keep, low_pass)
low_back.defvjp(back_keep, back_low)
NORM_EPS = 1e-12
MASKED = -1e+30
HIGH = lax.Precision.HIGHEST

def rounded(value):
    return low(low_back(value))

def product(left, right):
    return jnp.dot(left, right, precision=HIGH)

def layer_norm(rows, gain, bias):
    centered = rows - lax.optimization_barrier(jnp.mean(rows, axis=1, keepdims=True))
    inverse = lax.rsqrt(lax.optimization_barrier(jnp.mean(centered * centered, axis=1, keepdims=True)) + NORM_EPS)
    return centered * inverse * gain + bias

def segments_of(lengths):
    ends = jnp.cumsum(lengths, axis=1, dtype=jnp.int32)
    position = jnp.arange(GROUP_TOK, dtype=jnp.int32)
    return lax.optimization_barrier(jnp.sum((position[None, :, None] >= ends[:, None, :]).astype(jnp.int32), axis=2, dtype=jnp.int32))

def forward(dealt_tokens, w_in, b_in, dw_kernel, pw_weight, pw_bias, kern_weight, kern_bias, out_weight, out_bias, norm1_gain, norm1_bias, ffn_in, ffn_in_bias, ffn_out, ffn_out_bias, norm2_gain, norm2_bias, target, segment, inverse, deal):
    tokens = jnp.take_along_axis(dealt_tokens, inverse[:, :, None], axis=1)
    groups = tokens.shape[0]
    count = tokens.shape[1]
    half = KW // 2
    flat = tokens.reshape(groups * count, D)
    mixed = product(flat, w_in[:, :3 * A])
    query = rounded(mixed[:, :A] + b_in[0])
    keys = rounded(mixed[:, A:2 * A])
    values = rounded(mixed[:, 2 * A:] + b_in[1])
    conv_value = low_back(product(flat, w_in[:, 3 * A:]) + b_in[2]).reshape(groups, count, A)
    padded_seg = jnp.pad(segment, ((0, 0), (half, half)), constant_values=-1)
    padded_tok = jnp.pad(tokens, ((0, 0), (half, half), (0, 0)))
    padded_val = jnp.pad(conv_value, ((0, 0), (half, half), (0, 0)))
    near = [(padded_seg[:, tap:tap + count] == segment).astype(jnp.float32)[:, :, None] for tap in range(KW)]
    spread = sum((dw_kernel[tap] * near[tap] * padded_tok[:, tap:tap + count] for tap in range(KW)))
    spread = low(spread).reshape(groups * count, D)
    key_conv = low_back(product(spread, pw_weight) + pw_bias)
    conv_query = low(key_conv * query)
    logits = low_back(product(conv_query, kern_weight) + kern_bias)
    kernel = jax.nn.softmax(logits.reshape(groups, count, H, KW), axis=-1)
    value_taps = padded_val.reshape(groups, count + 2 * half, H, HD)
    conv_out = sum((kernel[..., tap:tap + 1] * near[tap][..., None] * value_taps[:, tap:tap + count] for tap in range(KW))).reshape(groups * count, A)
    block = math.gcd(count, 512)
    per_group = count // block
    query_blocks = query.reshape(groups * per_group, block, H, HD)
    seg_blocks = segment.reshape(groups * per_group, block)
    owner = jnp.repeat(jnp.arange(groups, dtype=jnp.int32), per_group)
    key_heads = keys.reshape(groups, count, H, HD)
    value_heads = values.reshape(groups, count, H, HD)
    scale = HD ** (-0.5)

    def attend(item):
        block_query, block_seg, index = item
        group_keys = key_heads[index]
        group_values = value_heads[index]
        group_seg = segment[index]
        scores = low_back(jnp.einsum('qhd,khd->hqk', block_query, group_keys, precision=HIGH) * scale)
        allowed = (block_seg[:, None] == group_seg[None, :])[None]
        scores = jnp.where(allowed, scores, MASKED)
        weights = low(jax.nn.softmax(scores, axis=-1))
        return jnp.einsum('hqk,khd->qhd', weights, group_values, precision=HIGH)
    attn_out = lax.map(jax.checkpoint(attend), (query_blocks, seg_blocks, owner)).reshape(groups * count, A)
    context = rounded(jnp.concatenate([attn_out, conv_out], axis=1))
    proj = low_back(product(context, out_weight) + out_bias)
    after_one = layer_norm(flat + proj, norm1_gain, norm1_bias)
    after_low = low(after_one).reshape(groups * count, NG, D // NG)
    pre_act = jnp.einsum('tgi,gio->tgo', after_low, ffn_in, precision=HIGH).reshape(groups * count, FF)
    pre_act = low_back(pre_act + ffn_in_bias)
    activated = low(jax.nn.gelu(pre_act, approximate=False)).reshape(groups * count, NG, FF // NG)
    ffn_result = jnp.einsum('tgi,gio->tgo', activated, ffn_out, precision=HIGH).reshape(groups * count, D)
    ffn_result = low_back(ffn_result + ffn_out_bias)
    result = layer_norm(after_one + ffn_result, norm2_gain, norm2_bias)
    valid = (segment < SEQS).astype(jnp.float32).reshape(groups * count, 1)
    natural_target = jnp.take_along_axis(target, inverse[:, :, None], axis=1)
    error = (result - natural_target.reshape(groups * count, D)) * valid
    dealt_result = jnp.take_along_axis(result.reshape(groups, count, D), deal[:, :, None], axis=1)
    return (dealt_result, jnp.sum(error * error))

def reference(hidden, teacher, lengths, deal, w_in, b_in, dw_kernel, pw_weight, pw_bias, kern_weight, kern_bias, out_weight, out_bias, norm1_gain, norm1_bias, ffn_in, ffn_in_bias, ffn_out, ffn_out_bias, norm2_gain, norm2_bias):
    segment = segments_of(lengths)
    inverse = jnp.argsort(deal, axis=1).astype(jnp.int32)
    total = jnp.sum(lengths).astype(jnp.float32)
    inputs = (hidden, w_in, b_in, dw_kernel, pw_weight, pw_bias, kern_weight, kern_bias, out_weight, out_bias, norm1_gain, norm1_bias, ffn_in, ffn_in_bias, ffn_out, ffn_out_bias, norm2_gain, norm2_bias)
    inputs = tuple((item.astype(jnp.float32) for item in inputs))
    target = teacher.astype(jnp.float32)

    def run(*params):
        return forward(*params, target, segment, inverse, deal)
    (result, squares), pull = jax.vjp(run, *inputs)
    grads = pull((jnp.zeros_like(result), jnp.full((), 0.5, squares.dtype)))
    loss = squares / (total * D)
    return (result.astype(jnp.bfloat16), loss, grads[0], grads[1], grads[2], grads[3], grads[4], grads[5], grads[6], grads[7], grads[8], grads[9], grads[10], grads[11], grads[12], grads[13], grads[14], grads[15], grads[16], grads[17])
```

```python
import functools

import jax
import jax.numpy as jnp
from jax import lax
from jax.experimental import pallas as pl
from jax.experimental.pallas import tpu as pltpu
from jax.sharding import PartitionSpec as P

D = 768
H = 6
HD = 64
FF = 3072
NG = 2
KW = 9
SEQS = 6
A = 384

NORM_EPS = 1e-12
MASKED = -1e30
ROOT_HALF = 0.7071067811865476
DENSITY_NORM = 0.3989422804014327
RIM = 16
MESH = pl.DeviceIdType.MESH
BF16 = jnp.bfloat16
F32 = jnp.float32
VMEM_LIMIT = 60 * 1024 * 1024


def remote(src, dst, send, recv, target):
    return pltpu.make_async_remote_copy(
        src_ref=src,
        dst_ref=dst,
        send_sem=send,
        recv_sem=recv,
        device_id=target,
        device_id_type=MESH,
    )


def greet(peers):
    barrier = pltpu.get_barrier_semaphore()
    total = 0
    for there, target in peers:

        @pl.when(there)
        def _(target=target):
            pl.semaphore_signal(barrier, inc=1, device_id=target, device_id_type=MESH)

        total = total + jnp.where(there, 1, 0)
    pl.semaphore_wait(barrier, total)


class Place:
    def __init__(self, count):
        self.count = count
        self.length = count // 2
        self.valid = count - count // 8
        self.window = count // 2
        self.me = lax.axis_index("ctx")
        self.line = lax.div(self.me, 2)
        self.side = lax.rem(self.me, 2)
        self.mate_index = self.me + 1 - 2 * self.side
        self.mate = {"ctx": self.mate_index}
        self.up = {"ctx": lax.rem(self.me + 2, count)}
        self.down = {"ctx": lax.rem(self.me + count - 2, count)}
        self.has_up = self.line < self.length - 1
        self.has_down = self.line > 0

    def others(self):
        return [
            (self.me >= 0, {"ctx": lax.rem(self.me + shift, self.count)}) for shift in range(1, self.count)
        ]


class PieceNeeds:
    def __init__(self, place, first, last):
        self.place, self.first, self.last = place, first, last

    def at(self, index, source):
        p = self.place
        return (
            (index < p.valid)
            & (self.first <= index + p.window)
            & (self.last >= index - p.window)
        )

    def above(self, line, source):
        p = self.place
        return (2 * line < p.valid) & (self.last >= 2 * line - p.window)

    def below(self, line, source):
        return self.first <= 2 * line + 1 + self.place.window

    def sent(self, source):
        return source >= 0


class BlockNeeds:
    def __init__(self, place):
        self.place = place

    def at(self, index, source):
        p = self.place
        near = (index <= source + p.window) & (index >= source - p.window)
        return near & (index < p.valid) & (source < p.valid)

    def above(self, line, source):
        p = self.place
        return (2 * line < p.valid) & (2 * line <= source + p.window) & (source < p.valid)

    def below(self, line, source):
        p = self.place
        return (2 * line + 1 >= source - p.window) & (source < p.valid)

    def sent(self, source):
        return source < self.place.valid


class Part:
    def __init__(self, place, needs, own, slot, send, recv):
        self.place, self.needs, self.own, self.slot = place, needs, own, slot
        self.send, self.recv = send, recv

    def copy(self, src, source, send, recv, target):
        return remote(src, self.slot(source), self.send.at[send], self.recv.at[recv], target)

    def go_up(self, source):
        p = self.place
        return p.has_up & self.needs.above(p.line + 1, source)

    def go_down(self, source):
        p = self.place
        return p.has_down & self.needs.below(p.line - 1, source)

    def from_below(self, s, source):
        p = self.place
        return (p.line - s >= 0) & self.needs.above(p.line, source)

    def from_above(self, s, source):
        p = self.place
        return (p.line + s < p.length) & self.needs.below(p.line, source)


class LinePart(Part):
    def start(self):
        p = self.place

        @pl.when(self.needs.at(p.mate_index, p.me))
        def _():
            self.copy(self.own, p.me, (2, 0), (2, 0), p.mate).start()

        @pl.when(self.go_up(p.me))
        def _():
            self.copy(self.own, p.me, (0, 0), (0, 1), p.up).start()

        @pl.when(self.go_down(p.me))
        def _():
            self.copy(self.own, p.me, (1, 0), (1, 1), p.down).start()

    def step(self, s):
        p = self.place
        for row, source, there, go, target in (
            (0, p.me - 2 * s, self.from_below, self.go_up, p.up),
            (1, p.me + 2 * s, self.from_above, self.go_down, p.down),
        ):

            @pl.when(there(s, source))
            def _(row=row, source=source, go=go, target=target):
                held = self.slot(source)
                self.copy(held, source, (2 + row, s), (row, s), p.mate).wait_recv()

                @pl.when(go(source))
                def _():
                    self.copy(held, source, (row, s), (row, s + 1), target).start()

                @pl.when(self.needs.at(p.mate_index, source))
                def _():
                    self.copy(held, source, (2 + row, s), (2 + row, s), p.mate).start()

    def finish(self):
        p = self.place
        for s in range(p.length):
            for row, source, exists, go, target in (
                (0, p.me - 2 * s, p.line - s >= 0, self.go_up, p.up),
                (1, p.me + 2 * s, p.line + s < p.length, self.go_down, p.down),
            ):
                held = self.slot(source)
                mates = source + 1 - 2 * p.side
                if s > 0 or row == 0:

                    @pl.when(exists & self.needs.at(p.me, mates))
                    def _(row=row, s=s, mates=mates):
                        theirs = self.slot(mates)
                        self.copy(theirs, mates, (2 + row, s), (2 + row, s), p.mate).wait_recv()

                    @pl.when(exists & self.needs.at(p.mate_index, source))
                    def _(row=row, s=s, held=held, source=source):
                        self.copy(held, source, (2 + row, s), (2 + row, s), p.mate).wait_send()

                @pl.when(exists & go(source) & ((s == 0) | self.arrived(row, source)))
                def _(row=row, s=s, held=held, source=source, target=target):
                    self.copy(held, source, (row, s), (row, s + 1), target).wait_send()

    def arrived(self, row, source):
        p = self.place
        return self.needs.above(p.line, source) if row == 0 else self.needs.below(p.line, source)


class PairPart(Part):
    def across(self):
        p = self.place

        @pl.when(self.needs.sent(p.me))
        def _():
            self.copy(self.own, p.me, (4, 0), (4, 0), p.mate).start()

    def along(self):
        p = self.place

        @pl.when(self.go_up(p.me))
        def _():
            self.copy(self.own, p.me, (0, 0), (0, 1), p.up).start()

        @pl.when(self.go_down(p.me))
        def _():
            self.copy(self.own, p.me, (1, 0), (1, 1), p.down).start()

    def middle(self):
        p = self.place
        source = p.mate_index
        held = self.slot(source)

        @pl.when(self.needs.sent(source))
        def _():
            self.copy(held, source, (4, 0), (4, 0), p.mate).wait_recv()

        @pl.when(self.go_up(source))
        def _():
            self.copy(held, source, (2, 0), (2, 1), p.up).start()

        @pl.when(self.go_down(source))
        def _():
            self.copy(held, source, (3, 0), (3, 1), p.down).start()

    def step(self, s):
        p = self.place
        for base, column in ((0, p.me), (2, p.mate_index)):
            for row, source, there, go, target in (
                (0, column - 2 * s, self.from_below, self.go_up, p.up),
                (1, column + 2 * s, self.from_above, self.go_down, p.down),
            ):

                @pl.when(there(s, source))
                def _(row=row + base, source=source, go=go, target=target):
                    held = self.slot(source)
                    self.copy(held, source, (row, s), (row, s), p.mate).wait_recv()

                    @pl.when(go(source))
                    def _():
                        self.copy(held, source, (row, s), (row, s + 1), target).start()

    def finish(self):
        p = self.place

        @pl.when(self.needs.sent(p.me))
        def _():
            self.copy(self.own, p.me, (4, 0), (4, 0), p.mate).wait_send()

        for s in range(p.length):
            for base, column in ((0, p.me), (2, p.mate_index)):
                for row, source, there, go, target in (
                    (0, column - 2 * s, self.from_below, self.go_up, p.up),
                    (1, column + 2 * s, self.from_above, self.go_down, p.down),
                ):
                    passed = there(s, source) if s > 0 else p.me >= 0

                    @pl.when(passed & go(source))
                    def _(row=row + base, s=s, source=source, target=target):
                        held = self.slot(source)
                        self.copy(held, source, (row, s), (row, s + 1), target).wait_send()


class Swap:
    def __init__(self, place, src, dst, send, recv):
        self.place, self.src, self.dst, self.send, self.recv = place, src, dst, send, recv

    def copy(self, shift):
        p = self.place
        there = lax.rem(p.me + shift, p.count)
        return remote(
            self.src.at[there], self.dst.at[p.me], self.send.at[shift], self.recv.at[shift], {"ctx": there}
        )

    def keep(self):
        p = self.place
        return pltpu.make_async_copy(self.src.at[p.me], self.dst.at[p.me], self.send.at[0])

    def start(self):
        for shift in range(1, self.place.count):
            self.copy(shift).start()
        self.keep().start()

    def finish(self):
        p = self.place
        self.keep().wait()
        for shift in range(1, p.count):
            self.copy(shift).wait_send()
            source = lax.rem(p.me + p.count - shift, p.count)
            held = self.dst.at[source]
            remote(held, held, self.send.at[shift], self.recv.at[shift], p.mate).wait_recv()


def part_sems(length):
    return [
        pltpu.SemaphoreType.DMA((5, length + 1)),
        pltpu.SemaphoreType.DMA((5, length + 1)),
    ]


def swap_sems(count):
    return [pltpu.SemaphoreType.DMA((count,)), pltpu.SemaphoreType.DMA((count,))]


N_SMALL = 4


def gather_body(count, spans, *refs):
    n = len(spans)
    inputs, refs = refs[: n + 13], refs[n + 13 :]
    x_ref, t_ref = inputs[:2]
    shards = list(inputs[2 : 2 + n])
    dw_ref, *rows_in, fb_in, b_in, pb_in, kern_in = inputs[2 + n :]
    out_ref, target_ref = refs[:2]
    fulls = list(refs[2 : 2 + n])
    vec_ref, small_ref, fb_ref, kw_ref = refs[2 + n : 6 + n]
    scratch = refs[6 + n :]
    own_small, all_small = scratch[:N_SMALL], scratch[N_SMALL : 2 * N_SMALL]
    local_sem, w_send, w_recv, pad_send, pad_recv = scratch[2 * N_SMALL : 2 * N_SMALL + 5]
    sems = scratch[2 * N_SMALL + 5 :]
    p = Place(count)
    k = lax.axis_index("wt")
    side = lax.rem(k, 2)
    core_mate = {"wt": k + 1 - 2 * side}
    far = lax.rem(k + 2, 4)
    far_mate = {"wt": far}

    wide, narrow, ffn, kern = own_small
    wide[...] = jnp.zeros(wide.shape, F32)
    wide[0:KW, :] = dw_ref[...].astype(F32)
    for i, row in enumerate(rows_in):
        wide[KW + i : KW + i + 1, :] = row[...].astype(F32)
    narrow[...] = jnp.zeros(narrow.shape, F32)
    narrow[0:3, : A // 4] = b_in[...].astype(F32)
    narrow[3:4, : A // 4] = pb_in[...].astype(F32)
    ffn[...] = jnp.zeros(ffn.shape, F32)
    ffn[0:1, :] = fb_in[...].astype(F32)
    kern[...] = jnp.zeros(kern.shape, F32)
    kern[:, : H * KW] = kern_in[...].astype(F32)

    def span(i, ref, index):
        if i >= n:
            return ref.at[index]
        axis, size = spans[i]
        window = pl.ds(pl.multiple_of(index * size, size), size)
        return ref.at[window] if axis == 0 else ref.at[:, window]

    shards += own_small
    fulls += all_small
    total = n + N_SMALL
    order = list(range(n, total)) + list(range(n))

    greet(p.others() + [(k >= 0, core_mate), (k >= 0, far_mate)])
    quarter, eighth = count // 4, count // 8
    cuts = [0, quarter, p.valid - quarter, p.valid - eighth, p.valid]
    parts = []
    for i, kind in enumerate((LinePart, LinePart, PairPart, PairPart)):
        first, end = cuts[i], cuts[i + 1]
        parts.append(
            kind(
                p,
                PieceNeeds(p, first, end - 1),
                x_ref.at[first:end],
                lambda j, first=first, end=end: out_ref.at[first:end, j],
                sems[2 * i],
                sems[2 * i + 1],
            )
        )
    low, high, *pairs = parts
    lines = [high, low]
    for part in pairs:
        part.across()
    for part in lines:
        part.start()
    for part in pairs:
        part.along()
    for i in order:
        held = span(i, fulls[i], k)
        remote(shards[i], held, w_send.at[0, i], w_recv.at[0, i], far_mate).start()
        remote(shards[i], held, w_send.at[1, i], w_recv.at[1, i], core_mate).start()

    def pad_copy(there):
        return remote(
            x_ref.at[p.valid :],
            out_ref.at[p.valid :, p.me],
            pad_send.at[there - p.valid],
            pad_recv.at[p.me],
            {"ctx": p.me * 0 + there},
        )

    for there in range(p.valid, count):

        @pl.when(p.me != there)
        def _(there=there):
            pad_copy(there).start()

    keeps = [pltpu.make_async_copy(x_ref, out_ref.at[:, p.me], local_sem.at[total])]
    for i in range(total):
        keeps.append(pltpu.make_async_copy(shards[i], span(i, fulls[i], k), local_sem.at[i]))
    for keep in keeps:
        keep.start()
    swap = Swap(p, t_ref, target_ref, sems[8], sems[9])

    def relay(i):
        held = span(i, fulls[i], far)
        remote(held, held, w_send.at[2, i], w_recv.at[0, i], core_mate).wait_recv()
        remote(held, held, w_send.at[2, i], w_recv.at[2, i], core_mate).start()

    for part in pairs:
        part.middle()
    done = 0
    for s in range(1, p.length):
        for part in lines + pairs:
            part.step(s)
        upto = total if s == p.length - 1 else min(total, done + 3)
        if s == p.length - 1:
            swap.start()
        for i in range(done, upto):
            relay(order[i])
        done = upto
    for keep in keeps:
        keep.wait()
    for i in range(total):
        held = span(i, fulls[i], k)
        remote(shards[i], held, w_send.at[0, i], w_recv.at[0, i], far_mate).wait_send()
        remote(shards[i], held, w_send.at[1, i], w_recv.at[1, i], core_mate).wait()
        remote(held, held, w_send.at[2, i], w_recv.at[2, i], core_mate).wait()

    def spread(ref, step, shape):
        row = lax.broadcasted_iota(jnp.int32, shape, 0)
        column = lax.broadcasted_iota(jnp.int32, shape, 1)
        value = 0.0
        for index in range(4):
            move = jnp.where((column == row + step * index) & (row < step), 1.0, 0.0).astype(BF16)
            value += jnp.dot(ref[index].astype(BF16), move, preferred_element_type=F32)
        return value

    vec_ref[...] = spread(all_small[0], D // 4, (D // 4, D))
    small_ref[...] = spread(all_small[1], A // 4, (128, A))
    for index in range(4):
        fb_ref[index : index + 1, :] = all_small[2][index, 0:1, :]
        kw_ref[A // 4 * index : A // 4 * index + A // 4, :] = all_small[3][index].astype(BF16)
    for part in pairs + lines:
        part.finish()
    for there in range(p.valid, count):

        @pl.when(p.me != there)
        def _(there=there):
            pad_copy(there).wait_send()

    @pl.when(p.me >= p.valid)
    def _():
        for shift in range(1, count):
            source = lax.rem(p.me + shift, count)
            held = out_ref.at[p.valid :, source]
            remote(held, held, pad_send.at[0], pad_recv.at[source], p.mate).wait_recv()

    swap.finish()


def gather_inputs(pieces, targets, shards, axes, smalls, ctx_count):
    length = ctx_count // 2
    fulls, spans = [], []
    for shard, axis in zip(shards, axes):
        shape = list(shard.shape)
        spans.append((axis, shape[axis]))
        shape[axis] *= 4
        fulls.append(jax.ShapeDtypeStruct(tuple(shape), shard.dtype))
    n = len(shards)
    total = n + N_SMALL
    small_shapes = [(16, D // 4), (8, 128), (8, D), (A // 4, 128)]
    vmem = pl.BlockSpec(memory_space=pltpu.VMEM)
    hbm = pl.BlockSpec(memory_space=pl.ANY)
    results = pl.pallas_call(
        functools.partial(gather_body, ctx_count, spans),
        out_shape=[
            jax.ShapeDtypeStruct((ctx_count,) + pieces.shape, pieces.dtype),
            jax.ShapeDtypeStruct(targets.shape, targets.dtype),
        ]
        + fulls
        + [
            jax.ShapeDtypeStruct((16, D), F32),
            jax.ShapeDtypeStruct((8, A), F32),
            jax.ShapeDtypeStruct((4, D), F32),
            jax.ShapeDtypeStruct((A, 128), BF16),
        ],
        in_specs=[vmem] * (2 + n + len(smalls)),
        out_specs=[hbm] * (2 + n) + [vmem] * 4,
        scratch_shapes=[pltpu.VMEM(shape, F32) for shape in small_shapes]
        + [pltpu.VMEM((4,) + shape, F32) for shape in small_shapes]
        + [
            pltpu.SemaphoreType.DMA((total + 1,)),
            pltpu.SemaphoreType.DMA((3, total)),
            pltpu.SemaphoreType.DMA((3, total)),
            pltpu.SemaphoreType.DMA((ctx_count // 8,)),
            pltpu.SemaphoreType.DMA((ctx_count,)),
        ]
        + part_sems(length) * 4
        + swap_sems(ctx_count),
        compiler_params=pltpu.CompilerParams(
            collective_id=0, has_side_effects=True, vmem_limit_bytes=VMEM_LIMIT
        ),
        name="gather_inputs",
    )(pieces, targets, *shards, *smalls)
    return results


def grads_gather_body(
    count, g_ref, stat_ref, res_ref, out_ref, edge_ref, all_ref, dealt_ref, local_sem, edge_send, edge_recv, *sems
):
    p = Place(count)
    rows = g_ref.shape[0]
    early = rows - 3 * rows // 8
    low = {"ctx": lax.rem(p.me + count - 1, count)}
    high = {"ctx": lax.rem(p.me + 1, count)}
    has_low, has_high = p.me > 0, p.me < count - 1
    greet(p.others())
    needs = BlockNeeds(p)
    pair = PairPart(p, needs, g_ref.at[early:, :A], lambda j: out_ref.at[j, early:], sems[0], sems[1])
    line = LinePart(p, needs, g_ref.at[:early, :A], lambda j: out_ref.at[j, :early], sems[2], sems[3])
    stats = LinePart(p, needs, stat_ref, lambda j: all_ref.at[j], sems[4], sems[5])
    swap = Swap(p, res_ref, dealt_ref, sems[6], sems[7])

    def to_low():
        return remote(g_ref.at[:RIM, A:], edge_ref.at[1], edge_send.at[0], edge_recv.at[1], low)

    def to_high():
        return remote(g_ref.at[rows - RIM :, A:], edge_ref.at[0], edge_send.at[1], edge_recv.at[0], high)

    @pl.when(has_low)
    def _():
        to_low().start()

    @pl.when(has_high)
    def _():
        to_high().start()

    parts = [stats, line, pair]
    stats.start()
    pair.across()
    line.start()
    pair.along()
    keeps = [
        pltpu.make_async_copy(g_ref.at[:, :A], out_ref.at[p.me], local_sem.at[0]),
        pltpu.make_async_copy(stat_ref, all_ref.at[p.me], local_sem.at[1]),
    ]
    for keep in keeps:
        keep.start()
    pair.middle()
    for s in range(1, p.length):
        if s == p.length - 1:
            swap.start()
        for part in parts:
            part.step(s)
    for keep in keeps:
        keep.wait()

    @pl.when(has_low)
    def _():
        to_low().wait_send()
        to_high().wait_recv()

    @pl.when(has_high)
    def _():
        to_high().wait_send()
        to_low().wait_recv()

    for part in parts:
        part.finish()
    swap.finish()


def gather_grads(grads, stats, results, ctx_count):
    length = ctx_count // 2
    rows = grads.shape[0]
    vmem = pl.BlockSpec(memory_space=pltpu.VMEM)
    return pl.pallas_call(
        functools.partial(grads_gather_body, ctx_count),
        out_shape=[
            jax.ShapeDtypeStruct((ctx_count, rows, A), grads.dtype),
            jax.ShapeDtypeStruct((2, RIM, A), grads.dtype),
            jax.ShapeDtypeStruct((ctx_count,) + stats.shape, stats.dtype),
            jax.ShapeDtypeStruct(results.shape, results.dtype),
        ],
        in_specs=[vmem] * 3,
        out_specs=[pl.BlockSpec(memory_space=pl.ANY)] * 4,
        scratch_shapes=[
            pltpu.SemaphoreType.DMA((2,)),
            pltpu.SemaphoreType.DMA((2,)),
            pltpu.SemaphoreType.DMA((2,)),
        ]
        + part_sems(length) * 3
        + swap_sems(ctx_count),
        compiler_params=pltpu.CompilerParams(
            collective_id=1, has_side_effects=True, vmem_limit_bytes=VMEM_LIMIT
        ),
        name="gather_grads",
    )(grads, stats, results)


def reduce_body(bits, shapes, *refs):
    n = len(shapes)
    stages = 2 + bits
    g_refs, f_ref, tok_ref = refs[:n], refs[n], refs[n + 1]
    out_refs, sum_ref, dealt_ref = refs[n + 2 : 2 * n + 2], refs[2 * n + 2], refs[2 * n + 3]
    scratch = refs[2 * n + 4 :]
    bufs = [scratch[stages * i : stages * i + stages] for i in range(n)]
    f_bufs, send, recv, f_send, f_recv, swap_send, swap_recv = scratch[stages * n :]
    p = Place(1 << bits)
    k = lax.axis_index("wt")
    me = lax.axis_index("ctx")
    core = lax.rem(k, 2)
    far = lax.div(k, 2)
    bit = [lax.rem(lax.div(me, 1 << b), 2) for b in range(bits)]
    targets = [{"wt": k + 1 - 2 * core}, {"wt": lax.rem(k + 2, 4)}]
    for b in range(bits):
        targets.append({"ctx": me + (1 << b) * (1 - 2 * bit[b])})
    greet(p.others() + [(k >= 0, target) for target in targets[:2]])
    swap = Swap(p, tok_ref, dealt_ref, swap_send, swap_recv)
    whole = slice(None)
    items = [(i, c) for i in range(n) for c in range(shapes[i][0])]

    def source(stage, item, kept):
        i, c = items[item]

        def pick(value):
            return value if kept else 1 - value

        if stage == 0:
            return g_refs[i].at[(whole, pick(core)) + (whole,) * bits + (c,)]
        if stage == 1:
            return bufs[i][0].at[c, pick(far)]
        b = stage - 2
        return bufs[i][stage - 1].at[(c,) + (whole,) * (bits - b - 1) + (pick(bit[b]),)]

    def spread(b, item, other):
        i, c = items[item]
        index = [bit[j] for j in range(b, -1, -1)]
        if other:
            index[0] = 1 - index[0]
        return out_refs[i].at[(whole,) * (bits - 1 - b) + tuple(index) + (c,)]

    def copy(stage, item):
        i, c = items[item]
        if stage < stages:
            src, dst, target = source(stage, item, False), bufs[i][stage].at[c], targets[stage]
        else:
            b = bits - 1 - (stage - stages)
            src, dst, target = spread(b, item, False), spread(b, item, False), targets[2 + b]
        return remote(src, dst, send.at[stage, item], recv.at[stage, item], target)

    def add(stage, item):
        i, c = items[item]
        mine, sums = source(stage, item, True), bufs[i][stage].at[c]
        lead = sums.shape[:-2]
        total = 1
        for size in lead:
            total *= size

        def one(at, _):
            index, rest = [], at
            for size in reversed(lead):
                index.append(lax.rem(rest, size))
                rest = lax.div(rest, size)
            index = tuple(reversed(index))
            value = mine[index].astype(F32) + sums[index].astype(F32)
            sums[index] = value.astype(BF16)
            return 0

        if lead:
            lax.fori_loop(0, total, one, 0)
        else:
            sums[...] = (mine[...].astype(F32) + sums[...].astype(F32)).astype(BF16)

    def f_copy(stage):
        return remote(
            f_bufs.at[0, stage], f_bufs.at[1, stage], f_send.at[stage], f_recv.at[stage], targets[stage]
        )

    last = stages + bits
    f_bufs[0, 0] = f_ref[...]
    f_copy(0).start()
    for item in range(len(items)):
        copy(0, item).start()
    swap.start()
    for t in range(1, len(items) + last):
        for item in range(len(items)):
            stage = t - item
            if not 1 <= stage <= last:
                continue
            before = stage - 1
            i, c = items[item]
            if before < stages:
                copy(before, item).wait_recv()
                add(before, item)
                if stage == stages:
                    out_refs[i][tuple(bit[j] for j in range(bits - 1, -1, -1)) + (c,)] = bufs[i][before][c]
            else:
                b = bits - 1 - (before - stages)
                held = spread(b, item, True)
                remote(held, held, send.at[before, item], recv.at[before, item], targets[2 + b]).wait_recv()
            if stage < last:
                copy(stage, item).start()
        if t <= stages:
            f_copy(t - 1).wait_recv()
            value = f_bufs[0, t - 1] + f_bufs[1, t - 1]
            if t < stages:
                f_bufs[0, t] = value
                f_copy(t).start()
            else:
                sum_ref[...] = value
    for stage in range(last):
        for item in range(len(items)):
            copy(stage, item).wait_send()
    for stage in range(stages):
        f_copy(stage).wait_send()
    swap.finish()


def reduce_grads(packs, vectors, tokens, ctx_count, size):
    bits = ctx_count.bit_length() - 1
    stages = 2 + bits
    twos = (2,) * bits
    shapes, outs, bufs, args = [], [], [], []
    for pack in packs:
        rows = pack.shape[1]
        piece = min(size, rows // ctx_count)
        chunks = rows // ctx_count // piece
        shapes.append((chunks, piece))
        outs.append(jax.ShapeDtypeStruct(twos + (chunks, piece, D), BF16))
        args.append(pack.reshape((2, 2) + twos + (chunks, piece, D)))
        bufs.append(pltpu.VMEM((chunks, 2) + twos + (piece, D), BF16))
        bufs.append(pltpu.VMEM((chunks,) + twos + (piece, D), BF16))
        for b in range(bits):
            bufs.append(pltpu.VMEM((chunks,) + twos[b + 1 :] + (piece, D), BF16))
    items = sum(chunks for chunks, _ in shapes)
    vmem = pl.BlockSpec(memory_space=pltpu.VMEM)
    results = pl.pallas_call(
        functools.partial(reduce_body, bits, shapes),
        out_shape=outs
        + [jax.ShapeDtypeStruct(vectors.shape, F32), jax.ShapeDtypeStruct(tokens.shape, BF16)],
        in_specs=[vmem] * (len(packs) + 2),
        out_specs=[vmem] * (len(packs) + 2),
        scratch_shapes=bufs
        + [
            pltpu.VMEM((2, stages) + vectors.shape, F32),
            pltpu.SemaphoreType.DMA((stages + bits, items)),
            pltpu.SemaphoreType.DMA((stages + bits, items)),
            pltpu.SemaphoreType.DMA((stages,)),
            pltpu.SemaphoreType.DMA((stages,)),
        ]
        + swap_sems(ctx_count),
        compiler_params=pltpu.CompilerParams(
            collective_id=2, has_side_effects=True, vmem_limit_bytes=VMEM_LIMIT
        ),
        name="reduce_grads",
    )(*args, vectors, tokens)
    return [out.reshape(-1, D) for out in results[:-2]], results[-2], results[-1]


def seg_of(position, bounds):
    seg = jnp.zeros(position.shape, jnp.int32)
    for i in range(SEQS):
        seg = seg + jnp.where(position >= bounds[i], 1, 0)
    return seg


def reach(bounds, first, last, group_rows):
    begin, end = jnp.int32(0), jnp.int32(group_rows)
    for i in range(SEQS):
        begin = jnp.where(bounds[i] <= first, bounds[i], begin)
    for i in reversed(range(SEQS)):
        end = jnp.where(bounds[i] > last, bounds[i], end)
    return begin, end


def half_masks(rows):
    lane = lax.broadcasted_iota(jnp.int32, (rows, 128), 1)
    low = jnp.where(lane < HD, 1.0, 0.0).astype(BF16)
    return low, (1.0 - low.astype(F32)).astype(BF16)


def dot_last(left, right):
    return lax.dot_general(left, right, (((1,), (1,)), ((), ())), preferred_element_type=F32)


def attend_body(tq, tk, bounds, q_ref, k_ref, v_ref, out_ref, lse_ref, m_ref, acc_ref):
    rows, group_rows = out_ref.shape[0], k_ref.shape[0]
    base = pl.multiple_of(bounds[SEQS], tq)
    q_masks, k_masks = half_masks(tq), half_masks(tk)
    lane = lax.broadcasted_iota(jnp.int32, (tq, 128), 1)
    low = lane < HD

    def tile(qi, _):
        q0 = pl.multiple_of(qi * tq, tq)
        first = pl.multiple_of(base + q0, tq)
        begin, end = reach(bounds, first, first + tq - 1, group_rows)
        q_seg = seg_of(first + lax.broadcasted_iota(jnp.int32, (tq, 1), 0), bounds)
        m_ref[...] = jnp.full(m_ref.shape, MASKED, F32)
        acc_ref[...] = jnp.zeros(acc_ref.shape, F32)

        def step(kt, _):
            k0 = pl.multiple_of(kt * tk, tk)
            k_seg = seg_of(k0 + lax.broadcasted_iota(jnp.int32, (1, tk), 1), bounds)
            bias = jnp.where(q_seg == k_seg, 0.0, MASKED)
            for pair in range(H // 2):
                cols = slice(128 * pair, 128 * pair + 128)
                q_pair = q_ref[pl.ds(first, tq), cols]
                k_pair = k_ref[pl.ds(k0, tk), cols]
                v_pair = v_ref[pl.ds(k0, tk), cols]
                for side in range(2):
                    head = 2 * pair + side
                    scores = dot_last(q_pair * q_masks[side], k_pair) + bias
                    old = m_ref[head]
                    new = jnp.maximum(old, jnp.max(scores, axis=1, keepdims=True))
                    weights = jnp.exp(scores - jnp.tile(new, (1, tk // 128)))
                    v_ones = v_pair * k_masks[side] + k_masks[1 - side]
                    acc_ref[head] = acc_ref[head] * jnp.exp(old - new) + jnp.dot(
                        weights.astype(BF16), v_ones, preferred_element_type=F32
                    )
                    m_ref[head] = new
            return 0

        lax.fori_loop(lax.div(begin, tk), lax.div(end + tk - 1, tk), step, 0)
        lse = jnp.zeros((tq, 128), F32)
        for pair in range(H // 2):
            left, right = acc_ref[2 * pair], acc_ref[2 * pair + 1]
            crossed = jnp.where(low, right, left)
            total = pltpu.roll(crossed, HD, 1)
            out_ref[pl.ds(q0, tq), 128 * pair : 128 * pair + 128] = jnp.where(low, left, right) / total
            lse = jnp.where(lane == 2 * pair, m_ref[2 * pair] + jnp.log(total), lse)
            lse = jnp.where(lane == 2 * pair + 1, m_ref[2 * pair + 1] + jnp.log(crossed), lse)
        lse_ref[pl.ds(q0, tq), :] = lse
        return 0

    lax.fori_loop(0, rows // tq, tile, 0)


def attend(bounds, query, keys, values, rows):
    tq, tk = min(256, rows), 512
    return pl.pallas_call(
        functools.partial(attend_body, tq, tk),
        out_shape=[
            jax.ShapeDtypeStruct((rows, A), F32),
            jax.ShapeDtypeStruct((rows, 128), F32),
        ],
        in_specs=[pl.BlockSpec(memory_space=pltpu.SMEM)]
        + [pl.BlockSpec(memory_space=pltpu.VMEM)] * 3,
        out_specs=[pl.BlockSpec(memory_space=pltpu.VMEM)] * 2,
        scratch_shapes=[pltpu.VMEM((H, tq, 128), F32), pltpu.VMEM((H, tq, 128), F32)],
        compiler_params=pltpu.CompilerParams(vmem_limit_bytes=VMEM_LIMIT),
        name="attend",
    )(bounds, query, keys, values)


def query_grads_body(tq, tk, bounds, q_ref, g_ref, stat_ref, k_ref, v_ref, out_ref, rep_ref):
    rows, group_rows = out_ref.shape[0], k_ref.shape[0]
    base = pl.multiple_of(bounds[SEQS], tq)
    q_masks, k_masks = half_masks(tq), half_masks(tk)

    def tile(qi, _):
        q0 = pl.multiple_of(qi * tq, tq)
        first = pl.multiple_of(base + q0, tq)
        begin, end = reach(bounds, first, first + tq - 1, group_rows)
        q_seg = seg_of(first + lax.broadcasted_iota(jnp.int32, (tq, 1), 0), bounds)
        stat = stat_ref[pl.ds(q0, tq), :]
        for head in range(H):
            rep_ref[head] = jnp.broadcast_to(stat[:, head : head + 1], (tq, 128))
            rep_ref[H + head] = jnp.broadcast_to(stat[:, 8 + head : 9 + head], (tq, 128))
        out_ref[pl.ds(q0, tq), :] = jnp.zeros((tq, A), F32)

        def step(kt, _):
            k0 = pl.multiple_of(kt * tk, tk)
            k_seg = seg_of(k0 + lax.broadcasted_iota(jnp.int32, (1, tk), 1), bounds)
            bias = jnp.where(q_seg == k_seg, 0.0, MASKED)
            for pair in range(H // 2):
                cols = slice(128 * pair, 128 * pair + 128)
                q_pair = q_ref[pl.ds(first, tq), cols]
                g_pair = g_ref[pl.ds(q0, tq), cols]
                k_pair = k_ref[pl.ds(k0, tk), cols]
                v_pair = v_ref[pl.ds(k0, tk), cols]
                total = jnp.zeros((tq, 128), F32)
                for side in range(2):
                    head = 2 * pair + side
                    scores = dot_last(q_pair * q_masks[side], k_pair) + bias
                    prob = jnp.exp(scores - jnp.tile(rep_ref[head], (1, tk // 128)))
                    back = dot_last(g_pair * q_masks[side], v_pair)
                    back = prob * (back - jnp.tile(rep_ref[H + head], (1, tk // 128)))
                    total = total + jnp.dot(
                        back.astype(BF16), k_pair * k_masks[side], preferred_element_type=F32
                    )
                out_ref[pl.ds(q0, tq), cols] += total
            return 0

        lax.fori_loop(lax.div(begin, tk), lax.div(end + tk - 1, tk), step, 0)
        return 0

    lax.fori_loop(0, rows // tq, tile, 0)


def query_grads(bounds, query, grads, stats, keys, values):
    rows = grads.shape[0]
    tq, tk = min(256, rows), 512
    return pl.pallas_call(
        functools.partial(query_grads_body, tq, tk),
        out_shape=jax.ShapeDtypeStruct((rows, A), F32),
        in_specs=[pl.BlockSpec(memory_space=pltpu.SMEM)]
        + [pl.BlockSpec(memory_space=pltpu.VMEM)] * 5,
        out_specs=pl.BlockSpec(memory_space=pltpu.VMEM),
        scratch_shapes=[pltpu.VMEM((2 * H, tq, 128), F32)],
        compiler_params=pltpu.CompilerParams(vmem_limit_bytes=VMEM_LIMIT),
        name="query_grads",
    )(bounds, query, grads, stats, keys, values)


def key_grads_body(tk, bounds, k_ref, v_ref, q_ref, g_ref, stat_ref, dk_ref, dv_ref):
    rows, group_rows = dk_ref.shape[0], q_ref.shape[0]
    tq = stat_ref.shape[2]
    base = pl.multiple_of(bounds[SEQS], tk)
    q_masks, k_masks = half_masks(tq), half_masks(tk)

    def tile(ki, _):
        k0 = pl.multiple_of(ki * tk, tk)
        first = pl.multiple_of(base + k0, tk)
        begin, end = reach(bounds, first, first + tk - 1, group_rows)
        k_seg = seg_of(first + lax.broadcasted_iota(jnp.int32, (tk, 1), 0), bounds)
        dk_ref[pl.ds(k0, tk), :] = jnp.zeros((tk, A), F32)
        dv_ref[pl.ds(k0, tk), :] = jnp.zeros((tk, A), F32)

        def step(qt, _):
            q0 = pl.multiple_of(qt * tq, tq)
            q_seg = seg_of(q0 + lax.broadcasted_iota(jnp.int32, (1, tq), 1), bounds)
            bias = jnp.where(k_seg == q_seg, 0.0, MASKED)
            for pair in range(H // 2):
                cols = slice(128 * pair, 128 * pair + 128)
                q_pair = q_ref[pl.ds(q0, tq), cols]
                g_pair = g_ref[pl.ds(q0, tq), cols]
                k_pair = k_ref[pl.ds(first, tk), cols]
                v_pair = v_ref[pl.ds(first, tk), cols]
                key_sum = jnp.zeros((tk, 128), F32)
                value_sum = jnp.zeros((tk, 128), F32)
                for side in range(2):
                    head = 2 * pair + side
                    scores = dot_last(k_pair * k_masks[side], q_pair) + bias
                    prob = jnp.exp(scores - stat_ref[qt, head : head + 1, :])
                    value_sum = value_sum + jnp.dot(
                        prob.astype(BF16), g_pair * q_masks[side], preferred_element_type=F32
                    )
                    back = dot_last(v_pair * k_masks[side], g_pair)
                    back = prob * (back - stat_ref[qt, 8 + head : 9 + head, :])
                    key_sum = key_sum + jnp.dot(
                        back.astype(BF16), q_pair * q_masks[side], preferred_element_type=F32
                    )
                dk_ref[pl.ds(k0, tk), cols] += key_sum
                dv_ref[pl.ds(k0, tk), cols] += value_sum
            return 0

        lax.fori_loop(lax.div(begin, tq), lax.div(end + tq - 1, tq), step, 0)
        return 0

    lax.fori_loop(0, rows // tk, tile, 0)


def key_grads(bounds, keys, values, queries, grads, stats):
    rows = stats.shape[2]
    tk = min(256, rows)
    return pl.pallas_call(
        functools.partial(key_grads_body, tk),
        out_shape=[jax.ShapeDtypeStruct((rows, A), F32)] * 2,
        in_specs=[pl.BlockSpec(memory_space=pltpu.SMEM)]
        + [pl.BlockSpec(memory_space=pltpu.VMEM)] * 5,
        out_specs=[pl.BlockSpec(memory_space=pltpu.VMEM)] * 2,
        compiler_params=pltpu.CompilerParams(vmem_limit_bytes=VMEM_LIMIT),
        name="key_grads",
    )(bounds, keys, values, queries, grads, stats)


def norm_back(grad_rows, normed, inverse, gain):
    scaled = grad_rows * gain
    return inverse * (
        scaled
        - jnp.mean(scaled, axis=1, keepdims=True)
        - normed * jnp.mean(scaled * normed, axis=1, keepdims=True)
    )


def dot_first(left, right):
    return lax.dot_general(left, right, (((0,), (0,)), ((), ())), preferred_element_type=F32)


def dot(left, right):
    return jnp.dot(left, right, preferred_element_type=F32)


def project_body(bounds, x_ref, w_ref, b_ref, q_ref, k_ref, v_ref):
    index = pl.program_id(0)

    @pl.when((index >= bounds[SEQS + 1]) & (index <= bounds[SEQS + 2]))
    def _():
        x = x_ref[...]
        query = (dot(x, w_ref[:, :A]) + b_ref[0:1, :]).astype(BF16).astype(F32)
        q_ref[...] = (query * (HD**-0.5)).astype(BF16)
        k_ref[...] = dot(x, w_ref[:, A : 2 * A]).astype(BF16)
        v_ref[...] = (dot(x, w_ref[:, 2 * A : 3 * A]) + b_ref[1:2, :]).astype(BF16)


def project(bounds, natural, w_in, smalls, rows):
    group_rows = natural.shape[0]

    def block(index, bounds):
        return (jnp.clip(index, bounds[SEQS + 1], bounds[SEQS + 2]), 0)

    def fixed(index, bounds):
        return (0, 0)

    return pl.pallas_call(
        project_body,
        out_shape=[jax.ShapeDtypeStruct((group_rows, A), BF16)] * 3,
        grid_spec=pltpu.PrefetchScalarGridSpec(
            num_scalar_prefetch=1,
            grid=(group_rows // rows,),
            in_specs=[
                pl.BlockSpec((rows, D), block),
                pl.BlockSpec((D, 3 * A), fixed),
                pl.BlockSpec((8, A), fixed),
            ],
            out_specs=[pl.BlockSpec((rows, A), block)] * 3,
        ),
        compiler_params=pltpu.CompilerParams(vmem_limit_bytes=VMEM_LIMIT),
        name="project",
    )(bounds, natural, w_in, smalls)


def tap_lanes(tap):
    row = lax.broadcasted_iota(jnp.int32, (128, A), 0)
    column = lax.broadcasted_iota(jnp.int32, (128, A), 1)
    return jnp.where(row == lax.div(column, HD) * KW + tap, 1.0, 0.0).astype(BF16)


def tap_pick(tap):
    row = lax.broadcasted_iota(jnp.int32, (A, 128), 0)
    column = lax.broadcasted_iota(jnp.int32, (A, 128), 1)
    first = row == lax.div(row, HD) * HD
    return jnp.where(first & (column == lax.div(row, HD) * KW + tap), 1.0, 0.0).astype(BF16)


def tap_weights(kw_ref, kb_ref, wide_ref, bias_ref):
    bias_ref[:, 0:128] = jnp.zeros((8, 128), F32)
    bias_ref[0:1, 0 : H * KW] = kb_ref[...].astype(F32)
    bias = bias_ref[:, 0:128].astype(BF16)
    for tap in range(KW):
        lanes = tap_lanes(tap)
        cols = slice(A * tap, A * tap + A)
        wide_ref[:, cols] = dot(kw_ref[...], lanes).astype(BF16)
        bias_ref[:, cols] = dot(bias, lanes)


def tap_near(bounds, group_rows, seg_ref, near_ref):
    span = near_ref.shape[1]
    position = bounds[SEQS] - RIM + lax.broadcasted_iota(jnp.int32, seg_ref.shape, 0)
    inside = (position >= 0) & (position < group_rows)
    seg_ref[...] = jnp.where(inside, seg_of(position, bounds), -1)
    seg = seg_ref[RIM // 2 : RIM // 2 + span, :]
    for tap in range(KW):
        shift = RIM // 2 - KW // 2 + tap
        near_ref[tap] = jnp.where((seg_ref[shift : shift + span, :] == seg) & (seg >= 0), 1.0, 0.0)


def tap_softmax(logits, bias_ref):
    parts = [logits[:, A * tap : A * tap + A] + bias_ref[0:1, A * tap : A * tap + A] for tap in range(KW)]
    largest = functools.reduce(jnp.maximum, parts)
    parts = [jnp.exp(part - largest) for part in parts]
    total = 1.0 / functools.reduce(jnp.add, parts)
    return [part * total for part in parts]


def wide3(value):
    return jnp.tile(value, (1, 3))


def conv_body(
    bounds, natural, w_ref, pw_ref, kw_ref, kb_ref, vec_ref, small_ref,
    out_ref, ext_ref, cv_ref, kc_ref, q_ref, cq_ref, sp_ref,
    extf_ref, seg_ref, near_ref, wide_ref, bias_ref, full_ref, sem,
):
    rows, group_rows = out_ref.shape[0], natural.shape[0]
    span = rows + RIM
    start = bounds[SEQS]
    copies = [
        pltpu.make_async_copy(
            natural.at[pl.ds(pl.multiple_of(jnp.maximum(start - RIM, 0), RIM), RIM)],
            ext_ref.at[0:RIM],
            sem.at[0],
        ),
        pltpu.make_async_copy(
            natural.at[pl.ds(pl.multiple_of(start, RIM), rows)], ext_ref.at[RIM : RIM + rows], sem.at[1]
        ),
        pltpu.make_async_copy(
            natural.at[pl.ds(pl.multiple_of(jnp.minimum(start + rows, group_rows - RIM), RIM), RIM)],
            ext_ref.at[RIM + rows : 2 * RIM + rows],
            sem.at[2],
        ),
    ]
    for copy in copies:
        copy.start()
    tap_weights(kw_ref, kb_ref, wide_ref, bias_ref)
    tap_near(bounds, group_rows, seg_ref, near_ref)
    for copy in copies:
        copy.wait()
    count = group_rows // rows
    place = lax.div(start, rows)
    padded = count - count // 8

    @pl.when((place == 0) | (place == padded))
    def _():
        ext_ref[0:RIM, :] = jnp.zeros((RIM, D), BF16)

    @pl.when((place == padded - 1) | (place == count - 1))
    def _():
        ext_ref[RIM + rows :, :] = jnp.zeros((RIM, D), BF16)

    ext = ext_ref[...]
    extf_ref[...] = ext.astype(F32)
    cv_ref[...] = dot(ext, w_ref[:, 3 * A :]) + small_ref[2:3, :]
    q_ref[...] = (dot(ext, w_ref[:, :A]) + small_ref[0:1, :]).astype(BF16).astype(F32)
    tile = span // 3
    for i in range(3):
        t0 = tile * i
        for c in range(6):
            cols = slice(128 * c, 128 * c + 128)
            window = extf_ref[t0 : t0 + tile + RIM, cols]
            total = 0.0
            for tap in range(KW):
                shift = RIM // 2 - KW // 2 + tap
                total += (
                    vec_ref[tap : tap + 1, cols]
                    * near_ref[tap, t0 : t0 + tile, :]
                    * window[shift : shift + tile]
                )
            sp_ref[t0 : t0 + tile, cols] = total.astype(BF16)
    kc_ref[...] = dot(sp_ref[...], pw_ref[...]) + small_ref[3:4, :]
    cq_ref[...] = (kc_ref[...] * q_ref[RIM // 2 : RIM // 2 + span, :]).astype(BF16)
    for i in range(3):
        t0 = tile * i
        kernel = tap_softmax(dot(cq_ref[t0 : t0 + tile, :], wide_ref[...]), bias_ref)
        window = cv_ref[t0 : t0 + tile + RIM, :]
        total = 0.0
        for tap in range(KW):
            shift = RIM // 2 - KW // 2 + tap
            total += kernel[tap] * wide3(near_ref[tap, t0 : t0 + tile, :]) * window[shift : shift + tile]
        full_ref[t0 : t0 + tile, :] = total
    out_ref[...] = full_ref[RIM // 2 : RIM // 2 + rows, :].astype(BF16)


def convolve(bounds, natural, w_in, pw, kw, kb, vectors, smalls, rows):
    span, wide = rows + RIM, rows + 2 * RIM
    vmem = pl.BlockSpec(memory_space=pltpu.VMEM)
    return pl.pallas_call(
        conv_body,
        out_shape=[
            jax.ShapeDtypeStruct((rows, A), BF16),
            jax.ShapeDtypeStruct((wide, D), BF16),
            jax.ShapeDtypeStruct((wide, A), F32),
            jax.ShapeDtypeStruct((span, A), F32),
            jax.ShapeDtypeStruct((wide, A), F32),
            jax.ShapeDtypeStruct((span, A), BF16),
            jax.ShapeDtypeStruct((span, D), BF16),
        ],
        in_specs=[pl.BlockSpec(memory_space=pltpu.SMEM), pl.BlockSpec(memory_space=pl.ANY)] + [vmem] * 6,
        out_specs=[vmem] * 7,
        scratch_shapes=[
            pltpu.VMEM((wide, D), F32),
            pltpu.VMEM((wide, 128), jnp.int32),
            pltpu.VMEM((KW, span, 128), F32),
            pltpu.VMEM((A, KW * A), BF16),
            pltpu.VMEM((8, KW * A), F32),
            pltpu.VMEM((span, A), F32),
            pltpu.SemaphoreType.DMA((3,)),
        ],
        compiler_params=pltpu.CompilerParams(vmem_limit_bytes=VMEM_LIMIT),
        name="convolve",
    )(bounds, natural, w_in, pw, kw, kb, vectors, smalls)


def norm_rows(x, gain, bias):
    centered = x - jnp.mean(x, axis=1, keepdims=True)
    inverse = lax.rsqrt(jnp.mean(centered * centered, axis=1, keepdims=True) + NORM_EPS)
    normed = centered * inverse
    return normed * gain + bias, normed, inverse


ROW_OUT_B, ROW_GAIN1, ROW_BIAS1, ROW_FFN_B, ROW_GAIN2, ROW_BIAS2 = range(KW, KW + 6)
FI_ROWS, FO_ROWS, OW_ROWS = 384, 384, 192
FIRST_PACK = 1024
SECOND_PACK = 512


def layer_body(
    bounds, attn_ref, lse_ref, conv_ref, ext_ref, tgt_ref, wo_ref, fi_ref, fo_ref, vec_ref, fb_ref,
    out_ref, gfirst_ref, gctx_ref, stat_ref, statt_ref, sums_ref, fbs_ref, pack_ref,
    ctx_s, low_s, act_s, slope_s, gfl_s, gpre_s, gproj_s,
):
    rows = out_ref.shape[0]
    tm = slope_s.shape[0]
    chunk = D
    wide = FF // NG
    part = D // NG
    row_of = lax.broadcasted_iota(jnp.int32, (A, 128), 0)
    column_of = lax.broadcasted_iota(jnp.int32, (A, 128), 1)
    head_pick = jnp.where(column_of == 8 + lax.div(row_of, HD), 1.0, 0.0).astype(BF16)
    sums_ref[...] = jnp.zeros(sums_ref.shape, F32)
    fbs_ref[...] = jnp.zeros(fbs_ref.shape, F32)

    def vec(row):
        return vec_ref[row : row + 1, :]

    def add_sum(row, value):
        sums_ref[row : row + 1, :] += jnp.sum(value, axis=0, keepdims=True)

    def tile(index, _):
        r0 = pl.multiple_of(index * tm, tm)
        here = pl.ds(r0, tm)
        attn = attn_ref[here, :]
        ctx_s[here, :A] = attn.astype(BF16)
        ctx_s[here, A:] = conv_ref[here, :]
        tokens = ext_ref[pl.ds(pl.multiple_of(r0 + RIM, RIM), tm), :].astype(F32)
        first = tokens + dot(ctx_s[here, :], wo_ref[...]) + vec(ROW_OUT_B)
        after, normed_one, inverse_one = norm_rows(first, vec(ROW_GAIN1), vec(ROW_BIAS1))
        low_s[here, :] = after.astype(BF16)
        results = []
        for g in range(NG):
            low = low_s[here, part * g : part * g + part]
            total = 0.0
            for c in range(wide // chunk):
                span = slice(chunk * c, chunk * c + chunk)
                whole = slice(wide * g + chunk * c, wide * g + chunk * c + chunk)
                pre = dot(low, fi_ref[g, :, span]) + fb_ref[2 * g + c : 2 * g + c + 1, :]
                phi = 0.5 * (1.0 + lax.erf(pre * ROOT_HALF))
                act = (pre * phi).astype(BF16)
                act_s[here, whole] = act
                slope_s[:, whole] = phi + pre * DENSITY_NORM * jnp.exp(-0.5 * pre * pre)
                total += dot(act, fo_ref[g, span, :])
            results.append(total)
        second = after + jnp.concatenate(results, axis=1) + vec(ROW_FFN_B)
        result, normed_two, inverse_two = norm_rows(second, vec(ROW_GAIN2), vec(ROW_BIAS2))
        out_ref[here, :] = result.astype(BF16)
        seg = seg_of(bounds[SEQS] + r0 + lax.broadcasted_iota(jnp.int32, (tm, 1), 0), bounds)
        error = jnp.where(seg < SEQS, result - tgt_ref[here, :].astype(F32), 0.0)
        add_sum(6, error * error)
        add_sum(4, error * normed_two)
        add_sum(5, error)
        grad_second = norm_back(error, normed_two, inverse_two, vec(ROW_GAIN2))
        gfl = grad_second.astype(BF16)
        gfl_s[here, :] = gfl
        add_sum(3, gfl.astype(F32))
        grads = []
        for g in range(NG):
            total = 0.0
            for c in range(wide // chunk):
                span = slice(chunk * c, chunk * c + chunk)
                whole = slice(wide * g + chunk * c, wide * g + chunk * c + chunk)
                gact = dot_last(gfl_s[here, part * g : part * g + part], fo_ref[g, span, :])
                gpre = (gact * slope_s[:, whole]).astype(BF16)
                gpre_s[here, whole] = gpre
                fbs_ref[0:1, whole] += jnp.sum(gpre.astype(F32), axis=0, keepdims=True)
                total += dot_last(gpre, fi_ref[g, :, span])
            grads.append(total)
        grad_after = jnp.concatenate(grads, axis=1) + grad_second
        add_sum(1, grad_after * normed_one)
        add_sum(2, grad_after)
        grad_first = norm_back(grad_after, normed_one, inverse_one, vec(ROW_GAIN1))
        gfirst_ref[here, :] = grad_first
        gproj = grad_first.astype(BF16)
        gproj_s[here, :] = gproj
        add_sum(0, gproj.astype(F32))
        gctx = dot_last(gproj, wo_ref[...]).astype(BF16)
        gctx_ref[here, :] = gctx
        product = gctx[:, :A].astype(F32) * attn
        high = product.astype(BF16)
        rest = (product - high.astype(F32)).astype(BF16)
        stat = lse_ref[here, :] + dot(high, head_pick) + dot(rest, head_pick)
        stat_ref[here, :] = stat
        return 0

    lax.fori_loop(0, rows // tm, tile, 0)
    statt_ref[...] = stat_ref[...].T[:16]
    for g in range(NG):
        for half in range(2):
            whole = slice(wide * g + D * half, wide * g + D * half + D)
            grad = dot_first(low_s[:, part * g : part * g + part], gpre_s[:, whole]).astype(BF16)
            r0 = 96 * (2 * g + half)
            for k in range(4):
                pack_ref[k, r0 : r0 + 96, :] = grad[96 * k : 96 * k + 96]
        for k in range(4):
            grad = dot_first(
                act_s[:, wide * g + A * k : wide * g + A * k + A], gfl_s[:, part * g : part * g + part]
            )
            pack_ref[k, FI_ROWS : FI_ROWS + FO_ROWS, part * g : part * g + part] = grad.astype(BF16)
    grad = dot_first(ctx_s[...], gproj_s[...]).astype(BF16)
    r0 = FI_ROWS + FO_ROWS
    for k in range(4):
        pack_ref[k, r0 : r0 + OW_ROWS, :] = grad[OW_ROWS * k : OW_ROWS * k + OW_ROWS]
        pack_ref[k, r0 + OW_ROWS :, :] = jnp.zeros((FIRST_PACK - r0 - OW_ROWS, D), BF16)


def layer(bounds, attn, lse, conv, ext, target, wo, fi, fo, vectors, fb):
    rows = attn.shape[0]
    tm = min(256, rows)
    vmem = pl.BlockSpec(memory_space=pltpu.VMEM)
    return pl.pallas_call(
        layer_body,
        out_shape=[
            jax.ShapeDtypeStruct((rows, D), BF16),
            jax.ShapeDtypeStruct((rows, D), F32),
            jax.ShapeDtypeStruct((rows, D), BF16),
            jax.ShapeDtypeStruct((rows, 128), F32),
            jax.ShapeDtypeStruct((16, rows), F32),
            jax.ShapeDtypeStruct((8, D), F32),
            jax.ShapeDtypeStruct((1, FF), F32),
            jax.ShapeDtypeStruct((4, FIRST_PACK, D), BF16),
        ],
        in_specs=[pl.BlockSpec(memory_space=pltpu.SMEM)] + [vmem] * 10,
        out_specs=[vmem] * 8,
        scratch_shapes=[
            pltpu.VMEM((rows, D), BF16),
            pltpu.VMEM((rows, D), BF16),
            pltpu.VMEM((rows, FF), BF16),
            pltpu.VMEM((tm, FF), F32),
            pltpu.VMEM((rows, D), BF16),
            pltpu.VMEM((rows, FF), BF16),
            pltpu.VMEM((rows, D), BF16),
        ],
        compiler_params=pltpu.CompilerParams(vmem_limit_bytes=VMEM_LIMIT),
        name="layer",
    )(bounds, attn, lse, conv, ext, target, wo, fi, fo, vectors, fb)


def conv_back_body(
    bounds, gctx_ref, edge_ref, dq_ref, dk_ref, dv_ref, gfirst_ref,
    ext_ref, cv_ref, kc_ref, q_ref, cq_ref, sp_ref, w_ref, pw_ref, kw_ref, kb_ref, vec_ref,
    gtok_ref, pack_ref, sums_ref, bsum_ref,
    extf_ref, seg_ref, near_ref, wide_ref, bias_ref, gc_ref, pc_ref, glc_ref, gsp_ref, gtc_ref, gm_ref,
    *, group_rows,
):
    rows = gctx_ref.shape[0]
    span = rows + RIM
    rim = RIM // 2
    place = bounds[SEQS + 3]
    tap_weights(kw_ref, kb_ref, wide_ref, bias_ref)
    tap_near(bounds, group_rows, seg_ref, near_ref)
    extf_ref[...] = ext_ref[...].astype(F32)
    low_edge = edge_ref[0].astype(F32)[RIM - rim :]
    high_edge = edge_ref[1].astype(F32)[:rim]
    gc_ref[0:rim, :] = jnp.where(place > 0, low_edge, 0.0)
    gc_ref[rim : rim + rows, :] = gctx_ref[:, A:].astype(F32)
    gc_ref[rim + rows :, :] = jnp.where(place < group_rows // rows - 1, high_edge, 0.0)
    blocks = jnp.where(
        lax.div(lax.broadcasted_iota(jnp.int32, (128, 128), 0), HD)
        == lax.div(lax.broadcasted_iota(jnp.int32, (128, 128), 1), HD),
        1.0,
        0.0,
    ).astype(BF16)
    tile = span // 3
    for i in range(3):
        t0 = tile * i
        here = slice(t0, t0 + tile)
        kernel = tap_softmax(dot(cq_ref[here, :], wide_ref[...]), bias_ref)
        window = cv_ref[t0 : t0 + tile + RIM, :]
        grad = gc_ref[here, :]
        inner = []
        total = 0.0
        for tap in range(KW):
            shift = rim - KW // 2 + tap
            near = wide3(near_ref[tap, here, :])
            product = (grad * window[shift : shift + tile]).astype(BF16)
            sums = jnp.concatenate(
                [dot(product[:, 128 * c : 128 * c + 128], blocks) for c in range(3)], axis=1
            )
            sums = sums * near
            inner.append(sums)
            total += kernel[tap] * sums
            pc_ref[tap, here, :] = kernel[tap] * near * grad
        picked = 0.0
        for tap in range(KW):
            logit = (kernel[tap] * (inner[tap] - total)).astype(BF16)
            picked += dot(logit, tap_pick(tap))
        glc_ref[here, :] = picked.astype(BF16)
    back = dot_last(glc_ref[...], kw_ref[...])
    query = q_ref[rim : rim + span, :]
    row = lax.broadcasted_iota(jnp.int32, (span, 1), 0)
    own = (row >= rim) & (row < rim + rows)
    grad_kc = (back * query).astype(BF16)
    gsp_ref[...] = dot_last(grad_kc, pw_ref[...])
    grad_query = back * kc_ref[...]
    own_kc = jnp.where(own, grad_kc.astype(F32), 0.0)
    own_logits = jnp.where(own, glc_ref[...].astype(F32), 0.0)
    grad_pw = dot_first(sp_ref[...], own_kc.astype(BF16)).astype(BF16)
    grad_kern = dot_first(cq_ref[...], own_logits.astype(BF16)).astype(BF16)
    for k in range(4):
        for half in range(2):
            r0 = 192 * k + 96 * half
            pack_ref[k, 384:480, A * half : A * half + A] = grad_pw[r0 : r0 + 96]
        for m in range(6):
            r0 = 96 * k + 16 * m
            pack_ref[k, 480:496, 128 * m : 128 * m + 128] = grad_kern[r0 : r0 + 16]
        pack_ref[k, 496:, :] = jnp.zeros((SECOND_PACK - 496, D), BF16)
    bsum_ref[...] = jnp.zeros(bsum_ref.shape, F32)
    bsum_ref[3:4, :] = jnp.sum(own_kc, axis=0, keepdims=True)
    bsum_ref[4:5, 0:128] = jnp.sum(own_logits, axis=0, keepdims=True)
    gm_ref[:, :A] = (dq_ref[...] * (HD**-0.5) + grad_query[rim : rim + rows]).astype(BF16)
    gm_ref[:, A : 2 * A] = dk_ref[...].astype(BF16)
    gm_ref[:, 2 * A : 3 * A] = dv_ref[...].astype(BF16)
    sums_ref[...] = jnp.zeros(sums_ref.shape, F32)
    step = 128
    for s0 in range(0, rows, step):
        for c in range(6):
            cols = slice(128 * c, 128 * c + 128)
            grads = gsp_ref[s0 + rim : s0 + rim + step, cols]
            tokens = extf_ref[s0 + rim : s0 + rim + step + RIM, cols]
            spread = gsp_ref[s0 : s0 + step + RIM, cols]
            total = 0.0
            for tap in range(KW):
                shift = rim - KW // 2 + tap
                value = near_ref[tap, s0 + rim : s0 + rim + step, :] * grads * tokens[shift : shift + step]
                sums_ref[tap : tap + 1, cols] += jnp.sum(value, axis=0, keepdims=True)
                shift = rim + KW // 2 - tap
                moved = near_ref[tap, s0 : s0 + step + RIM, :] * spread
                total += vec_ref[tap : tap + 1, cols] * moved[shift : shift + step]
            gtc_ref[s0 : s0 + step, cols] = total
        for c in range(3):
            cols = slice(128 * c, 128 * c + 128)
            total = 0.0
            for tap in range(KW):
                shift = rim + KW // 2 - tap
                total += pc_ref[tap, s0 : s0 + step + RIM, cols][shift : shift + step]
            gm_ref[s0 : s0 + step, 3 * A + 128 * c : 3 * A + 128 * c + 128] = total.astype(BF16)
    bsum_ref[0:1, :] = jnp.sum(gm_ref[:, :A].astype(F32), axis=0, keepdims=True)
    bsum_ref[1:2, :] = jnp.sum(gm_ref[:, 2 * A : 3 * A].astype(F32), axis=0, keepdims=True)
    bsum_ref[2:3, :] = jnp.sum(gm_ref[:, 3 * A :].astype(F32), axis=0, keepdims=True)
    gtok_ref[...] = (dot_last(gm_ref[...], w_ref[...]) + gfirst_ref[...] + gtc_ref[...]).astype(BF16)
    for half in range(2):
        grad = dot_first(ext_ref[RIM : RIM + rows, :], gm_ref[:, D * half : D * half + D]).astype(BF16)
        for k in range(4):
            pack_ref[k, 192 * half : 192 * half + 192, :] = grad[192 * k : 192 * k + 192]


def conv_back(bounds, group_rows, *args):
    rows = args[0].shape[0]
    span, wide = rows + RIM, rows + 2 * RIM
    vmem = pl.BlockSpec(memory_space=pltpu.VMEM)
    return pl.pallas_call(
        functools.partial(conv_back_body, group_rows=group_rows),
        out_shape=[
            jax.ShapeDtypeStruct((rows, D), BF16),
            jax.ShapeDtypeStruct((4, SECOND_PACK, D), BF16),
            jax.ShapeDtypeStruct((16, D), F32),
            jax.ShapeDtypeStruct((8, A), F32),
        ],
        in_specs=[pl.BlockSpec(memory_space=pltpu.SMEM)] + [vmem] * len(args),
        out_specs=[vmem] * 4,
        scratch_shapes=[
            pltpu.VMEM((wide, D), F32),
            pltpu.VMEM((wide, 128), jnp.int32),
            pltpu.VMEM((KW, span, 128), F32),
            pltpu.VMEM((A, KW * A), BF16),
            pltpu.VMEM((8, KW * A), F32),
            pltpu.VMEM((span, A), F32),
            pltpu.VMEM((KW, span, A), F32),
            pltpu.VMEM((span, 128), BF16),
            pltpu.VMEM((span, D), F32),
            pltpu.VMEM((rows, D), F32),
            pltpu.VMEM((rows, 4 * A), BF16),
        ],
        compiler_params=pltpu.CompilerParams(vmem_limit_bytes=VMEM_LIMIT),
        name="conv_back",
    )(bounds, *args)


def finish_body(
    place, arrange_ref, out_in, tok_in, first_ref, second_ref, sum_ref,
    out_ref, tok_ref, w_ref, b_ref, dw_ref, pw_ref, pb_ref, kern_ref, vec_ref, ow_ref, fi_ref, fb_ref, fo_ref,
    loss_ref, kb_ref,
):
    rows = out_ref.shape[0]
    slot = lax.broadcasted_iota(jnp.int32, (rows, rows), 0)
    sort = jnp.where(slot == arrange_ref[...], 1.0, 0.0).astype(BF16)
    out_ref[...] = dot_first(sort, out_in[...]).astype(BF16)
    tok_ref[...] = dot_first(sort, tok_in[...])
    for half in range(2):
        w_ref[:, D * half : D * half + D] = second_ref[192 * half : 192 * half + 192, :].astype(F32)
        pw_ref[96 * half : 96 * half + 96, :] = second_ref[384:480, A * half : A * half + A].astype(F32)
    for m in range(6):
        kern_ref[16 * m : 16 * m + 16, :] = second_ref[480:496, 128 * m : 128 * m + H * KW].astype(F32)
    for g in range(NG):
        for half in range(2):
            r0 = 96 * (2 * g + half)
            fi_ref[g, :, D * half : D * half + D] = first_ref[r0 : r0 + 96, :].astype(F32)
        fo_ref[g] = first_ref[384:768, A * g : A * g + A].astype(F32)
    ow_ref[...] = first_ref[768:960, :].astype(F32)
    total = jnp.sum(sum_ref[15:16, :], axis=1, keepdims=True)
    loss_ref[...] = total / (place[1].astype(F32) * D)
    kb_ref[...] = sum_ref[22:23, 0 : H * KW]
    for k in range(4):

        @pl.when(place[0] == k)
        def _(k=k):
            cols = slice(D // 4 * k, D // 4 * k + D // 4)
            dw_ref[...] = sum_ref[0:KW, cols]
            vec_ref[...] = sum_ref[KW : KW + 6, cols]
            fb_ref[...] = sum_ref[16 + k : 17 + k, :]
            part = slice(A // 4 * k, A // 4 * k + A // 4)
            second = slice(A + A // 4 * k, A + A // 4 * k + A // 4)
            b_ref[0:1, :] = sum_ref[20:21, part]
            b_ref[1:2, :] = sum_ref[20:21, second]
            b_ref[2:3, :] = sum_ref[21:22, part]
            pb_ref[...] = sum_ref[21:22, second]


def finish(place, arrange, *args):
    rows = args[0].shape[0]
    vmem = pl.BlockSpec(memory_space=pltpu.VMEM)
    shapes = [
        (rows, D), (D // 4, 4 * A), (3, A // 4), (KW, D // 4), (D // 4, A), (1, A // 4), (A // 4, H * KW),
        (6, D // 4), (D // 4, D), (NG, A // 4, FF // NG), (1, D), (NG, A, A), (1, 1), (1, H * KW),
    ]
    return pl.pallas_call(
        finish_body,
        out_shape=[jax.ShapeDtypeStruct((rows, D), BF16)] + [jax.ShapeDtypeStruct(shape, F32) for shape in shapes],
        in_specs=[pl.BlockSpec(memory_space=pltpu.SMEM)] + [vmem] * (len(args) + 1),
        out_specs=[vmem] * 15,
        compiler_params=pltpu.CompilerParams(vmem_limit_bytes=VMEM_LIMIT),
        name="finish",
    )(place, arrange, *args)


def local(
    hidden,
    teacher,
    lengths,
    deal,
    w_in,
    b_in,
    dw_kernel,
    pw_weight,
    pw_bias,
    kern_weight,
    kern_bias,
    out_weight,
    out_bias,
    norm1_gain,
    norm1_bias,
    ffn_in,
    ffn_in_bias,
    ffn_out,
    ffn_out_bias,
    norm2_gain,
    norm2_bias,
):
    rows = hidden.shape[1]
    ctx_count = lax.axis_size("ctx")
    group_rows = rows * ctx_count
    piece_rows = rows // ctx_count
    group = lax.axis_index("wt")
    place = lax.axis_index("ctx")
    own_lengths = lax.dynamic_slice_in_dim(lengths, group, 1, 0)[0]
    ends = jnp.cumsum(own_lengths, dtype=jnp.int32)
    begin = jnp.max(jnp.where(ends <= place * rows, ends, 0))
    end = jnp.min(jnp.where(ends >= place * rows + rows, ends, group_rows))
    bounds = jnp.concatenate(
        [ends, jnp.stack([place * rows, begin // rows, (end - 1) // rows, place])]
    ).astype(jnp.int32)

    own_slots = lax.dynamic_slice_in_dim(deal[0], place * rows, rows, 0)
    arrange = own_slots // rows * piece_rows + own_slots % rows - place * piece_rows
    sort = (jnp.arange(rows, dtype=jnp.int32)[:, None] == arrange[None, :]).astype(BF16)

    def sorted_rows(values):
        return jnp.dot(sort, values, preferred_element_type=F32).astype(BF16)

    pieces_shape = (ctx_count, piece_rows, D)
    natural, target, full_w_in, full_pw, full_out_w, full_ffn_in, full_ffn_out, vectors, smalls, ffn_in_b, full_kern = (
        gather_inputs(
            sorted_rows(hidden[0]).reshape(pieces_shape),
            sorted_rows(teacher[0]).reshape(pieces_shape),
            (w_in, pw_weight, out_weight, ffn_in, ffn_out),
            (0, 0, 0, 1, 1),
            [dw_kernel]
            + [
                item[None]
                for item in (
                    out_bias, norm1_gain, norm1_bias, ffn_out_bias, norm2_gain, norm2_bias, ffn_in_bias
                )
            ]
            + [b_in, pw_bias[None], kern_weight],
            ctx_count,
        )
    )
    natural = natural.reshape(group_rows, D)
    target = target.reshape(rows, D)
    kern_b = kern_bias[None]

    all_q8, all_keys, all_values = project(bounds, natural, full_w_in, smalls, rows)
    conv_out, extended, conv_value, key_conv, query_ext, conv_query, spread = convolve(
        bounds, natural, full_w_in, full_pw, full_kern, kern_b, vectors, smalls, rows
    )
    attn_out, lse = attend(bounds, all_q8, all_keys, all_values, rows)
    result, grad_first, grad_context, stats, stats_t, layer_sums, ffn_in_sums, first_pack = layer(
        bounds, attn_out, lse, conv_out, extended, target,
        full_out_w, full_ffn_in, full_ffn_out, vectors, ffn_in_b,
    )
    all_grads, edges, all_stats, output = gather_grads(
        grad_context, stats_t, result.reshape(pieces_shape), ctx_count
    )
    grad_query = query_grads(bounds, all_q8, grad_context, stats, all_keys, all_values)
    grad_keys, grad_values = key_grads(
        bounds, all_keys, all_values, all_q8, all_grads.reshape(group_rows, A), all_stats
    )
    grad_tokens, second_pack, tap_sums, bias_sums = conv_back(
        bounds, group_rows, grad_context, edges, grad_query, grad_keys, grad_values, grad_first,
        extended, conv_value, key_conv, query_ext, conv_query, spread,
        full_w_in, full_pw, full_kern, kern_b, vectors,
    )
    sums = jnp.concatenate(
        [tap_sums[:KW], layer_sums[:7], ffn_in_sums.reshape(4, D), bias_sums.reshape(4, D)], axis=0
    )
    (first, second), totals, moved = reduce_grads(
        [first_pack, second_pack], sums, grad_tokens.reshape(pieces_shape), ctx_count, 32
    )
    (
        dealt_out, dealt_grad, g_w_in, g_b_in, g_dw, g_pw, g_pw_b, g_kern, g_vec, g_out, g_ffn_in, g_ffn_in_b,
        g_ffn_out, loss, g_kern_b,
    ) = finish(
        jnp.stack([group, jnp.sum(lengths)]).astype(jnp.int32), arrange[None],
        output.reshape(rows, D), moved.reshape(rows, D), first, second, totals,
    )
    return (
        dealt_out[None],
        loss[0, 0],
        dealt_grad[None],
        g_w_in,
        g_b_in,
        g_dw,
        g_pw,
        g_pw_b[0],
        g_kern,
        g_kern_b[0],
        g_out,
        g_vec[0],
        g_vec[1],
        g_vec[2],
        g_ffn_in,
        g_ffn_in_b[0],
        g_ffn_out,
        g_vec[3],
        g_vec[4],
        g_vec[5],
    )


def solution(mesh):
    return jax.shard_map(
        local,
        mesh=mesh,
        in_specs=(
            P("wt", "ctx", None),
            P("wt", "ctx", None),
            P(),
            P("wt", None),
            P("wt", None),
            P(None, "wt"),
            P(None, "wt"),
            P("wt", None),
            P("wt"),
            P("wt", None),
            P(),
            P("wt", None),
            P("wt"),
            P("wt"),
            P("wt"),
            P(None, "wt", None),
            P("wt"),
            P(None, "wt", None),
            P("wt"),
            P("wt"),
            P("wt"),
        ),
        out_specs=(
            P("wt", "ctx", None),
            P(),
            P("wt", "ctx", None),
            P("wt", None),
            P(None, "wt"),
            P(None, "wt"),
            P("wt", None),
            P("wt"),
            P("wt", None),
            P(),
            P("wt", None),
            P("wt"),
            P("wt"),
            P("wt"),
            P(None, "wt", None),
            P("wt"),
            P(None, "wt", None),
            P("wt"),
            P("wt"),
            P("wt"),
        ),
        check_vma=False,
    )
```

```python
import functools

import jax
import jax.numpy as jnp
from jax import lax
from jax.experimental import pallas as pl
from jax.experimental.pallas import tpu as pltpu
from jax.sharding import PartitionSpec as P

D = 768
H = 6
HD = 64
FF = 3072
NG = 2
KW = 9
SEQS = 6
A = 384

NORM_EPS = 1e-12
MASKED = -1e30
ROOT_HALF = 0.7071067811865476
DENSITY_NORM = 0.3989422804014327
RIM = 16
MESH = pl.DeviceIdType.MESH
BF16 = jnp.bfloat16
F32 = jnp.float32
VMEM_LIMIT = 60 * 1024 * 1024


def remote(src, dst, send, recv, target):
    return pltpu.make_async_remote_copy(
        src_ref=src,
        dst_ref=dst,
        send_sem=send,
        recv_sem=recv,
        device_id=target,
        device_id_type=MESH,
    )


def greet(peers):
    barrier = pltpu.get_barrier_semaphore()
    total = 0
    for there, target in peers:

        @pl.when(there)
        def _(target=target):
            pl.semaphore_signal(barrier, inc=1, device_id=target, device_id_type=MESH)

        total = total + jnp.where(there, 1, 0)
    pl.semaphore_wait(barrier, total)


class Place:
    def __init__(self, count):
        self.count = count
        self.length = count // 2
        self.valid = count - count // 8
        self.window = count // 2
        self.me = lax.axis_index("ctx")
        self.line = lax.div(self.me, 2)
        self.side = lax.rem(self.me, 2)
        self.mate_index = self.me + 1 - 2 * self.side
        self.mate = {"ctx": self.mate_index}
        self.up = {"ctx": lax.rem(self.me + 2, count)}
        self.down = {"ctx": lax.rem(self.me + count - 2, count)}
        self.has_up = self.line < self.length - 1
        self.has_down = self.line > 0

    def others(self):
        return [
            (self.me >= 0, {"ctx": lax.rem(self.me + shift, self.count)}) for shift in range(1, self.count)
        ]


class PieceNeeds:
    def __init__(self, place, first, last):
        self.place, self.first, self.last = place, first, last

    def at(self, index, source):
        p = self.place
        return (
            (index < p.valid)
            & (self.first <= index + p.window)
            & (self.last >= index - p.window)
        )

    def above(self, line, source):
        p = self.place
        return (2 * line < p.valid) & (self.last >= 2 * line - p.window)

    def below(self, line, source):
        return self.first <= 2 * line + 1 + self.place.window

    def sent(self, source):
        return source >= 0


class BlockNeeds:
    def __init__(self, place):
        self.place = place

    def at(self, index, source):
        p = self.place
        near = (index <= source + p.window) & (index >= source - p.window)
        return near & (index < p.valid) & (source < p.valid)

    def above(self, line, source):
        p = self.place
        return (2 * line < p.valid) & (2 * line <= source + p.window) & (source < p.valid)

    def below(self, line, source):
        p = self.place
        return (2 * line + 1 >= source - p.window) & (source < p.valid)

    def sent(self, source):
        return source < self.place.valid


class AllNeeds:
    def __init__(self, place):
        self.place = place

    def at(self, index, source):
        return source * 0 == 0

    def above(self, line, source):
        return source * 0 == 0

    def below(self, line, source):
        return source * 0 == 0

    def sent(self, source):
        return source * 0 == 0


class Part:
    def __init__(self, place, needs, own, slot, send, recv):
        self.place, self.needs, self.own, self.slot = place, needs, own, slot
        self.send, self.recv = send, recv

    def copy(self, src, source, send, recv, target):
        return remote(src, self.slot(source), self.send.at[send], self.recv.at[recv], target)

    def go_up(self, source):
        p = self.place
        return p.has_up & self.needs.above(p.line + 1, source)

    def go_down(self, source):
        p = self.place
        return p.has_down & self.needs.below(p.line - 1, source)

    def from_below(self, s, source):
        p = self.place
        return (p.line - s >= 0) & self.needs.above(p.line, source)

    def from_above(self, s, source):
        p = self.place
        return (p.line + s < p.length) & self.needs.below(p.line, source)


class LinePart(Part):
    def start(self):
        p = self.place

        @pl.when(self.needs.at(p.mate_index, p.me))
        def _():
            self.copy(self.own, p.me, (2, 0), (2, 0), p.mate).start()

        @pl.when(self.go_up(p.me))
        def _():
            self.copy(self.own, p.me, (0, 0), (0, 1), p.up).start()

        @pl.when(self.go_down(p.me))
        def _():
            self.copy(self.own, p.me, (1, 0), (1, 1), p.down).start()

    def step(self, s):
        p = self.place
        for row, source, there, go, target in (
            (0, p.me - 2 * s, self.from_below, self.go_up, p.up),
            (1, p.me + 2 * s, self.from_above, self.go_down, p.down),
        ):

            @pl.when(there(s, source))
            def _(row=row, source=source, go=go, target=target):
                held = self.slot(source)
                self.copy(held, source, (2 + row, s), (row, s), p.mate).wait_recv()

                @pl.when(go(source))
                def _():
                    self.copy(held, source, (row, s), (row, s + 1), target).start()

                @pl.when(self.needs.at(p.mate_index, source))
                def _():
                    self.copy(held, source, (2 + row, s), (2 + row, s), p.mate).start()

    def finish(self):
        p = self.place
        for s in range(p.length):
            for row, source, exists, go, target in (
                (0, p.me - 2 * s, p.line - s >= 0, self.go_up, p.up),
                (1, p.me + 2 * s, p.line + s < p.length, self.go_down, p.down),
            ):
                held = self.slot(source)
                mates = source + 1 - 2 * p.side
                if s > 0 or row == 0:

                    @pl.when(exists & self.needs.at(p.me, mates))
                    def _(row=row, s=s, mates=mates):
                        theirs = self.slot(mates)
                        self.copy(theirs, mates, (2 + row, s), (2 + row, s), p.mate).wait_recv()

                    @pl.when(exists & self.needs.at(p.mate_index, source))
                    def _(row=row, s=s, held=held, source=source):
                        self.copy(held, source, (2 + row, s), (2 + row, s), p.mate).wait_send()

                @pl.when(exists & go(source) & ((s == 0) | self.arrived(row, source)))
                def _(row=row, s=s, held=held, source=source, target=target):
                    self.copy(held, source, (row, s), (row, s + 1), target).wait_send()

    def arrived(self, row, source):
        p = self.place
        return self.needs.above(p.line, source) if row == 0 else self.needs.below(p.line, source)


class PairPart(Part):
    def across(self):
        p = self.place

        @pl.when(self.needs.sent(p.me))
        def _():
            self.copy(self.own, p.me, (4, 0), (4, 0), p.mate).start()

    def along(self):
        p = self.place

        @pl.when(self.go_up(p.me))
        def _():
            self.copy(self.own, p.me, (0, 0), (0, 1), p.up).start()

        @pl.when(self.go_down(p.me))
        def _():
            self.copy(self.own, p.me, (1, 0), (1, 1), p.down).start()

    def middle(self):
        p = self.place
        source = p.mate_index
        held = self.slot(source)

        @pl.when(self.needs.sent(source))
        def _():
            self.copy(held, source, (4, 0), (4, 0), p.mate).wait_recv()

        @pl.when(self.go_up(source))
        def _():
            self.copy(held, source, (2, 0), (2, 1), p.up).start()

        @pl.when(self.go_down(source))
        def _():
            self.copy(held, source, (3, 0), (3, 1), p.down).start()

    def step(self, s):
        p = self.place
        for base, column in ((0, p.me), (2, p.mate_index)):
            for row, source, there, go, target in (
                (0, column - 2 * s, self.from_below, self.go_up, p.up),
                (1, column + 2 * s, self.from_above, self.go_down, p.down),
            ):

                @pl.when(there(s, source))
                def _(row=row + base, source=source, go=go, target=target):
                    held = self.slot(source)
                    self.copy(held, source, (row, s), (row, s), p.mate).wait_recv()

                    @pl.when(go(source))
                    def _():
                        self.copy(held, source, (row, s), (row, s + 1), target).start()

    def finish(self):
        p = self.place

        @pl.when(self.needs.sent(p.me))
        def _():
            self.copy(self.own, p.me, (4, 0), (4, 0), p.mate).wait_send()

        for s in range(p.length):
            for base, column in ((0, p.me), (2, p.mate_index)):
                for row, source, there, go, target in (
                    (0, column - 2 * s, self.from_below, self.go_up, p.up),
                    (1, column + 2 * s, self.from_above, self.go_down, p.down),
                ):
                    passed = there(s, source) if s > 0 else p.me >= 0

                    @pl.when(passed & go(source))
                    def _(row=row + base, s=s, source=source, target=target):
                        held = self.slot(source)
                        self.copy(held, source, (row, s), (row, s + 1), target).wait_send()


class Swap:
    def __init__(self, place, src, dst, send, recv):
        self.place, self.src, self.dst, self.send, self.recv = place, src, dst, send, recv

    def copy(self, shift):
        p = self.place
        there = lax.rem(p.me + shift, p.count)
        return remote(
            self.src.at[there], self.dst.at[p.me], self.send.at[shift], self.recv.at[shift], {"ctx": there}
        )

    def keep(self):
        p = self.place
        return pltpu.make_async_copy(self.src.at[p.me], self.dst.at[p.me], self.send.at[0])

    def start(self):
        for shift in range(1, self.place.count):
            self.copy(shift).start()
        self.keep().start()

    def finish(self):
        p = self.place
        self.keep().wait()
        for shift in range(1, p.count):
            self.copy(shift).wait_send()
            source = lax.rem(p.me + p.count - shift, p.count)
            held = self.dst.at[source]
            remote(held, held, self.send.at[shift], self.recv.at[shift], p.mate).wait_recv()


def part_sems(length):
    return [
        pltpu.SemaphoreType.DMA((5, length + 1)),
        pltpu.SemaphoreType.DMA((5, length + 1)),
    ]


def swap_sems(count):
    return [pltpu.SemaphoreType.DMA((count,)), pltpu.SemaphoreType.DMA((count,))]


def dot(left, right):
    return jnp.dot(left, right, preferred_element_type=F32)


def setup_body(
    lengths, deal_ref, x_ref, t_ref, dw_ref, *refs
):
    rows_in, refs = refs[:6], refs[6:]
    fb_in, b_in, pb_in, kern_in = refs[:4]
    sx_ref, st_ref, arrange_ref, bounds, wide, narrow, ffn, kern = refs[4:]
    count, piece = sx_ref.shape[:2]
    rows = count * piece
    group = lax.axis_index("wt")
    place = lax.axis_index("ctx")
    start = place * rows
    end = jnp.int32(0)
    total = jnp.int32(0)
    first, last = jnp.int32(0), jnp.int32(rows * count)
    ends = []
    for i in range(SEQS):
        end = end + lengths[group, i]
        ends.append(end)
        bounds[i] = end
        for g in range(4):
            total = total + lengths[g, i]
    for i in range(SEQS):
        first = jnp.where(ends[i] <= start, ends[i], first)
    for i in reversed(range(SEQS)):
        last = jnp.where(ends[i] >= start + rows, ends[i], last)
    bounds[SEQS] = start
    bounds[SEQS + 1] = lax.div(first, rows)
    bounds[SEQS + 2] = lax.div(last - 1, rows)
    bounds[SEQS + 3] = place
    bounds[SEQS + 4] = group
    bounds[SEQS + 5] = total
    slots = deal_ref[0:1, pl.ds(pl.multiple_of(start, 128), rows)]
    block = lax.div(slots, rows)
    arrange = block * piece + (slots - block * rows) - place * piece
    arrange_ref[...] = arrange
    sort = jnp.where(lax.broadcasted_iota(jnp.int32, (rows, rows), 0) == arrange, 1.0, 0.0).astype(BF16)
    for src, dst in ((x_ref, sx_ref), (t_ref, st_ref)):
        moved = dot(sort, src[...]).astype(BF16)
        for j in range(count):
            dst[j] = moved[piece * j : piece * j + piece]
    wide[...] = jnp.zeros(wide.shape, F32)
    wide[0:KW, :] = dw_ref[...].astype(F32)
    for i, row in enumerate(rows_in):
        wide[KW + i : KW + i + 1, :] = row[...].astype(F32).reshape(1, D // 4)
    narrow[...] = jnp.zeros(narrow.shape, F32)
    narrow[0:3, : A // 4] = b_in[...].astype(F32)
    narrow[3:4, : A // 4] = pb_in[...].astype(F32).reshape(1, A // 4)
    ffn[...] = jnp.zeros(ffn.shape, F32)
    ffn[0:1, :] = fb_in[...].astype(F32).reshape(1, D)
    kern[...] = jnp.zeros(kern.shape, F32)
    kern[:, : H * KW] = kern_in[...].astype(F32)


SMALL_SHAPES = [(16, D // 4), (8, 128), (8, D), (A // 4, 128)]


def setup(lengths, deal, hidden, teacher, smalls, count):
    rows = hidden.shape[0]
    vmem = pl.BlockSpec(memory_space=pltpu.VMEM)
    smem = pl.BlockSpec(memory_space=pltpu.SMEM)
    pieces = jax.ShapeDtypeStruct((count, rows // count, D), BF16)
    return pl.pallas_call(
        setup_body,
        out_shape=[
            pieces,
            pieces,
            jax.ShapeDtypeStruct((1, rows), jnp.int32),
            jax.ShapeDtypeStruct((SEQS + 6,), jnp.int32),
        ]
        + [jax.ShapeDtypeStruct(shape, F32) for shape in SMALL_SHAPES],
        in_specs=[smem] + [vmem] * (3 + len(smalls)),
        out_specs=[vmem] * 3 + [smem] + [vmem] * 4,
        compiler_params=pltpu.CompilerParams(vmem_limit_bytes=VMEM_LIMIT),
        name="setup",
    )(lengths, deal, hidden, teacher, *smalls)


N_SMALL = 4


def gather_body(count, spans, *refs):
    n = len(spans)
    inputs, refs = refs[: n + 2 + N_SMALL], refs[n + 2 + N_SMALL :]
    x_ref, t_ref = inputs[:2]
    shards = list(inputs[2 : 2 + n])
    own_small = list(inputs[2 + n :])
    out_ref, target_ref = refs[:2]
    fulls = list(refs[2 : 2 + n])
    vec_ref, small_ref, fb_ref, kw_ref = refs[2 + n : 6 + n]
    scratch = refs[6 + n :]
    all_small = scratch[:N_SMALL]
    local_sem, w_send, w_recv, pad_send, pad_recv = scratch[N_SMALL : N_SMALL + 5]
    sems = scratch[N_SMALL + 5 :]
    p = Place(count)
    k = lax.axis_index("wt")
    side = lax.rem(k, 2)
    core_mate = {"wt": k + 1 - 2 * side}
    far = lax.rem(k + 2, 4)
    far_mate = {"wt": far}

    def span(i, ref, index):
        if i >= n:
            return ref.at[index]
        axis, size = spans[i]
        window = pl.ds(pl.multiple_of(index * size, size), size)
        return ref.at[window] if axis == 0 else ref.at[:, window]

    shards += own_small
    fulls += all_small
    total = n + N_SMALL
    order = list(range(n, total)) + list(range(n))

    greet(p.others() + [(k >= 0, core_mate), (k >= 0, far_mate)])
    quarter, eighth = count // 4, count // 8
    cuts = [0, quarter, p.valid - quarter, p.valid - eighth, p.valid]
    parts = []
    for i, kind in enumerate((LinePart, LinePart, PairPart, PairPart)):
        first, end = cuts[i], cuts[i + 1]
        parts.append(
            kind(
                p,
                PieceNeeds(p, first, end - 1),
                x_ref.at[first:end],
                lambda j, first=first, end=end: out_ref.at[first:end, j],
                sems[2 * i],
                sems[2 * i + 1],
            )
        )
    low, high, *pairs = parts
    lines = [high, low]
    for part in pairs:
        part.across()
    for part in lines:
        part.start()
    for part in pairs:
        part.along()
    for i in order:
        held = span(i, fulls[i], k)
        remote(shards[i], held, w_send.at[0, i], w_recv.at[0, i], far_mate).start()
        remote(shards[i], held, w_send.at[1, i], w_recv.at[1, i], core_mate).start()

    def pad_copy(there):
        return remote(
            x_ref.at[p.valid :],
            out_ref.at[p.valid :, p.me],
            pad_send.at[there - p.valid],
            pad_recv.at[p.me],
            {"ctx": p.me * 0 + there},
        )

    def pads():
        for there in range(p.valid, count):

            @pl.when(p.me != there)
            def _(there=there):
                pad_copy(there).start()

    keeps = [pltpu.make_async_copy(x_ref, out_ref.at[:, p.me], local_sem.at[total])]
    for i in range(total):
        keeps.append(pltpu.make_async_copy(shards[i], span(i, fulls[i], k), local_sem.at[i]))
    for keep in keeps:
        keep.start()
    swap = Swap(p, t_ref, target_ref, sems[8], sems[9])

    def relay(i):
        held = span(i, fulls[i], far)
        remote(held, held, w_send.at[2, i], w_recv.at[0, i], core_mate).wait_recv()
        remote(held, held, w_send.at[2, i], w_recv.at[2, i], core_mate).start()

    for part in pairs:
        part.middle()
    done = 0
    for s in range(1, p.length):
        for part in lines + pairs:
            part.step(s)
        upto = total if s == p.length - 1 else min(total, done + 3)
        if s == p.length - 1:
            swap.start()
            pads()
        for i in range(done, upto):
            relay(order[i])
        done = upto
    for keep in keeps:
        keep.wait()
    for i in range(total):
        held = span(i, fulls[i], k)
        remote(shards[i], held, w_send.at[0, i], w_recv.at[0, i], far_mate).wait_send()
        remote(shards[i], held, w_send.at[1, i], w_recv.at[1, i], core_mate).wait()
        remote(held, held, w_send.at[2, i], w_recv.at[2, i], core_mate).wait()

    def spread(ref, step, shape):
        row = lax.broadcasted_iota(jnp.int32, shape, 0)
        column = lax.broadcasted_iota(jnp.int32, shape, 1)
        value = 0.0
        for index in range(4):
            move = jnp.where((column == row + step * index) & (row < step), 1.0, 0.0).astype(BF16)
            value += jnp.dot(ref[index].astype(BF16), move, preferred_element_type=F32)
        return value

    vec_ref[...] = spread(all_small[0], D // 4, (D // 4, D))
    small_ref[...] = spread(all_small[1], A // 4, (128, A))
    for index in range(4):
        fb_ref[index : index + 1, :] = all_small[2][index, 0:1, :]
        kw_ref[A // 4 * index : A // 4 * index + A // 4, :] = all_small[3][index].astype(BF16)
    for part in pairs + lines:
        part.finish()
    for there in range(p.valid, count):

        @pl.when(p.me != there)
        def _(there=there):
            pad_copy(there).wait_send()

    @pl.when(p.me >= p.valid)
    def _():
        for shift in range(1, count):
            source = lax.rem(p.me + shift, count)
            held = out_ref.at[p.valid :, source]
            remote(held, held, pad_send.at[0], pad_recv.at[source], p.mate).wait_recv()

    swap.finish()


def gather_inputs(pieces, targets, shards, axes, smalls, ctx_count):
    length = ctx_count // 2
    fulls, spans = [], []
    for shard, axis in zip(shards, axes):
        shape = list(shard.shape)
        spans.append((axis, shape[axis]))
        shape[axis] *= 4
        fulls.append(jax.ShapeDtypeStruct(tuple(shape), shard.dtype))
    n = len(shards)
    total = n + N_SMALL
    vmem = pl.BlockSpec(memory_space=pltpu.VMEM)
    hbm = pl.BlockSpec(memory_space=pl.ANY)
    results = pl.pallas_call(
        functools.partial(gather_body, ctx_count, spans),
        out_shape=[
            jax.ShapeDtypeStruct((ctx_count,) + pieces.shape, pieces.dtype),
            jax.ShapeDtypeStruct(targets.shape, targets.dtype),
        ]
        + fulls
        + [
            jax.ShapeDtypeStruct((16, D), F32),
            jax.ShapeDtypeStruct((8, A), F32),
            jax.ShapeDtypeStruct((4, D), F32),
            jax.ShapeDtypeStruct((A, 128), BF16),
        ],
        in_specs=[vmem] * (2 + n + len(smalls)),
        out_specs=[hbm] * (2 + n) + [vmem] * 4,
        scratch_shapes=[pltpu.VMEM((4,) + shape, F32) for shape in SMALL_SHAPES]
        + [
            pltpu.SemaphoreType.DMA((total + 1,)),
            pltpu.SemaphoreType.DMA((3, total)),
            pltpu.SemaphoreType.DMA((3, total)),
            pltpu.SemaphoreType.DMA((ctx_count // 8,)),
            pltpu.SemaphoreType.DMA((ctx_count,)),
        ]
        + part_sems(length) * 4
        + swap_sems(ctx_count),
        compiler_params=pltpu.CompilerParams(
            collective_id=0, has_side_effects=True, vmem_limit_bytes=VMEM_LIMIT
        ),
        name="gather_inputs",
    )(pieces, targets, *shards, *smalls)
    return results


class Sum:
    def __init__(self, bits, chunks, packed, bufs, out, send, recv):
        self.bits, self.chunks, self.packed, self.bufs, self.out = bits, chunks, packed, bufs, out
        self.send, self.recv = send, recv
        self.stages = 2 + bits
        self.last = self.stages + bits
        k = lax.axis_index("wt")
        me = lax.axis_index("ctx")
        self.core = lax.rem(k, 2)
        self.far = lax.div(k, 2)
        self.bit = [lax.rem(lax.div(me, 1 << b), 2) for b in range(bits)]
        self.targets = [{"wt": k + 1 - 2 * self.core}, {"wt": lax.rem(k + 2, 4)}]
        for b in range(bits):
            self.targets.append({"ctx": me + (1 << b) * (1 - 2 * self.bit[b])})

    def source(self, stage, c, kept):
        whole = slice(None)

        def pick(value):
            return value if kept else 1 - value

        if stage == 0:
            return self.packed.at[(whole, pick(self.core)) + (whole,) * self.bits + (c,)]
        if stage == 1:
            return self.bufs[0].at[c, pick(self.far)]
        b = stage - 2
        return self.bufs[stage - 1].at[(c,) + (whole,) * (self.bits - b - 1) + (pick(self.bit[b]),)]

    def spread(self, b, c, other):
        index = [self.bit[j] for j in range(b, -1, -1)]
        if other:
            index[0] = 1 - index[0]
        return self.out.at[(slice(None),) * (self.bits - 1 - b) + tuple(index) + (c,)]

    def place_own(self, c, value):
        self.out[tuple(self.bit[j] for j in range(self.bits - 1, -1, -1)) + (c,)] = value

    def copy(self, stage, c):
        if stage < self.stages:
            src, dst, target = self.source(stage, c, False), self.bufs[stage].at[c], self.targets[stage]
        else:
            b = self.bits - 1 - (stage - self.stages)
            src, dst, target = self.spread(b, c, False), self.spread(b, c, False), self.targets[2 + b]
        return remote(src, dst, self.send.at[stage, c], self.recv.at[stage, c], target)

    def start(self, stage, c):
        self.copy(stage, c).start()

    def take(self, stage, c):
        if stage >= self.stages:
            b = self.bits - 1 - (stage - self.stages)
            held = self.spread(b, c, True)
            remote(
                held, held, self.send.at[stage, c], self.recv.at[stage, c], self.targets[2 + b]
            ).wait_recv()
            return
        self.copy(stage, c).wait_recv()
        mine, sums = self.source(stage, c, True), self.bufs[stage].at[c]
        lead = sums.shape[:-2]
        total = 1
        for size in lead:
            total *= size

        def one(at, _):
            index, rest = [], at
            for size in reversed(lead):
                index.append(lax.rem(rest, size))
                rest = lax.div(rest, size)
            index = tuple(reversed(index))
            value = mine[index].astype(F32) + sums[index].astype(F32)
            sums[index] = value.astype(BF16)
            return 0

        if lead:
            lax.fori_loop(0, total, one, 0)
        else:
            sums[...] = (mine[...].astype(F32) + sums[...].astype(F32)).astype(BF16)

    def sent(self, stage, c):
        self.copy(stage, c).wait_send()

    def open(self):
        for c in range(min(4, self.chunks)):
            self.start(0, c)

    def across(self, first, end):
        for c in range(first, min(end, self.chunks)):
            self.take(0, c)
            self.start(1, c)
            if c + 4 < self.chunks:
                self.start(0, c + 4)


def sum_shapes(ctx_count, rows, size):
    bits = ctx_count.bit_length() - 1
    piece = min(size, rows // ctx_count)
    chunks = rows // ctx_count // piece
    twos = (2,) * bits
    bufs = [
        pltpu.VMEM((chunks, 2) + twos + (piece, D), BF16),
        pltpu.VMEM((chunks,) + twos + (piece, D), BF16),
    ]
    for b in range(bits):
        bufs.append(pltpu.VMEM((chunks,) + twos[b + 1 :] + (piece, D), BF16))
    tail = (chunks, piece, D)
    return bits, chunks, (2, 2) + twos + tail, twos + tail, bufs


def seg_of(position, bounds):
    seg = jnp.zeros(position.shape, jnp.int32)
    for i in range(SEQS):
        seg = seg + jnp.where(position >= bounds[i], 1, 0)
    return seg


def reach(bounds, first, last, group_rows):
    begin, end = jnp.int32(0), jnp.int32(group_rows)
    for i in range(SEQS):
        begin = jnp.where(bounds[i] <= first, bounds[i], begin)
    for i in reversed(range(SEQS)):
        end = jnp.where(bounds[i] > last, bounds[i], end)
    return begin, end


def half_masks(rows):
    lane = lax.broadcasted_iota(jnp.int32, (rows, 128), 1)
    low = jnp.where(lane < HD, 1.0, 0.0).astype(BF16)
    return low, (1.0 - low.astype(F32)).astype(BF16)


def dot_last(left, right):
    return lax.dot_general(left, right, (((1,), (1,)), ((), ())), preferred_element_type=F32)


def attend_body(tq, tk, bounds, q_ref, k_ref, v_ref, out_ref, lse_ref, m_ref, acc_ref):
    rows, group_rows = out_ref.shape[0], k_ref.shape[0]
    base = pl.multiple_of(bounds[SEQS], tq)
    q_masks, k_masks = half_masks(tq), half_masks(tk)
    lane = lax.broadcasted_iota(jnp.int32, (tq, 128), 1)
    low = lane < HD

    def tile(qi, _):
        q0 = pl.multiple_of(qi * tq, tq)
        first = pl.multiple_of(base + q0, tq)
        begin, end = reach(bounds, first, first + tq - 1, group_rows)
        q_seg = seg_of(first + lax.broadcasted_iota(jnp.int32, (tq, 1), 0), bounds)
        m_ref[...] = jnp.full(m_ref.shape, MASKED, F32)
        acc_ref[...] = jnp.zeros(acc_ref.shape, F32)

        def step(kt, _):
            k0 = pl.multiple_of(kt * tk, tk)
            k_seg = seg_of(k0 + lax.broadcasted_iota(jnp.int32, (1, tk), 1), bounds)
            bias = jnp.where(q_seg == k_seg, 0.0, MASKED)
            for pair in range(H // 2):
                cols = slice(128 * pair, 128 * pair + 128)
                q_pair = q_ref[pl.ds(first, tq), cols]
                k_pair = k_ref[pl.ds(k0, tk), cols]
                v_pair = v_ref[pl.ds(k0, tk), cols]
                for side in range(2):
                    head = 2 * pair + side
                    scores = dot_last(q_pair * q_masks[side], k_pair) + bias
                    old = m_ref[head]
                    new = jnp.maximum(old, jnp.max(scores, axis=1, keepdims=True))
                    weights = jnp.exp(scores - jnp.tile(new, (1, tk // 128)))
                    v_ones = v_pair * k_masks[side] + k_masks[1 - side]
                    acc_ref[head] = acc_ref[head] * jnp.exp(old - new) + jnp.dot(
                        weights.astype(BF16), v_ones, preferred_element_type=F32
                    )
                    m_ref[head] = new
            return 0

        lax.fori_loop(lax.div(begin, tk), lax.div(end + tk - 1, tk), step, 0)
        lse = jnp.zeros((tq, 128), F32)
        for pair in range(H // 2):
            left, right = acc_ref[2 * pair], acc_ref[2 * pair + 1]
            crossed = jnp.where(low, right, left)
            total = pltpu.roll(crossed, HD, 1)
            out_ref[pl.ds(q0, tq), 128 * pair : 128 * pair + 128] = jnp.where(low, left, right) / total
            lse = jnp.where(lane == 2 * pair, m_ref[2 * pair] + jnp.log(total), lse)
            lse = jnp.where(lane == 2 * pair + 1, m_ref[2 * pair + 1] + jnp.log(crossed), lse)
        lse_ref[pl.ds(q0, tq), :] = lse
        return 0

    lax.fori_loop(0, rows // tq, tile, 0)


def attend(bounds, query, keys, values, rows):
    tq, tk = min(256, rows), 512
    return pl.pallas_call(
        functools.partial(attend_body, tq, tk),
        out_shape=[
            jax.ShapeDtypeStruct((rows, A), F32),
            jax.ShapeDtypeStruct((rows, 128), F32),
        ],
        in_specs=[pl.BlockSpec(memory_space=pltpu.SMEM)]
        + [pl.BlockSpec(memory_space=pltpu.VMEM)] * 3,
        out_specs=[pl.BlockSpec(memory_space=pltpu.VMEM)] * 2,
        scratch_shapes=[pltpu.VMEM((H, tq, 128), F32), pltpu.VMEM((H, tq, 128), F32)],
        compiler_params=pltpu.CompilerParams(vmem_limit_bytes=VMEM_LIMIT),
        name="attend",
    )(bounds, query, keys, values)


def query_grads_body(tq, tk, bounds, q_ref, g_ref, stat_ref, k_ref, v_ref, out_ref, rep_ref):
    rows, group_rows = out_ref.shape[0], k_ref.shape[0]
    base = pl.multiple_of(bounds[SEQS], tq)
    q_masks, k_masks = half_masks(tq), half_masks(tk)

    def tile(qi, _):
        q0 = pl.multiple_of(qi * tq, tq)
        first = pl.multiple_of(base + q0, tq)
        begin, end = reach(bounds, first, first + tq - 1, group_rows)
        q_seg = seg_of(first + lax.broadcasted_iota(jnp.int32, (tq, 1), 0), bounds)
        stat = stat_ref[pl.ds(q0, tq), :]
        for head in range(H):
            rep_ref[head] = jnp.broadcast_to(stat[:, head : head + 1], (tq, 128))
            rep_ref[H + head] = jnp.broadcast_to(stat[:, 8 + head : 9 + head], (tq, 128))
        out_ref[pl.ds(q0, tq), :] = jnp.zeros((tq, A), F32)

        def step(kt, _):
            k0 = pl.multiple_of(kt * tk, tk)
            k_seg = seg_of(k0 + lax.broadcasted_iota(jnp.int32, (1, tk), 1), bounds)
            bias = jnp.where(q_seg == k_seg, 0.0, MASKED)
            for pair in range(H // 2):
                cols = slice(128 * pair, 128 * pair + 128)
                q_pair = q_ref[pl.ds(first, tq), cols]
                g_pair = g_ref[pl.ds(q0, tq), cols]
                k_pair = k_ref[pl.ds(k0, tk), cols]
                v_pair = v_ref[pl.ds(k0, tk), cols]
                total = jnp.zeros((tq, 128), F32)
                for side in range(2):
                    head = 2 * pair + side
                    scores = dot_last(q_pair * q_masks[side], k_pair) + bias
                    prob = jnp.exp(scores - jnp.tile(rep_ref[head], (1, tk // 128)))
                    back = dot_last(g_pair * q_masks[side], v_pair)
                    back = prob * (back - jnp.tile(rep_ref[H + head], (1, tk // 128)))
                    total = total + jnp.dot(
                        back.astype(BF16), k_pair * k_masks[side], preferred_element_type=F32
                    )
                out_ref[pl.ds(q0, tq), cols] += total
            return 0

        lax.fori_loop(lax.div(begin, tk), lax.div(end + tk - 1, tk), step, 0)
        return 0

    lax.fori_loop(0, rows // tq, tile, 0)


def query_grads(bounds, query, grads, stats, keys, values):
    rows = grads.shape[0]
    tq, tk = min(256, rows), 512
    return pl.pallas_call(
        functools.partial(query_grads_body, tq, tk),
        out_shape=jax.ShapeDtypeStruct((rows, A), F32),
        in_specs=[pl.BlockSpec(memory_space=pltpu.SMEM)]
        + [pl.BlockSpec(memory_space=pltpu.VMEM)] * 5,
        out_specs=pl.BlockSpec(memory_space=pltpu.VMEM),
        scratch_shapes=[pltpu.VMEM((2 * H, tq, 128), F32)],
        compiler_params=pltpu.CompilerParams(vmem_limit_bytes=VMEM_LIMIT),
        name="query_grads",
    )(bounds, query, grads, stats, keys, values)


def key_grads_body(tk, bounds, k_ref, v_ref, q_ref, g_ref, stat_ref, dk_ref, dv_ref):
    rows, group_rows = dk_ref.shape[0], q_ref.shape[0]
    tq = stat_ref.shape[2]
    base = pl.multiple_of(bounds[SEQS], tk)
    q_masks, k_masks = half_masks(tq), half_masks(tk)

    def tile(ki, _):
        k0 = pl.multiple_of(ki * tk, tk)
        first = pl.multiple_of(base + k0, tk)
        begin, end = reach(bounds, first, first + tk - 1, group_rows)
        k_seg = seg_of(first + lax.broadcasted_iota(jnp.int32, (tk, 1), 0), bounds)
        dk_ref[pl.ds(k0, tk), :] = jnp.zeros((tk, A), F32)
        dv_ref[pl.ds(k0, tk), :] = jnp.zeros((tk, A), F32)

        def step(qt, _):
            q0 = pl.multiple_of(qt * tq, tq)
            q_seg = seg_of(q0 + lax.broadcasted_iota(jnp.int32, (1, tq), 1), bounds)
            bias = jnp.where(k_seg == q_seg, 0.0, MASKED)
            for pair in range(H // 2):
                cols = slice(128 * pair, 128 * pair + 128)
                q_pair = q_ref[pl.ds(q0, tq), cols]
                g_pair = g_ref[pl.ds(q0, tq), cols]
                k_pair = k_ref[pl.ds(first, tk), cols]
                v_pair = v_ref[pl.ds(first, tk), cols]
                key_sum = jnp.zeros((tk, 128), F32)
                value_sum = jnp.zeros((tk, 128), F32)
                for side in range(2):
                    head = 2 * pair + side
                    scores = dot_last(k_pair * k_masks[side], q_pair) + bias
                    prob = jnp.exp(scores - stat_ref[qt, head : head + 1, :])
                    value_sum = value_sum + jnp.dot(
                        prob.astype(BF16), g_pair * q_masks[side], preferred_element_type=F32
                    )
                    back = dot_last(v_pair * k_masks[side], g_pair)
                    back = prob * (back - stat_ref[qt, 8 + head : 9 + head, :])
                    key_sum = key_sum + jnp.dot(
                        back.astype(BF16), q_pair * q_masks[side], preferred_element_type=F32
                    )
                dk_ref[pl.ds(k0, tk), cols] += key_sum
                dv_ref[pl.ds(k0, tk), cols] += value_sum
            return 0

        lax.fori_loop(lax.div(begin, tq), lax.div(end + tq - 1, tq), step, 0)
        return 0

    lax.fori_loop(0, rows // tk, tile, 0)


def key_grads(bounds, keys, values, queries, grads, stats):
    rows = stats.shape[2]
    tk = min(256, rows)
    return pl.pallas_call(
        functools.partial(key_grads_body, tk),
        out_shape=[jax.ShapeDtypeStruct((rows, A), F32)] * 2,
        in_specs=[pl.BlockSpec(memory_space=pltpu.SMEM)]
        + [pl.BlockSpec(memory_space=pltpu.VMEM)] * 5,
        out_specs=[pl.BlockSpec(memory_space=pltpu.VMEM)] * 2,
        compiler_params=pltpu.CompilerParams(vmem_limit_bytes=VMEM_LIMIT),
        name="key_grads",
    )(bounds, keys, values, queries, grads, stats)


def norm_back(grad_rows, normed, inverse, gain):
    scaled = grad_rows * gain
    return inverse * (
        scaled
        - jnp.mean(scaled, axis=1, keepdims=True)
        - normed * jnp.mean(scaled * normed, axis=1, keepdims=True)
    )


def dot_first(left, right):
    return lax.dot_general(left, right, (((0,), (0,)), ((), ())), preferred_element_type=F32)


def project_body(bounds, x_ref, w_ref, b_ref, q_ref, k_ref, v_ref):
    index = pl.program_id(0)

    @pl.when((index >= bounds[SEQS + 1]) & (index <= bounds[SEQS + 2]))
    def _():
        x = x_ref[...]
        query = (dot(x, w_ref[:, :A]) + b_ref[0:1, :]).astype(BF16).astype(F32)
        q_ref[...] = (query * (HD**-0.5)).astype(BF16)
        k_ref[...] = dot(x, w_ref[:, A : 2 * A]).astype(BF16)
        v_ref[...] = (dot(x, w_ref[:, 2 * A : 3 * A]) + b_ref[1:2, :]).astype(BF16)


def project(bounds, natural, w_in, smalls, rows):
    group_rows = natural.shape[0]

    def block(index, bounds):
        return (jnp.clip(index, bounds[SEQS + 1], bounds[SEQS + 2]), 0)

    def fixed(index, bounds):
        return (0, 0)

    return pl.pallas_call(
        project_body,
        out_shape=[jax.ShapeDtypeStruct((group_rows, A), BF16)] * 3,
        grid_spec=pltpu.PrefetchScalarGridSpec(
            num_scalar_prefetch=1,
            grid=(group_rows // rows,),
            in_specs=[
                pl.BlockSpec((rows, D), block),
                pl.BlockSpec((D, 3 * A), fixed),
                pl.BlockSpec((8, A), fixed),
            ],
            out_specs=[pl.BlockSpec((rows, A), block)] * 3,
        ),
        compiler_params=pltpu.CompilerParams(vmem_limit_bytes=VMEM_LIMIT),
        name="project",
    )(bounds, natural, w_in, smalls)


def tap_lanes(tap):
    row = lax.broadcasted_iota(jnp.int32, (128, A), 0)
    column = lax.broadcasted_iota(jnp.int32, (128, A), 1)
    return jnp.where(row == lax.div(column, HD) * KW + tap, 1.0, 0.0).astype(BF16)


def tap_pick(tap):
    row = lax.broadcasted_iota(jnp.int32, (A, 128), 0)
    column = lax.broadcasted_iota(jnp.int32, (A, 128), 1)
    first = row == lax.div(row, HD) * HD
    return jnp.where(first & (column == lax.div(row, HD) * KW + tap), 1.0, 0.0).astype(BF16)


def tap_weights(kw_ref, kb_ref, wide_ref, bias_ref):
    bias_ref[:, 0:128] = jnp.zeros((8, 128), F32)
    bias_ref[0:1, 0 : H * KW] = kb_ref[...].astype(F32)
    bias = bias_ref[:, 0:128].astype(BF16)
    for tap in range(KW):
        lanes = tap_lanes(tap)
        cols = slice(A * tap, A * tap + A)
        wide_ref[:, cols] = dot(kw_ref[...], lanes).astype(BF16)
        bias_ref[:, cols] = dot(bias, lanes)


def tap_near(bounds, group_rows, seg_ref, near_ref):
    span = near_ref.shape[1]
    position = bounds[SEQS] - RIM + lax.broadcasted_iota(jnp.int32, seg_ref.shape, 0)
    inside = (position >= 0) & (position < group_rows)
    seg_ref[...] = jnp.where(inside, seg_of(position, bounds), -1)
    seg = seg_ref[RIM // 2 : RIM // 2 + span, :]
    for tap in range(KW):
        shift = RIM // 2 - KW // 2 + tap
        near_ref[tap] = jnp.where((seg_ref[shift : shift + span, :] == seg) & (seg >= 0), 1.0, 0.0)


def tap_softmax(logits, bias_ref):
    parts = [logits[:, A * tap : A * tap + A] + bias_ref[0:1, A * tap : A * tap + A] for tap in range(KW)]
    largest = functools.reduce(jnp.maximum, parts)
    parts = [jnp.exp(part - largest) for part in parts]
    total = 1.0 / functools.reduce(jnp.add, parts)
    return [part * total for part in parts]


def wide3(value):
    return jnp.tile(value, (1, 3))


def conv_body(
    bounds, natural, w_ref, pw_ref, kw_ref, kb_ref, vec_ref, small_ref,
    out_ref, ext_ref, cv_ref, kc_ref, q_ref, cq_ref, sp_ref,
    extf_ref, seg_ref, near_ref, wide_ref, bias_ref, full_ref, sem,
):
    rows, group_rows = out_ref.shape[0], natural.shape[0]
    span = rows + RIM
    start = bounds[SEQS]
    copies = [
        pltpu.make_async_copy(
            natural.at[pl.ds(pl.multiple_of(jnp.maximum(start - RIM, 0), RIM), RIM)],
            ext_ref.at[0:RIM],
            sem.at[0],
        ),
        pltpu.make_async_copy(
            natural.at[pl.ds(pl.multiple_of(start, RIM), rows)], ext_ref.at[RIM : RIM + rows], sem.at[1]
        ),
        pltpu.make_async_copy(
            natural.at[pl.ds(pl.multiple_of(jnp.minimum(start + rows, group_rows - RIM), RIM), RIM)],
            ext_ref.at[RIM + rows : 2 * RIM + rows],
            sem.at[2],
        ),
    ]
    for copy in copies:
        copy.start()
    tap_weights(kw_ref, kb_ref, wide_ref, bias_ref)
    tap_near(bounds, group_rows, seg_ref, near_ref)
    for copy in copies:
        copy.wait()
    count = group_rows // rows
    place = lax.div(start, rows)
    padded = count - count // 8

    @pl.when((place == 0) | (place == padded))
    def _():
        ext_ref[0:RIM, :] = jnp.zeros((RIM, D), BF16)

    @pl.when((place == padded - 1) | (place == count - 1))
    def _():
        ext_ref[RIM + rows :, :] = jnp.zeros((RIM, D), BF16)

    ext = ext_ref[...]
    extf_ref[...] = ext.astype(F32)
    cv_ref[...] = dot(ext, w_ref[:, 3 * A :]) + small_ref[2:3, :]
    q_ref[...] = (dot(ext, w_ref[:, :A]) + small_ref[0:1, :]).astype(BF16).astype(F32)
    tile = span // 3
    for i in range(3):
        t0 = tile * i
        for c in range(6):
            cols = slice(128 * c, 128 * c + 128)
            window = extf_ref[t0 : t0 + tile + RIM, cols]
            total = 0.0
            for tap in range(KW):
                shift = RIM // 2 - KW // 2 + tap
                total += (
                    vec_ref[tap : tap + 1, cols]
                    * near_ref[tap, t0 : t0 + tile, :]
                    * window[shift : shift + tile]
                )
            sp_ref[t0 : t0 + tile, cols] = total.astype(BF16)
    kc_ref[...] = dot(sp_ref[...], pw_ref[...]) + small_ref[3:4, :]
    cq_ref[...] = (kc_ref[...] * q_ref[RIM // 2 : RIM // 2 + span, :]).astype(BF16)
    for i in range(3):
        t0 = tile * i
        kernel = tap_softmax(dot(cq_ref[t0 : t0 + tile, :], wide_ref[...]), bias_ref)
        window = cv_ref[t0 : t0 + tile + RIM, :]
        total = 0.0
        for tap in range(KW):
            shift = RIM // 2 - KW // 2 + tap
            total += kernel[tap] * wide3(near_ref[tap, t0 : t0 + tile, :]) * window[shift : shift + tile]
        full_ref[t0 : t0 + tile, :] = total
    out_ref[...] = full_ref[RIM // 2 : RIM // 2 + rows, :].astype(BF16)


def convolve(bounds, natural, w_in, pw, kw, kb, vectors, smalls, rows):
    span, wide = rows + RIM, rows + 2 * RIM
    vmem = pl.BlockSpec(memory_space=pltpu.VMEM)
    return pl.pallas_call(
        conv_body,
        out_shape=[
            jax.ShapeDtypeStruct((rows, A), BF16),
            jax.ShapeDtypeStruct((wide, D), BF16),
            jax.ShapeDtypeStruct((wide, A), F32),
            jax.ShapeDtypeStruct((span, A), F32),
            jax.ShapeDtypeStruct((wide, A), F32),
            jax.ShapeDtypeStruct((span, A), BF16),
            jax.ShapeDtypeStruct((span, D), BF16),
        ],
        in_specs=[pl.BlockSpec(memory_space=pltpu.SMEM), pl.BlockSpec(memory_space=pl.ANY)] + [vmem] * 6,
        out_specs=[vmem] * 7,
        scratch_shapes=[
            pltpu.VMEM((wide, D), F32),
            pltpu.VMEM((wide, 128), jnp.int32),
            pltpu.VMEM((KW, span, 128), F32),
            pltpu.VMEM((A, KW * A), BF16),
            pltpu.VMEM((8, KW * A), F32),
            pltpu.VMEM((span, A), F32),
            pltpu.SemaphoreType.DMA((3,)),
        ],
        compiler_params=pltpu.CompilerParams(vmem_limit_bytes=VMEM_LIMIT),
        name="convolve",
    )(bounds, natural, w_in, pw, kw, kb, vectors, smalls)


def norm_rows(x, gain, bias):
    centered = x - jnp.mean(x, axis=1, keepdims=True)
    inverse = lax.rsqrt(jnp.mean(centered * centered, axis=1, keepdims=True) + NORM_EPS)
    normed = centered * inverse
    return normed * gain + bias, normed, inverse


ROW_OUT_B, ROW_GAIN1, ROW_BIAS1, ROW_FFN_B, ROW_GAIN2, ROW_BIAS2 = range(KW, KW + 6)
FI_ROWS, FO_ROWS, OW_ROWS = 384, 384, 192
FIRST_PACK = 1024
SECOND_PACK = 512


def layer_body(
    bounds, attn_ref, lse_ref, conv_ref, ext_ref, tgt_ref, wo_ref, fi_ref, fo_ref, vec_ref, fb_ref,
    out_ref, gfirst_ref, gctx_ref, stat_ref, statt_ref, sums_ref, fbs_ref, pack_ref,
    ctx_s, low_s, act_s, slope_s, gfl_s, gpre_s, gproj_s,
):
    rows = out_ref.shape[0]
    tm = slope_s.shape[0]
    chunk = D
    wide = FF // NG
    part = D // NG
    row_of = lax.broadcasted_iota(jnp.int32, (A, 128), 0)
    column_of = lax.broadcasted_iota(jnp.int32, (A, 128), 1)
    head_pick = jnp.where(column_of == 8 + lax.div(row_of, HD), 1.0, 0.0).astype(BF16)
    sums_ref[...] = jnp.zeros(sums_ref.shape, F32)
    fbs_ref[...] = jnp.zeros(fbs_ref.shape, F32)

    def vec(row):
        return vec_ref[row : row + 1, :]

    def add_sum(row, value):
        sums_ref[row : row + 1, :] += jnp.sum(value, axis=0, keepdims=True)

    def tile(index, _):
        r0 = pl.multiple_of(index * tm, tm)
        here = pl.ds(r0, tm)
        attn = attn_ref[here, :]
        ctx_s[here, :A] = attn.astype(BF16)
        ctx_s[here, A:] = conv_ref[here, :]
        tokens = ext_ref[pl.ds(pl.multiple_of(r0 + RIM, RIM), tm), :].astype(F32)
        first = tokens + dot(ctx_s[here, :], wo_ref[...]) + vec(ROW_OUT_B)
        after, normed_one, inverse_one = norm_rows(first, vec(ROW_GAIN1), vec(ROW_BIAS1))
        low_s[here, :] = after.astype(BF16)
        results = []
        for g in range(NG):
            low = low_s[here, part * g : part * g + part]
            total = 0.0
            for c in range(wide // chunk):
                span = slice(chunk * c, chunk * c + chunk)
                whole = slice(wide * g + chunk * c, wide * g + chunk * c + chunk)
                pre = dot(low, fi_ref[g, :, span]) + fb_ref[2 * g + c : 2 * g + c + 1, :]
                phi = 0.5 * (1.0 + lax.erf(pre * ROOT_HALF))
                act = (pre * phi).astype(BF16)
                act_s[here, whole] = act
                slope_s[:, whole] = phi + pre * DENSITY_NORM * jnp.exp(-0.5 * pre * pre)
                total += dot(act, fo_ref[g, span, :])
            results.append(total)
        second = after + jnp.concatenate(results, axis=1) + vec(ROW_FFN_B)
        result, normed_two, inverse_two = norm_rows(second, vec(ROW_GAIN2), vec(ROW_BIAS2))
        out_ref[here, :] = result.astype(BF16)
        seg = seg_of(bounds[SEQS] + r0 + lax.broadcasted_iota(jnp.int32, (tm, 1), 0), bounds)
        error = jnp.where(seg < SEQS, result - tgt_ref[here, :].astype(F32), 0.0)
        add_sum(6, error * error)
        add_sum(4, error * normed_two)
        add_sum(5, error)
        grad_second = norm_back(error, normed_two, inverse_two, vec(ROW_GAIN2))
        gfl = grad_second.astype(BF16)
        gfl_s[here, :] = gfl
        add_sum(3, gfl.astype(F32))
        grads = []
        for g in range(NG):
            total = 0.0
            for c in range(wide // chunk):
                span = slice(chunk * c, chunk * c + chunk)
                whole = slice(wide * g + chunk * c, wide * g + chunk * c + chunk)
                gact = dot_last(gfl_s[here, part * g : part * g + part], fo_ref[g, span, :])
                gpre = (gact * slope_s[:, whole]).astype(BF16)
                gpre_s[here, whole] = gpre
                fbs_ref[2 * g + c : 2 * g + c + 1, :] += jnp.sum(gpre.astype(F32), axis=0, keepdims=True)
                total += dot_last(gpre, fi_ref[g, :, span])
            grads.append(total)
        grad_after = jnp.concatenate(grads, axis=1) + grad_second
        add_sum(1, grad_after * normed_one)
        add_sum(2, grad_after)
        grad_first = norm_back(grad_after, normed_one, inverse_one, vec(ROW_GAIN1))
        gfirst_ref[here, :] = grad_first
        gproj = grad_first.astype(BF16)
        gproj_s[here, :] = gproj
        add_sum(0, gproj.astype(F32))
        gctx = dot_last(gproj, wo_ref[...]).astype(BF16)
        gctx_ref[here, :] = gctx
        product = gctx[:, :A].astype(F32) * attn
        high = product.astype(BF16)
        rest = (product - high.astype(F32)).astype(BF16)
        stat = lse_ref[here, :] + dot(high, head_pick) + dot(rest, head_pick)
        stat_ref[here, :] = stat
        return 0

    lax.fori_loop(0, rows // tm, tile, 0)
    statt_ref[...] = stat_ref[...].T[:16]
    for g in range(NG):
        for half in range(2):
            whole = slice(wide * g + D * half, wide * g + D * half + D)
            grad = dot_first(low_s[:, part * g : part * g + part], gpre_s[:, whole]).astype(BF16)
            r0 = 96 * (2 * g + half)
            for k in range(4):
                pack_ref[k, r0 : r0 + 96, :] = grad[96 * k : 96 * k + 96]
        for k in range(4):
            grad = dot_first(
                act_s[:, wide * g + A * k : wide * g + A * k + A], gfl_s[:, part * g : part * g + part]
            )
            pack_ref[k, FI_ROWS : FI_ROWS + FO_ROWS, part * g : part * g + part] = grad.astype(BF16)
    grad = dot_first(ctx_s[...], gproj_s[...]).astype(BF16)
    r0 = FI_ROWS + FO_ROWS
    for k in range(4):
        pack_ref[k, r0 : r0 + OW_ROWS, :] = grad[OW_ROWS * k : OW_ROWS * k + OW_ROWS]
        pack_ref[k, r0 + OW_ROWS :, :] = jnp.zeros((FIRST_PACK - r0 - OW_ROWS, D), BF16)


def layer(bounds, attn, lse, conv, ext, target, wo, fi, fo, vectors, fb):
    rows = attn.shape[0]
    tm = min(256, rows)
    vmem = pl.BlockSpec(memory_space=pltpu.VMEM)
    return pl.pallas_call(
        layer_body,
        out_shape=[
            jax.ShapeDtypeStruct((rows, D), BF16),
            jax.ShapeDtypeStruct((rows, D), F32),
            jax.ShapeDtypeStruct((rows, D), BF16),
            jax.ShapeDtypeStruct((rows, 128), F32),
            jax.ShapeDtypeStruct((16, rows), F32),
            jax.ShapeDtypeStruct((8, D), F32),
            jax.ShapeDtypeStruct((4, D), F32),
            jax.ShapeDtypeStruct((4, FIRST_PACK, D), BF16),
        ],
        in_specs=[pl.BlockSpec(memory_space=pltpu.SMEM)] + [vmem] * 10,
        out_specs=[vmem] * 8,
        scratch_shapes=[
            pltpu.VMEM((rows, D), BF16),
            pltpu.VMEM((rows, D), BF16),
            pltpu.VMEM((rows, FF), BF16),
            pltpu.VMEM((tm, FF), F32),
            pltpu.VMEM((rows, D), BF16),
            pltpu.VMEM((rows, FF), BF16),
            pltpu.VMEM((rows, D), BF16),
        ],
        compiler_params=pltpu.CompilerParams(vmem_limit_bytes=VMEM_LIMIT),
        name="layer",
    )(bounds, attn, lse, conv, ext, target, wo, fi, fo, vectors, fb)


TAIL_ROWS = 128


def middle_body(
    count, sums, *refs, group_rows
):
    bits, chunks = sums
    (
        bounds, g_ref, stat_ref, res_ref, pack_ref,
        ext_ref, cv_ref, kc_ref, q_ref, cq_ref, sp_ref, pw_ref, kw_ref, kb_ref, vec_ref,
        out_ref, all_ref, dealt_ref, own_ref, gq_ref, gcv_ref, gtc_ref, tail_ref, sums_ref, bsum_ref,
        edge_ref, extf_ref, seg_ref, near_ref, wide_ref, bias_ref, gc_ref, pc_ref, glc_ref, gsp_ref,
        *rest,
    ) = refs
    bufs, rest = rest[: 2 + bits], rest[2 + bits :]
    sum_send, sum_recv, local_sem, edge_send, edge_recv, *sems = rest
    p = Place(count)
    rows = g_ref.shape[0]
    span = rows + RIM
    rim = RIM // 2
    place = p.me
    total = Sum(bits, chunks, pack_ref, bufs, None, sum_send, sum_recv)
    early = rows - 3 * rows // 8
    low = {"ctx": lax.rem(p.me + count - 1, count)}
    high = {"ctx": lax.rem(p.me + 1, count)}
    has_low, has_high = p.me > 0, p.me < count - 1
    greet(p.others() + [(p.me >= 0, target) for target in total.targets[:2]])
    needs = BlockNeeds(p)
    pair = PairPart(p, needs, g_ref.at[early:, :A], lambda j: out_ref.at[j, early:], sems[0], sems[1])
    line = LinePart(p, needs, g_ref.at[:early, :A], lambda j: out_ref.at[j, :early], sems[2], sems[3])
    stats = LinePart(p, needs, stat_ref, lambda j: all_ref.at[j], sems[4], sems[5])
    swap = Swap(p, res_ref, dealt_ref, sems[6], sems[7])

    def to_low():
        return remote(g_ref.at[:RIM, A:], edge_ref.at[1], edge_send.at[0], edge_recv.at[1], low)

    def to_high():
        return remote(g_ref.at[rows - RIM :, A:], edge_ref.at[0], edge_send.at[1], edge_recv.at[0], high)

    def advance(t):
        for c in range(chunks):
            stage = t - c
            if 1 <= stage <= total.stages:
                total.take(stage - 1, c)
                if stage < total.stages:
                    total.start(stage, c)
                else:
                    own_ref[c] = bufs[stage - 1][c]

    @pl.when(has_low)
    def _():
        to_low().start()

    @pl.when(has_high)
    def _():
        to_high().start()

    total.open()
    parts = [stats, line, pair]
    stats.start()
    pair.across()
    line.start()
    pair.along()
    keeps = [
        pltpu.make_async_copy(g_ref.at[:, :A], out_ref.at[p.me], local_sem.at[0]),
        pltpu.make_async_copy(stat_ref, all_ref.at[p.me], local_sem.at[1]),
    ]
    for keep in keeps:
        keep.start()
    advance(1)
    tap_weights(kw_ref, kb_ref, wide_ref, bias_ref)
    pair.middle()
    tap_near(bounds, group_rows, seg_ref, near_ref)
    extf_ref[...] = ext_ref[...].astype(F32)

    @pl.when(has_low)
    def _():
        to_low().wait_send()
        to_high().wait_recv()

    @pl.when(has_high)
    def _():
        to_high().wait_send()
        to_low().wait_recv()

    gc_ref[0:rim, :] = jnp.where(place > 0, edge_ref[0].astype(F32)[RIM - rim :], 0.0)
    gc_ref[rim : rim + rows, :] = g_ref[:, A:].astype(F32)
    gc_ref[rim + rows :, :] = jnp.where(place < count - 1, edge_ref[1].astype(F32)[:rim], 0.0)
    blocks = jnp.where(
        lax.div(lax.broadcasted_iota(jnp.int32, (128, 128), 0), HD)
        == lax.div(lax.broadcasted_iota(jnp.int32, (128, 128), 1), HD),
        1.0,
        0.0,
    ).astype(BF16)
    tile = span // 3

    def tap_tile(i):
        t0 = tile * i
        here = slice(t0, t0 + tile)
        kernel = tap_softmax(dot(cq_ref[here, :], wide_ref[...]), bias_ref)
        window = cv_ref[t0 : t0 + tile + RIM, :]
        grad = gc_ref[here, :]
        inner = []
        mean = 0.0
        for tap in range(KW):
            shift = rim - KW // 2 + tap
            near = wide3(near_ref[tap, here, :])
            product = (grad * window[shift : shift + tile]).astype(BF16)
            terms = jnp.concatenate(
                [dot(product[:, 128 * c : 128 * c + 128], blocks) for c in range(3)], axis=1
            )
            terms = terms * near
            inner.append(terms)
            mean += kernel[tap] * terms
            pc_ref[tap, here, :] = kernel[tap] * near * grad
        picked = 0.0
        for tap in range(KW):
            logit = (kernel[tap] * (inner[tap] - mean)).astype(BF16)
            picked += dot(logit, tap_pick(tap))
        glc_ref[here, :] = picked.astype(BF16)

    tap_tile(0)
    for part in parts:
        part.step(1)
    advance(2)
    tap_tile(1)
    for s in range(2, p.length):
        for part in parts:
            part.step(s)
        if s == 2:
            swap.start()
            advance(3)
            tap_tile(2)
    advance(4)
    back = dot_last(glc_ref[...], kw_ref[...])
    query = q_ref[rim : rim + span, :]
    row = lax.broadcasted_iota(jnp.int32, (span, 1), 0)
    own = (row >= rim) & (row < rim + rows)
    grad_kc = (back * query).astype(BF16)
    gsp_ref[...] = dot_last(grad_kc, pw_ref[...])
    gq_ref[...] = (back * kc_ref[...])[rim : rim + rows]
    own_kc = jnp.where(own, grad_kc.astype(F32), 0.0)
    own_logits = jnp.where(own, glc_ref[...].astype(F32), 0.0)
    grad_pw = dot_first(sp_ref[...], own_kc.astype(BF16)).astype(BF16)
    grad_kern = dot_first(cq_ref[...], own_logits.astype(BF16)).astype(BF16)
    for k in range(4):
        for half in range(2):
            r0 = 192 * k + 96 * half
            tail_ref[k, 0:96, A * half : A * half + A] = grad_pw[r0 : r0 + 96]
        for m in range(6):
            r0 = 96 * k + 16 * m
            tail_ref[k, 96:112, 128 * m : 128 * m + 128] = grad_kern[r0 : r0 + 16]
        tail_ref[k, 112:, :] = jnp.zeros((TAIL_ROWS - 112, D), BF16)
    bsum_ref[...] = jnp.zeros(bsum_ref.shape, F32)
    bsum_ref[0:1, :] = jnp.sum(own_kc, axis=0, keepdims=True)
    bsum_ref[1:2, 0:128] = jnp.sum(own_logits, axis=0, keepdims=True)
    advance(5)
    sums_ref[...] = jnp.zeros(sums_ref.shape, F32)
    step = 128
    for s0 in range(0, rows, step):
        for c in range(6):
            cols = slice(128 * c, 128 * c + 128)
            grads = gsp_ref[s0 + rim : s0 + rim + step, cols]
            tokens = extf_ref[s0 + rim : s0 + rim + step + RIM, cols]
            spread = gsp_ref[s0 : s0 + step + RIM, cols]
            sofar = 0.0
            for tap in range(KW):
                shift = rim - KW // 2 + tap
                value = near_ref[tap, s0 + rim : s0 + rim + step, :] * grads * tokens[shift : shift + step]
                sums_ref[tap : tap + 1, cols] += jnp.sum(value, axis=0, keepdims=True)
                shift = rim + KW // 2 - tap
                moved = near_ref[tap, s0 : s0 + step + RIM, :] * spread
                sofar += vec_ref[tap : tap + 1, cols] * moved[shift : shift + step]
            gtc_ref[s0 : s0 + step, cols] = sofar
        for c in range(3):
            cols = slice(128 * c, 128 * c + 128)
            sofar = 0.0
            for tap in range(KW):
                shift = rim + KW // 2 - tap
                sofar += pc_ref[tap, s0 : s0 + step + RIM, cols][shift : shift + step]
            gcv_ref[s0 : s0 + step, cols] = sofar.astype(BF16)
        if s0 == rows // 2 - step:
            advance(6)
    for t in range(7, chunks + total.stages):
        advance(t)
    for keep in keeps:
        keep.wait()
    for part in parts:
        part.finish()
    swap.finish()
    for stage in range(total.stages):
        for c in range(chunks):
            total.sent(stage, c)


def middle(bounds, group_rows, ctx_count, grads, stats, results, pack, *args):
    length = ctx_count // 2
    rows = grads.shape[0]
    span, wide = rows + RIM, rows + 2 * RIM
    bits, chunks, packed_shape, out_shape, bufs = sum_shapes(ctx_count, pack.shape[1], 32)
    vmem = pl.BlockSpec(memory_space=pltpu.VMEM)
    hbm = pl.BlockSpec(memory_space=pl.ANY)
    return pl.pallas_call(
        functools.partial(middle_body, ctx_count, (bits, chunks), group_rows=group_rows),
        out_shape=[
            jax.ShapeDtypeStruct((ctx_count, rows, A), grads.dtype),
            jax.ShapeDtypeStruct((ctx_count,) + stats.shape, stats.dtype),
            jax.ShapeDtypeStruct(results.shape, results.dtype),
            jax.ShapeDtypeStruct(out_shape[-3:], BF16),
            jax.ShapeDtypeStruct((rows, A), F32),
            jax.ShapeDtypeStruct((rows, A), BF16),
            jax.ShapeDtypeStruct((rows, D), F32),
            jax.ShapeDtypeStruct((4, TAIL_ROWS, D), BF16),
            jax.ShapeDtypeStruct((16, D), F32),
            jax.ShapeDtypeStruct((8, A), F32),
        ],
        in_specs=[pl.BlockSpec(memory_space=pltpu.SMEM)] + [vmem] * (len(args) + 4),
        out_specs=[hbm] * 3 + [vmem] * 7,
        scratch_shapes=[
            pltpu.VMEM((2, RIM, A), BF16),
            pltpu.VMEM((wide, D), F32),
            pltpu.VMEM((wide, 128), jnp.int32),
            pltpu.VMEM((KW, span, 128), F32),
            pltpu.VMEM((A, KW * A), BF16),
            pltpu.VMEM((8, KW * A), F32),
            pltpu.VMEM((span, A), F32),
            pltpu.VMEM((KW, span, A), F32),
            pltpu.VMEM((span, 128), BF16),
            pltpu.VMEM((span, D), F32),
        ]
        + bufs
        + [
            pltpu.SemaphoreType.DMA((2 + bits, chunks)),
            pltpu.SemaphoreType.DMA((2 + bits, chunks)),
            pltpu.SemaphoreType.DMA((2,)),
            pltpu.SemaphoreType.DMA((2,)),
            pltpu.SemaphoreType.DMA((2,)),
        ]
        + part_sems(length) * 3
        + swap_sems(ctx_count),
        compiler_params=pltpu.CompilerParams(
            collective_id=1, has_side_effects=True, vmem_limit_bytes=VMEM_LIMIT
        ),
        name="middle",
    )(bounds, grads, stats, results, pack.reshape(packed_shape), *args)


def ending_body(count, sums, *refs):
    bits, second_chunks = sums
    (
        dq_ref, dk_ref, dv_ref, gq_ref, gcv_ref, gtc_ref, gfirst_ref, ext_ref, w_ref, tail_ref, own_ref,
        tap_ref, bsum_ref, layer_ref, ffn_ref,
        first_ref, second_ref, sum_ref, dealt_ref,
        gm_ref, gtok_ref, pack_ref, f_bufs, *rest,
    ) = refs
    bufs, rest = rest[: 2 + bits], rest[2 + bits :]
    first_send, first_recv, second_send, second_recv, f_send, f_recv, keep_sem, swap_send, swap_recv = rest
    p = Place(count)
    rows = gm_ref.shape[0]
    piece = pack_ref.shape[-2]
    first = LinePart(p, AllNeeds(p), own_ref, lambda j: first_ref.at[j], first_send, first_recv)
    second = Sum(bits, second_chunks, pack_ref, bufs, second_ref, second_send, second_recv)
    swap = Swap(p, gtok_ref, dealt_ref, swap_send, swap_recv)
    stages, last = second.stages, second.last
    greet(p.others() + [(p.me >= 0, target) for target in second.targets[:2]])
    first.start()
    keep = pltpu.make_async_copy(own_ref, first_ref.at[p.me], keep_sem)
    keep.start()

    def store(k, r0, value):
        for at in range(0, value.shape[0], piece):
            row = (r0 + at) // piece
            index = []
            rest, c = row // second_chunks, row % second_chunks
            for b in range(bits):
                index.insert(0, rest % 2)
                rest //= 2
            pack_ref[(k // 2, k % 2) + tuple(index) + (c,)] = value[at : at + piece]

    gm_ref[:, :A] = (dq_ref[...] * (HD**-0.5) + gq_ref[...]).astype(BF16)
    gm_ref[:, A : 2 * A] = dk_ref[...].astype(BF16)
    gm_ref[:, 2 * A : 3 * A] = dv_ref[...].astype(BF16)
    gm_ref[:, 3 * A :] = gcv_ref[...]
    for half in range(2):
        grad = dot_first(ext_ref[RIM : RIM + rows, :], gm_ref[:, D * half : D * half + D]).astype(BF16)
        for k in range(4):
            store(k, 192 * half, grad[192 * k : 192 * k + 192])
    for k in range(4):
        store(k, 384, tail_ref[k])
    second.open()
    second.across(0, second_chunks)
    first.step(1)
    f_bufs[0, 0] = jnp.zeros(f_bufs.shape[2:], F32)
    f_bufs[0, 0, 0:KW, :] = tap_ref[0:KW, :]
    f_bufs[0, 0, KW : KW + 7, :] = layer_ref[0:7, :]
    f_bufs[0, 0, 16:20, :] = ffn_ref[...]
    f_bufs[0, 0, 20:21, :A] = jnp.sum(gm_ref[:, :A].astype(F32), axis=0, keepdims=True)
    f_bufs[0, 0, 20:21, A:] = jnp.sum(gm_ref[:, 2 * A : 3 * A].astype(F32), axis=0, keepdims=True)
    f_bufs[0, 0, 21:22, :A] = jnp.sum(gm_ref[:, 3 * A :].astype(F32), axis=0, keepdims=True)
    f_bufs[0, 0, 21:22, A:] = bsum_ref[0:1, :]
    f_bufs[0, 0, 22:23, :A] = bsum_ref[1:2, :]

    def f_copy(stage):
        return remote(
            f_bufs.at[0, stage], f_bufs.at[1, stage], f_send.at[stage], f_recv.at[stage], second.targets[stage]
        )

    f_copy(0).start()
    grad = dot_last(gm_ref[...], w_ref[...]) + gfirst_ref[...] + gtc_ref[...]
    size = rows // count
    for j in range(count):
        gtok_ref[j] = grad[size * j : size * j + size].astype(BF16)
    swap.start()
    for t in range(1, second_chunks + last - 1):
        if 2 <= t + 1 < p.length:
            first.step(t + 1)
        for c in reversed(range(second_chunks)):
            stage = t - c + 1
            if not 2 <= stage <= last:
                continue
            second.take(stage - 1, c)
            if stage == stages:
                second.place_own(c, bufs[stage - 1][c])
            if stage < last:
                second.start(stage, c)
        if t <= stages:
            f_copy(t - 1).wait_recv()
            value = f_bufs[0, t - 1] + f_bufs[1, t - 1]
            if t < stages:
                f_bufs[0, t] = value
                f_copy(t).start()
            else:
                sum_ref[...] = value
    for s in range(second_chunks + last, p.length):
        first.step(s)
    first.finish()
    keep.wait()
    for stage in range(last):
        for c in range(second_chunks):
            second.sent(stage, c)
    for stage in range(stages):
        f_copy(stage).wait_send()
    swap.finish()


def ending(ctx_count, *args):
    rows = args[0].shape[0]
    bits, second_chunks, packed_shape, second_shape, bufs = sum_shapes(ctx_count, SECOND_PACK, 16)
    vmem = pl.BlockSpec(memory_space=pltpu.VMEM)
    pieces = (ctx_count, rows // ctx_count, D)
    first, second, totals, moved = pl.pallas_call(
        functools.partial(ending_body, ctx_count, (bits, second_chunks)),
        out_shape=[
            jax.ShapeDtypeStruct((ctx_count, FIRST_PACK // ctx_count, D), BF16),
            jax.ShapeDtypeStruct(second_shape, BF16),
            jax.ShapeDtypeStruct((24, D), F32),
            jax.ShapeDtypeStruct(pieces, BF16),
        ],
        in_specs=[vmem] * len(args),
        out_specs=[vmem] * 4,
        scratch_shapes=[
            pltpu.VMEM((rows, 4 * A), BF16),
            pltpu.VMEM(pieces, BF16),
            pltpu.VMEM(packed_shape, BF16),
            pltpu.VMEM((2, 2 + bits, 24, D), F32),
        ]
        + bufs
        + part_sems(ctx_count // 2)
        + [
            pltpu.SemaphoreType.DMA((2 + 2 * bits, second_chunks)),
            pltpu.SemaphoreType.DMA((2 + 2 * bits, second_chunks)),
            pltpu.SemaphoreType.DMA((2 + bits,)),
            pltpu.SemaphoreType.DMA((2 + bits,)),
            pltpu.SemaphoreType.DMA,
        ]
        + swap_sems(ctx_count),
        compiler_params=pltpu.CompilerParams(
            collective_id=2, has_side_effects=True, vmem_limit_bytes=VMEM_LIMIT
        ),
        name="ending",
    )(*args)
    return first.reshape(-1, D), second.reshape(-1, D), totals, moved.reshape(rows, D)


def finish_body(
    place, arrange_ref, out_in, tok_in, first_ref, second_ref, sum_ref,
    out_ref, tok_ref, w_ref, b_ref, dw_ref, pw_ref, pb_ref, kern_ref, vec_ref, ow_ref, fi_ref, fb_ref, fo_ref,
    loss_ref, kb_ref,
):
    rows = out_ref.shape[0]
    slot = lax.broadcasted_iota(jnp.int32, (rows, rows), 0)
    sort = jnp.where(slot == arrange_ref[...], 1.0, 0.0).astype(BF16)
    out_ref[...] = dot_first(sort, out_in[...]).astype(BF16)
    tok_ref[...] = dot_first(sort, tok_in[...])
    for half in range(2):
        w_ref[:, D * half : D * half + D] = second_ref[192 * half : 192 * half + 192, :].astype(F32)
        pw_ref[96 * half : 96 * half + 96, :] = second_ref[384:480, A * half : A * half + A].astype(F32)
    for m in range(6):
        kern_ref[16 * m : 16 * m + 16, :] = second_ref[480:496, 128 * m : 128 * m + H * KW].astype(F32)
    for g in range(NG):
        for half in range(2):
            r0 = 96 * (2 * g + half)
            fi_ref[g, :, D * half : D * half + D] = first_ref[r0 : r0 + 96, :].astype(F32)
        fo_ref[g] = first_ref[384:768, A * g : A * g + A].astype(F32)
    ow_ref[...] = first_ref[768:960, :].astype(F32)
    total = jnp.sum(sum_ref[15:16, :], axis=1, keepdims=True)
    loss_ref[...] = total / (place[SEQS + 5].astype(F32) * D)
    kb_ref[...] = sum_ref[22:23, 0 : H * KW]
    for k in range(4):

        @pl.when(place[SEQS + 4] == k)
        def _(k=k):
            cols = slice(D // 4 * k, D // 4 * k + D // 4)
            dw_ref[...] = sum_ref[0:KW, cols]
            vec_ref[...] = sum_ref[KW : KW + 6, cols]
            fb_ref[...] = sum_ref[16 + k : 17 + k, :]
            part = slice(A // 4 * k, A // 4 * k + A // 4)
            second = slice(A + A // 4 * k, A + A // 4 * k + A // 4)
            b_ref[0:1, :] = sum_ref[20:21, part]
            b_ref[1:2, :] = sum_ref[20:21, second]
            b_ref[2:3, :] = sum_ref[21:22, part]
            pb_ref[...] = sum_ref[21:22, second]


def finish(place, arrange, *args):
    rows = args[0].shape[0]
    vmem = pl.BlockSpec(memory_space=pltpu.VMEM)
    shapes = [
        (rows, D), (D // 4, 4 * A), (3, A // 4), (KW, D // 4), (D // 4, A), (1, A // 4), (A // 4, H * KW),
        (6, D // 4), (D // 4, D), (NG, A // 4, FF // NG), (1, D), (NG, A, A), (1, 1), (1, H * KW),
    ]
    return pl.pallas_call(
        finish_body,
        out_shape=[jax.ShapeDtypeStruct((rows, D), BF16)] + [jax.ShapeDtypeStruct(shape, F32) for shape in shapes],
        in_specs=[pl.BlockSpec(memory_space=pltpu.SMEM)] + [vmem] * (len(args) + 1),
        out_specs=[vmem] * 15,
        compiler_params=pltpu.CompilerParams(vmem_limit_bytes=VMEM_LIMIT),
        name="finish",
    )(place, arrange, *args)


def local(
    hidden,
    teacher,
    lengths,
    deal,
    w_in,
    b_in,
    dw_kernel,
    pw_weight,
    pw_bias,
    kern_weight,
    kern_bias,
    out_weight,
    out_bias,
    norm1_gain,
    norm1_bias,
    ffn_in,
    ffn_in_bias,
    ffn_out,
    ffn_out_bias,
    norm2_gain,
    norm2_bias,
):
    rows = hidden.shape[1]
    ctx_count = lax.axis_size("ctx")
    group_rows = rows * ctx_count
    piece_rows = rows // ctx_count
    sorted_hidden, sorted_teacher, arrange, bounds, *smalls = setup(
        lengths, deal, hidden[0], teacher[0],
        [
            dw_kernel, out_bias, norm1_gain, norm1_bias, ffn_out_bias, norm2_gain, norm2_bias, ffn_in_bias,
            b_in, pw_bias, kern_weight,
        ],
        ctx_count,
    )
    pieces_shape = (ctx_count, piece_rows, D)
    natural, target, full_w_in, full_pw, full_out_w, full_ffn_in, full_ffn_out, vectors, smalls, ffn_in_b, full_kern = (
        gather_inputs(
            sorted_hidden,
            sorted_teacher,
            (w_in, pw_weight, out_weight, ffn_in, ffn_out),
            (0, 0, 0, 1, 1),
            smalls,
            ctx_count,
        )
    )
    natural = natural.reshape(group_rows, D)
    target = target.reshape(rows, D)
    kern_b = kern_bias[None]

    all_q8, all_keys, all_values = project(bounds, natural, full_w_in, smalls, rows)
    conv_out, extended, conv_value, key_conv, query_ext, conv_query, spread = convolve(
        bounds, natural, full_w_in, full_pw, full_kern, kern_b, vectors, smalls, rows
    )
    attn_out, lse = attend(bounds, all_q8, all_keys, all_values, rows)
    result, grad_first, grad_context, stats, stats_t, layer_sums, ffn_in_sums, first_pack = layer(
        bounds, attn_out, lse, conv_out, extended, target,
        full_out_w, full_ffn_in, full_ffn_out, vectors, ffn_in_b,
    )
    (
        all_grads, all_stats, output, first_own, grad_query_conv, grad_cov, grad_tokens_conv, tail, tap_sums,
        bias_sums,
    ) = middle(
        bounds, group_rows, ctx_count, grad_context, stats_t, result.reshape(pieces_shape), first_pack,
        extended, conv_value, key_conv, query_ext, conv_query, spread, full_pw, full_kern, kern_b, vectors,
    )
    grad_query = query_grads(bounds, all_q8, grad_context, stats, all_keys, all_values)
    grad_keys, grad_values = key_grads(
        bounds, all_keys, all_values, all_q8, all_grads.reshape(group_rows, A), all_stats
    )
    first, second, totals, moved = ending(
        ctx_count, grad_query, grad_keys, grad_values, grad_query_conv, grad_cov, grad_tokens_conv, grad_first,
        extended, full_w_in, tail, first_own.reshape(-1, D), tap_sums, bias_sums, layer_sums, ffn_in_sums,
    )
    (
        dealt_out, dealt_grad, g_w_in, g_b_in, g_dw, g_pw, g_pw_b, g_kern, g_vec, g_out, g_ffn_in, g_ffn_in_b,
        g_ffn_out, loss, g_kern_b,
    ) = finish(
        bounds, arrange,
        output.reshape(rows, D), moved, first, second, totals,
    )
    return (
        dealt_out[None],
        loss[0, 0],
        dealt_grad[None],
        g_w_in,
        g_b_in,
        g_dw,
        g_pw,
        g_pw_b[0],
        g_kern,
        g_kern_b[0],
        g_out,
        g_vec[0],
        g_vec[1],
        g_vec[2],
        g_ffn_in,
        g_ffn_in_b[0],
        g_ffn_out,
        g_vec[3],
        g_vec[4],
        g_vec[5],
    )


def solution(mesh):
    return jax.shard_map(
        local,
        mesh=mesh,
        in_specs=(
            P("wt", "ctx", None),
            P("wt", "ctx", None),
            P(),
            P("wt", None),
            P("wt", None),
            P(None, "wt"),
            P(None, "wt"),
            P("wt", None),
            P("wt"),
            P("wt", None),
            P(),
            P("wt", None),
            P("wt"),
            P("wt"),
            P("wt"),
            P(None, "wt", None),
            P("wt"),
            P(None, "wt", None),
            P("wt"),
            P("wt"),
            P("wt"),
        ),
        out_specs=(
            P("wt", "ctx", None),
            P(),
            P("wt", "ctx", None),
            P("wt", None),
            P(None, "wt"),
            P(None, "wt"),
            P("wt", None),
            P("wt"),
            P("wt", None),
            P(),
            P("wt", None),
            P("wt"),
            P("wt"),
            P("wt"),
            P(None, "wt", None),
            P("wt"),
            P(None, "wt", None),
            P("wt"),
            P("wt"),
            P("wt"),
        ),
        check_vma=False,
    )
```

```python
import functools

import jax
import jax.numpy as jnp
from jax import lax
from jax.experimental import pallas as pl
from jax.experimental.pallas import tpu as pltpu
from jax.sharding import PartitionSpec as P

D = 768
H = 6
HD = 64
FF = 3072
NG = 2
KW = 9
SEQS = 6
A = 384

NORM_EPS = 1e-12
MASKED = -1e30
ROOT_HALF = 0.7071067811865476
DENSITY_NORM = 0.3989422804014327
RIM = 16
MESH = pl.DeviceIdType.MESH
BF16 = jnp.bfloat16
F32 = jnp.float32
VMEM_LIMIT = 60 * 1024 * 1024


def remote(src, dst, send, recv, target):
    return pltpu.make_async_remote_copy(
        src_ref=src,
        dst_ref=dst,
        send_sem=send,
        recv_sem=recv,
        device_id=target,
        device_id_type=MESH,
    )


def greet(peers):
    barrier = pltpu.get_barrier_semaphore()
    total = 0
    for there, target in peers:

        @pl.when(there)
        def _(target=target):
            pl.semaphore_signal(barrier, inc=1, device_id=target, device_id_type=MESH)

        total = total + jnp.where(there, 1, 0)
    pl.semaphore_wait(barrier, total)


class Place:
    def __init__(self, count):
        self.count = count
        self.length = count // 2
        self.valid = count - count // 8
        self.window = count // 2
        self.me = lax.axis_index("ctx")
        self.line = lax.div(self.me, 2)
        self.side = lax.rem(self.me, 2)
        self.mate_index = self.me + 1 - 2 * self.side
        self.mate = {"ctx": self.mate_index}
        self.up = {"ctx": lax.rem(self.me + 2, count)}
        self.down = {"ctx": lax.rem(self.me + count - 2, count)}
        self.has_up = self.line < self.length - 1
        self.has_down = self.line > 0

    def others(self):
        return [
            (self.me >= 0, {"ctx": lax.rem(self.me + shift, self.count)}) for shift in range(1, self.count)
        ]


class PieceNeeds:
    def __init__(self, place, first, last):
        self.place, self.first, self.last = place, first, last

    def at(self, index, source):
        p = self.place
        return (
            (index < p.valid)
            & (self.first <= index + p.window)
            & (self.last >= index - p.window)
        )

    def above(self, line, source):
        p = self.place
        return (2 * line < p.valid) & (self.last >= 2 * line - p.window)

    def below(self, line, source):
        return self.first <= 2 * line + 1 + self.place.window

    def sent(self, source):
        return source >= 0


class BlockNeeds:
    def __init__(self, place):
        self.place = place

    def at(self, index, source):
        p = self.place
        near = (index <= source + p.window) & (index >= source - p.window)
        return near & (index < p.valid) & (source < p.valid)

    def above(self, line, source):
        p = self.place
        return (2 * line < p.valid) & (2 * line <= source + p.window) & (source < p.valid)

    def below(self, line, source):
        p = self.place
        return (2 * line + 1 >= source - p.window) & (source < p.valid)

    def sent(self, source):
        return source < self.place.valid


class AllNeeds:
    def __init__(self, place):
        self.place = place

    def at(self, index, source):
        return source * 0 == 0

    def above(self, line, source):
        return source * 0 == 0

    def below(self, line, source):
        return source * 0 == 0

    def sent(self, source):
        return source * 0 == 0


class Part:
    def __init__(self, place, needs, own, slot, send, recv):
        self.place, self.needs, self.own, self.slot = place, needs, own, slot
        self.send, self.recv = send, recv

    def copy(self, src, source, send, recv, target):
        return remote(src, self.slot(source), self.send.at[send], self.recv.at[recv], target)

    def go_up(self, source):
        p = self.place
        return p.has_up & self.needs.above(p.line + 1, source)

    def go_down(self, source):
        p = self.place
        return p.has_down & self.needs.below(p.line - 1, source)

    def from_below(self, s, source):
        p = self.place
        return (p.line - s >= 0) & self.needs.above(p.line, source)

    def from_above(self, s, source):
        p = self.place
        return (p.line + s < p.length) & self.needs.below(p.line, source)


class LinePart(Part):
    def start(self):
        p = self.place

        @pl.when(self.needs.at(p.mate_index, p.me))
        def _():
            self.copy(self.own, p.me, (2, 0), (2, 0), p.mate).start()

        @pl.when(self.go_up(p.me))
        def _():
            self.copy(self.own, p.me, (0, 0), (0, 1), p.up).start()

        @pl.when(self.go_down(p.me))
        def _():
            self.copy(self.own, p.me, (1, 0), (1, 1), p.down).start()

    def step(self, s):
        p = self.place
        for row, source, there, go, target in (
            (0, p.me - 2 * s, self.from_below, self.go_up, p.up),
            (1, p.me + 2 * s, self.from_above, self.go_down, p.down),
        ):

            @pl.when(there(s, source))
            def _(row=row, source=source, go=go, target=target):
                held = self.slot(source)
                self.copy(held, source, (2 + row, s), (row, s), p.mate).wait_recv()

                @pl.when(go(source))
                def _():
                    self.copy(held, source, (row, s), (row, s + 1), target).start()

                @pl.when(self.needs.at(p.mate_index, source))
                def _():
                    self.copy(held, source, (2 + row, s), (2 + row, s), p.mate).start()

    def finish(self, taken=False):
        p = self.place
        for s in range(p.length):
            for row, source, exists, go, target in (
                (0, p.me - 2 * s, p.line - s >= 0, self.go_up, p.up),
                (1, p.me + 2 * s, p.line + s < p.length, self.go_down, p.down),
            ):
                held = self.slot(source)
                mates = source + 1 - 2 * p.side
                if s > 0 or row == 0:

                    @pl.when(exists & self.needs.at(p.me, mates) & (not taken))
                    def _(row=row, s=s, mates=mates):
                        theirs = self.slot(mates)
                        self.copy(theirs, mates, (2 + row, s), (2 + row, s), p.mate).wait_recv()

                    @pl.when(exists & self.needs.at(p.mate_index, source))
                    def _(row=row, s=s, held=held, source=source):
                        self.copy(held, source, (2 + row, s), (2 + row, s), p.mate).wait_send()

                @pl.when(exists & go(source) & ((s == 0) | self.arrived(row, source)))
                def _(row=row, s=s, held=held, source=source, target=target):
                    self.copy(held, source, (row, s), (row, s + 1), target).wait_send()

    def arrived(self, row, source):
        p = self.place
        return self.needs.above(p.line, source) if row == 0 else self.needs.below(p.line, source)


class PairPart(Part):
    def across(self):
        p = self.place

        @pl.when(self.needs.sent(p.me))
        def _():
            self.copy(self.own, p.me, (4, 0), (4, 0), p.mate).start()

    def along(self):
        p = self.place

        @pl.when(self.go_up(p.me))
        def _():
            self.copy(self.own, p.me, (0, 0), (0, 1), p.up).start()

        @pl.when(self.go_down(p.me))
        def _():
            self.copy(self.own, p.me, (1, 0), (1, 1), p.down).start()

    def middle(self):
        p = self.place
        source = p.mate_index
        held = self.slot(source)

        @pl.when(self.needs.sent(source))
        def _():
            self.copy(held, source, (4, 0), (4, 0), p.mate).wait_recv()

        @pl.when(self.go_up(source))
        def _():
            self.copy(held, source, (2, 0), (2, 1), p.up).start()

        @pl.when(self.go_down(source))
        def _():
            self.copy(held, source, (3, 0), (3, 1), p.down).start()

    def step(self, s):
        p = self.place
        for base, column in ((0, p.me), (2, p.mate_index)):
            for row, source, there, go, target in (
                (0, column - 2 * s, self.from_below, self.go_up, p.up),
                (1, column + 2 * s, self.from_above, self.go_down, p.down),
            ):

                @pl.when(there(s, source))
                def _(row=row + base, source=source, go=go, target=target):
                    held = self.slot(source)
                    self.copy(held, source, (row, s), (row, s), p.mate).wait_recv()

                    @pl.when(go(source))
                    def _():
                        self.copy(held, source, (row, s), (row, s + 1), target).start()

    def finish(self):
        p = self.place

        @pl.when(self.needs.sent(p.me))
        def _():
            self.copy(self.own, p.me, (4, 0), (4, 0), p.mate).wait_send()

        for s in range(p.length):
            for base, column in ((0, p.me), (2, p.mate_index)):
                for row, source, there, go, target in (
                    (0, column - 2 * s, self.from_below, self.go_up, p.up),
                    (1, column + 2 * s, self.from_above, self.go_down, p.down),
                ):
                    passed = there(s, source) if s > 0 else p.me >= 0

                    @pl.when(passed & go(source))
                    def _(row=row + base, s=s, source=source, target=target):
                        held = self.slot(source)
                        self.copy(held, source, (row, s), (row, s + 1), target).wait_send()


class Swap:
    def __init__(self, place, src, dst, send, recv):
        self.place, self.src, self.dst, self.send, self.recv = place, src, dst, send, recv

    def copy(self, shift):
        p = self.place
        there = lax.rem(p.me + shift, p.count)
        return remote(
            self.src.at[there], self.dst.at[p.me], self.send.at[shift], self.recv.at[shift], {"ctx": there}
        )

    def keep(self):
        p = self.place
        return pltpu.make_async_copy(self.src.at[p.me], self.dst.at[p.me], self.send.at[0])

    def start(self):
        for shift in range(1, self.place.count):
            self.copy(shift).start()
        self.keep().start()

    def finish(self):
        p = self.place
        self.keep().wait()
        for shift in range(1, p.count):
            self.copy(shift).wait_send()
            source = lax.rem(p.me + p.count - shift, p.count)
            held = self.dst.at[source]
            remote(held, held, self.send.at[shift], self.recv.at[shift], p.mate).wait_recv()


def part_sems(length):
    return [
        pltpu.SemaphoreType.DMA((5, length + 1)),
        pltpu.SemaphoreType.DMA((5, length + 1)),
    ]


def swap_sems(count):
    return [pltpu.SemaphoreType.DMA((count,)), pltpu.SemaphoreType.DMA((count,))]


def dot(left, right):
    return jnp.dot(left, right, preferred_element_type=F32)


def setup_body(
    lengths, deal_ref, x_ref, t_ref, dw_ref, *refs
):
    rows_in, refs = refs[:6], refs[6:]
    fb_in, b_in, pb_in, kern_in = refs[:4]
    sx_ref, st_ref, arrange_ref, bounds, wide, narrow, ffn, kern = refs[4:]
    count, piece = sx_ref.shape[:2]
    rows = count * piece
    group = lax.axis_index("wt")
    place = lax.axis_index("ctx")
    start = place * rows
    end = jnp.int32(0)
    total = jnp.int32(0)
    first, last = jnp.int32(0), jnp.int32(rows * count)
    ends = []
    for i in range(SEQS):
        end = end + lengths[group, i]
        ends.append(end)
        bounds[i] = end
        for g in range(4):
            total = total + lengths[g, i]
    for i in range(SEQS):
        first = jnp.where(ends[i] <= start, ends[i], first)
    for i in reversed(range(SEQS)):
        last = jnp.where(ends[i] >= start + rows, ends[i], last)
    bounds[SEQS] = start
    bounds[SEQS + 1] = lax.div(first, rows)
    bounds[SEQS + 2] = lax.div(last - 1, rows)
    bounds[SEQS + 3] = place
    bounds[SEQS + 4] = group
    bounds[SEQS + 5] = total
    slots = deal_ref[0:1, pl.ds(pl.multiple_of(start, 128), rows)]
    block = lax.div(slots, rows)
    arrange = block * piece + (slots - block * rows) - place * piece
    arrange_ref[...] = arrange
    sort = jnp.where(lax.broadcasted_iota(jnp.int32, (rows, rows), 0) == arrange, 1.0, 0.0).astype(BF16)
    for src, dst in ((x_ref, sx_ref), (t_ref, st_ref)):
        moved = dot(sort, src[...]).astype(BF16)
        for j in range(count):
            dst[j] = moved[piece * j : piece * j + piece]
    wide[...] = jnp.zeros(wide.shape, F32)
    wide[0:KW, :] = dw_ref[...].astype(F32)
    for i, row in enumerate(rows_in):
        wide[KW + i : KW + i + 1, :] = row[...].astype(F32).reshape(1, D // 4)
    narrow[...] = jnp.zeros(narrow.shape, F32)
    narrow[0:3, : A // 4] = b_in[...].astype(F32)
    narrow[3:4, : A // 4] = pb_in[...].astype(F32).reshape(1, A // 4)
    ffn[...] = jnp.zeros(ffn.shape, F32)
    ffn[0:1, :] = fb_in[...].astype(F32).reshape(1, D)
    kern[...] = jnp.zeros(kern.shape, F32)
    kern[:, : H * KW] = kern_in[...].astype(F32)


SMALL_SHAPES = [(16, D // 4), (8, 128), (8, D), (A // 4, 128)]


def setup(lengths, deal, hidden, teacher, smalls, count):
    rows = hidden.shape[0]
    vmem = pl.BlockSpec(memory_space=pltpu.VMEM)
    smem = pl.BlockSpec(memory_space=pltpu.SMEM)
    pieces = jax.ShapeDtypeStruct((count, rows // count, D), BF16)
    return pl.pallas_call(
        setup_body,
        out_shape=[
            pieces,
            pieces,
            jax.ShapeDtypeStruct((1, rows), jnp.int32),
            jax.ShapeDtypeStruct((SEQS + 6,), jnp.int32),
        ]
        + [jax.ShapeDtypeStruct(shape, F32) for shape in SMALL_SHAPES],
        in_specs=[smem] + [vmem] * (3 + len(smalls)),
        out_specs=[vmem] * 3 + [smem] + [vmem] * 4,
        compiler_params=pltpu.CompilerParams(vmem_limit_bytes=VMEM_LIMIT),
        name="setup",
    )(lengths, deal, hidden, teacher, *smalls)


N_SMALL = 4


def gather_body(count, spans, fused, *refs):
    n = len(spans)
    inputs, refs = refs[: n + 4 + N_SMALL], refs[n + 4 + N_SMALL :]
    x_ref, t_ref = inputs[:2]
    shards = list(inputs[2 : 2 + n])
    own_small = list(inputs[2 + n : 2 + n + N_SMALL])
    bounds, kb_ref = inputs[2 + n + N_SMALL :]
    target_ref = refs[0]
    fulls = list(refs[1 : 1 + n])
    vec_ref, small_ref, fb_ref, kw_ref = refs[1 + n : 5 + n]
    refs = refs[5 + n :]
    if fused:
        out_hbm, conv_outs, refs = refs[:3], refs[3:10], refs[10:]
        out_ref, held_out, conv_scratch, project_sem, refs = refs[0], refs[1:4], refs[4:10], refs[10], refs[11:]
    else:
        out_ref, refs = refs[0], refs[1:]
    all_small = refs[:N_SMALL]
    local_sem, w_send, w_recv, pad_send, pad_recv = refs[N_SMALL : N_SMALL + 5]
    sems = refs[N_SMALL + 5 :]
    p = Place(count)
    k = lax.axis_index("wt")
    side = lax.rem(k, 2)
    core_mate = {"wt": k + 1 - 2 * side}
    far = lax.rem(k + 2, 4)
    far_mate = {"wt": far}

    def span(i, ref, index):
        if i >= n:
            return ref.at[index]
        axis, size = spans[i]
        window = pl.ds(pl.multiple_of(index * size, size), size)
        return ref.at[window] if axis == 0 else ref.at[:, window]

    shards += own_small
    fulls += all_small
    total = n + N_SMALL
    order = list(range(n, total)) + list(range(n))

    greet(p.others() + [(k >= 0, core_mate), (k >= 0, far_mate)])
    quarter, eighth = count // 4, count // 8
    cuts = [0, quarter, p.valid - quarter, p.valid - eighth, p.valid]
    parts = []
    for i, kind in enumerate((LinePart, LinePart, PairPart, PairPart)):
        first, end = cuts[i], cuts[i + 1]
        parts.append(
            kind(
                p,
                PieceNeeds(p, first, end - 1),
                x_ref.at[first:end],
                lambda j, first=first, end=end: out_ref.at[first:end, j],
                sems[2 * i],
                sems[2 * i + 1],
            )
        )
    low, high, *pairs = parts
    lines = [high, low]
    for part in pairs:
        part.across()
    for part in lines:
        part.start()
    for part in pairs:
        part.along()
    for i in order:
        held = span(i, fulls[i], k)
        remote(shards[i], held, w_send.at[0, i], w_recv.at[0, i], far_mate).start()
        remote(shards[i], held, w_send.at[1, i], w_recv.at[1, i], core_mate).start()

    def pad_copy(there):
        return remote(
            x_ref.at[p.valid :],
            out_ref.at[p.valid :, p.me],
            pad_send.at[there - p.valid],
            pad_recv.at[p.me],
            {"ctx": p.me * 0 + there},
        )

    def pads():
        for there in range(p.valid, count):

            @pl.when(p.me != there)
            def _(there=there):
                pad_copy(there).start()

    own_copy = pltpu.make_async_copy(x_ref, out_ref.at[:, p.me], local_sem.at[total])
    keeps = [
        pltpu.make_async_copy(shards[i], span(i, fulls[i], k), local_sem.at[i]) for i in range(total)
    ]
    for keep in [own_copy] + keeps:
        keep.start()
    swap = Swap(p, t_ref, target_ref, sems[8], sems[9])

    def relay(i):
        held = span(i, fulls[i], far)
        remote(held, held, w_send.at[2, i], w_recv.at[0, i], core_mate).wait_recv()
        remote(held, held, w_send.at[2, i], w_recv.at[2, i], core_mate).start()

    def whole(i):
        keeps[i].wait()
        held = span(i, fulls[i], k)
        remote(shards[i], held, w_send.at[1, i], w_recv.at[1, i], core_mate).wait_recv()
        remote(held, held, w_send.at[2, i], w_recv.at[2, i], core_mate).wait_recv()

    def spread(ref, step, shape):
        row = lax.broadcasted_iota(jnp.int32, shape, 0)
        column = lax.broadcasted_iota(jnp.int32, shape, 1)
        value = 0.0
        for index in range(4):
            move = jnp.where((column == row + step * index) & (row < step), 1.0, 0.0).astype(BF16)
            value += dot(ref[index].astype(BF16), move)
        return value

    def smalls():
        for i in range(n, total):
            whole(i)
        vec_ref[...] = spread(all_small[0], D // 4, (D // 4, D))
        small_ref[...] = spread(all_small[1], A // 4, (128, A))
        for index in range(4):
            fb_ref[index : index + 1, :] = all_small[2][index, 0:1, :]
            kw_ref[A // 4 * index : A // 4 * index + A // 4, :] = all_small[3][index].astype(BF16)

    def project_rows(x, blocks, sources):
        lead = out_ref[blocks, sources].shape[:-1]
        w_ref = fulls[0]
        query = (dot(x, w_ref[:, :A]) + small_ref[0:1, :]).astype(BF16).astype(F32)
        keys = dot(x, w_ref[:, A : 2 * A])
        values = dot(x, w_ref[:, 2 * A : 3 * A]) + small_ref[1:2, :]
        for value, held in zip((query * (HD**-0.5), keys, values), held_out):
            held[blocks, sources] = value.astype(BF16).reshape(lead + (A,))

    def project_copies(source):
        return [
            pltpu.make_async_copy(
                held_out[i].at[: p.valid, source], out_hbm[i].at[: p.valid, source], project_sem.at[i, source]
            )
            for i in range(3)
        ]

    def project_source(source):
        blocks = slice(0, p.valid)
        project_rows(out_ref[blocks, source].reshape(-1, D), blocks, source)
        for copy in project_copies(source):
            copy.start()

    def pad_copies():
        return [
            pltpu.make_async_copy(held_out[i].at[p.valid :], out_hbm[i].at[p.valid :], project_sem.at[i, 0])
            for i in range(3)
        ]

    def wait_pads():
        for shift in range(1, count):
            source = lax.rem(p.me + shift, count)
            held = out_ref.at[p.valid :, source]
            remote(held, held, pad_send.at[0], pad_recv.at[source], p.mate).wait_recv()

    def project_column(s):
        for there, source in ((p.line - s >= 0, p.me - 2 * s), (p.line + s < p.length, p.me + 2 * s)):

            @pl.when(there & (p.me < p.valid))
            def _(source=source):
                project_source(source)

            if s == 0:
                break

    def project_mates(s):
        for row, there, source in (
            (2, p.line - s >= 0, p.mate_index - 2 * s),
            (3, p.line + s < p.length, p.mate_index + 2 * s),
        ):

            @pl.when(there & (p.me < p.valid))
            def _(row=row, source=source):
                for part in lines:

                    @pl.when(part.needs.at(p.me, source))
                    def _(part=part):
                        theirs = part.slot(source)
                        part.copy(theirs, source, (row, s), (row, s), p.mate).wait_recv()

                project_source(source)

            if s == 0:
                break

    for part in pairs:
        part.middle()
    for s in range(1, p.length - 1):
        for part in lines + pairs:
            part.step(s)
        if s == 1:
            for i in order[: N_SMALL + 1]:
                relay(i)
    swap.start()
    pads()
    smalls()
    whole(0)
    if fused:
        own_copy.wait()
        for s in range(p.length - 1):
            project_column(s)
        project_mates(0)
    for part in lines + pairs:
        part.step(p.length - 1)
    for i in order[N_SMALL + 1 :]:
        relay(i)
    if fused:
        project_column(p.length - 1)
        for s in range(1, p.length):
            project_mates(s)

        @pl.when(p.me >= p.valid)
        def _():
            wait_pads()
            blocks = slice(p.valid, count)
            project_rows(out_ref[blocks].reshape(-1, D), blocks, slice(0, count))
            for copy in pad_copies():
                copy.start()

        piece = x_ref.shape[1]
        conv_out, ext_ref, cv_ref = conv_outs[:3]
        before = jnp.maximum(p.me - 1, 0)
        after = jnp.minimum(p.me + 1, count - 1)
        ext_ref[0:RIM, :] = out_ref[before, count - 1, piece - RIM :, :]
        for j in range(count):
            ext_ref[RIM + piece * j : RIM + piece * j + piece, :] = out_ref[p.me, j]
        ext_ref[RIM + piece * count :, :] = out_ref[after, 0, :RIM, :]
        whole(1)
        conv_core(
            bounds, count * count * piece, fulls[0], fulls[1], kw_ref, kb_ref, vec_ref, small_ref,
            *conv_outs, *conv_scratch,
        )

        @pl.when(p.me < p.valid)
        def _():
            for source in range(count):
                for copy in project_copies(source):
                    copy.wait()

        @pl.when(p.me >= p.valid)
        def _():
            for copy in pad_copies():
                copy.wait()

    else:
        own_copy.wait()
        whole(1)

        @pl.when(p.me >= p.valid)
        def _():
            wait_pads()

    for i in range(2, n):
        whole(i)
    for i in range(total):
        held = span(i, fulls[i], k)
        remote(shards[i], held, w_send.at[0, i], w_recv.at[0, i], far_mate).wait_send()
        remote(shards[i], held, w_send.at[1, i], w_recv.at[1, i], core_mate).wait_send()
        remote(held, held, w_send.at[2, i], w_recv.at[2, i], core_mate).wait_send()
    for part in pairs:
        part.finish()
    for part in lines:
        part.finish(taken=fused)
    for there in range(p.valid, count):

        @pl.when(p.me != there)
        def _(there=there):
            pad_copy(there).wait_send()

    swap.finish()


def gather_inputs(bounds, pieces, targets, shards, axes, smalls, kern_bias, ctx_count, fused):
    length = ctx_count // 2
    rows = pieces.shape[0] * pieces.shape[1]
    fulls, spans = [], []
    for shard, axis in zip(shards, axes):
        shape = list(shard.shape)
        spans.append((axis, shape[axis]))
        shape[axis] *= 4
        fulls.append(jax.ShapeDtypeStruct(tuple(shape), shard.dtype))
    n = len(shards)
    total = n + N_SMALL
    vmem = pl.BlockSpec(memory_space=pltpu.VMEM)
    hbm = pl.BlockSpec(memory_space=pl.ANY)
    natural = (ctx_count,) + pieces.shape
    heads = (ctx_count,) + pieces.shape[:-1] + (A,)
    outs = (
        [jax.ShapeDtypeStruct(targets.shape, targets.dtype)]
        + fulls
        + [
            jax.ShapeDtypeStruct((16, D), F32),
            jax.ShapeDtypeStruct((8, A), F32),
            jax.ShapeDtypeStruct((4, D), F32),
            jax.ShapeDtypeStruct((A, 128), BF16),
        ]
    )
    specs = [hbm] + [vmem] * 2 + [hbm] * (n - 2) + [vmem] * 4
    scratch = []
    if fused:
        conv_outs, conv_scratch = conv_shapes(rows)
        outs += [jax.ShapeDtypeStruct(heads, BF16)] * 3 + conv_outs
        specs += [hbm] * 3 + [vmem] * 7
        scratch += [pltpu.VMEM(natural, BF16)] + [pltpu.VMEM(heads, BF16)] * 3 + conv_scratch
        scratch += [pltpu.SemaphoreType.DMA((3, ctx_count))]
    else:
        outs.append(jax.ShapeDtypeStruct(natural, BF16))
        specs.append(hbm)
    return pl.pallas_call(
        functools.partial(gather_body, ctx_count, spans, fused),
        out_shape=outs,
        in_specs=[vmem] * (2 + n + len(smalls)) + [pl.BlockSpec(memory_space=pltpu.SMEM), vmem],
        out_specs=specs,
        scratch_shapes=scratch
        + [pltpu.VMEM((4,) + shape, F32) for shape in SMALL_SHAPES]
        + [
            pltpu.SemaphoreType.DMA((total + 1,)),
            pltpu.SemaphoreType.DMA((3, total)),
            pltpu.SemaphoreType.DMA((3, total)),
            pltpu.SemaphoreType.DMA((ctx_count // 8,)),
            pltpu.SemaphoreType.DMA((ctx_count,)),
        ]
        + part_sems(length) * 4
        + swap_sems(ctx_count),
        compiler_params=pltpu.CompilerParams(
            collective_id=0, has_side_effects=True, vmem_limit_bytes=VMEM_LIMIT
        ),
        name="gather_inputs",
    )(pieces, targets, *shards, *smalls, bounds, kern_bias)


class Sum:
    def __init__(self, bits, chunks, packed, bufs, out, send, recv):
        self.bits, self.chunks, self.packed, self.bufs, self.out = bits, chunks, packed, bufs, out
        self.send, self.recv = send, recv
        self.stages = 2 + bits
        self.last = self.stages + bits
        k = lax.axis_index("wt")
        me = lax.axis_index("ctx")
        self.core = lax.rem(k, 2)
        self.far = lax.div(k, 2)
        self.bit = [lax.rem(lax.div(me, 1 << b), 2) for b in range(bits)]
        self.targets = [{"wt": k + 1 - 2 * self.core}, {"wt": lax.rem(k + 2, 4)}]
        for b in range(bits):
            self.targets.append({"ctx": me + (1 << b) * (1 - 2 * self.bit[b])})

    def source(self, stage, c, kept):
        whole = slice(None)

        def pick(value):
            return value if kept else 1 - value

        if stage == 0:
            return self.packed.at[(whole, pick(self.core)) + (whole,) * self.bits + (c,)]
        if stage == 1:
            return self.bufs[0].at[c, pick(self.far)]
        b = stage - 2
        return self.bufs[stage - 1].at[(c,) + (whole,) * (self.bits - b - 1) + (pick(self.bit[b]),)]

    def spread(self, b, c, other):
        index = [self.bit[j] for j in range(b, -1, -1)]
        if other:
            index[0] = 1 - index[0]
        return self.out.at[(slice(None),) * (self.bits - 1 - b) + tuple(index) + (c,)]

    def place_own(self, c, value):
        self.out[tuple(self.bit[j] for j in range(self.bits - 1, -1, -1)) + (c,)] = value

    def copy(self, stage, c):
        if stage < self.stages:
            src, dst, target = self.source(stage, c, False), self.bufs[stage].at[c], self.targets[stage]
        else:
            b = self.bits - 1 - (stage - self.stages)
            src, dst, target = self.spread(b, c, False), self.spread(b, c, False), self.targets[2 + b]
        return remote(src, dst, self.send.at[stage, c], self.recv.at[stage, c], target)

    def start(self, stage, c):
        self.copy(stage, c).start()

    def take(self, stage, c):
        if stage >= self.stages:
            b = self.bits - 1 - (stage - self.stages)
            held = self.spread(b, c, True)
            remote(
                held, held, self.send.at[stage, c], self.recv.at[stage, c], self.targets[2 + b]
            ).wait_recv()
            return
        self.copy(stage, c).wait_recv()
        mine, sums = self.source(stage, c, True), self.bufs[stage].at[c]
        lead = sums.shape[:-2]
        total = 1
        for size in lead:
            total *= size

        def one(at, _):
            index, rest = [], at
            for size in reversed(lead):
                index.append(lax.rem(rest, size))
                rest = lax.div(rest, size)
            index = tuple(reversed(index))
            value = mine[index].astype(F32) + sums[index].astype(F32)
            sums[index] = value.astype(BF16)
            return 0

        if lead:
            lax.fori_loop(0, total, one, 0)
        else:
            sums[...] = (mine[...].astype(F32) + sums[...].astype(F32)).astype(BF16)

    def sent(self, stage, c):
        self.copy(stage, c).wait_send()

    def open(self):
        for c in range(min(4, self.chunks)):
            self.start(0, c)

    def across(self, first, end):
        for c in range(first, min(end, self.chunks)):
            self.take(0, c)
            self.start(1, c)
            if c + 4 < self.chunks:
                self.start(0, c + 4)


def sum_shapes(ctx_count, rows, size):
    bits = ctx_count.bit_length() - 1
    piece = min(size, rows // ctx_count)
    chunks = rows // ctx_count // piece
    twos = (2,) * bits
    bufs = [
        pltpu.VMEM((chunks, 2) + twos + (piece, D), BF16),
        pltpu.VMEM((chunks,) + twos + (piece, D), BF16),
    ]
    for b in range(bits):
        bufs.append(pltpu.VMEM((chunks,) + twos[b + 1 :] + (piece, D), BF16))
    tail = (chunks, piece, D)
    return bits, chunks, (2, 2) + twos + tail, twos + tail, bufs


def seg_of(position, bounds):
    seg = jnp.zeros(position.shape, jnp.int32)
    for i in range(SEQS):
        seg = seg + jnp.where(position >= bounds[i], 1, 0)
    return seg


def reach(bounds, first, last, group_rows):
    begin, end = jnp.int32(0), jnp.int32(group_rows)
    for i in range(SEQS):
        begin = jnp.where(bounds[i] <= first, bounds[i], begin)
    for i in reversed(range(SEQS)):
        end = jnp.where(bounds[i] > last, bounds[i], end)
    return begin, end


def half_masks(rows):
    lane = lax.broadcasted_iota(jnp.int32, (rows, 128), 1)
    low = jnp.where(lane < HD, 1.0, 0.0).astype(BF16)
    return low, (1.0 - low.astype(F32)).astype(BF16)


def dot_last(left, right):
    return lax.dot_general(left, right, (((1,), (1,)), ((), ())), preferred_element_type=F32)


def attend_body(tq, tk, bounds, q_ref, k_ref, v_ref, out_ref, lse_ref, m_ref, acc_ref):
    rows, group_rows = out_ref.shape[0], k_ref.shape[0]
    base = pl.multiple_of(bounds[SEQS], tq)
    q_masks, k_masks = half_masks(tq), half_masks(tk)
    lane = lax.broadcasted_iota(jnp.int32, (tq, 128), 1)
    low = lane < HD

    def tile(qi, _):
        q0 = pl.multiple_of(qi * tq, tq)
        first = pl.multiple_of(base + q0, tq)
        begin, end = reach(bounds, first, first + tq - 1, group_rows)
        q_seg = seg_of(first + lax.broadcasted_iota(jnp.int32, (tq, 1), 0), bounds)
        m_ref[...] = jnp.full(m_ref.shape, MASKED, F32)
        acc_ref[...] = jnp.zeros(acc_ref.shape, F32)

        def step(kt, _):
            k0 = pl.multiple_of(kt * tk, tk)
            k_seg = seg_of(k0 + lax.broadcasted_iota(jnp.int32, (1, tk), 1), bounds)
            bias = jnp.where(q_seg == k_seg, 0.0, MASKED)
            for pair in range(H // 2):
                cols = slice(128 * pair, 128 * pair + 128)
                q_pair = q_ref[pl.ds(first, tq), cols]
                k_pair = k_ref[pl.ds(k0, tk), cols]
                v_pair = v_ref[pl.ds(k0, tk), cols]
                for side in range(2):
                    head = 2 * pair + side
                    scores = dot_last(q_pair * q_masks[side], k_pair) + bias
                    old = m_ref[head]
                    new = jnp.maximum(old, jnp.max(scores, axis=1, keepdims=True))
                    weights = jnp.exp(scores - jnp.tile(new, (1, tk // 128)))
                    v_ones = v_pair * k_masks[side] + k_masks[1 - side]
                    acc_ref[head] = acc_ref[head] * jnp.exp(old - new) + jnp.dot(
                        weights.astype(BF16), v_ones, preferred_element_type=F32
                    )
                    m_ref[head] = new
            return 0

        lax.fori_loop(lax.div(begin, tk), lax.div(end + tk - 1, tk), step, 0)
        lse = jnp.zeros((tq, 128), F32)
        for pair in range(H // 2):
            left, right = acc_ref[2 * pair], acc_ref[2 * pair + 1]
            crossed = jnp.where(low, right, left)
            total = pltpu.roll(crossed, HD, 1)
            out_ref[pl.ds(q0, tq), 128 * pair : 128 * pair + 128] = jnp.where(low, left, right) / total
            lse = jnp.where(lane == 2 * pair, m_ref[2 * pair] + jnp.log(total), lse)
            lse = jnp.where(lane == 2 * pair + 1, m_ref[2 * pair + 1] + jnp.log(crossed), lse)
        lse_ref[pl.ds(q0, tq), :] = lse
        return 0

    lax.fori_loop(0, rows // tq, tile, 0)


def attend(bounds, query, keys, values, rows):
    tq, tk = rows, rows // 2
    return pl.pallas_call(
        functools.partial(attend_body, tq, tk),
        out_shape=[
            jax.ShapeDtypeStruct((rows, A), F32),
            jax.ShapeDtypeStruct((rows, 128), F32),
        ],
        in_specs=[pl.BlockSpec(memory_space=pltpu.SMEM)]
        + [pl.BlockSpec(memory_space=pltpu.VMEM)] * 3,
        out_specs=[pl.BlockSpec(memory_space=pltpu.VMEM)] * 2,
        scratch_shapes=[pltpu.VMEM((H, tq, 128), F32), pltpu.VMEM((H, tq, 128), F32)],
        compiler_params=pltpu.CompilerParams(vmem_limit_bytes=VMEM_LIMIT),
        name="attend",
    )(bounds, query, keys, values)


def query_grads_body(tq, tk, bounds, q_ref, g_ref, stat_ref, k_ref, v_ref, out_ref, rep_ref):
    rows, group_rows = out_ref.shape[0], k_ref.shape[0]
    base = pl.multiple_of(bounds[SEQS], tq)
    q_masks, k_masks = half_masks(tq), half_masks(tk)

    def tile(qi, _):
        q0 = pl.multiple_of(qi * tq, tq)
        first = pl.multiple_of(base + q0, tq)
        begin, end = reach(bounds, first, first + tq - 1, group_rows)
        q_seg = seg_of(first + lax.broadcasted_iota(jnp.int32, (tq, 1), 0), bounds)
        stat = stat_ref[pl.ds(q0, tq), :]
        for head in range(H):
            rep_ref[head] = jnp.broadcast_to(stat[:, head : head + 1], (tq, 128))
            rep_ref[H + head] = jnp.broadcast_to(stat[:, 8 + head : 9 + head], (tq, 128))
        out_ref[pl.ds(q0, tq), :] = jnp.zeros((tq, A), F32)

        def step(kt, _):
            k0 = pl.multiple_of(kt * tk, tk)
            k_seg = seg_of(k0 + lax.broadcasted_iota(jnp.int32, (1, tk), 1), bounds)
            bias = jnp.where(q_seg == k_seg, 0.0, MASKED)
            for pair in range(H // 2):
                cols = slice(128 * pair, 128 * pair + 128)
                q_pair = q_ref[pl.ds(first, tq), cols]
                g_pair = g_ref[pl.ds(q0, tq), cols]
                k_pair = k_ref[pl.ds(k0, tk), cols]
                v_pair = v_ref[pl.ds(k0, tk), cols]
                total = jnp.zeros((tq, 128), F32)
                for side in range(2):
                    head = 2 * pair + side
                    scores = dot_last(q_pair * q_masks[side], k_pair) + bias
                    prob = jnp.exp(scores - jnp.tile(rep_ref[head], (1, tk // 128)))
                    back = dot_last(g_pair * q_masks[side], v_pair)
                    back = prob * (back - jnp.tile(rep_ref[H + head], (1, tk // 128)))
                    total = total + jnp.dot(
                        back.astype(BF16), k_pair * k_masks[side], preferred_element_type=F32
                    )
                out_ref[pl.ds(q0, tq), cols] += total
            return 0

        lax.fori_loop(lax.div(begin, tk), lax.div(end + tk - 1, tk), step, 0)
        return 0

    lax.fori_loop(0, rows // tq, tile, 0)


def query_grads(bounds, query, grads, stats, keys, values):
    rows = grads.shape[0]
    tq, tk = rows, rows // 2
    return pl.pallas_call(
        functools.partial(query_grads_body, tq, tk),
        out_shape=jax.ShapeDtypeStruct((rows, A), F32),
        in_specs=[pl.BlockSpec(memory_space=pltpu.SMEM)]
        + [pl.BlockSpec(memory_space=pltpu.VMEM)] * 5,
        out_specs=pl.BlockSpec(memory_space=pltpu.VMEM),
        scratch_shapes=[pltpu.VMEM((2 * H, tq, 128), F32)],
        compiler_params=pltpu.CompilerParams(vmem_limit_bytes=VMEM_LIMIT),
        name="query_grads",
    )(bounds, query, grads, stats, keys, values)


def key_grads_body(tk, bounds, k_ref, v_ref, q_ref, g_ref, stat_ref, dk_ref, dv_ref):
    rows, group_rows = dk_ref.shape[0], q_ref.shape[0]
    tq = stat_ref.shape[2]
    base = pl.multiple_of(bounds[SEQS], tk)
    q_masks, k_masks = half_masks(tq), half_masks(tk)

    def tile(ki, _):
        k0 = pl.multiple_of(ki * tk, tk)
        first = pl.multiple_of(base + k0, tk)
        begin, end = reach(bounds, first, first + tk - 1, group_rows)
        k_seg = seg_of(first + lax.broadcasted_iota(jnp.int32, (tk, 1), 0), bounds)
        dk_ref[pl.ds(k0, tk), :] = jnp.zeros((tk, A), F32)
        dv_ref[pl.ds(k0, tk), :] = jnp.zeros((tk, A), F32)

        def step(qt, _):
            q0 = pl.multiple_of(qt * tq, tq)
            q_seg = seg_of(q0 + lax.broadcasted_iota(jnp.int32, (1, tq), 1), bounds)
            bias = jnp.where(k_seg == q_seg, 0.0, MASKED)
            for pair in range(H // 2):
                cols = slice(128 * pair, 128 * pair + 128)
                q_pair = q_ref[pl.ds(q0, tq), cols]
                g_pair = g_ref[pl.ds(q0, tq), cols]
                k_pair = k_ref[pl.ds(first, tk), cols]
                v_pair = v_ref[pl.ds(first, tk), cols]
                key_sum = jnp.zeros((tk, 128), F32)
                value_sum = jnp.zeros((tk, 128), F32)
                for side in range(2):
                    head = 2 * pair + side
                    scores = dot_last(k_pair * k_masks[side], q_pair) + bias
                    prob = jnp.exp(scores - stat_ref[qt, head : head + 1, :])
                    value_sum = value_sum + jnp.dot(
                        prob.astype(BF16), g_pair * q_masks[side], preferred_element_type=F32
                    )
                    back = dot_last(v_pair * k_masks[side], g_pair)
                    back = prob * (back - stat_ref[qt, 8 + head : 9 + head, :])
                    key_sum = key_sum + jnp.dot(
                        back.astype(BF16), q_pair * q_masks[side], preferred_element_type=F32
                    )
                dk_ref[pl.ds(k0, tk), cols] += key_sum
                dv_ref[pl.ds(k0, tk), cols] += value_sum
            return 0

        lax.fori_loop(lax.div(begin, tq), lax.div(end + tq - 1, tq), step, 0)
        return 0

    lax.fori_loop(0, rows // tk, tile, 0)


def key_grads(bounds, keys, values, queries, grads, stats):
    rows = stats.shape[2]
    tk = rows
    return pl.pallas_call(
        functools.partial(key_grads_body, tk),
        out_shape=[jax.ShapeDtypeStruct((rows, A), F32)] * 2,
        in_specs=[pl.BlockSpec(memory_space=pltpu.SMEM)]
        + [pl.BlockSpec(memory_space=pltpu.VMEM)] * 5,
        out_specs=[pl.BlockSpec(memory_space=pltpu.VMEM)] * 2,
        compiler_params=pltpu.CompilerParams(vmem_limit_bytes=VMEM_LIMIT),
        name="key_grads",
    )(bounds, keys, values, queries, grads, stats)


def norm_back(grad_rows, normed, inverse, gain):
    scaled = grad_rows * gain
    return inverse * (
        scaled
        - jnp.mean(scaled, axis=1, keepdims=True)
        - normed * jnp.mean(scaled * normed, axis=1, keepdims=True)
    )


def dot_first(left, right):
    return lax.dot_general(left, right, (((0,), (0,)), ((), ())), preferred_element_type=F32)


def project_body(bounds, x_ref, w_ref, b_ref, q_ref, k_ref, v_ref):
    index = pl.program_id(0)

    @pl.when((index >= bounds[SEQS + 1]) & (index <= bounds[SEQS + 2]))
    def _():
        x = x_ref[...]
        query = (dot(x, w_ref[:, :A]) + b_ref[0:1, :]).astype(BF16).astype(F32)
        q_ref[...] = (query * (HD**-0.5)).astype(BF16)
        k_ref[...] = dot(x, w_ref[:, A : 2 * A]).astype(BF16)
        v_ref[...] = (dot(x, w_ref[:, 2 * A : 3 * A]) + b_ref[1:2, :]).astype(BF16)


def project(bounds, natural, w_in, smalls, rows):
    group_rows = natural.shape[0]

    def block(index, bounds):
        return (jnp.clip(index, bounds[SEQS + 1], bounds[SEQS + 2]), 0)

    def fixed(index, bounds):
        return (0, 0)

    return pl.pallas_call(
        project_body,
        out_shape=[jax.ShapeDtypeStruct((group_rows, A), BF16)] * 3,
        grid_spec=pltpu.PrefetchScalarGridSpec(
            num_scalar_prefetch=1,
            grid=(group_rows // rows,),
            in_specs=[
                pl.BlockSpec((rows, D), block),
                pl.BlockSpec((D, 3 * A), fixed),
                pl.BlockSpec((8, A), fixed),
            ],
            out_specs=[pl.BlockSpec((rows, A), block)] * 3,
        ),
        compiler_params=pltpu.CompilerParams(vmem_limit_bytes=VMEM_LIMIT),
        name="project",
    )(bounds, natural, w_in, smalls)


def tap_lanes(tap):
    row = lax.broadcasted_iota(jnp.int32, (128, A), 0)
    column = lax.broadcasted_iota(jnp.int32, (128, A), 1)
    return jnp.where(row == lax.div(column, HD) * KW + tap, 1.0, 0.0).astype(BF16)


def tap_pick(tap):
    row = lax.broadcasted_iota(jnp.int32, (A, 128), 0)
    column = lax.broadcasted_iota(jnp.int32, (A, 128), 1)
    first = row == lax.div(row, HD) * HD
    return jnp.where(first & (column == lax.div(row, HD) * KW + tap), 1.0, 0.0).astype(BF16)


def tap_weights(kw_ref, kb_ref, wide_ref, bias_ref):
    bias_ref[:, 0:128] = jnp.zeros((8, 128), F32)
    bias_ref[0:1, 0 : H * KW] = kb_ref[...].astype(F32)
    bias = bias_ref[:, 0:128].astype(BF16)
    for tap in range(KW):
        lanes = tap_lanes(tap)
        cols = slice(A * tap, A * tap + A)
        wide_ref[:, cols] = dot(kw_ref[...], lanes).astype(BF16)
        bias_ref[:, cols] = dot(bias, lanes)


def tap_near(bounds, group_rows, seg_ref, near_ref):
    span = near_ref.shape[1]
    start = lax.axis_index("ctx") * (span - RIM)
    position = start - RIM + lax.broadcasted_iota(jnp.int32, seg_ref.shape, 0)
    inside = (position >= 0) & (position < group_rows)
    seg_ref[...] = jnp.where(inside, seg_of(position, bounds), -1)
    seg = seg_ref[RIM // 2 : RIM // 2 + span, :]
    for tap in range(KW):
        shift = RIM // 2 - KW // 2 + tap
        near_ref[tap] = jnp.where((seg_ref[shift : shift + span, :] == seg) & (seg >= 0), 1.0, 0.0)


def tap_softmax(logits, bias_ref):
    parts = [logits[:, A * tap : A * tap + A] + bias_ref[0:1, A * tap : A * tap + A] for tap in range(KW)]
    largest = functools.reduce(jnp.maximum, parts)
    parts = [jnp.exp(part - largest) for part in parts]
    total = 1.0 / functools.reduce(jnp.add, parts)
    return [part * total for part in parts]


def wide3(value):
    return jnp.tile(value, (1, 3))


def conv_body(
    bounds, natural, w_ref, pw_ref, kw_ref, kb_ref, vec_ref, small_ref,
    out_ref, ext_ref, cv_ref, kc_ref, q_ref, cq_ref, sp_ref,
    extf_ref, seg_ref, near_ref, wide_ref, bias_ref, full_ref, sem,
):
    rows, group_rows = out_ref.shape[0], natural.shape[0]
    start = bounds[SEQS]
    copies = [
        pltpu.make_async_copy(
            natural.at[pl.ds(pl.multiple_of(jnp.maximum(start - RIM, 0), RIM), RIM)],
            ext_ref.at[0:RIM],
            sem.at[0],
        ),
        pltpu.make_async_copy(
            natural.at[pl.ds(pl.multiple_of(start, RIM), rows)], ext_ref.at[RIM : RIM + rows], sem.at[1]
        ),
        pltpu.make_async_copy(
            natural.at[pl.ds(pl.multiple_of(jnp.minimum(start + rows, group_rows - RIM), RIM), RIM)],
            ext_ref.at[RIM + rows : 2 * RIM + rows],
            sem.at[2],
        ),
    ]
    for copy in copies:
        copy.start()
    for copy in copies:
        copy.wait()
    conv_core(
        bounds, group_rows, w_ref, pw_ref, kw_ref, kb_ref, vec_ref, small_ref,
        out_ref, ext_ref, cv_ref, kc_ref, q_ref, cq_ref, sp_ref,
        extf_ref, seg_ref, near_ref, wide_ref, bias_ref, full_ref,
    )


def conv_core(
    bounds, group_rows, w_ref, pw_ref, kw_ref, kb_ref, vec_ref, small_ref,
    out_ref, ext_ref, cv_ref, kc_ref, q_ref, cq_ref, sp_ref,
    extf_ref, seg_ref, near_ref, wide_ref, bias_ref, full_ref,
):
    rows = out_ref.shape[0]
    span = rows + RIM
    tap_weights(kw_ref, kb_ref, wide_ref, bias_ref)
    tap_near(bounds, group_rows, seg_ref, near_ref)
    count = group_rows // rows
    place = lax.axis_index("ctx")
    padded = count - count // 8

    @pl.when((place == 0) | (place == padded))
    def _():
        ext_ref[0:RIM, :] = jnp.zeros((RIM, D), BF16)

    @pl.when((place == padded - 1) | (place == count - 1))
    def _():
        ext_ref[RIM + rows :, :] = jnp.zeros((RIM, D), BF16)

    ext = ext_ref[...]
    extf_ref[...] = ext.astype(F32)
    cv_ref[...] = dot(ext, w_ref[:, 3 * A :]) + small_ref[2:3, :]
    q_ref[...] = (dot(ext, w_ref[:, :A]) + small_ref[0:1, :]).astype(BF16).astype(F32)
    tile = span // 3
    for i in range(3):
        t0 = tile * i
        for c in range(6):
            cols = slice(128 * c, 128 * c + 128)
            window = extf_ref[t0 : t0 + tile + RIM, cols]
            total = 0.0
            for tap in range(KW):
                shift = RIM // 2 - KW // 2 + tap
                total += (
                    vec_ref[tap : tap + 1, cols]
                    * near_ref[tap, t0 : t0 + tile, :]
                    * window[shift : shift + tile]
                )
            sp_ref[t0 : t0 + tile, cols] = total.astype(BF16)
    kc_ref[...] = dot(sp_ref[...], pw_ref[...]) + small_ref[3:4, :]
    cq_ref[...] = (kc_ref[...] * q_ref[RIM // 2 : RIM // 2 + span, :]).astype(BF16)
    for i in range(3):
        t0 = tile * i
        kernel = tap_softmax(dot(cq_ref[t0 : t0 + tile, :], wide_ref[...]), bias_ref)
        window = cv_ref[t0 : t0 + tile + RIM, :]
        total = 0.0
        for tap in range(KW):
            shift = RIM // 2 - KW // 2 + tap
            total += kernel[tap] * wide3(near_ref[tap, t0 : t0 + tile, :]) * window[shift : shift + tile]
        full_ref[t0 : t0 + tile, :] = total
    out_ref[...] = full_ref[RIM // 2 : RIM // 2 + rows, :].astype(BF16)


def conv_shapes(rows):
    span, wide = rows + RIM, rows + 2 * RIM
    outs = [
        jax.ShapeDtypeStruct((rows, A), BF16),
        jax.ShapeDtypeStruct((wide, D), BF16),
        jax.ShapeDtypeStruct((wide, A), F32),
        jax.ShapeDtypeStruct((span, A), F32),
        jax.ShapeDtypeStruct((wide, A), F32),
        jax.ShapeDtypeStruct((span, A), BF16),
        jax.ShapeDtypeStruct((span, D), BF16),
    ]
    scratch = [
        pltpu.VMEM((wide, D), F32),
        pltpu.VMEM((wide, 128), jnp.int32),
        pltpu.VMEM((KW, span, 128), F32),
        pltpu.VMEM((A, KW * A), BF16),
        pltpu.VMEM((8, KW * A), F32),
        pltpu.VMEM((span, A), F32),
    ]
    return outs, scratch


def convolve(bounds, natural, w_in, pw, kw, kb, vectors, smalls, rows):
    outs, scratch = conv_shapes(rows)
    vmem = pl.BlockSpec(memory_space=pltpu.VMEM)
    return pl.pallas_call(
        conv_body,
        out_shape=outs,
        in_specs=[pl.BlockSpec(memory_space=pltpu.SMEM), pl.BlockSpec(memory_space=pl.ANY)] + [vmem] * 6,
        out_specs=[vmem] * 7,
        scratch_shapes=scratch + [pltpu.SemaphoreType.DMA((3,))],
        compiler_params=pltpu.CompilerParams(vmem_limit_bytes=VMEM_LIMIT),
        name="convolve",
    )(bounds, natural, w_in, pw, kw, kb, vectors, smalls)


def norm_rows(x, gain, bias):
    centered = x - jnp.mean(x, axis=1, keepdims=True)
    inverse = lax.rsqrt(jnp.mean(centered * centered, axis=1, keepdims=True) + NORM_EPS)
    normed = centered * inverse
    return normed * gain + bias, normed, inverse


ROW_OUT_B, ROW_GAIN1, ROW_BIAS1, ROW_FFN_B, ROW_GAIN2, ROW_BIAS2 = range(KW, KW + 6)
FI_ROWS, FO_ROWS, OW_ROWS = 384, 384, 192
FIRST_PACK = 1024
SECOND_PACK = 512


def layer_body(
    bounds, attn_ref, lse_ref, conv_ref, ext_ref, tgt_ref, wo_ref, fi_ref, fo_ref, vec_ref, fb_ref,
    out_ref, gfirst_ref, gctx_ref, stat_ref, statt_ref, sums_ref, fbs_ref, pack_ref,
    ctx_s, low_s, act_s, slope_s, gfl_s, gpre_s, gproj_s,
):
    rows = out_ref.shape[0]
    tm = slope_s.shape[0]
    chunk = D
    wide = FF // NG
    part = D // NG
    row_of = lax.broadcasted_iota(jnp.int32, (A, 128), 0)
    column_of = lax.broadcasted_iota(jnp.int32, (A, 128), 1)
    head_pick = jnp.where(column_of == 8 + lax.div(row_of, HD), 1.0, 0.0).astype(BF16)
    sums_ref[...] = jnp.zeros(sums_ref.shape, F32)
    fbs_ref[...] = jnp.zeros(fbs_ref.shape, F32)

    def vec(row):
        return vec_ref[row : row + 1, :]

    def add_sum(row, value):
        sums_ref[row : row + 1, :] += jnp.sum(value, axis=0, keepdims=True)

    def tile(index, _):
        r0 = pl.multiple_of(index * tm, tm)
        here = pl.ds(r0, tm)
        attn = attn_ref[here, :]
        ctx_s[here, :A] = attn.astype(BF16)
        ctx_s[here, A:] = conv_ref[here, :]
        tokens = ext_ref[pl.ds(pl.multiple_of(r0 + RIM, RIM), tm), :].astype(F32)
        first = tokens + dot(ctx_s[here, :], wo_ref[...]) + vec(ROW_OUT_B)
        after, normed_one, inverse_one = norm_rows(first, vec(ROW_GAIN1), vec(ROW_BIAS1))
        low_s[here, :] = after.astype(BF16)
        results = []
        for g in range(NG):
            low = low_s[here, part * g : part * g + part]
            total = 0.0
            for c in range(wide // chunk):
                span = slice(chunk * c, chunk * c + chunk)
                whole = slice(wide * g + chunk * c, wide * g + chunk * c + chunk)
                pre = dot(low, fi_ref[g, :, span]) + fb_ref[2 * g + c : 2 * g + c + 1, :]
                phi = 0.5 * (1.0 + lax.erf(pre * ROOT_HALF))
                act = (pre * phi).astype(BF16)
                act_s[here, whole] = act
                slope_s[:, whole] = phi + pre * DENSITY_NORM * jnp.exp(-0.5 * pre * pre)
                total += dot(act, fo_ref[g, span, :])
            results.append(total)
        second = after + jnp.concatenate(results, axis=1) + vec(ROW_FFN_B)
        result, normed_two, inverse_two = norm_rows(second, vec(ROW_GAIN2), vec(ROW_BIAS2))
        out_ref[here, :] = result.astype(BF16)
        seg = seg_of(bounds[SEQS] + r0 + lax.broadcasted_iota(jnp.int32, (tm, 1), 0), bounds)
        error = jnp.where(seg < SEQS, result - tgt_ref[here, :].astype(F32), 0.0)
        add_sum(6, error * error)
        add_sum(4, error * normed_two)
        add_sum(5, error)
        grad_second = norm_back(error, normed_two, inverse_two, vec(ROW_GAIN2))
        gfl = grad_second.astype(BF16)
        gfl_s[here, :] = gfl
        add_sum(3, gfl.astype(F32))
        grads = []
        for g in range(NG):
            total = 0.0
            for c in range(wide // chunk):
                span = slice(chunk * c, chunk * c + chunk)
                whole = slice(wide * g + chunk * c, wide * g + chunk * c + chunk)
                gact = dot_last(gfl_s[here, part * g : part * g + part], fo_ref[g, span, :])
                gpre = (gact * slope_s[:, whole]).astype(BF16)
                gpre_s[here, whole] = gpre
                fbs_ref[2 * g + c : 2 * g + c + 1, :] += jnp.sum(gpre.astype(F32), axis=0, keepdims=True)
                total += dot_last(gpre, fi_ref[g, :, span])
            grads.append(total)
        grad_after = jnp.concatenate(grads, axis=1) + grad_second
        add_sum(1, grad_after * normed_one)
        add_sum(2, grad_after)
        grad_first = norm_back(grad_after, normed_one, inverse_one, vec(ROW_GAIN1))
        gfirst_ref[here, :] = grad_first
        gproj = grad_first.astype(BF16)
        gproj_s[here, :] = gproj
        add_sum(0, gproj.astype(F32))
        gctx = dot_last(gproj, wo_ref[...]).astype(BF16)
        gctx_ref[here, :] = gctx
        product = gctx[:, :A].astype(F32) * attn
        high = product.astype(BF16)
        rest = (product - high.astype(F32)).astype(BF16)
        stat = lse_ref[here, :] + dot(high, head_pick) + dot(rest, head_pick)
        stat_ref[here, :] = stat
        return 0

    lax.fori_loop(0, rows // tm, tile, 0)
    statt_ref[...] = stat_ref[...].T[:16]
    for g in range(NG):
        for half in range(2):
            whole = slice(wide * g + D * half, wide * g + D * half + D)
            grad = dot_first(low_s[:, part * g : part * g + part], gpre_s[:, whole]).astype(BF16)
            r0 = 96 * (2 * g + half)
            for k in range(4):
                pack_ref[k, r0 : r0 + 96, :] = grad[96 * k : 96 * k + 96]
        for k in range(4):
            grad = dot_first(
                act_s[:, wide * g + A * k : wide * g + A * k + A], gfl_s[:, part * g : part * g + part]
            )
            pack_ref[k, FI_ROWS : FI_ROWS + FO_ROWS, part * g : part * g + part] = grad.astype(BF16)
    grad = dot_first(ctx_s[...], gproj_s[...]).astype(BF16)
    r0 = FI_ROWS + FO_ROWS
    for k in range(4):
        pack_ref[k, r0 : r0 + OW_ROWS, :] = grad[OW_ROWS * k : OW_ROWS * k + OW_ROWS]
        pack_ref[k, r0 + OW_ROWS :, :] = jnp.zeros((FIRST_PACK - r0 - OW_ROWS, D), BF16)


def layer(bounds, attn, lse, conv, ext, target, wo, fi, fo, vectors, fb):
    rows = attn.shape[0]
    tm = min(256, rows)
    vmem = pl.BlockSpec(memory_space=pltpu.VMEM)
    return pl.pallas_call(
        layer_body,
        out_shape=[
            jax.ShapeDtypeStruct((rows, D), BF16),
            jax.ShapeDtypeStruct((rows, D), F32),
            jax.ShapeDtypeStruct((rows, D), BF16),
            jax.ShapeDtypeStruct((rows, 128), F32),
            jax.ShapeDtypeStruct((16, rows), F32),
            jax.ShapeDtypeStruct((8, D), F32),
            jax.ShapeDtypeStruct((4, D), F32),
            jax.ShapeDtypeStruct((4, FIRST_PACK, D), BF16),
        ],
        in_specs=[pl.BlockSpec(memory_space=pltpu.SMEM)] + [vmem] * 10,
        out_specs=[vmem] * 8,
        scratch_shapes=[
            pltpu.VMEM((rows, D), BF16),
            pltpu.VMEM((rows, D), BF16),
            pltpu.VMEM((rows, FF), BF16),
            pltpu.VMEM((tm, FF), F32),
            pltpu.VMEM((rows, D), BF16),
            pltpu.VMEM((rows, FF), BF16),
            pltpu.VMEM((rows, D), BF16),
        ],
        compiler_params=pltpu.CompilerParams(vmem_limit_bytes=VMEM_LIMIT),
        name="layer",
    )(bounds, attn, lse, conv, ext, target, wo, fi, fo, vectors, fb)


TAIL_ROWS = 128


def middle_body(
    count, sums, *refs, group_rows
):
    bits, chunks = sums
    (
        bounds, g_ref, stat_ref, res_ref, pack_ref,
        ext_ref, cv_ref, kc_ref, q_ref, cq_ref, sp_ref, pw_ref, kw_ref, kb_ref, vec_ref,
        out_ref, all_ref, dealt_ref, own_ref, gq_ref, gcv_ref, gtc_ref, tail_ref, sums_ref, bsum_ref,
        edge_ref, extf_ref, seg_ref, near_ref, wide_ref, bias_ref, gc_ref, pc_ref, glc_ref, gsp_ref,
        *rest,
    ) = refs
    bufs, rest = rest[: 2 + bits], rest[2 + bits :]
    sum_send, sum_recv, local_sem, edge_send, edge_recv, *sems = rest
    p = Place(count)
    rows = g_ref.shape[0]
    span = rows + RIM
    rim = RIM // 2
    place = p.me
    total = Sum(bits, chunks, pack_ref, bufs, None, sum_send, sum_recv)
    early = rows - 3 * rows // 8
    low = {"ctx": lax.rem(p.me + count - 1, count)}
    high = {"ctx": lax.rem(p.me + 1, count)}
    has_low, has_high = p.me > 0, p.me < count - 1
    greet(p.others() + [(p.me >= 0, target) for target in total.targets[:2]])
    needs = BlockNeeds(p)
    pair = PairPart(p, needs, g_ref.at[early:, :A], lambda j: out_ref.at[j, early:], sems[0], sems[1])
    line = LinePart(p, needs, g_ref.at[:early, :A], lambda j: out_ref.at[j, :early], sems[2], sems[3])
    stats = LinePart(p, needs, stat_ref, lambda j: all_ref.at[j], sems[4], sems[5])
    swap = Swap(p, res_ref, dealt_ref, sems[6], sems[7])

    def to_low():
        return remote(g_ref.at[:RIM, A:], edge_ref.at[1], edge_send.at[0], edge_recv.at[1], low)

    def to_high():
        return remote(g_ref.at[rows - RIM :, A:], edge_ref.at[0], edge_send.at[1], edge_recv.at[0], high)

    def advance(t):
        for c in range(chunks):
            stage = t - c
            if 1 <= stage <= total.stages:
                total.take(stage - 1, c)
                if stage < total.stages:
                    total.start(stage, c)
                else:
                    own_ref[c] = bufs[stage - 1][c]

    @pl.when(has_low)
    def _():
        to_low().start()

    @pl.when(has_high)
    def _():
        to_high().start()

    total.open()
    parts = [stats, line, pair]
    stats.start()
    pair.across()
    line.start()
    pair.along()
    keeps = [
        pltpu.make_async_copy(g_ref.at[:, :A], out_ref.at[p.me], local_sem.at[0]),
        pltpu.make_async_copy(stat_ref, all_ref.at[p.me], local_sem.at[1]),
    ]
    for keep in keeps:
        keep.start()
    advance(1)
    tap_weights(kw_ref, kb_ref, wide_ref, bias_ref)
    pair.middle()
    tap_near(bounds, group_rows, seg_ref, near_ref)
    extf_ref[...] = ext_ref[...].astype(F32)

    @pl.when(has_low)
    def _():
        to_low().wait_send()
        to_high().wait_recv()

    @pl.when(has_high)
    def _():
        to_high().wait_send()
        to_low().wait_recv()

    gc_ref[0:rim, :] = jnp.where(place > 0, edge_ref[0].astype(F32)[RIM - rim :], 0.0)
    gc_ref[rim : rim + rows, :] = g_ref[:, A:].astype(F32)
    gc_ref[rim + rows :, :] = jnp.where(place < count - 1, edge_ref[1].astype(F32)[:rim], 0.0)
    blocks = jnp.where(
        lax.div(lax.broadcasted_iota(jnp.int32, (128, 128), 0), HD)
        == lax.div(lax.broadcasted_iota(jnp.int32, (128, 128), 1), HD),
        1.0,
        0.0,
    ).astype(BF16)
    tile = span // 3

    def tap_tile(i):
        t0 = tile * i
        here = slice(t0, t0 + tile)
        kernel = tap_softmax(dot(cq_ref[here, :], wide_ref[...]), bias_ref)
        window = cv_ref[t0 : t0 + tile + RIM, :]
        grad = gc_ref[here, :]
        inner = []
        mean = 0.0
        for tap in range(KW):
            shift = rim - KW // 2 + tap
            near = wide3(near_ref[tap, here, :])
            product = (grad * window[shift : shift + tile]).astype(BF16)
            terms = jnp.concatenate(
                [dot(product[:, 128 * c : 128 * c + 128], blocks) for c in range(3)], axis=1
            )
            terms = terms * near
            inner.append(terms)
            mean += kernel[tap] * terms
            pc_ref[tap, here, :] = kernel[tap] * near * grad
        picked = 0.0
        for tap in range(KW):
            logit = (kernel[tap] * (inner[tap] - mean)).astype(BF16)
            picked += dot(logit, tap_pick(tap))
        glc_ref[here, :] = picked.astype(BF16)

    tap_tile(0)
    for part in parts:
        part.step(1)
    advance(2)
    tap_tile(1)
    for s in range(2, p.length):
        for part in parts:
            part.step(s)
        if s == 2:
            swap.start()
            advance(3)
            tap_tile(2)
    advance(4)
    back = dot_last(glc_ref[...], kw_ref[...])
    query = q_ref[rim : rim + span, :]
    row = lax.broadcasted_iota(jnp.int32, (span, 1), 0)
    own = (row >= rim) & (row < rim + rows)
    grad_kc = (back * query).astype(BF16)
    gsp_ref[...] = dot_last(grad_kc, pw_ref[...])
    gq_ref[...] = (back * kc_ref[...])[rim : rim + rows]
    own_kc = jnp.where(own, grad_kc.astype(F32), 0.0)
    own_logits = jnp.where(own, glc_ref[...].astype(F32), 0.0)
    grad_pw = dot_first(sp_ref[...], own_kc.astype(BF16)).astype(BF16)
    grad_kern = dot_first(cq_ref[...], own_logits.astype(BF16)).astype(BF16)
    for k in range(4):
        for half in range(2):
            r0 = 192 * k + 96 * half
            tail_ref[k, 0:96, A * half : A * half + A] = grad_pw[r0 : r0 + 96]
        for m in range(6):
            r0 = 96 * k + 16 * m
            tail_ref[k, 96:112, 128 * m : 128 * m + 128] = grad_kern[r0 : r0 + 16]
        tail_ref[k, 112:, :] = jnp.zeros((TAIL_ROWS - 112, D), BF16)
    bsum_ref[...] = jnp.zeros(bsum_ref.shape, F32)
    bsum_ref[0:1, :] = jnp.sum(own_kc, axis=0, keepdims=True)
    bsum_ref[1:2, 0:128] = jnp.sum(own_logits, axis=0, keepdims=True)
    advance(5)
    sums_ref[...] = jnp.zeros(sums_ref.shape, F32)
    step = 128
    for s0 in range(0, rows, step):
        for c in range(6):
            cols = slice(128 * c, 128 * c + 128)
            grads = gsp_ref[s0 + rim : s0 + rim + step, cols]
            tokens = extf_ref[s0 + rim : s0 + rim + step + RIM, cols]
            spread = gsp_ref[s0 : s0 + step + RIM, cols]
            sofar = 0.0
            for tap in range(KW):
                shift = rim - KW // 2 + tap
                value = near_ref[tap, s0 + rim : s0 + rim + step, :] * grads * tokens[shift : shift + step]
                sums_ref[tap : tap + 1, cols] += jnp.sum(value, axis=0, keepdims=True)
                shift = rim + KW // 2 - tap
                moved = near_ref[tap, s0 : s0 + step + RIM, :] * spread
                sofar += vec_ref[tap : tap + 1, cols] * moved[shift : shift + step]
            gtc_ref[s0 : s0 + step, cols] = sofar
        for c in range(3):
            cols = slice(128 * c, 128 * c + 128)
            sofar = 0.0
            for tap in range(KW):
                shift = rim + KW // 2 - tap
                sofar += pc_ref[tap, s0 : s0 + step + RIM, cols][shift : shift + step]
            gcv_ref[s0 : s0 + step, cols] = sofar.astype(BF16)
        if s0 == rows // 2 - step:
            advance(6)
    for t in range(7, chunks + total.stages):
        advance(t)
    for keep in keeps:
        keep.wait()
    for part in parts:
        part.finish()
    swap.finish()
    for stage in range(total.stages):
        for c in range(chunks):
            total.sent(stage, c)


def middle(bounds, group_rows, ctx_count, grads, stats, results, pack, *args):
    length = ctx_count // 2
    rows = grads.shape[0]
    span, wide = rows + RIM, rows + 2 * RIM
    bits, chunks, packed_shape, out_shape, bufs = sum_shapes(ctx_count, pack.shape[1], 32)
    vmem = pl.BlockSpec(memory_space=pltpu.VMEM)
    hbm = pl.BlockSpec(memory_space=pl.ANY)
    return pl.pallas_call(
        functools.partial(middle_body, ctx_count, (bits, chunks), group_rows=group_rows),
        out_shape=[
            jax.ShapeDtypeStruct((ctx_count, rows, A), grads.dtype),
            jax.ShapeDtypeStruct((ctx_count,) + stats.shape, stats.dtype),
            jax.ShapeDtypeStruct(results.shape, results.dtype),
            jax.ShapeDtypeStruct(out_shape[-3:], BF16),
            jax.ShapeDtypeStruct((rows, A), F32),
            jax.ShapeDtypeStruct((rows, A), BF16),
            jax.ShapeDtypeStruct((rows, D), F32),
            jax.ShapeDtypeStruct((4, TAIL_ROWS, D), BF16),
            jax.ShapeDtypeStruct((16, D), F32),
            jax.ShapeDtypeStruct((8, A), F32),
        ],
        in_specs=[pl.BlockSpec(memory_space=pltpu.SMEM)] + [vmem] * (len(args) + 4),
        out_specs=[hbm] * 3 + [vmem] * 7,
        scratch_shapes=[
            pltpu.VMEM((2, RIM, A), BF16),
            pltpu.VMEM((wide, D), F32),
            pltpu.VMEM((wide, 128), jnp.int32),
            pltpu.VMEM((KW, span, 128), F32),
            pltpu.VMEM((A, KW * A), BF16),
            pltpu.VMEM((8, KW * A), F32),
            pltpu.VMEM((span, A), F32),
            pltpu.VMEM((KW, span, A), F32),
            pltpu.VMEM((span, 128), BF16),
            pltpu.VMEM((span, D), F32),
        ]
        + bufs
        + [
            pltpu.SemaphoreType.DMA((2 + bits, chunks)),
            pltpu.SemaphoreType.DMA((2 + bits, chunks)),
            pltpu.SemaphoreType.DMA((2,)),
            pltpu.SemaphoreType.DMA((2,)),
            pltpu.SemaphoreType.DMA((2,)),
        ]
        + part_sems(length) * 3
        + swap_sems(ctx_count),
        compiler_params=pltpu.CompilerParams(
            collective_id=1, has_side_effects=True, vmem_limit_bytes=VMEM_LIMIT
        ),
        name="middle",
    )(bounds, grads, stats, results, pack.reshape(packed_shape), *args)


def ending_body(count, sums, *refs):
    bits, second_chunks = sums
    (
        dq_ref, dk_ref, dv_ref, gq_ref, gcv_ref, gtc_ref, gfirst_ref, ext_ref, w_ref, tail_ref, own_ref,
        tap_ref, bsum_ref, layer_ref, ffn_ref,
        first_ref, second_ref, sum_ref, dealt_ref,
        gm_ref, gtok_ref, pack_ref, f_bufs, *rest,
    ) = refs
    bufs, rest = rest[: 2 + bits], rest[2 + bits :]
    first_send, first_recv, second_send, second_recv, f_send, f_recv, keep_sem, swap_send, swap_recv = rest
    p = Place(count)
    rows = gm_ref.shape[0]
    piece = pack_ref.shape[-2]
    first = LinePart(p, AllNeeds(p), own_ref, lambda j: first_ref.at[j], first_send, first_recv)
    second = Sum(bits, second_chunks, pack_ref, bufs, second_ref, second_send, second_recv)
    swap = Swap(p, gtok_ref, dealt_ref, swap_send, swap_recv)
    stages, last = second.stages, second.last
    greet(p.others() + [(p.me >= 0, target) for target in second.targets[:2]])
    first.start()
    keep = pltpu.make_async_copy(own_ref, first_ref.at[p.me], keep_sem)
    keep.start()

    def store(k, r0, value):
        for at in range(0, value.shape[0], piece):
            row = (r0 + at) // piece
            index = []
            rest, c = row // second_chunks, row % second_chunks
            for b in range(bits):
                index.insert(0, rest % 2)
                rest //= 2
            pack_ref[(k // 2, k % 2) + tuple(index) + (c,)] = value[at : at + piece]

    gm_ref[:, :A] = (dq_ref[...] * (HD**-0.5) + gq_ref[...]).astype(BF16)
    gm_ref[:, A : 2 * A] = dk_ref[...].astype(BF16)
    gm_ref[:, 2 * A : 3 * A] = dv_ref[...].astype(BF16)
    gm_ref[:, 3 * A :] = gcv_ref[...]
    for half in range(2):
        grad = dot_first(ext_ref[RIM : RIM + rows, :], gm_ref[:, D * half : D * half + D]).astype(BF16)
        for k in range(4):
            store(k, 192 * half, grad[192 * k : 192 * k + 192])
    for k in range(4):
        store(k, 384, tail_ref[k])
    second.open()
    second.across(0, second_chunks)
    first.step(1)
    f_bufs[0, 0] = jnp.zeros(f_bufs.shape[2:], F32)
    f_bufs[0, 0, 0:KW, :] = tap_ref[0:KW, :]
    f_bufs[0, 0, KW : KW + 7, :] = layer_ref[0:7, :]
    f_bufs[0, 0, 16:20, :] = ffn_ref[...]
    f_bufs[0, 0, 20:21, :A] = jnp.sum(gm_ref[:, :A].astype(F32), axis=0, keepdims=True)
    f_bufs[0, 0, 20:21, A:] = jnp.sum(gm_ref[:, 2 * A : 3 * A].astype(F32), axis=0, keepdims=True)
    f_bufs[0, 0, 21:22, :A] = jnp.sum(gm_ref[:, 3 * A :].astype(F32), axis=0, keepdims=True)
    f_bufs[0, 0, 21:22, A:] = bsum_ref[0:1, :]
    f_bufs[0, 0, 22:23, :A] = bsum_ref[1:2, :]

    def f_copy(stage):
        return remote(
            f_bufs.at[0, stage], f_bufs.at[1, stage], f_send.at[stage], f_recv.at[stage], second.targets[stage]
        )

    f_copy(0).start()
    grad = dot_last(gm_ref[...], w_ref[...]) + gfirst_ref[...] + gtc_ref[...]
    size = rows // count
    for j in range(count):
        gtok_ref[j] = grad[size * j : size * j + size].astype(BF16)
    swap.start()
    for t in range(1, second_chunks + last - 1):
        if 2 <= t + 1 < p.length:
            first.step(t + 1)
        for c in reversed(range(second_chunks)):
            stage = t - c + 1
            if not 2 <= stage <= last:
                continue
            second.take(stage - 1, c)
            if stage == stages:
                second.place_own(c, bufs[stage - 1][c])
            if stage < last:
                second.start(stage, c)
        if t <= stages:
            f_copy(t - 1).wait_recv()
            value = f_bufs[0, t - 1] + f_bufs[1, t - 1]
            if t < stages:
                f_bufs[0, t] = value
                f_copy(t).start()
            else:
                sum_ref[...] = value
    for s in range(second_chunks + last, p.length):
        first.step(s)
    first.finish()
    keep.wait()
    for stage in range(last):
        for c in range(second_chunks):
            second.sent(stage, c)
    for stage in range(stages):
        f_copy(stage).wait_send()
    swap.finish()


def ending(ctx_count, *args):
    rows = args[0].shape[0]
    bits, second_chunks, packed_shape, second_shape, bufs = sum_shapes(ctx_count, SECOND_PACK, 16)
    vmem = pl.BlockSpec(memory_space=pltpu.VMEM)
    pieces = (ctx_count, rows // ctx_count, D)
    first, second, totals, moved = pl.pallas_call(
        functools.partial(ending_body, ctx_count, (bits, second_chunks)),
        out_shape=[
            jax.ShapeDtypeStruct((ctx_count, FIRST_PACK // ctx_count, D), BF16),
            jax.ShapeDtypeStruct(second_shape, BF16),
            jax.ShapeDtypeStruct((24, D), F32),
            jax.ShapeDtypeStruct(pieces, BF16),
        ],
        in_specs=[vmem] * len(args),
        out_specs=[vmem] * 4,
        scratch_shapes=[
            pltpu.VMEM((rows, 4 * A), BF16),
            pltpu.VMEM(pieces, BF16),
            pltpu.VMEM(packed_shape, BF16),
            pltpu.VMEM((2, 2 + bits, 24, D), F32),
        ]
        + bufs
        + part_sems(ctx_count // 2)
        + [
            pltpu.SemaphoreType.DMA((2 + 2 * bits, second_chunks)),
            pltpu.SemaphoreType.DMA((2 + 2 * bits, second_chunks)),
            pltpu.SemaphoreType.DMA((2 + bits,)),
            pltpu.SemaphoreType.DMA((2 + bits,)),
            pltpu.SemaphoreType.DMA,
        ]
        + swap_sems(ctx_count),
        compiler_params=pltpu.CompilerParams(
            collective_id=2, has_side_effects=True, vmem_limit_bytes=VMEM_LIMIT
        ),
        name="ending",
    )(*args)
    return first.reshape(-1, D), second.reshape(-1, D), totals, moved.reshape(rows, D)


def finish_body(
    place, arrange_ref, out_in, tok_in, first_ref, second_ref, sum_ref,
    out_ref, tok_ref, w_ref, b_ref, dw_ref, pw_ref, pb_ref, kern_ref, vec_ref, ow_ref, fi_ref, fb_ref, fo_ref,
    loss_ref, kb_ref,
):
    rows = out_ref.shape[0]
    slot = lax.broadcasted_iota(jnp.int32, (rows, rows), 0)
    sort = jnp.where(slot == arrange_ref[...], 1.0, 0.0).astype(BF16)
    out_ref[...] = dot_first(sort, out_in[...]).astype(BF16)
    tok_ref[...] = dot_first(sort, tok_in[...])
    for half in range(2):
        w_ref[:, D * half : D * half + D] = second_ref[192 * half : 192 * half + 192, :].astype(F32)
        pw_ref[96 * half : 96 * half + 96, :] = second_ref[384:480, A * half : A * half + A].astype(F32)
    for m in range(6):
        kern_ref[16 * m : 16 * m + 16, :] = second_ref[480:496, 128 * m : 128 * m + H * KW].astype(F32)
    for g in range(NG):
        for half in range(2):
            r0 = 96 * (2 * g + half)
            fi_ref[g, :, D * half : D * half + D] = first_ref[r0 : r0 + 96, :].astype(F32)
        fo_ref[g] = first_ref[384:768, A * g : A * g + A].astype(F32)
    ow_ref[...] = first_ref[768:960, :].astype(F32)
    total = jnp.sum(sum_ref[15:16, :], axis=1, keepdims=True)
    loss_ref[...] = total / (place[SEQS + 5].astype(F32) * D)
    kb_ref[...] = sum_ref[22:23, 0 : H * KW]
    for k in range(4):

        @pl.when(place[SEQS + 4] == k)
        def _(k=k):
            cols = slice(D // 4 * k, D // 4 * k + D // 4)
            dw_ref[...] = sum_ref[0:KW, cols]
            vec_ref[...] = sum_ref[KW : KW + 6, cols]
            fb_ref[...] = sum_ref[16 + k : 17 + k, :]
            part = slice(A // 4 * k, A // 4 * k + A // 4)
            second = slice(A + A // 4 * k, A + A // 4 * k + A // 4)
            b_ref[0:1, :] = sum_ref[20:21, part]
            b_ref[1:2, :] = sum_ref[20:21, second]
            b_ref[2:3, :] = sum_ref[21:22, part]
            pb_ref[...] = sum_ref[21:22, second]


def finish(place, arrange, *args):
    rows = args[0].shape[0]
    vmem = pl.BlockSpec(memory_space=pltpu.VMEM)
    shapes = [
        (rows, D), (D // 4, 4 * A), (3, A // 4), (KW, D // 4), (D // 4, A), (1, A // 4), (A // 4, H * KW),
        (6, D // 4), (D // 4, D), (NG, A // 4, FF // NG), (1, D), (NG, A, A), (1, 1), (1, H * KW),
    ]
    return pl.pallas_call(
        finish_body,
        out_shape=[jax.ShapeDtypeStruct((rows, D), BF16)] + [jax.ShapeDtypeStruct(shape, F32) for shape in shapes],
        in_specs=[pl.BlockSpec(memory_space=pltpu.SMEM)] + [vmem] * (len(args) + 1),
        out_specs=[vmem] * 15,
        compiler_params=pltpu.CompilerParams(vmem_limit_bytes=VMEM_LIMIT),
        name="finish",
    )(place, arrange, *args)


def local(
    hidden,
    teacher,
    lengths,
    deal,
    w_in,
    b_in,
    dw_kernel,
    pw_weight,
    pw_bias,
    kern_weight,
    kern_bias,
    out_weight,
    out_bias,
    norm1_gain,
    norm1_bias,
    ffn_in,
    ffn_in_bias,
    ffn_out,
    ffn_out_bias,
    norm2_gain,
    norm2_bias,
):
    rows = hidden.shape[1]
    ctx_count = lax.axis_size("ctx")
    group_rows = rows * ctx_count
    piece_rows = rows // ctx_count
    sorted_hidden, sorted_teacher, arrange, bounds, *smalls = setup(
        lengths, deal, hidden[0], teacher[0],
        [
            dw_kernel, out_bias, norm1_gain, norm1_bias, ffn_out_bias, norm2_gain, norm2_bias, ffn_in_bias,
            b_in, pw_bias, kern_weight,
        ],
        ctx_count,
    )
    pieces_shape = (ctx_count, piece_rows, D)
    kern_b = kern_bias[None]
    fused = group_rows <= 4096
    target, full_w_in, full_pw, full_out_w, full_ffn_in, full_ffn_out, vectors, smalls, ffn_in_b, full_kern, *rest = (
        gather_inputs(
            bounds,
            sorted_hidden,
            sorted_teacher,
            (w_in, pw_weight, out_weight, ffn_in, ffn_out),
            (0, 0, 0, 1, 1),
            smalls,
            kern_b,
            ctx_count,
            fused,
        )
    )
    target = target.reshape(rows, D)
    if fused:
        all_q8, all_keys, all_values = (item.reshape(group_rows, A) for item in rest[:3])
        conv_parts = rest[3:]
    else:
        natural = rest[0].reshape(group_rows, D)
        all_q8, all_keys, all_values = project(bounds, natural, full_w_in, smalls, rows)
        conv_parts = convolve(
            bounds, natural, full_w_in, full_pw, full_kern, kern_b, vectors, smalls, rows
        )
    conv_out, extended, conv_value, key_conv, query_ext, conv_query, spread = conv_parts
    attn_out, lse = attend(bounds, all_q8, all_keys, all_values, rows)
    result, grad_first, grad_context, stats, stats_t, layer_sums, ffn_in_sums, first_pack = layer(
        bounds, attn_out, lse, conv_out, extended, target,
        full_out_w, full_ffn_in, full_ffn_out, vectors, ffn_in_b,
    )
    (
        all_grads, all_stats, output, first_own, grad_query_conv, grad_cov, grad_tokens_conv, tail, tap_sums,
        bias_sums,
    ) = middle(
        bounds, group_rows, ctx_count, grad_context, stats_t, result.reshape(pieces_shape), first_pack,
        extended, conv_value, key_conv, query_ext, conv_query, spread, full_pw, full_kern, kern_b, vectors,
    )
    grad_query = query_grads(bounds, all_q8, grad_context, stats, all_keys, all_values)
    grad_keys, grad_values = key_grads(
        bounds, all_keys, all_values, all_q8, all_grads.reshape(group_rows, A), all_stats
    )
    first, second, totals, moved = ending(
        ctx_count, grad_query, grad_keys, grad_values, grad_query_conv, grad_cov, grad_tokens_conv, grad_first,
        extended, full_w_in, tail, first_own.reshape(-1, D), tap_sums, bias_sums, layer_sums, ffn_in_sums,
    )
    (
        dealt_out, dealt_grad, g_w_in, g_b_in, g_dw, g_pw, g_pw_b, g_kern, g_vec, g_out, g_ffn_in, g_ffn_in_b,
        g_ffn_out, loss, g_kern_b,
    ) = finish(
        bounds, arrange,
        output.reshape(rows, D), moved, first, second, totals,
    )
    return (
        dealt_out[None],
        loss[0, 0],
        dealt_grad[None],
        g_w_in,
        g_b_in,
        g_dw,
        g_pw,
        g_pw_b[0],
        g_kern,
        g_kern_b[0],
        g_out,
        g_vec[0],
        g_vec[1],
        g_vec[2],
        g_ffn_in,
        g_ffn_in_b[0],
        g_ffn_out,
        g_vec[3],
        g_vec[4],
        g_vec[5],
    )


def solution(mesh):
    return jax.shard_map(
        local,
        mesh=mesh,
        in_specs=(
            P("wt", "ctx", None),
            P("wt", "ctx", None),
            P(),
            P("wt", None),
            P("wt", None),
            P(None, "wt"),
            P(None, "wt"),
            P("wt", None),
            P("wt"),
            P("wt", None),
            P(),
            P("wt", None),
            P("wt"),
            P("wt"),
            P("wt"),
            P(None, "wt", None),
            P("wt"),
            P(None, "wt", None),
            P("wt"),
            P("wt"),
            P("wt"),
        ),
        out_specs=(
            P("wt", "ctx", None),
            P(),
            P("wt", "ctx", None),
            P("wt", None),
            P(None, "wt"),
            P(None, "wt"),
            P("wt", None),
            P("wt"),
            P("wt", None),
            P(),
            P("wt", None),
            P("wt"),
            P("wt"),
            P("wt"),
            P(None, "wt", None),
            P("wt"),
            P(None, "wt", None),
            P("wt"),
            P("wt"),
            P("wt"),
        ),
        check_vma=False,
    )
```

```python
import functools

import jax
import jax.numpy as jnp
from jax import lax
from jax.experimental import pallas as pl
from jax.experimental.pallas import tpu as pltpu
from jax.sharding import PartitionSpec as P

D = 768
H = 6
HD = 64
FF = 3072
NG = 2
KW = 9
SEQS = 6
A = 384

NORM_EPS = 1e-12
MASKED = -1e30
ROOT_HALF = 0.7071067811865476
DENSITY_NORM = 0.3989422804014327
RIM = 16
MESH = pl.DeviceIdType.MESH
BF16 = jnp.bfloat16
F32 = jnp.float32
VMEM_LIMIT = 60 * 1024 * 1024


def remote(src, dst, send, recv, target):
    return pltpu.make_async_remote_copy(
        src_ref=src,
        dst_ref=dst,
        send_sem=send,
        recv_sem=recv,
        device_id=target,
        device_id_type=MESH,
    )


def greet(peers):
    barrier = pltpu.get_barrier_semaphore()
    total = 0
    for there, target in peers:

        @pl.when(there)
        def _(target=target):
            pl.semaphore_signal(barrier, inc=1, device_id=target, device_id_type=MESH)

        total = total + jnp.where(there, 1, 0)
    pl.semaphore_wait(barrier, total)


class Place:
    def __init__(self, count):
        self.count = count
        self.length = count // 2
        self.valid = count - count // 8
        self.window = count // 2
        self.me = lax.axis_index("ctx")
        self.line = lax.div(self.me, 2)
        self.side = lax.rem(self.me, 2)
        self.mate_index = self.me + 1 - 2 * self.side
        self.mate = {"ctx": self.mate_index}
        self.up = {"ctx": lax.rem(self.me + 2, count)}
        self.down = {"ctx": lax.rem(self.me + count - 2, count)}
        self.has_up = self.line < self.length - 1
        self.has_down = self.line > 0

    def others(self):
        return [
            (self.me >= 0, {"ctx": lax.rem(self.me + shift, self.count)}) for shift in range(1, self.count)
        ]


class PieceNeeds:
    def __init__(self, place, first, last):
        self.place, self.first, self.last = place, first, last

    def at(self, index, source):
        p = self.place
        return (
            (index < p.valid)
            & (self.first <= index + p.window)
            & (self.last >= index - p.window)
        )

    def above(self, line, source):
        p = self.place
        return (2 * line < p.valid) & (self.last >= 2 * line - p.window)

    def below(self, line, source):
        return self.first <= 2 * line + 1 + self.place.window

    def sent(self, source):
        return source >= 0


class BlockNeeds:
    def __init__(self, place):
        self.place = place

    def at(self, index, source):
        p = self.place
        near = (index <= source + p.window) & (index >= source - p.window)
        return near & (index < p.valid) & (source < p.valid)

    def above(self, line, source):
        p = self.place
        return (2 * line < p.valid) & (2 * line <= source + p.window) & (source < p.valid)

    def below(self, line, source):
        p = self.place
        return (2 * line + 1 >= source - p.window) & (source < p.valid)

    def sent(self, source):
        return source < self.place.valid


class AllNeeds:
    def __init__(self, place):
        self.place = place

    def at(self, index, source):
        return source * 0 == 0

    def above(self, line, source):
        return source * 0 == 0

    def below(self, line, source):
        return source * 0 == 0

    def sent(self, source):
        return source * 0 == 0


class Part:
    def __init__(self, place, needs, own, slot, send, recv):
        self.place, self.needs, self.own, self.slot = place, needs, own, slot
        self.send, self.recv = send, recv

    def copy(self, src, source, send, recv, target):
        return remote(src, self.slot(source), self.send.at[send], self.recv.at[recv], target)

    def go_up(self, source):
        p = self.place
        return p.has_up & self.needs.above(p.line + 1, source)

    def go_down(self, source):
        p = self.place
        return p.has_down & self.needs.below(p.line - 1, source)

    def from_below(self, s, source):
        p = self.place
        return (p.line - s >= 0) & self.needs.above(p.line, source)

    def from_above(self, s, source):
        p = self.place
        return (p.line + s < p.length) & self.needs.below(p.line, source)


class LinePart(Part):
    def start(self):
        p = self.place

        @pl.when(self.needs.at(p.mate_index, p.me))
        def _():
            self.copy(self.own, p.me, (2, 0), (2, 0), p.mate).start()

        @pl.when(self.go_up(p.me))
        def _():
            self.copy(self.own, p.me, (0, 0), (0, 1), p.up).start()

        @pl.when(self.go_down(p.me))
        def _():
            self.copy(self.own, p.me, (1, 0), (1, 1), p.down).start()

    def step(self, s):
        p = self.place
        for row, source, there, go, target in (
            (0, p.me - 2 * s, self.from_below, self.go_up, p.up),
            (1, p.me + 2 * s, self.from_above, self.go_down, p.down),
        ):

            @pl.when(there(s, source))
            def _(row=row, source=source, go=go, target=target):
                held = self.slot(source)
                self.copy(held, source, (2 + row, s), (row, s), p.mate).wait_recv()

                @pl.when(go(source))
                def _():
                    self.copy(held, source, (row, s), (row, s + 1), target).start()

                @pl.when(self.needs.at(p.mate_index, source))
                def _():
                    self.copy(held, source, (2 + row, s), (2 + row, s), p.mate).start()

    def finish(self, taken=False):
        p = self.place
        for s in range(p.length):
            for row, source, exists, go, target in (
                (0, p.me - 2 * s, p.line - s >= 0, self.go_up, p.up),
                (1, p.me + 2 * s, p.line + s < p.length, self.go_down, p.down),
            ):
                held = self.slot(source)
                mates = source + 1 - 2 * p.side
                if s > 0 or row == 0:

                    @pl.when(exists & self.needs.at(p.me, mates) & (not taken))
                    def _(row=row, s=s, mates=mates):
                        theirs = self.slot(mates)
                        self.copy(theirs, mates, (2 + row, s), (2 + row, s), p.mate).wait_recv()

                    @pl.when(exists & self.needs.at(p.mate_index, source))
                    def _(row=row, s=s, held=held, source=source):
                        self.copy(held, source, (2 + row, s), (2 + row, s), p.mate).wait_send()

                @pl.when(exists & go(source) & ((s == 0) | self.arrived(row, source)))
                def _(row=row, s=s, held=held, source=source, target=target):
                    self.copy(held, source, (row, s), (row, s + 1), target).wait_send()

    def arrived(self, row, source):
        p = self.place
        return self.needs.above(p.line, source) if row == 0 else self.needs.below(p.line, source)


class PairPart(Part):
    def across(self):
        p = self.place

        @pl.when(self.needs.sent(p.me))
        def _():
            self.copy(self.own, p.me, (4, 0), (4, 0), p.mate).start()

    def along(self):
        p = self.place

        @pl.when(self.go_up(p.me))
        def _():
            self.copy(self.own, p.me, (0, 0), (0, 1), p.up).start()

        @pl.when(self.go_down(p.me))
        def _():
            self.copy(self.own, p.me, (1, 0), (1, 1), p.down).start()

    def middle(self):
        p = self.place
        source = p.mate_index
        held = self.slot(source)

        @pl.when(self.needs.sent(source))
        def _():
            self.copy(held, source, (4, 0), (4, 0), p.mate).wait_recv()

        @pl.when(self.go_up(source))
        def _():
            self.copy(held, source, (2, 0), (2, 1), p.up).start()

        @pl.when(self.go_down(source))
        def _():
            self.copy(held, source, (3, 0), (3, 1), p.down).start()

    def step(self, s):
        p = self.place
        for base, column in ((0, p.me), (2, p.mate_index)):
            for row, source, there, go, target in (
                (0, column - 2 * s, self.from_below, self.go_up, p.up),
                (1, column + 2 * s, self.from_above, self.go_down, p.down),
            ):

                @pl.when(there(s, source))
                def _(row=row + base, source=source, go=go, target=target):
                    held = self.slot(source)
                    self.copy(held, source, (row, s), (row, s), p.mate).wait_recv()

                    @pl.when(go(source))
                    def _():
                        self.copy(held, source, (row, s), (row, s + 1), target).start()

    def finish(self):
        p = self.place

        @pl.when(self.needs.sent(p.me))
        def _():
            self.copy(self.own, p.me, (4, 0), (4, 0), p.mate).wait_send()

        for s in range(p.length):
            for base, column in ((0, p.me), (2, p.mate_index)):
                for row, source, there, go, target in (
                    (0, column - 2 * s, self.from_below, self.go_up, p.up),
                    (1, column + 2 * s, self.from_above, self.go_down, p.down),
                ):
                    passed = there(s, source) if s > 0 else p.me >= 0

                    @pl.when(passed & go(source))
                    def _(row=row + base, s=s, source=source, target=target):
                        held = self.slot(source)
                        self.copy(held, source, (row, s), (row, s + 1), target).wait_send()


class Swap:
    def __init__(self, place, src, dst, send, recv):
        self.place, self.src, self.dst, self.send, self.recv = place, src, dst, send, recv

    def copy(self, shift):
        p = self.place
        there = lax.rem(p.me + shift, p.count)
        return remote(
            self.src.at[there], self.dst.at[p.me], self.send.at[shift], self.recv.at[shift], {"ctx": there}
        )

    def keep(self):
        p = self.place
        return pltpu.make_async_copy(self.src.at[p.me], self.dst.at[p.me], self.send.at[0])

    def start(self):
        for shift in range(1, self.place.count):
            self.copy(shift).start()
        self.keep().start()

    def finish(self):
        p = self.place
        self.keep().wait()
        for shift in range(1, p.count):
            self.copy(shift).wait_send()
            source = lax.rem(p.me + p.count - shift, p.count)
            held = self.dst.at[source]
            remote(held, held, self.send.at[shift], self.recv.at[shift], p.mate).wait_recv()


def part_sems(length):
    return [
        pltpu.SemaphoreType.DMA((5, length + 1)),
        pltpu.SemaphoreType.DMA((5, length + 1)),
    ]


def swap_sems(count):
    return [pltpu.SemaphoreType.DMA((count,)), pltpu.SemaphoreType.DMA((count,))]


def dot(left, right):
    return jnp.dot(left, right, preferred_element_type=F32)


def setup_body(
    lengths, deal_ref, x_ref, t_ref, dw_ref, *refs
):
    rows_in, refs = refs[:6], refs[6:]
    fb_in, b_in, pb_in, kern_in = refs[:4]
    sx_ref, st_ref, arrange_ref, bounds, wide, narrow, ffn, kern, kern_s = refs[4:]
    count, piece = sx_ref.shape[:2]
    rows = count * piece
    group = lax.axis_index("wt")
    place = lax.axis_index("ctx")
    start = place * rows
    end = jnp.int32(0)
    total = jnp.int32(0)
    first, last = jnp.int32(0), jnp.int32(rows * count)
    ends = []
    for i in range(SEQS):
        end = end + lengths[group, i]
        ends.append(end)
        bounds[i] = end
        for g in range(4):
            total = total + lengths[g, i]
    for i in range(SEQS):
        first = jnp.where(ends[i] <= start, ends[i], first)
    for i in reversed(range(SEQS)):
        last = jnp.where(ends[i] >= start + rows, ends[i], last)
    bounds[SEQS] = start
    bounds[SEQS + 1] = lax.div(first, rows)
    bounds[SEQS + 2] = lax.div(last - 1, rows)
    bounds[SEQS + 3] = place
    bounds[SEQS + 4] = group
    bounds[SEQS + 5] = total
    slots = deal_ref[0:1, pl.ds(pl.multiple_of(start, 128), rows)]
    block = lax.div(slots, rows)
    arrange = block * piece + (slots - block * rows) - place * piece
    arrange_ref[...] = arrange
    sort = jnp.where(lax.broadcasted_iota(jnp.int32, (rows, rows), 0) == arrange, 1.0, 0.0).astype(BF16)
    for src, dst in ((x_ref, sx_ref), (t_ref, st_ref)):
        moved = dot(sort, src[...]).astype(BF16)
        for j in range(count):
            dst[j] = moved[piece * j : piece * j + piece]
    wide[...] = jnp.zeros(wide.shape, F32)
    wide[0:KW, :] = dw_ref[...].astype(F32)
    for i, row in enumerate(rows_in):
        wide[KW + i : KW + i + 1, :] = row[...].astype(F32).reshape(1, D // 4)
    narrow[...] = jnp.zeros(narrow.shape, F32)
    narrow[0:3, : A // 4] = b_in[...].astype(F32)
    narrow[3:4, : A // 4] = pb_in[...].astype(F32).reshape(1, A // 4)
    ffn[...] = jnp.zeros(ffn.shape, F32)
    ffn[0:1, :] = fb_in[...].astype(F32).reshape(1, D)
    kern_s[...] = jnp.zeros(kern_s.shape, F32)
    kern_s[: H * KW, : A // 4] = kern_in[...].astype(F32)
    kern[...] = kern_s[...].T[: A // 4]


SMALL_SHAPES = [(16, D // 4), (8, 128), (8, D), (A // 4, 128)]


def setup(lengths, deal, hidden, teacher, smalls, count):
    rows = hidden.shape[0]
    vmem = pl.BlockSpec(memory_space=pltpu.VMEM)
    smem = pl.BlockSpec(memory_space=pltpu.SMEM)
    pieces = jax.ShapeDtypeStruct((count, rows // count, D), BF16)
    return pl.pallas_call(
        setup_body,
        out_shape=[
            pieces,
            pieces,
            jax.ShapeDtypeStruct((1, rows), jnp.int32),
            jax.ShapeDtypeStruct((SEQS + 6,), jnp.int32),
        ]
        + [jax.ShapeDtypeStruct(shape, F32) for shape in SMALL_SHAPES],
        in_specs=[smem] + [vmem] * (3 + len(smalls)),
        out_specs=[vmem] * 3 + [smem] + [vmem] * 4,
        scratch_shapes=[pltpu.VMEM((128, 128), F32)],
        compiler_params=pltpu.CompilerParams(vmem_limit_bytes=VMEM_LIMIT),
        name="setup",
    )(lengths, deal, hidden, teacher, *smalls)


N_SMALL = 4


def gather_body(count, spans, fused, *refs):
    n = len(spans)
    inputs, refs = refs[: n + 4 + N_SMALL], refs[n + 4 + N_SMALL :]
    x_ref, t_ref = inputs[:2]
    shards = list(inputs[2 : 2 + n])
    own_small = list(inputs[2 + n : 2 + n + N_SMALL])
    bounds, kb_ref = inputs[2 + n + N_SMALL :]
    target_ref = refs[0]
    fulls = list(refs[1 : 1 + n])
    vec_ref, small_ref, fb_ref, kw_ref = refs[1 + n : 5 + n]
    refs = refs[5 + n :]
    if fused:
        out_hbm, conv_outs, refs = refs[:3], refs[3:10], refs[10:]
        out_ref, held_out, conv_scratch, project_sem, refs = refs[0], refs[1:4], refs[4:10], refs[10], refs[11:]
    else:
        out_ref, refs = refs[0], refs[1:]
    all_small = refs[:N_SMALL]
    local_sem, w_send, w_recv, pad_send, pad_recv = refs[N_SMALL : N_SMALL + 5]
    sems = refs[N_SMALL + 5 :]
    p = Place(count)
    k = lax.axis_index("wt")
    side = lax.rem(k, 2)
    core_mate = {"wt": k + 1 - 2 * side}
    far = lax.rem(k + 2, 4)
    far_mate = {"wt": far}

    def span(i, ref, index):
        if i >= n:
            return ref.at[index]
        axis, size = spans[i]
        window = pl.ds(pl.multiple_of(index * size, size), size)
        return ref.at[window] if axis == 0 else ref.at[:, window]

    shards += own_small
    fulls += all_small
    total = n + N_SMALL
    order = list(range(n, total)) + list(range(n))

    greet(p.others() + [(k >= 0, core_mate), (k >= 0, far_mate)])
    quarter, eighth = count // 4, count // 8
    cuts = [0, quarter, p.valid - quarter, p.valid - eighth, p.valid]
    parts = []
    for i, kind in enumerate((LinePart, LinePart, PairPart, PairPart)):
        first, end = cuts[i], cuts[i + 1]
        parts.append(
            kind(
                p,
                PieceNeeds(p, first, end - 1),
                x_ref.at[first:end],
                lambda j, first=first, end=end: out_ref.at[first:end, j],
                sems[2 * i],
                sems[2 * i + 1],
            )
        )
    low, high, *pairs = parts
    lines = [high, low]
    for part in pairs:
        part.across()
    for part in lines:
        part.start()
    for part in pairs:
        part.along()
    for i in order:
        held = span(i, fulls[i], k)
        remote(shards[i], held, w_send.at[0, i], w_recv.at[0, i], far_mate).start()
        remote(shards[i], held, w_send.at[1, i], w_recv.at[1, i], core_mate).start()

    def pad_copy(there):
        return remote(
            x_ref.at[p.valid :],
            out_ref.at[p.valid :, p.me],
            pad_send.at[there - p.valid],
            pad_recv.at[p.me],
            {"ctx": p.me * 0 + there},
        )

    def pads():
        for there in range(p.valid, count):

            @pl.when(p.me != there)
            def _(there=there):
                pad_copy(there).start()

    own_copy = pltpu.make_async_copy(x_ref, out_ref.at[:, p.me], local_sem.at[total])
    keeps = [
        pltpu.make_async_copy(shards[i], span(i, fulls[i], k), local_sem.at[i]) for i in range(total)
    ]
    for keep in [own_copy] + keeps:
        keep.start()
    swap = Swap(p, t_ref, target_ref, sems[8], sems[9])

    def relay(i):
        held = span(i, fulls[i], far)
        remote(held, held, w_send.at[2, i], w_recv.at[0, i], core_mate).wait_recv()
        remote(held, held, w_send.at[2, i], w_recv.at[2, i], core_mate).start()

    def whole(i):
        keeps[i].wait()
        held = span(i, fulls[i], k)
        remote(shards[i], held, w_send.at[1, i], w_recv.at[1, i], core_mate).wait_recv()
        remote(held, held, w_send.at[2, i], w_recv.at[2, i], core_mate).wait_recv()

    def spread(ref, step, shape):
        row = lax.broadcasted_iota(jnp.int32, shape, 0)
        column = lax.broadcasted_iota(jnp.int32, shape, 1)
        value = 0.0
        for index in range(4):
            move = jnp.where((column == row + step * index) & (row < step), 1.0, 0.0).astype(BF16)
            value += dot(ref[index].astype(BF16), move)
        return value

    def smalls():
        for i in range(n, total):
            whole(i)
        vec_ref[...] = spread(all_small[0], D // 4, (D // 4, D))
        small_ref[...] = spread(all_small[1], A // 4, (128, A))
        for index in range(4):
            fb_ref[index : index + 1, :] = all_small[2][index, 0:1, :]
            kw_ref[A // 4 * index : A // 4 * index + A // 4, :] = all_small[3][index].astype(BF16)

    def project_rows(x, blocks, sources):
        lead = out_ref[blocks, sources].shape[:-1]
        w_ref = fulls[0]
        query = (dot(x, w_ref[:, :A]) + small_ref[0:1, :]).astype(BF16).astype(F32)
        keys = dot(x, w_ref[:, A : 2 * A])
        values = dot(x, w_ref[:, 2 * A : 3 * A]) + small_ref[1:2, :]
        for value, held in zip((query * (HD**-0.5), keys, values), held_out):
            held[blocks, sources] = value.astype(BF16).reshape(lead + (A,))

    def project_copies(source):
        return [
            pltpu.make_async_copy(
                held_out[i].at[: p.valid, source], out_hbm[i].at[: p.valid, source], project_sem.at[i, source]
            )
            for i in range(3)
        ]

    def project_source(source):
        blocks = slice(0, p.valid)
        project_rows(out_ref[blocks, source].reshape(-1, D), blocks, source)
        for copy in project_copies(source):
            copy.start()

    def pad_copies():
        return [
            pltpu.make_async_copy(held_out[i].at[p.valid :], out_hbm[i].at[p.valid :], project_sem.at[i, 0])
            for i in range(3)
        ]

    def wait_pads():
        for shift in range(1, count):
            source = lax.rem(p.me + shift, count)
            held = out_ref.at[p.valid :, source]
            remote(held, held, pad_send.at[0], pad_recv.at[source], p.mate).wait_recv()

    def candidates(first, end, column, mates):
        def one(i, _):
            s = lax.div(i + 1, 2)
            odd = lax.rem(i, 2)
            line = p.line + (2 * odd - 1) * s
            source = column + (2 * odd - 1) * 2 * s

            @pl.when((line >= 0) & (line < p.length) & (p.me < p.valid))
            def _():
                if mates:
                    for part in lines:

                        @pl.when(part.needs.at(p.me, source))
                        def _(part=part):
                            theirs = part.slot(source)
                            at = (2 + odd, s)
                            part.copy(theirs, source, at, at, p.mate).wait_recv()

                project_source(source)

            return 0

        lax.fori_loop(first, end, one, 0)

    for part in pairs:
        part.middle()
    for s in range(1, p.length - 1):
        for part in lines + pairs:
            part.step(s)
        if s == 1:
            for i in order[: N_SMALL + 1]:
                relay(i)
    swap.start()
    pads()
    smalls()
    whole(0)
    if fused:
        own_copy.wait()
        candidates(0, 2 * p.length - 3, p.me, False)
        candidates(0, 1, p.mate_index, True)
    for part in lines + pairs:
        part.step(p.length - 1)
    for i in order[N_SMALL + 1 :]:
        relay(i)
    if fused:
        candidates(2 * p.length - 3, 2 * p.length - 1, p.me, False)
        candidates(1, 2 * p.length - 1, p.mate_index, True)

        @pl.when(p.me >= p.valid)
        def _():
            wait_pads()
            blocks = slice(p.valid, count)
            project_rows(out_ref[blocks].reshape(-1, D), blocks, slice(0, count))
            for copy in pad_copies():
                copy.start()

        piece = x_ref.shape[1]
        conv_out, ext_ref, cv_ref = conv_outs[:3]
        before = jnp.maximum(p.me - 1, 0)
        after = jnp.minimum(p.me + 1, count - 1)
        ext_ref[0:RIM, :] = out_ref[before, count - 1, piece - RIM :, :]
        for j in range(count):
            ext_ref[RIM + piece * j : RIM + piece * j + piece, :] = out_ref[p.me, j]
        ext_ref[RIM + piece * count :, :] = out_ref[after, 0, :RIM, :]
        whole(1)
        conv_core(
            bounds, count * count * piece, fulls[0], fulls[1], kw_ref, kb_ref, vec_ref, small_ref,
            *conv_outs, *conv_scratch,
        )

        @pl.when(p.me < p.valid)
        def _():
            for source in range(count):
                for copy in project_copies(source):
                    copy.wait()

        @pl.when(p.me >= p.valid)
        def _():
            for copy in pad_copies():
                copy.wait()

    else:
        own_copy.wait()
        whole(1)

        @pl.when(p.me >= p.valid)
        def _():
            wait_pads()

    for i in range(2, n):
        whole(i)
    for i in range(total):
        held = span(i, fulls[i], k)
        remote(shards[i], held, w_send.at[0, i], w_recv.at[0, i], far_mate).wait_send()
        remote(shards[i], held, w_send.at[1, i], w_recv.at[1, i], core_mate).wait_send()
        remote(held, held, w_send.at[2, i], w_recv.at[2, i], core_mate).wait_send()
    for part in pairs:
        part.finish()
    for part in lines:
        part.finish(taken=fused)
    for there in range(p.valid, count):

        @pl.when(p.me != there)
        def _(there=there):
            pad_copy(there).wait_send()

    swap.finish()


def gather_inputs(bounds, pieces, targets, shards, axes, smalls, kern_bias, ctx_count, fused):
    length = ctx_count // 2
    rows = pieces.shape[0] * pieces.shape[1]
    fulls, spans = [], []
    for shard, axis in zip(shards, axes):
        shape = list(shard.shape)
        spans.append((axis, shape[axis]))
        shape[axis] *= 4
        fulls.append(jax.ShapeDtypeStruct(tuple(shape), shard.dtype))
    n = len(shards)
    total = n + N_SMALL
    vmem = pl.BlockSpec(memory_space=pltpu.VMEM)
    hbm = pl.BlockSpec(memory_space=pl.ANY)
    natural = (ctx_count,) + pieces.shape
    heads = (ctx_count,) + pieces.shape[:-1] + (A,)
    outs = (
        [jax.ShapeDtypeStruct(targets.shape, targets.dtype)]
        + fulls
        + [
            jax.ShapeDtypeStruct((16, D), F32),
            jax.ShapeDtypeStruct((8, A), F32),
            jax.ShapeDtypeStruct((4, D), F32),
            jax.ShapeDtypeStruct((A, 128), BF16),
        ]
    )
    specs = [hbm] + [vmem] * 2 + [hbm] * (n - 2) + [vmem] * 4
    scratch = []
    if fused:
        conv_outs, conv_scratch = conv_shapes(rows)
        outs += [jax.ShapeDtypeStruct(heads, BF16)] * 3 + conv_outs
        specs += [hbm] * 3 + [vmem] * 7
        scratch += [pltpu.VMEM(natural, BF16)] + [pltpu.VMEM(heads, BF16)] * 3 + conv_scratch
        scratch += [pltpu.SemaphoreType.DMA((3, ctx_count))]
    else:
        outs.append(jax.ShapeDtypeStruct(natural, BF16))
        specs.append(hbm)
    return pl.pallas_call(
        functools.partial(gather_body, ctx_count, spans, fused),
        out_shape=outs,
        in_specs=[vmem] * (2 + n + len(smalls)) + [pl.BlockSpec(memory_space=pltpu.SMEM), vmem],
        out_specs=specs,
        scratch_shapes=scratch
        + [pltpu.VMEM((4,) + shape, F32) for shape in SMALL_SHAPES]
        + [
            pltpu.SemaphoreType.DMA((total + 1,)),
            pltpu.SemaphoreType.DMA((3, total)),
            pltpu.SemaphoreType.DMA((3, total)),
            pltpu.SemaphoreType.DMA((ctx_count // 8,)),
            pltpu.SemaphoreType.DMA((ctx_count,)),
        ]
        + part_sems(length) * 4
        + swap_sems(ctx_count),
        compiler_params=pltpu.CompilerParams(
            collective_id=0, has_side_effects=True, vmem_limit_bytes=VMEM_LIMIT
        ),
        name="gather_inputs",
    )(pieces, targets, *shards, *smalls, bounds, kern_bias)


class Sum:
    def __init__(self, bits, chunks, packed, bufs, out, send, recv, mine=None):
        self.bits, self.chunks, self.packed, self.bufs, self.out = bits, chunks, packed, bufs, out
        self.mine = mine
        self.send, self.recv = send, recv
        self.stages = 2 + bits
        self.last = self.stages + bits
        k = lax.axis_index("wt")
        me = lax.axis_index("ctx")
        self.core = lax.rem(k, 2)
        self.far = lax.div(k, 2)
        self.bit = [lax.rem(lax.div(me, 1 << b), 2) for b in range(bits)]
        self.targets = [{"wt": k + 1 - 2 * self.core}, {"wt": lax.rem(k + 2, 4)}]
        for b in range(bits):
            self.targets.append({"ctx": me + (1 << b) * (1 - 2 * self.bit[b])})

    def source(self, stage, c, kept):
        whole = slice(None)

        def pick(value):
            return value if kept else 1 - value

        if stage == 0 and kept and self.mine is not None:
            return self.mine.at[(whole,) * (self.bits + 1) + (c,)]
        if stage == 0:
            return self.packed.at[(whole, pick(self.core)) + (whole,) * self.bits + (c,)]
        if stage == 1:
            return self.bufs[0].at[c, pick(self.far)]
        b = stage - 2
        return self.bufs[stage - 1].at[(c,) + (whole,) * (self.bits - b - 1) + (pick(self.bit[b]),)]

    def spread(self, b, c, other):
        index = [self.bit[j] for j in range(b, -1, -1)]
        if other:
            index[0] = 1 - index[0]
        return self.out.at[(slice(None),) * (self.bits - 1 - b) + tuple(index) + (c,)]

    def place_own(self, c, value):
        self.out[tuple(self.bit[j] for j in range(self.bits - 1, -1, -1)) + (c,)] = value

    def copy(self, stage, c):
        if stage < self.stages:
            src, dst, target = self.source(stage, c, False), self.bufs[stage].at[c], self.targets[stage]
        else:
            b = self.bits - 1 - (stage - self.stages)
            src, dst, target = self.spread(b, c, False), self.spread(b, c, False), self.targets[2 + b]
        return remote(src, dst, self.send.at[stage, c], self.recv.at[stage, c], target)

    def start(self, stage, c):
        self.copy(stage, c).start()

    def take(self, stage, c):
        if stage >= self.stages:
            b = self.bits - 1 - (stage - self.stages)
            held = self.spread(b, c, True)
            remote(
                held, held, self.send.at[stage, c], self.recv.at[stage, c], self.targets[2 + b]
            ).wait_recv()
            return
        self.copy(stage, c).wait_recv()
        mine, sums = self.source(stage, c, True), self.bufs[stage].at[c]
        lead = sums.shape[:-2]
        total = 1
        for size in lead:
            total *= size

        def one(at, _):
            index, rest = [], at
            for size in reversed(lead):
                index.append(lax.rem(rest, size))
                rest = lax.div(rest, size)
            index = tuple(reversed(index))
            value = mine[index].astype(F32) + sums[index].astype(F32)
            sums[index] = value.astype(BF16)
            return 0

        if lead:
            lax.fori_loop(0, total, one, 0)
        else:
            sums[...] = (mine[...].astype(F32) + sums[...].astype(F32)).astype(BF16)

    def sent(self, stage, c):
        self.copy(stage, c).wait_send()

    def open(self):
        for c in range(min(4, self.chunks)):
            self.start(0, c)

    def across(self, first, end):
        for c in range(first, min(end, self.chunks)):
            self.take(0, c)
            self.start(1, c)
            if c + 4 < self.chunks:
                self.start(0, c + 4)


def sum_shapes(ctx_count, rows, size):
    bits = ctx_count.bit_length() - 1
    piece = min(size, rows // ctx_count)
    chunks = rows // ctx_count // piece
    twos = (2,) * bits
    bufs = [
        pltpu.VMEM((chunks, 2) + twos + (piece, D), BF16),
        pltpu.VMEM((chunks,) + twos + (piece, D), BF16),
    ]
    for b in range(bits):
        bufs.append(pltpu.VMEM((chunks,) + twos[b + 1 :] + (piece, D), BF16))
    tail = (chunks, piece, D)
    return bits, chunks, (2, 2) + twos + tail, twos + tail, bufs


def seg_of(position, bounds):
    seg = jnp.zeros(position.shape, jnp.int32)
    for i in range(SEQS):
        seg = seg + jnp.where(position >= bounds[i], 1, 0)
    return seg


def reach(bounds, first, last, group_rows):
    begin, end = jnp.int32(0), jnp.int32(group_rows)
    for i in range(SEQS):
        begin = jnp.where(bounds[i] <= first, bounds[i], begin)
    for i in reversed(range(SEQS)):
        end = jnp.where(bounds[i] > last, bounds[i], end)
    return begin, end


def half_masks(rows):
    lane = lax.broadcasted_iota(jnp.int32, (rows, 128), 1)
    low = jnp.where(lane < HD, 1.0, 0.0).astype(BF16)
    return low, (1.0 - low.astype(F32)).astype(BF16)


def dot_last(left, right):
    return lax.dot_general(left, right, (((1,), (1,)), ((), ())), preferred_element_type=F32)


def attend_body(tq, tk, bounds, q_ref, k_ref, v_ref, out_ref, lse_ref, m_ref, acc_ref):
    rows, group_rows = out_ref.shape[0], k_ref.shape[0]
    base = pl.multiple_of(bounds[SEQS], tq)
    q_masks, k_masks = half_masks(tq), half_masks(tk)
    lane = lax.broadcasted_iota(jnp.int32, (tq, 128), 1)
    low = lane < HD

    def tile(qi, _):
        q0 = pl.multiple_of(qi * tq, tq)
        first = pl.multiple_of(base + q0, tq)
        begin, end = reach(bounds, first, first + tq - 1, group_rows)
        q_seg = seg_of(first + lax.broadcasted_iota(jnp.int32, (tq, 1), 0), bounds)
        m_ref[...] = jnp.full(m_ref.shape, MASKED, F32)
        acc_ref[...] = jnp.zeros(acc_ref.shape, F32)

        def step(kt, _):
            k0 = pl.multiple_of(kt * tk, tk)
            k_seg = seg_of(k0 + lax.broadcasted_iota(jnp.int32, (1, tk), 1), bounds)
            bias = jnp.where(q_seg == k_seg, 0.0, MASKED)
            for pair in range(H // 2):
                cols = slice(128 * pair, 128 * pair + 128)
                q_pair = q_ref[pl.ds(first, tq), cols]
                k_pair = k_ref[pl.ds(k0, tk), cols]
                v_pair = v_ref[pl.ds(k0, tk), cols]
                for side in range(2):
                    head = 2 * pair + side
                    scores = dot_last(q_pair * q_masks[side], k_pair) + bias
                    old = m_ref[head]
                    new = jnp.maximum(old, jnp.max(scores, axis=1, keepdims=True))
                    weights = jnp.exp(scores - jnp.tile(new, (1, tk // 128)))
                    v_ones = v_pair * k_masks[side] + k_masks[1 - side]
                    acc_ref[head] = acc_ref[head] * jnp.exp(old - new) + jnp.dot(
                        weights.astype(BF16), v_ones, preferred_element_type=F32
                    )
                    m_ref[head] = new
            return 0

        lax.fori_loop(lax.div(begin, tk), lax.div(end + tk - 1, tk), step, 0)
        lse = jnp.zeros((tq, 128), F32)
        for pair in range(H // 2):
            left, right = acc_ref[2 * pair], acc_ref[2 * pair + 1]
            crossed = jnp.where(low, right, left)
            total = pltpu.roll(crossed, HD, 1)
            out_ref[pl.ds(q0, tq), 128 * pair : 128 * pair + 128] = jnp.where(low, left, right) / total
            lse = jnp.where(lane == 2 * pair, m_ref[2 * pair] + jnp.log(total), lse)
            lse = jnp.where(lane == 2 * pair + 1, m_ref[2 * pair + 1] + jnp.log(crossed), lse)
        lse_ref[pl.ds(q0, tq), :] = lse
        return 0

    lax.fori_loop(0, rows // tq, tile, 0)


def attend(bounds, query, keys, values, rows):
    tq, tk = rows, rows // 2
    return pl.pallas_call(
        functools.partial(attend_body, tq, tk),
        out_shape=[
            jax.ShapeDtypeStruct((rows, A), F32),
            jax.ShapeDtypeStruct((rows, 128), F32),
        ],
        in_specs=[pl.BlockSpec(memory_space=pltpu.SMEM)]
        + [pl.BlockSpec(memory_space=pltpu.VMEM)] * 3,
        out_specs=[pl.BlockSpec(memory_space=pltpu.VMEM)] * 2,
        scratch_shapes=[pltpu.VMEM((H, tq, 128), F32), pltpu.VMEM((H, tq, 128), F32)],
        compiler_params=pltpu.CompilerParams(vmem_limit_bytes=VMEM_LIMIT),
        name="attend",
    )(bounds, query, keys, values)


def query_grads_body(tq, tk, bounds, q_ref, g_ref, stat_ref, k_ref, v_ref, out_ref, rep_ref):
    rows, group_rows = out_ref.shape[0], k_ref.shape[0]
    base = pl.multiple_of(bounds[SEQS], tq)
    q_masks, k_masks = half_masks(tq), half_masks(tk)

    def tile(qi, _):
        q0 = pl.multiple_of(qi * tq, tq)
        first = pl.multiple_of(base + q0, tq)
        begin, end = reach(bounds, first, first + tq - 1, group_rows)
        q_seg = seg_of(first + lax.broadcasted_iota(jnp.int32, (tq, 1), 0), bounds)
        stat = stat_ref[pl.ds(q0, tq), :]
        for head in range(H):
            rep_ref[head] = jnp.broadcast_to(stat[:, head : head + 1], (tq, 128))
            rep_ref[H + head] = jnp.broadcast_to(stat[:, 8 + head : 9 + head], (tq, 128))
        out_ref[pl.ds(q0, tq), :] = jnp.zeros((tq, A), F32)

        def step(kt, _):
            k0 = pl.multiple_of(kt * tk, tk)
            k_seg = seg_of(k0 + lax.broadcasted_iota(jnp.int32, (1, tk), 1), bounds)
            bias = jnp.where(q_seg == k_seg, 0.0, MASKED)
            for pair in range(H // 2):
                cols = slice(128 * pair, 128 * pair + 128)
                q_pair = q_ref[pl.ds(first, tq), cols]
                g_pair = g_ref[pl.ds(q0, tq), cols]
                k_pair = k_ref[pl.ds(k0, tk), cols]
                v_pair = v_ref[pl.ds(k0, tk), cols]
                total = jnp.zeros((tq, 128), F32)
                for side in range(2):
                    head = 2 * pair + side
                    scores = dot_last(q_pair * q_masks[side], k_pair) + bias
                    prob = jnp.exp(scores - jnp.tile(rep_ref[head], (1, tk // 128)))
                    back = dot_last(g_pair * q_masks[side], v_pair)
                    back = prob * (back - jnp.tile(rep_ref[H + head], (1, tk // 128)))
                    total = total + jnp.dot(
                        back.astype(BF16), k_pair * k_masks[side], preferred_element_type=F32
                    )
                out_ref[pl.ds(q0, tq), cols] += total
            return 0

        lax.fori_loop(lax.div(begin, tk), lax.div(end + tk - 1, tk), step, 0)
        return 0

    lax.fori_loop(0, rows // tq, tile, 0)


def query_grads(bounds, query, grads, stats, keys, values):
    rows = grads.shape[0]
    tq, tk = rows, rows // 2
    return pl.pallas_call(
        functools.partial(query_grads_body, tq, tk),
        out_shape=jax.ShapeDtypeStruct((rows, A), F32),
        in_specs=[pl.BlockSpec(memory_space=pltpu.SMEM)]
        + [pl.BlockSpec(memory_space=pltpu.VMEM)] * 5,
        out_specs=pl.BlockSpec(memory_space=pltpu.VMEM),
        scratch_shapes=[pltpu.VMEM((2 * H, tq, 128), F32)],
        compiler_params=pltpu.CompilerParams(vmem_limit_bytes=VMEM_LIMIT),
        name="query_grads",
    )(bounds, query, grads, stats, keys, values)


def key_grads_body(
    tk, bounds, k_all, v_all, q_ref, g_ref, stat_ref, dk_ref, dv_ref, k_ref, v_ref, sem
):
    rows, group_rows = dk_ref.shape[0], q_ref.shape[0]
    own = pl.ds(pl.multiple_of(bounds[SEQS], rows), rows)
    for copy in fetch([k_all.at[own], v_all.at[own]], [k_ref, v_ref], sem):
        copy.wait()
    tq = stat_ref.shape[2]
    base = pl.multiple_of(bounds[SEQS], tk)
    q_masks, k_masks = half_masks(tq), half_masks(tk)

    def tile(ki, _):
        k0 = pl.multiple_of(ki * tk, tk)
        first = pl.multiple_of(base + k0, tk)
        begin, end = reach(bounds, first, first + tk - 1, group_rows)
        k_seg = seg_of(first + lax.broadcasted_iota(jnp.int32, (tk, 1), 0), bounds)
        dk_ref[pl.ds(k0, tk), :] = jnp.zeros((tk, A), F32)
        dv_ref[pl.ds(k0, tk), :] = jnp.zeros((tk, A), F32)

        def step(qt, _):
            q0 = pl.multiple_of(qt * tq, tq)
            q_seg = seg_of(q0 + lax.broadcasted_iota(jnp.int32, (1, tq), 1), bounds)
            bias = jnp.where(k_seg == q_seg, 0.0, MASKED)
            for pair in range(H // 2):
                cols = slice(128 * pair, 128 * pair + 128)
                q_pair = q_ref[pl.ds(q0, tq), cols]
                g_pair = g_ref[pl.ds(q0, tq), cols]
                k_pair = k_ref[pl.ds(k0, tk), cols]
                v_pair = v_ref[pl.ds(k0, tk), cols]
                key_sum = jnp.zeros((tk, 128), F32)
                value_sum = jnp.zeros((tk, 128), F32)
                for side in range(2):
                    head = 2 * pair + side
                    scores = dot_last(k_pair * k_masks[side], q_pair) + bias
                    prob = jnp.exp(scores - stat_ref[qt, head : head + 1, :])
                    value_sum = value_sum + jnp.dot(
                        prob.astype(BF16), g_pair * q_masks[side], preferred_element_type=F32
                    )
                    back = dot_last(v_pair * k_masks[side], g_pair)
                    back = prob * (back - stat_ref[qt, 8 + head : 9 + head, :])
                    key_sum = key_sum + jnp.dot(
                        back.astype(BF16), q_pair * q_masks[side], preferred_element_type=F32
                    )
                dk_ref[pl.ds(k0, tk), cols] += key_sum
                dv_ref[pl.ds(k0, tk), cols] += value_sum
            return 0

        lax.fori_loop(lax.div(begin, tq), lax.div(end + tq - 1, tq), step, 0)
        return 0

    lax.fori_loop(0, rows // tk, tile, 0)


def key_grads(bounds, keys, values, queries, grads, stats):
    rows = stats.shape[2]
    tk = rows
    return pl.pallas_call(
        functools.partial(key_grads_body, tk),
        out_shape=[jax.ShapeDtypeStruct((rows, A), F32)] * 2,
        in_specs=[pl.BlockSpec(memory_space=pltpu.SMEM)]
        + [pl.BlockSpec(memory_space=pl.ANY)] * 2
        + [pl.BlockSpec(memory_space=pltpu.VMEM)] * 3,
        out_specs=[pl.BlockSpec(memory_space=pltpu.VMEM)] * 2,
        scratch_shapes=[pltpu.VMEM((rows, A), BF16)] * 2 + [pltpu.SemaphoreType.DMA((2,))],
        compiler_params=pltpu.CompilerParams(vmem_limit_bytes=VMEM_LIMIT),
        name="key_grads",
    )(bounds, keys, values, queries, grads, stats)


def norm_back(grad_rows, normed, inverse, gain):
    scaled = grad_rows * gain
    return inverse * (
        scaled
        - jnp.mean(scaled, axis=1, keepdims=True)
        - normed * jnp.mean(scaled * normed, axis=1, keepdims=True)
    )


def dot_first(left, right):
    return lax.dot_general(left, right, (((0,), (0,)), ((), ())), preferred_element_type=F32)


def project_body(bounds, x_ref, w_ref, b_ref, q_ref, k_ref, v_ref):
    index = pl.program_id(0)

    @pl.when((index >= bounds[SEQS + 1]) & (index <= bounds[SEQS + 2]))
    def _():
        x = x_ref[...]
        query = (dot(x, w_ref[:, :A]) + b_ref[0:1, :]).astype(BF16).astype(F32)
        q_ref[...] = (query * (HD**-0.5)).astype(BF16)
        k_ref[...] = dot(x, w_ref[:, A : 2 * A]).astype(BF16)
        v_ref[...] = (dot(x, w_ref[:, 2 * A : 3 * A]) + b_ref[1:2, :]).astype(BF16)


def project(bounds, natural, w_in, smalls, rows):
    group_rows = natural.shape[0]

    def block(index, bounds):
        return (jnp.clip(index, bounds[SEQS + 1], bounds[SEQS + 2]), 0)

    def fixed(index, bounds):
        return (0, 0)

    return pl.pallas_call(
        project_body,
        out_shape=[jax.ShapeDtypeStruct((group_rows, A), BF16)] * 3,
        grid_spec=pltpu.PrefetchScalarGridSpec(
            num_scalar_prefetch=1,
            grid=(group_rows // rows,),
            in_specs=[
                pl.BlockSpec((rows, D), block),
                pl.BlockSpec((D, 3 * A), fixed),
                pl.BlockSpec((8, A), fixed),
            ],
            out_specs=[pl.BlockSpec((rows, A), block)] * 3,
        ),
        compiler_params=pltpu.CompilerParams(vmem_limit_bytes=VMEM_LIMIT),
        name="project",
    )(bounds, natural, w_in, smalls)


def tap_lanes(tap):
    row = lax.broadcasted_iota(jnp.int32, (128, A), 0)
    column = lax.broadcasted_iota(jnp.int32, (128, A), 1)
    return jnp.where(row == lax.div(column, HD) * KW + tap, 1.0, 0.0).astype(BF16)


def tap_pick(tap):
    row = lax.broadcasted_iota(jnp.int32, (A, 128), 0)
    column = lax.broadcasted_iota(jnp.int32, (A, 128), 1)
    first = row == lax.div(row, HD) * HD
    return jnp.where(first & (column == lax.div(row, HD) * KW + tap), 1.0, 0.0).astype(BF16)


def tap_weights(kw_ref, kb_ref, wide_ref, bias_ref):
    bias_ref[:, 0:128] = jnp.zeros((8, 128), F32)
    bias_ref[0:1, 0 : H * KW] = kb_ref[...].astype(F32)
    bias = bias_ref[:, 0:128].astype(BF16)
    for tap in range(KW):
        lanes = tap_lanes(tap)
        cols = slice(A * tap, A * tap + A)
        wide_ref[:, cols] = dot(kw_ref[...], lanes).astype(BF16)
        bias_ref[:, cols] = dot(bias, lanes)


def tap_near(bounds, group_rows, seg_ref, near_ref):
    span = near_ref.shape[1]
    start = lax.axis_index("ctx") * (span - RIM)
    position = start - RIM + lax.broadcasted_iota(jnp.int32, seg_ref.shape, 0)
    inside = (position >= 0) & (position < group_rows)
    seg_ref[...] = jnp.where(inside, seg_of(position, bounds), -1)
    seg = seg_ref[RIM // 2 : RIM // 2 + span, :]
    for tap in range(KW):
        shift = RIM // 2 - KW // 2 + tap
        near_ref[tap] = jnp.where((seg_ref[shift : shift + span, :] == seg) & (seg >= 0), 1.0, 0.0)


def tap_softmax(logits, bias_ref):
    parts = [logits[:, A * tap : A * tap + A] + bias_ref[0:1, A * tap : A * tap + A] for tap in range(KW)]
    largest = functools.reduce(jnp.maximum, parts)
    parts = [jnp.exp(part - largest) for part in parts]
    total = 1.0 / functools.reduce(jnp.add, parts)
    return [part * total for part in parts]


def wide3(value):
    return jnp.tile(value, (1, 3))


def conv_body(
    bounds, natural, w_ref, pw_ref, kw_ref, kb_ref, vec_ref, small_ref,
    out_ref, ext_ref, cv_ref, kc_ref, q_ref, cq_ref, sp_ref,
    extf_ref, seg_ref, near_ref, wide_ref, bias_ref, full_ref, sem,
):
    rows, group_rows = out_ref.shape[0], natural.shape[0]
    start = bounds[SEQS]
    copies = [
        pltpu.make_async_copy(
            natural.at[pl.ds(pl.multiple_of(jnp.maximum(start - RIM, 0), RIM), RIM)],
            ext_ref.at[0:RIM],
            sem.at[0],
        ),
        pltpu.make_async_copy(
            natural.at[pl.ds(pl.multiple_of(start, RIM), rows)], ext_ref.at[RIM : RIM + rows], sem.at[1]
        ),
        pltpu.make_async_copy(
            natural.at[pl.ds(pl.multiple_of(jnp.minimum(start + rows, group_rows - RIM), RIM), RIM)],
            ext_ref.at[RIM + rows : 2 * RIM + rows],
            sem.at[2],
        ),
    ]
    for copy in copies:
        copy.start()
    for copy in copies:
        copy.wait()
    conv_core(
        bounds, group_rows, w_ref, pw_ref, kw_ref, kb_ref, vec_ref, small_ref,
        out_ref, ext_ref, cv_ref, kc_ref, q_ref, cq_ref, sp_ref,
        extf_ref, seg_ref, near_ref, wide_ref, bias_ref, full_ref,
    )


def conv_core(
    bounds, group_rows, w_ref, pw_ref, kw_ref, kb_ref, vec_ref, small_ref,
    out_ref, ext_ref, cv_ref, kc_ref, q_ref, cq_ref, sp_ref,
    extf_ref, seg_ref, near_ref, wide_ref, bias_ref, full_ref,
):
    rows = out_ref.shape[0]
    span = rows + RIM
    tap_weights(kw_ref, kb_ref, wide_ref, bias_ref)
    tap_near(bounds, group_rows, seg_ref, near_ref)
    count = group_rows // rows
    place = lax.axis_index("ctx")
    padded = count - count // 8

    @pl.when((place == 0) | (place == padded))
    def _():
        ext_ref[0:RIM, :] = jnp.zeros((RIM, D), BF16)

    @pl.when((place == padded - 1) | (place == count - 1))
    def _():
        ext_ref[RIM + rows :, :] = jnp.zeros((RIM, D), BF16)

    ext = ext_ref[...]
    extf_ref[...] = ext.astype(F32)
    cv_ref[...] = dot(ext, w_ref[:, 3 * A :]) + small_ref[2:3, :]
    q_ref[...] = (dot(ext, w_ref[:, :A]) + small_ref[0:1, :]).astype(BF16).astype(F32)
    tile = span // 3

    def spread_tile(i, _):
        t0 = pl.multiple_of(tile * i, 16)
        here = pl.ds(t0, tile)
        for c in range(6):
            cols = slice(128 * c, 128 * c + 128)
            window = extf_ref[pl.ds(t0, tile + RIM), cols]
            total = 0.0
            for tap in range(KW):
                shift = RIM // 2 - KW // 2 + tap
                total += vec_ref[tap : tap + 1, cols] * near_ref[tap, here, :] * window[shift : shift + tile]
            sp_ref[here, cols] = total.astype(BF16)
        return 0

    lax.fori_loop(0, 3, spread_tile, 0)
    kc_ref[...] = dot(sp_ref[...], pw_ref[...]) + small_ref[3:4, :]
    cq_ref[...] = (kc_ref[...] * q_ref[RIM // 2 : RIM // 2 + span, :]).astype(BF16)

    def mix_tile(i, _):
        t0 = pl.multiple_of(tile * i, 16)
        here = pl.ds(t0, tile)
        kernel = tap_softmax(dot(cq_ref[here, :], wide_ref[...]), bias_ref)
        window = cv_ref[pl.ds(t0, tile + RIM), :]
        total = 0.0
        for tap in range(KW):
            shift = RIM // 2 - KW // 2 + tap
            total += kernel[tap] * wide3(near_ref[tap, here, :]) * window[shift : shift + tile]
        full_ref[here, :] = total
        return 0

    lax.fori_loop(0, 3, mix_tile, 0)
    out_ref[...] = full_ref[RIM // 2 : RIM // 2 + rows, :].astype(BF16)


def conv_shapes(rows):
    span, wide = rows + RIM, rows + 2 * RIM
    outs = [
        jax.ShapeDtypeStruct((rows, A), BF16),
        jax.ShapeDtypeStruct((wide, D), BF16),
        jax.ShapeDtypeStruct((wide, A), F32),
        jax.ShapeDtypeStruct((span, A), F32),
        jax.ShapeDtypeStruct((wide, A), F32),
        jax.ShapeDtypeStruct((span, A), BF16),
        jax.ShapeDtypeStruct((span, D), BF16),
    ]
    scratch = [
        pltpu.VMEM((wide, D), F32),
        pltpu.VMEM((wide, 128), jnp.int32),
        pltpu.VMEM((KW, span, 128), F32),
        pltpu.VMEM((A, KW * A), BF16),
        pltpu.VMEM((8, KW * A), F32),
        pltpu.VMEM((span, A), F32),
    ]
    return outs, scratch


def convolve(bounds, natural, w_in, pw, kw, kb, vectors, smalls, rows):
    outs, scratch = conv_shapes(rows)
    vmem = pl.BlockSpec(memory_space=pltpu.VMEM)
    return pl.pallas_call(
        conv_body,
        out_shape=outs,
        in_specs=[pl.BlockSpec(memory_space=pltpu.SMEM), pl.BlockSpec(memory_space=pl.ANY)] + [vmem] * 6,
        out_specs=[vmem] * 7,
        scratch_shapes=scratch + [pltpu.SemaphoreType.DMA((3,))],
        compiler_params=pltpu.CompilerParams(vmem_limit_bytes=VMEM_LIMIT),
        name="convolve",
    )(bounds, natural, w_in, pw, kw, kb, vectors, smalls)


def norm_rows(x, gain, bias):
    centered = x - jnp.mean(x, axis=1, keepdims=True)
    inverse = lax.rsqrt(jnp.mean(centered * centered, axis=1, keepdims=True) + NORM_EPS)
    normed = centered * inverse
    return normed * gain + bias, normed, inverse


ROW_OUT_B, ROW_GAIN1, ROW_BIAS1, ROW_FFN_B, ROW_GAIN2, ROW_BIAS2 = range(KW, KW + 6)
FI_ROWS, FO_ROWS, OW_ROWS = 384, 384, 192
FIRST_PACK = 1024
SECOND_PACK = 512


def layer_body(
    bounds, attn_ref, lse_ref, conv_ref, ext_ref, tgt_ref, wo_ref, fi_ref, fo_ref, vec_ref, fb_ref,
    out_ref, gfirst_ref, gctx_ref, stat_ref, statt_ref, sums_ref, fbs_ref, pack_ref,
    ctx_s, low_s, act_s, slope_s, gfl_s, gpre_s, gproj_s,
):
    rows = out_ref.shape[0]
    tm = slope_s.shape[0]
    chunk = D
    wide = FF // NG
    part = D // NG
    row_of = lax.broadcasted_iota(jnp.int32, (A, 128), 0)
    column_of = lax.broadcasted_iota(jnp.int32, (A, 128), 1)
    head_pick = jnp.where(column_of == 8 + lax.div(row_of, HD), 1.0, 0.0).astype(BF16)
    sums_ref[...] = jnp.zeros(sums_ref.shape, F32)
    fbs_ref[...] = jnp.zeros(fbs_ref.shape, F32)

    def vec(row):
        return vec_ref[row : row + 1, :]

    def add_sum(row, value):
        sums_ref[row : row + 1, :] += jnp.sum(value, axis=0, keepdims=True)

    def tile(index, _):
        r0 = pl.multiple_of(index * tm, tm)
        here = pl.ds(r0, tm)
        attn = attn_ref[here, :]
        ctx_s[here, :A] = attn.astype(BF16)
        ctx_s[here, A:] = conv_ref[here, :]
        tokens = ext_ref[pl.ds(pl.multiple_of(r0 + RIM, RIM), tm), :].astype(F32)
        first = tokens + dot(ctx_s[here, :], wo_ref[...]) + vec(ROW_OUT_B)
        after, normed_one, inverse_one = norm_rows(first, vec(ROW_GAIN1), vec(ROW_BIAS1))
        low_s[here, :] = after.astype(BF16)
        results = []
        for g in range(NG):
            low = low_s[here, part * g : part * g + part]
            total = 0.0
            for c in range(wide // chunk):
                span = slice(chunk * c, chunk * c + chunk)
                whole = slice(wide * g + chunk * c, wide * g + chunk * c + chunk)
                pre = dot(low, fi_ref[g, :, span]) + fb_ref[2 * g + c : 2 * g + c + 1, :]
                phi = 0.5 * (1.0 + lax.erf(pre * ROOT_HALF))
                act = (pre * phi).astype(BF16)
                act_s[here, whole] = act
                slope_s[:, whole] = phi + pre * DENSITY_NORM * jnp.exp(-0.5 * pre * pre)
                total += dot(act, fo_ref[g, span, :])
            results.append(total)
        second = after + jnp.concatenate(results, axis=1) + vec(ROW_FFN_B)
        result, normed_two, inverse_two = norm_rows(second, vec(ROW_GAIN2), vec(ROW_BIAS2))
        out_ref[here, :] = result.astype(BF16)
        seg = seg_of(bounds[SEQS] + r0 + lax.broadcasted_iota(jnp.int32, (tm, 1), 0), bounds)
        error = jnp.where(seg < SEQS, result - tgt_ref[here, :].astype(F32), 0.0)
        add_sum(6, error * error)
        add_sum(4, error * normed_two)
        add_sum(5, error)
        grad_second = norm_back(error, normed_two, inverse_two, vec(ROW_GAIN2))
        gfl = grad_second.astype(BF16)
        gfl_s[here, :] = gfl
        add_sum(3, gfl.astype(F32))
        grads = []
        for g in range(NG):
            total = 0.0
            for c in range(wide // chunk):
                span = slice(chunk * c, chunk * c + chunk)
                whole = slice(wide * g + chunk * c, wide * g + chunk * c + chunk)
                gact = dot_last(gfl_s[here, part * g : part * g + part], fo_ref[g, span, :])
                gpre = (gact * slope_s[:, whole]).astype(BF16)
                gpre_s[here, whole] = gpre
                fbs_ref[2 * g + c : 2 * g + c + 1, :] += jnp.sum(gpre.astype(F32), axis=0, keepdims=True)
                total += dot_last(gpre, fi_ref[g, :, span])
            grads.append(total)
        grad_after = jnp.concatenate(grads, axis=1) + grad_second
        add_sum(1, grad_after * normed_one)
        add_sum(2, grad_after)
        grad_first = norm_back(grad_after, normed_one, inverse_one, vec(ROW_GAIN1))
        gfirst_ref[here, :] = grad_first
        gproj = grad_first.astype(BF16)
        gproj_s[here, :] = gproj
        add_sum(0, gproj.astype(F32))
        gctx = dot_last(gproj, wo_ref[...]).astype(BF16)
        gctx_ref[here, :] = gctx
        product = gctx[:, :A].astype(F32) * attn
        high = product.astype(BF16)
        rest = (product - high.astype(F32)).astype(BF16)
        stat = lse_ref[here, :] + dot(high, head_pick) + dot(rest, head_pick)
        stat_ref[here, :] = stat
        return 0

    lax.fori_loop(0, rows // tm, tile, 0)
    statt_ref[...] = stat_ref[...].T[:16]
    for g in range(NG):
        for half in range(2):
            whole = slice(wide * g + D * half, wide * g + D * half + D)
            grad = dot_first(low_s[:, part * g : part * g + part], gpre_s[:, whole]).astype(BF16)
            r0 = 96 * (2 * g + half)
            for k in range(4):
                pack_ref[k, r0 : r0 + 96, :] = grad[96 * k : 96 * k + 96]
        for k in range(4):
            grad = dot_first(
                act_s[:, wide * g + A * k : wide * g + A * k + A], gfl_s[:, part * g : part * g + part]
            )
            pack_ref[k, FI_ROWS : FI_ROWS + FO_ROWS, part * g : part * g + part] = grad.astype(BF16)
    grad = dot_first(ctx_s[...], gproj_s[...]).astype(BF16)
    r0 = FI_ROWS + FO_ROWS
    for k in range(4):
        pack_ref[k, r0 : r0 + OW_ROWS, :] = grad[OW_ROWS * k : OW_ROWS * k + OW_ROWS]
        pack_ref[k, r0 + OW_ROWS :, :] = jnp.zeros((FIRST_PACK - r0 - OW_ROWS, D), BF16)


def layer(bounds, attn, lse, conv, ext, target, wo, fi, fo, vectors, fb):
    rows = attn.shape[0]
    tm = min(256, rows)
    vmem = pl.BlockSpec(memory_space=pltpu.VMEM)
    return pl.pallas_call(
        layer_body,
        out_shape=[
            jax.ShapeDtypeStruct((rows, D), BF16),
            jax.ShapeDtypeStruct((rows, D), F32),
            jax.ShapeDtypeStruct((rows, D), BF16),
            jax.ShapeDtypeStruct((rows, 128), F32),
            jax.ShapeDtypeStruct((16, rows), F32),
            jax.ShapeDtypeStruct((8, D), F32),
            jax.ShapeDtypeStruct((4, D), F32),
            jax.ShapeDtypeStruct((4, FIRST_PACK, D), BF16),
        ],
        in_specs=[pl.BlockSpec(memory_space=pltpu.SMEM)] + [vmem] * 10,
        out_specs=[vmem] * 8,
        scratch_shapes=[
            pltpu.VMEM((rows, D), BF16),
            pltpu.VMEM((rows, D), BF16),
            pltpu.VMEM((rows, FF), BF16),
            pltpu.VMEM((tm, FF), F32),
            pltpu.VMEM((rows, D), BF16),
            pltpu.VMEM((rows, FF), BF16),
            pltpu.VMEM((rows, D), BF16),
        ],
        compiler_params=pltpu.CompilerParams(vmem_limit_bytes=VMEM_LIMIT),
        name="layer",
    )(bounds, attn, lse, conv, ext, target, wo, fi, fo, vectors, fb)


TAIL_ROWS = 128


def fetch(sources, targets, sem):
    copies = [
        pltpu.make_async_copy(src, dst, sem.at[i]) for i, (src, dst) in enumerate(zip(sources, targets))
    ]
    for copy in copies:
        copy.start()
    return copies


LATE = 7


def middle_body(
    count, sums, *refs, group_rows
):
    bits, chunks = sums
    (
        bounds, g_ref, stat_ref, res_ref, pack_ref, late0, late1, late2, late3, late4, late5, late6, kw_ref, kb_ref, vec_ref,
        out_ref, all_ref, dealt_ref, own_ref, gq_ref, gcv_ref, gtc_ref, tail_ref, sums_ref, bsum_ref,
        edge_ref, extf_ref, seg_ref, near_ref, wide_ref, bias_ref, gc_ref, pc_ref, glc_ref, gsp_ref,
        *rest,
    ) = refs
    late = [late0, late1, late2, late3, late4, late5, late6]
    early_refs, rest = rest[:LATE], rest[LATE:]
    ext_ref, cv_ref, kc_ref, q_ref, cq_ref, sp_ref, pw_ref = early_refs
    mine_ref, late_sem, mine_sem, *rest = rest
    bufs, rest = rest[: 2 + bits], rest[2 + bits :]
    sum_send, sum_recv, local_sem, edge_send, edge_recv, *sems = rest
    p = Place(count)
    core = lax.rem(lax.axis_index("wt"), 2)
    mine_copy = pltpu.make_async_copy(pack_ref.at[:, core], mine_ref, mine_sem)
    mine_copy.start()
    loads = fetch(late, early_refs, late_sem)
    rows = g_ref.shape[0]
    span = rows + RIM
    rim = RIM // 2
    place = p.me
    total = Sum(bits, chunks, pack_ref, bufs, None, sum_send, sum_recv, mine_ref)
    early = rows - 3 * rows // 8
    low = {"ctx": lax.rem(p.me + count - 1, count)}
    high = {"ctx": lax.rem(p.me + 1, count)}
    has_low, has_high = p.me > 0, p.me < count - 1
    greet(p.others() + [(p.me >= 0, target) for target in total.targets[:2]])
    needs = BlockNeeds(p)
    pair = PairPart(p, needs, g_ref.at[early:, :A], lambda j: out_ref.at[j, early:], sems[0], sems[1])
    line = LinePart(p, needs, g_ref.at[:early, :A], lambda j: out_ref.at[j, :early], sems[2], sems[3])
    stats = LinePart(p, needs, stat_ref, lambda j: all_ref.at[j], sems[4], sems[5])
    swap = Swap(p, res_ref, dealt_ref, sems[6], sems[7])

    def to_low():
        return remote(g_ref.at[:RIM, A:], edge_ref.at[1], edge_send.at[0], edge_recv.at[1], low)

    def to_high():
        return remote(g_ref.at[rows - RIM :, A:], edge_ref.at[0], edge_send.at[1], edge_recv.at[0], high)

    def advance(t):
        for c in range(chunks):
            stage = t - c
            if 1 <= stage <= total.stages:
                total.take(stage - 1, c)
                if stage < total.stages:
                    total.start(stage, c)
                else:
                    own_ref[c] = bufs[stage - 1][c]

    @pl.when(has_low)
    def _():
        to_low().start()

    @pl.when(has_high)
    def _():
        to_high().start()

    total.open()
    parts = [stats, line, pair]
    stats.start()
    pair.across()
    line.start()
    pair.along()
    keeps = [
        pltpu.make_async_copy(g_ref.at[:, :A], out_ref.at[p.me], local_sem.at[0]),
        pltpu.make_async_copy(stat_ref, all_ref.at[p.me], local_sem.at[1]),
    ]
    for keep in keeps:
        keep.start()
    mine_copy.wait()
    advance(1)
    tap_weights(kw_ref, kb_ref, wide_ref, bias_ref)
    pair.middle()
    for load in loads:
        load.wait()
    tap_near(bounds, group_rows, seg_ref, near_ref)
    extf_ref[...] = ext_ref[...].astype(F32)

    @pl.when(has_low)
    def _():
        to_low().wait_send()
        to_high().wait_recv()

    @pl.when(has_high)
    def _():
        to_high().wait_send()
        to_low().wait_recv()

    gc_ref[0:rim, :] = jnp.where(place > 0, edge_ref[0].astype(F32)[RIM - rim :], 0.0)
    gc_ref[rim : rim + rows, :] = g_ref[:, A:].astype(F32)
    gc_ref[rim + rows :, :] = jnp.where(place < count - 1, edge_ref[1].astype(F32)[:rim], 0.0)
    blocks = jnp.where(
        lax.div(lax.broadcasted_iota(jnp.int32, (128, 128), 0), HD)
        == lax.div(lax.broadcasted_iota(jnp.int32, (128, 128), 1), HD),
        1.0,
        0.0,
    ).astype(BF16)
    tile = span // 3

    def tap_tile(i):
        t0 = pl.multiple_of(tile * i, 16)
        here = pl.ds(t0, tile)
        kernel = tap_softmax(dot(cq_ref[here, :], wide_ref[...]), bias_ref)
        window = cv_ref[pl.ds(t0, tile + RIM), :]
        grad = gc_ref[here, :]
        inner = []
        mean = 0.0
        for tap in range(KW):
            shift = rim - KW // 2 + tap
            near = wide3(near_ref[tap, here, :])
            product = (grad * window[shift : shift + tile]).astype(BF16)
            terms = jnp.concatenate(
                [dot(product[:, 128 * c : 128 * c + 128], blocks) for c in range(3)], axis=1
            )
            terms = terms * near
            inner.append(terms)
            mean += kernel[tap] * terms
            pc_ref[tap, here, :] = kernel[tap] * near * grad
        picked = 0.0
        for tap in range(KW):
            logit = (kernel[tap] * (inner[tap] - mean)).astype(BF16)
            picked += dot(logit, tap_pick(tap))
        glc_ref[here, :] = picked.astype(BF16)

    def round_of(i, _):
        tap_tile(i)
        for s in range(1, min(3, p.length)):

            @pl.when(i == s - 1)
            def _(s=s):
                for part in parts:
                    part.step(s)
                advance(s + 1)

        return 0

    lax.fori_loop(0, 3, round_of, 0)
    for s in range(3, p.length):
        for part in parts:
            part.step(s)
    swap.start()
    advance(4)
    back = dot_last(glc_ref[...], kw_ref[...])
    query = q_ref[rim : rim + span, :]
    row = lax.broadcasted_iota(jnp.int32, (span, 1), 0)
    own = (row >= rim) & (row < rim + rows)
    grad_kc = (back * query).astype(BF16)
    gsp_ref[...] = dot_last(grad_kc, pw_ref[...])
    gq_ref[...] = (back * kc_ref[...])[rim : rim + rows]
    own_kc = jnp.where(own, grad_kc.astype(F32), 0.0)
    own_logits = jnp.where(own, glc_ref[...].astype(F32), 0.0)
    grad_pw = dot_first(sp_ref[...], own_kc.astype(BF16)).astype(BF16)
    grad_kern = dot_first(cq_ref[...], own_logits.astype(BF16)).astype(BF16)
    for k in range(4):
        for half in range(2):
            r0 = 192 * k + 96 * half
            tail_ref[k, 0:96, A * half : A * half + A] = grad_pw[r0 : r0 + 96]
        for m in range(6):
            r0 = 96 * k + 16 * m
            tail_ref[k, 96:112, 128 * m : 128 * m + 128] = grad_kern[r0 : r0 + 16]
        tail_ref[k, 112:, :] = jnp.zeros((TAIL_ROWS - 112, D), BF16)
    bsum_ref[...] = jnp.zeros(bsum_ref.shape, F32)
    bsum_ref[0:1, :] = jnp.sum(own_kc, axis=0, keepdims=True)
    bsum_ref[1:2, 0:128] = jnp.sum(own_logits, axis=0, keepdims=True)
    advance(5)
    sums_ref[...] = jnp.zeros(sums_ref.shape, F32)
    step = 128

    def back_tile(i, _):
        s0 = pl.multiple_of(step * i, step)
        here = pl.ds(s0, step)
        inner = pl.ds(pl.multiple_of(s0 + rim, 8), step)
        for c in range(6):
            cols = slice(128 * c, 128 * c + 128)
            grads = gsp_ref[inner, cols]
            tokens = extf_ref[pl.ds(pl.multiple_of(s0 + rim, 8), step + RIM), cols]
            spread = gsp_ref[pl.ds(s0, step + RIM), cols]
            sofar = 0.0
            for tap in range(KW):
                shift = rim - KW // 2 + tap
                value = near_ref[tap, inner, :] * grads * tokens[shift : shift + step]
                sums_ref[tap : tap + 1, cols] += jnp.sum(value, axis=0, keepdims=True)
                shift = rim + KW // 2 - tap
                moved = near_ref[tap, pl.ds(s0, step + RIM), :] * spread
                sofar += vec_ref[tap : tap + 1, cols] * moved[shift : shift + step]
            gtc_ref[here, cols] = sofar
        for c in range(3):
            cols = slice(128 * c, 128 * c + 128)
            sofar = 0.0
            for tap in range(KW):
                shift = rim + KW // 2 - tap
                sofar += pc_ref[tap, pl.ds(s0, step + RIM), cols][shift : shift + step]
            gcv_ref[here, cols] = sofar.astype(BF16)

        @pl.when(i == rows // step // 2 - 1)
        def _():
            advance(6)

        return 0

    lax.fori_loop(0, rows // step, back_tile, 0)
    for t in range(7, chunks + total.stages):
        advance(t)
    for keep in keeps:
        keep.wait()
    for part in parts:
        part.finish()
    swap.finish()
    for stage in range(total.stages):
        for c in range(chunks):
            total.sent(stage, c)


def middle(bounds, group_rows, ctx_count, grads, stats, results, pack, *args):
    length = ctx_count // 2
    rows = grads.shape[0]
    span, wide = rows + RIM, rows + 2 * RIM
    bits, chunks, packed_shape, out_shape, bufs = sum_shapes(ctx_count, pack.shape[1], 32)
    vmem = pl.BlockSpec(memory_space=pltpu.VMEM)
    hbm = pl.BlockSpec(memory_space=pl.ANY)
    return pl.pallas_call(
        functools.partial(middle_body, ctx_count, (bits, chunks), group_rows=group_rows),
        out_shape=[
            jax.ShapeDtypeStruct((ctx_count, rows, A), grads.dtype),
            jax.ShapeDtypeStruct((ctx_count,) + stats.shape, stats.dtype),
            jax.ShapeDtypeStruct(results.shape, results.dtype),
            jax.ShapeDtypeStruct(out_shape[-3:], BF16),
            jax.ShapeDtypeStruct((rows, A), F32),
            jax.ShapeDtypeStruct((rows, A), BF16),
            jax.ShapeDtypeStruct((rows, D), F32),
            jax.ShapeDtypeStruct((4, TAIL_ROWS, D), BF16),
            jax.ShapeDtypeStruct((16, D), F32),
            jax.ShapeDtypeStruct((8, A), F32),
        ],
        in_specs=[pl.BlockSpec(memory_space=pltpu.SMEM)]
        + [vmem] * 3
        + [hbm] * (1 + LATE)
        + [vmem] * (len(args) - LATE),
        out_specs=[hbm] * 3 + [vmem] * 7,
        scratch_shapes=[
            pltpu.VMEM((2, RIM, A), BF16),
            pltpu.VMEM((wide, D), F32),
            pltpu.VMEM((wide, 128), jnp.int32),
            pltpu.VMEM((KW, span, 128), F32),
            pltpu.VMEM((A, KW * A), BF16),
            pltpu.VMEM((8, KW * A), F32),
            pltpu.VMEM((span, A), F32),
            pltpu.VMEM((KW, span, A), F32),
            pltpu.VMEM((span, 128), BF16),
            pltpu.VMEM((span, D), F32),
        ]
        + [pltpu.VMEM(item.shape, item.dtype) for item in args[:LATE]]
        + [
            pltpu.VMEM(packed_shape[1:], BF16),
            pltpu.SemaphoreType.DMA((LATE,)),
            pltpu.SemaphoreType.DMA,
        ]
        + bufs
        + [
            pltpu.SemaphoreType.DMA((2 + bits, chunks)),
            pltpu.SemaphoreType.DMA((2 + bits, chunks)),
            pltpu.SemaphoreType.DMA((2,)),
            pltpu.SemaphoreType.DMA((2,)),
            pltpu.SemaphoreType.DMA((2,)),
        ]
        + part_sems(length) * 3
        + swap_sems(ctx_count),
        compiler_params=pltpu.CompilerParams(
            collective_id=1, has_side_effects=True, vmem_limit_bytes=VMEM_LIMIT
        ),
        name="middle",
    )(bounds, grads, stats, results, pack.reshape(packed_shape), *args)


def ending_body(count, sums, *refs):
    bits, second_chunks = sums
    (
        dq_ref, dk_ref, dv_ref, gq_ref, gcv_ref, late0, late1, late2, ext_ref, tail_ref, own_ref,
        tap_ref, bsum_ref, layer_ref, ffn_ref,
        first_ref, second_ref, sum_ref, dealt_ref,
        gm_ref, gtok_ref, pack_ref, f_bufs, gtc_ref, gfirst_ref, w_ref, late_sem, *rest,
    ) = refs
    loads = fetch([late0, late1, late2], [gtc_ref, gfirst_ref, w_ref], late_sem)
    bufs, rest = rest[: 2 + bits], rest[2 + bits :]
    first_send, first_recv, second_send, second_recv, f_send, f_recv, keep_sem, swap_send, swap_recv = rest
    p = Place(count)
    rows = gm_ref.shape[0]
    piece = pack_ref.shape[-2]
    first = LinePart(p, AllNeeds(p), own_ref, lambda j: first_ref.at[j], first_send, first_recv)
    second = Sum(bits, second_chunks, pack_ref, bufs, second_ref, second_send, second_recv)
    swap = Swap(p, gtok_ref, dealt_ref, swap_send, swap_recv)
    stages, last = second.stages, second.last
    greet(p.others() + [(p.me >= 0, target) for target in second.targets[:2]])
    first.start()
    keep = pltpu.make_async_copy(own_ref, first_ref.at[p.me], keep_sem)
    keep.start()

    def store(k, r0, value):
        for at in range(0, value.shape[0], piece):
            row = (r0 + at) // piece
            index = []
            rest, c = row // second_chunks, row % second_chunks
            for b in range(bits):
                index.insert(0, rest % 2)
                rest //= 2
            pack_ref[(k // 2, k % 2) + tuple(index) + (c,)] = value[at : at + piece]

    gm_ref[:, :A] = (dq_ref[...] * (HD**-0.5) + gq_ref[...]).astype(BF16)
    gm_ref[:, A : 2 * A] = dk_ref[...].astype(BF16)
    gm_ref[:, 2 * A : 3 * A] = dv_ref[...].astype(BF16)
    gm_ref[:, 3 * A :] = gcv_ref[...]
    for half in range(2):
        grad = dot_first(ext_ref[RIM : RIM + rows, :], gm_ref[:, D * half : D * half + D]).astype(BF16)
        for k in range(4):
            store(k, 192 * half, grad[192 * k : 192 * k + 192])
    for k in range(4):
        store(k, 384, tail_ref[k])
    second.open()
    first.step(1)
    second.across(0, second_chunks)
    f_bufs[0, 0] = jnp.zeros(f_bufs.shape[2:], F32)
    f_bufs[0, 0, 0:KW, :] = tap_ref[0:KW, :]
    f_bufs[0, 0, KW : KW + 7, :] = layer_ref[0:7, :]
    f_bufs[0, 0, 16:20, :] = ffn_ref[...]
    f_bufs[0, 0, 20:21, :A] = jnp.sum(gm_ref[:, :A].astype(F32), axis=0, keepdims=True)
    f_bufs[0, 0, 20:21, A:] = jnp.sum(gm_ref[:, 2 * A : 3 * A].astype(F32), axis=0, keepdims=True)
    f_bufs[0, 0, 21:22, :A] = jnp.sum(gm_ref[:, 3 * A :].astype(F32), axis=0, keepdims=True)
    f_bufs[0, 0, 21:22, A:] = bsum_ref[0:1, :]
    f_bufs[0, 0, 22:23, :A] = bsum_ref[1:2, :]

    def f_copy(stage):
        return remote(
            f_bufs.at[0, stage], f_bufs.at[1, stage], f_send.at[stage], f_recv.at[stage], second.targets[stage]
        )

    f_copy(0).start()
    def advance(t):
        for c in reversed(range(second_chunks)):
            stage = t - c + 1
            if not 2 <= stage <= last:
                continue
            second.take(stage - 1, c)
            if stage == stages:
                second.place_own(c, bufs[stage - 1][c])
            if stage < last:
                second.start(stage, c)
        if t <= stages:
            f_copy(t - 1).wait_recv()
            value = f_bufs[0, t - 1] + f_bufs[1, t - 1]
            if t < stages:
                f_bufs[0, t] = value
                f_copy(t).start()
            else:
                sum_ref[...] = value

    for load in loads:
        load.wait()
    grad = dot_last(gm_ref[...], w_ref[...]) + gfirst_ref[...] + gtc_ref[...]
    size = rows // count
    for j in range(count):
        gtok_ref[j] = grad[size * j : size * j + size].astype(BF16)
    for s in range(2, p.length):
        first.step(s)
        if s == 2:
            advance(1)
    swap.start()
    for t in range(2, second_chunks + last - 1):
        advance(t)
    first.finish()
    keep.wait()
    for stage in range(last):
        for c in range(second_chunks):
            second.sent(stage, c)
    for stage in range(stages):
        f_copy(stage).wait_send()
    swap.finish()


def ending(ctx_count, *args):
    rows = args[0].shape[0]
    bits, second_chunks, packed_shape, second_shape, bufs = sum_shapes(ctx_count, SECOND_PACK, 16)
    vmem = pl.BlockSpec(memory_space=pltpu.VMEM)
    pieces = (ctx_count, rows // ctx_count, D)
    first, second, totals, moved = pl.pallas_call(
        functools.partial(ending_body, ctx_count, (bits, second_chunks)),
        out_shape=[
            jax.ShapeDtypeStruct((ctx_count, FIRST_PACK // ctx_count, D), BF16),
            jax.ShapeDtypeStruct(second_shape, BF16),
            jax.ShapeDtypeStruct((24, D), F32),
            jax.ShapeDtypeStruct(pieces, BF16),
        ],
        in_specs=[vmem] * 5 + [pl.BlockSpec(memory_space=pl.ANY)] * 3 + [vmem] * (len(args) - 8),
        out_specs=[vmem] * 4,
        scratch_shapes=[
            pltpu.VMEM((rows, 4 * A), BF16),
            pltpu.VMEM(pieces, BF16),
            pltpu.VMEM(packed_shape, BF16),
            pltpu.VMEM((2, 2 + bits, 24, D), F32),
        ]
        + [pltpu.VMEM(item.shape, item.dtype) for item in args[5:8]]
        + [pltpu.SemaphoreType.DMA((3,))]
        + bufs
        + part_sems(ctx_count // 2)
        + [
            pltpu.SemaphoreType.DMA((2 + 2 * bits, second_chunks)),
            pltpu.SemaphoreType.DMA((2 + 2 * bits, second_chunks)),
            pltpu.SemaphoreType.DMA((2 + bits,)),
            pltpu.SemaphoreType.DMA((2 + bits,)),
            pltpu.SemaphoreType.DMA,
        ]
        + swap_sems(ctx_count),
        compiler_params=pltpu.CompilerParams(
            collective_id=2, has_side_effects=True, vmem_limit_bytes=VMEM_LIMIT
        ),
        name="ending",
    )(*args)
    return first.reshape(-1, D), second.reshape(-1, D), totals, moved.reshape(rows, D)


def finish_body(
    place, arrange_ref, out_in, tok_in, first_ref, second_ref, sum_ref,
    out_ref, tok_ref, w_ref, b_ref, dw_ref, pw_ref, pb_ref, kern_ref, ow_ref, fi_ref, fb_ref, fo_ref,
    loss_ref, kb_ref, v0_ref, v1_ref, v2_ref, v3_ref, v4_ref, v5_ref, kern_s,
):
    rows = out_ref.shape[0]
    slot = lax.broadcasted_iota(jnp.int32, (rows, rows), 0)
    sort = jnp.where(slot == arrange_ref[...], 1.0, 0.0).astype(BF16)
    out_ref[...] = dot_first(sort, out_in[...]).astype(BF16)
    tok_ref[...] = dot_first(sort, tok_in[...])
    for half in range(2):
        w_ref[:, D * half : D * half + D] = second_ref[192 * half : 192 * half + 192, :].astype(F32)
        pw_ref[96 * half : 96 * half + 96, :] = second_ref[384:480, A * half : A * half + A].astype(F32)
    for m in range(6):
        kern_s[16 * m : 16 * m + 16, :] = second_ref[480:496, 128 * m : 128 * m + 128].astype(F32)
    kern_s[A // 4 :, :] = jnp.zeros((128 - A // 4, 128), F32)
    kern_ref[...] = kern_s[...].T[: H * KW, : A // 4]
    for g in range(NG):
        for half in range(2):
            r0 = 96 * (2 * g + half)
            fi_ref[g, :, D * half : D * half + D] = first_ref[r0 : r0 + 96, :].astype(F32)
        fo_ref[g] = first_ref[384:768, A * g : A * g + A].astype(F32)
    ow_ref[...] = first_ref[768:960, :].astype(F32)
    total = jnp.sum(sum_ref[15:16, :], axis=1, keepdims=True)
    loss_ref[...] = total / (place[SEQS + 5].astype(F32) * D)
    kb_ref[...] = sum_ref[22:23, 0 : H * KW].reshape(H * KW)
    for k in range(4):

        @pl.when(place[SEQS + 4] == k)
        def _(k=k):
            cols = slice(D // 4 * k, D // 4 * k + D // 4)
            dw_ref[...] = sum_ref[0:KW, cols]
            for i, v_ref in enumerate((v0_ref, v1_ref, v2_ref, v3_ref, v4_ref, v5_ref)):
                v_ref[...] = sum_ref[KW + i : KW + i + 1, cols].reshape(D // 4)
            fb_ref[...] = sum_ref[16 + k : 17 + k, :].reshape(D)
            part = slice(A // 4 * k, A // 4 * k + A // 4)
            second = slice(A + A // 4 * k, A + A // 4 * k + A // 4)
            b_ref[0:1, :] = sum_ref[20:21, part]
            b_ref[1:2, :] = sum_ref[20:21, second]
            b_ref[2:3, :] = sum_ref[21:22, part]
            pb_ref[...] = sum_ref[21:22, second].reshape(A // 4)


def finish(place, arrange, *args):
    rows = args[0].shape[0]
    vmem = pl.BlockSpec(memory_space=pltpu.VMEM)
    shapes = [
        (rows, D), (D // 4, 4 * A), (3, A // 4), (KW, D // 4), (D // 4, A), (A // 4,), (H * KW, A // 4),
        (D // 4, D), (NG, A // 4, FF // NG), (D,), (NG, A, A), (1, 1), (H * KW,),
    ] + [(D // 4,)] * 6
    return pl.pallas_call(
        finish_body,
        out_shape=[jax.ShapeDtypeStruct((rows, D), BF16)] + [jax.ShapeDtypeStruct(shape, F32) for shape in shapes],
        in_specs=[pl.BlockSpec(memory_space=pltpu.SMEM)] + [vmem] * (len(args) + 1),
        out_specs=[vmem] * 20,
        scratch_shapes=[pltpu.VMEM((128, 128), F32)],
        compiler_params=pltpu.CompilerParams(vmem_limit_bytes=VMEM_LIMIT),
        name="finish",
    )(place, arrange, *args)


def local(
    hidden,
    teacher,
    lengths,
    deal,
    w_in,
    b_in,
    dw_kernel,
    pw_weight,
    pw_bias,
    kern_weight,
    kern_bias,
    out_weight,
    out_bias,
    norm1_gain,
    norm1_bias,
    ffn_in,
    ffn_in_bias,
    ffn_out,
    ffn_out_bias,
    norm2_gain,
    norm2_bias,
):
    rows = hidden.shape[1]
    ctx_count = lax.axis_size("ctx")
    group_rows = rows * ctx_count
    piece_rows = rows // ctx_count
    sorted_hidden, sorted_teacher, arrange, bounds, *smalls = setup(
        lengths, deal, hidden[0], teacher[0],
        [
            dw_kernel, out_bias, norm1_gain, norm1_bias, ffn_out_bias, norm2_gain, norm2_bias, ffn_in_bias,
            b_in, pw_bias, kern_weight.T,
        ],
        ctx_count,
    )
    pieces_shape = (ctx_count, piece_rows, D)
    kern_b = kern_bias[None]
    fused = group_rows <= 4096
    target, full_w_in, full_pw, full_out_w, full_ffn_in, full_ffn_out, vectors, smalls, ffn_in_b, full_kern, *rest = (
        gather_inputs(
            bounds,
            sorted_hidden,
            sorted_teacher,
            (w_in, pw_weight, out_weight, ffn_in, ffn_out),
            (0, 0, 0, 1, 1),
            smalls,
            kern_b,
            ctx_count,
            fused,
        )
    )
    target = target.reshape(rows, D)
    if fused:
        all_q8, all_keys, all_values = (item.reshape(group_rows, A) for item in rest[:3])
        conv_parts = rest[3:]
    else:
        natural = rest[0].reshape(group_rows, D)
        all_q8, all_keys, all_values = project(bounds, natural, full_w_in, smalls, rows)
        conv_parts = convolve(
            bounds, natural, full_w_in, full_pw, full_kern, kern_b, vectors, smalls, rows
        )
    conv_out, extended, conv_value, key_conv, query_ext, conv_query, spread = conv_parts
    attn_out, lse = attend(bounds, all_q8, all_keys, all_values, rows)
    result, grad_first, grad_context, stats, stats_t, layer_sums, ffn_in_sums, first_pack = layer(
        bounds, attn_out, lse, conv_out, extended, target,
        full_out_w, full_ffn_in, full_ffn_out, vectors, ffn_in_b,
    )
    (
        all_grads, all_stats, output, first_own, grad_query_conv, grad_cov, grad_tokens_conv, tail, tap_sums,
        bias_sums,
    ) = middle(
        bounds, group_rows, ctx_count, grad_context, stats_t, result.reshape(pieces_shape), first_pack,
        extended, conv_value, key_conv, query_ext, conv_query, spread, full_pw, full_kern, kern_b, vectors,
    )
    grad_query = query_grads(bounds, all_q8, grad_context, stats, all_keys, all_values)
    grad_keys, grad_values = key_grads(
        bounds, all_keys, all_values, all_q8, all_grads.reshape(group_rows, A), all_stats
    )
    first, second, totals, moved = ending(
        ctx_count, grad_query, grad_keys, grad_values, grad_query_conv, grad_cov, grad_tokens_conv, grad_first,
        full_w_in, extended, tail, first_own.reshape(-1, D), tap_sums, bias_sums, layer_sums, ffn_in_sums,
    )
    (
        dealt_out, dealt_grad, g_w_in, g_b_in, g_dw, g_pw, g_pw_b, g_kern, g_out, g_ffn_in, g_ffn_in_b,
        g_ffn_out, loss, g_kern_b, *g_vec,
    ) = finish(
        bounds, arrange,
        output.reshape(rows, D), moved, first, second, totals,
    )
    return (
        dealt_out[None],
        loss[0, 0],
        dealt_grad[None],
        g_w_in,
        g_b_in,
        g_dw,
        g_pw,
        g_pw_b,
        g_kern.T,
        g_kern_b,
        g_out,
        g_vec[0],
        g_vec[1],
        g_vec[2],
        g_ffn_in,
        g_ffn_in_b,
        g_ffn_out,
        g_vec[3],
        g_vec[4],
        g_vec[5],
    )


def solution(mesh):
    return jax.shard_map(
        local,
        mesh=mesh,
        in_specs=(
            P("wt", "ctx", None),
            P("wt", "ctx", None),
            P(),
            P("wt", None),
            P("wt", None),
            P(None, "wt"),
            P(None, "wt"),
            P("wt", None),
            P("wt"),
            P("wt", None),
            P(),
            P("wt", None),
            P("wt"),
            P("wt"),
            P("wt"),
            P(None, "wt", None),
            P("wt"),
            P(None, "wt", None),
            P("wt"),
            P("wt"),
            P("wt"),
        ),
        out_specs=(
            P("wt", "ctx", None),
            P(),
            P("wt", "ctx", None),
            P("wt", None),
            P(None, "wt"),
            P(None, "wt"),
            P("wt", None),
            P("wt"),
            P("wt", None),
            P(),
            P("wt", None),
            P("wt"),
            P("wt"),
            P("wt"),
            P(None, "wt", None),
            P("wt"),
            P(None, "wt", None),
            P("wt"),
            P("wt"),
            P("wt"),
        ),
        check_vma=False,
    )
```

```python
import functools

import jax
import jax.numpy as jnp
from jax import lax
from jax.experimental import pallas as pl
from jax.experimental.pallas import tpu as pltpu
from jax.sharding import PartitionSpec as P

D = 768
H = 6
HD = 64
FF = 3072
NG = 2
KW = 9
SEQS = 6
A = 384

NORM_EPS = 1e-12
MASKED = -1e30
ROOT_HALF = 0.7071067811865476
DENSITY_NORM = 0.3989422804014327
RIM = 16
MESH = pl.DeviceIdType.MESH
BF16 = jnp.bfloat16
F32 = jnp.float32
VMEM_LIMIT = 60 * 1024 * 1024


def remote(src, dst, send, recv, target):
    return pltpu.make_async_remote_copy(
        src_ref=src,
        dst_ref=dst,
        send_sem=send,
        recv_sem=recv,
        device_id=target,
        device_id_type=MESH,
    )


def greet(peers):
    barrier = pltpu.get_barrier_semaphore()
    total = 0
    for there, target in peers:

        @pl.when(there)
        def _(target=target):
            pl.semaphore_signal(barrier, inc=1, device_id=target, device_id_type=MESH)

        total = total + jnp.where(there, 1, 0)
    pl.semaphore_wait(barrier, total)


class Place:
    def __init__(self, count):
        self.count = count
        self.length = count // 2
        self.valid = count - count // 8
        self.window = count // 2
        self.me = lax.axis_index("ctx")
        self.line = lax.div(self.me, 2)
        self.side = lax.rem(self.me, 2)
        self.mate_index = self.me + 1 - 2 * self.side
        self.mate = {"ctx": self.mate_index}
        self.up = {"ctx": lax.rem(self.me + 2, count)}
        self.down = {"ctx": lax.rem(self.me + count - 2, count)}
        self.has_up = self.line < self.length - 1
        self.has_down = self.line > 0

    def others(self):
        return [
            (self.me >= 0, {"ctx": lax.rem(self.me + shift, self.count)}) for shift in range(1, self.count)
        ]


class PieceNeeds:
    def __init__(self, place, first, last):
        self.place, self.first, self.last = place, first, last

    def at(self, index, source):
        p = self.place
        return (
            (index < p.valid)
            & (self.first <= index + p.window)
            & (self.last >= index - p.window)
        )

    def above(self, line, source):
        p = self.place
        return (2 * line < p.valid) & (self.last >= 2 * line - p.window)

    def below(self, line, source):
        return self.first <= 2 * line + 1 + self.place.window

    def sent(self, source):
        return source >= 0


class BlockNeeds:
    def __init__(self, place):
        self.place = place

    def at(self, index, source):
        p = self.place
        near = (index <= source + p.window) & (index >= source - p.window)
        return near & (index < p.valid) & (source < p.valid)

    def above(self, line, source):
        p = self.place
        return (2 * line < p.valid) & (2 * line <= source + p.window) & (source < p.valid)

    def below(self, line, source):
        p = self.place
        return (2 * line + 1 >= source - p.window) & (source < p.valid)

    def sent(self, source):
        return source < self.place.valid


class AllNeeds:
    def __init__(self, place):
        self.place = place

    def at(self, index, source):
        return source * 0 == 0

    def above(self, line, source):
        return source * 0 == 0

    def below(self, line, source):
        return source * 0 == 0

    def sent(self, source):
        return source * 0 == 0


class Part:
    def __init__(self, place, needs, own, slot, send, recv):
        self.place, self.needs, self.own, self.slot = place, needs, own, slot
        self.send, self.recv = send, recv

    def copy(self, src, source, send, recv, target):
        return remote(src, self.slot(source), self.send.at[send], self.recv.at[recv], target)

    def go_up(self, source):
        p = self.place
        return p.has_up & self.needs.above(p.line + 1, source)

    def go_down(self, source):
        p = self.place
        return p.has_down & self.needs.below(p.line - 1, source)

    def from_below(self, s, source):
        p = self.place
        return (p.line - s >= 0) & self.needs.above(p.line, source)

    def from_above(self, s, source):
        p = self.place
        return (p.line + s < p.length) & self.needs.below(p.line, source)


class LinePart(Part):
    def start(self):
        p = self.place

        @pl.when(self.needs.at(p.mate_index, p.me))
        def _():
            self.copy(self.own, p.me, (2, 0), (2, 0), p.mate).start()

        @pl.when(self.go_up(p.me))
        def _():
            self.copy(self.own, p.me, (0, 0), (0, 1), p.up).start()

        @pl.when(self.go_down(p.me))
        def _():
            self.copy(self.own, p.me, (1, 0), (1, 1), p.down).start()

    def step(self, s):
        p = self.place
        for row, source, there, go, target in (
            (0, p.me - 2 * s, self.from_below, self.go_up, p.up),
            (1, p.me + 2 * s, self.from_above, self.go_down, p.down),
        ):

            @pl.when(there(s, source))
            def _(row=row, source=source, go=go, target=target):
                held = self.slot(source)
                self.copy(held, source, (2 + row, s), (row, s), p.mate).wait_recv()

                @pl.when(go(source))
                def _():
                    self.copy(held, source, (row, s), (row, s + 1), target).start()

                @pl.when(self.needs.at(p.mate_index, source))
                def _():
                    self.copy(held, source, (2 + row, s), (2 + row, s), p.mate).start()

    def finish(self, taken=False):
        p = self.place
        for s in range(p.length):
            for row, source, exists, go, target in (
                (0, p.me - 2 * s, p.line - s >= 0, self.go_up, p.up),
                (1, p.me + 2 * s, p.line + s < p.length, self.go_down, p.down),
            ):
                held = self.slot(source)
                mates = source + 1 - 2 * p.side
                if s > 0 or row == 0:

                    @pl.when(exists & self.needs.at(p.me, mates) & (not taken))
                    def _(row=row, s=s, mates=mates):
                        theirs = self.slot(mates)
                        self.copy(theirs, mates, (2 + row, s), (2 + row, s), p.mate).wait_recv()

                    @pl.when(exists & self.needs.at(p.mate_index, source))
                    def _(row=row, s=s, held=held, source=source):
                        self.copy(held, source, (2 + row, s), (2 + row, s), p.mate).wait_send()

                @pl.when(exists & go(source) & ((s == 0) | self.arrived(row, source)))
                def _(row=row, s=s, held=held, source=source, target=target):
                    self.copy(held, source, (row, s), (row, s + 1), target).wait_send()

    def arrived(self, row, source):
        p = self.place
        return self.needs.above(p.line, source) if row == 0 else self.needs.below(p.line, source)


class PairPart(Part):
    def across(self):
        p = self.place

        @pl.when(self.needs.sent(p.me))
        def _():
            self.copy(self.own, p.me, (4, 0), (4, 0), p.mate).start()

    def along(self):
        p = self.place

        @pl.when(self.go_up(p.me))
        def _():
            self.copy(self.own, p.me, (0, 0), (0, 1), p.up).start()

        @pl.when(self.go_down(p.me))
        def _():
            self.copy(self.own, p.me, (1, 0), (1, 1), p.down).start()

    def middle(self):
        p = self.place
        source = p.mate_index
        held = self.slot(source)

        @pl.when(self.needs.sent(source))
        def _():
            self.copy(held, source, (4, 0), (4, 0), p.mate).wait_recv()

        @pl.when(self.go_up(source))
        def _():
            self.copy(held, source, (2, 0), (2, 1), p.up).start()

        @pl.when(self.go_down(source))
        def _():
            self.copy(held, source, (3, 0), (3, 1), p.down).start()

    def step(self, s):
        p = self.place
        for base, column in ((0, p.me), (2, p.mate_index)):
            for row, source, there, go, target in (
                (0, column - 2 * s, self.from_below, self.go_up, p.up),
                (1, column + 2 * s, self.from_above, self.go_down, p.down),
            ):

                @pl.when(there(s, source))
                def _(row=row + base, source=source, go=go, target=target):
                    held = self.slot(source)
                    self.copy(held, source, (row, s), (row, s), p.mate).wait_recv()

                    @pl.when(go(source))
                    def _():
                        self.copy(held, source, (row, s), (row, s + 1), target).start()

    def finish(self):
        p = self.place

        @pl.when(self.needs.sent(p.me))
        def _():
            self.copy(self.own, p.me, (4, 0), (4, 0), p.mate).wait_send()

        for s in range(p.length):
            for base, column in ((0, p.me), (2, p.mate_index)):
                for row, source, there, go, target in (
                    (0, column - 2 * s, self.from_below, self.go_up, p.up),
                    (1, column + 2 * s, self.from_above, self.go_down, p.down),
                ):
                    passed = there(s, source) if s > 0 else p.me >= 0

                    @pl.when(passed & go(source))
                    def _(row=row + base, s=s, source=source, target=target):
                        held = self.slot(source)
                        self.copy(held, source, (row, s), (row, s + 1), target).wait_send()


class Swap:
    def __init__(self, place, src, dst, send, recv):
        self.place, self.src, self.dst, self.send, self.recv = place, src, dst, send, recv

    def copy(self, shift):
        p = self.place
        there = lax.rem(p.me + shift, p.count)
        return remote(
            self.src.at[there], self.dst.at[p.me], self.send.at[shift], self.recv.at[shift], {"ctx": there}
        )

    def keep(self):
        p = self.place
        return pltpu.make_async_copy(self.src.at[p.me], self.dst.at[p.me], self.send.at[0])

    def start(self):
        for shift in range(1, self.place.count):
            self.copy(shift).start()
        self.keep().start()

    def finish(self):
        p = self.place
        self.keep().wait()
        for shift in range(1, p.count):
            self.copy(shift).wait_send()
            source = lax.rem(p.me + p.count - shift, p.count)
            held = self.dst.at[source]
            remote(held, held, self.send.at[shift], self.recv.at[shift], p.mate).wait_recv()


def part_sems(length):
    return [
        pltpu.SemaphoreType.DMA((5, length + 1)),
        pltpu.SemaphoreType.DMA((5, length + 1)),
    ]


def swap_sems(count):
    return [pltpu.SemaphoreType.DMA((count,)), pltpu.SemaphoreType.DMA((count,))]


def dot(left, right):
    return jnp.dot(left, right, preferred_element_type=F32)


def setup_body(
    lengths, deal_ref, x_ref, t_ref, dw_ref, *refs
):
    rows_in, refs = refs[:6], refs[6:]
    fb_in, b_in, pb_in, kern_in = refs[:4]
    sx_ref, st_ref, arrange_ref, bounds, wide, narrow, ffn, kern, kern_s = refs[4:]
    count, piece = sx_ref.shape[:2]
    rows = count * piece
    group = lax.axis_index("wt")
    place = lax.axis_index("ctx")
    start = place * rows
    end = jnp.int32(0)
    total = jnp.int32(0)
    first, last = jnp.int32(0), jnp.int32(rows * count)
    ends = []
    for i in range(SEQS):
        end = end + lengths[group, i]
        ends.append(end)
        bounds[i] = end
        for g in range(4):
            total = total + lengths[g, i]
    for i in range(SEQS):
        first = jnp.where(ends[i] <= start, ends[i], first)
    for i in reversed(range(SEQS)):
        last = jnp.where(ends[i] >= start + rows, ends[i], last)
    bounds[SEQS] = start
    bounds[SEQS + 1] = lax.div(first, rows)
    bounds[SEQS + 2] = lax.div(last - 1, rows)
    bounds[SEQS + 3] = place
    bounds[SEQS + 4] = group
    bounds[SEQS + 5] = total
    slots = deal_ref[0:1, pl.ds(pl.multiple_of(start, 128), rows)]
    block = lax.div(slots, rows)
    arrange = block * piece + (slots - block * rows) - place * piece
    arrange_ref[...] = arrange
    sort = jnp.where(lax.broadcasted_iota(jnp.int32, (rows, rows), 0) == arrange, 1.0, 0.0).astype(BF16)
    for src, dst in ((x_ref, sx_ref), (t_ref, st_ref)):
        moved = dot(sort, src[...]).astype(BF16)
        for j in range(count):
            dst[j] = moved[piece * j : piece * j + piece]
    wide[...] = jnp.zeros(wide.shape, F32)
    wide[0:KW, :] = dw_ref[...].astype(F32)
    for i, row in enumerate(rows_in):
        wide[KW + i : KW + i + 1, :] = row[...].astype(F32).reshape(1, D // 4)
    narrow[...] = jnp.zeros(narrow.shape, F32)
    narrow[0:3, : A // 4] = b_in[...].astype(F32)
    narrow[3:4, : A // 4] = pb_in[...].astype(F32).reshape(1, A // 4)
    ffn[...] = jnp.zeros(ffn.shape, F32)
    ffn[0:1, :] = fb_in[...].astype(F32).reshape(1, D)
    kern_s[...] = jnp.zeros(kern_s.shape, F32)
    kern_s[: H * KW, : A // 4] = kern_in[...].astype(F32)
    kern[...] = kern_s[...].T[: A // 4]


SMALL_SHAPES = [(16, D // 4), (8, 128), (8, D), (A // 4, 128)]


def setup(lengths, deal, hidden, teacher, smalls, count):
    rows = hidden.shape[0]
    vmem = pl.BlockSpec(memory_space=pltpu.VMEM)
    smem = pl.BlockSpec(memory_space=pltpu.SMEM)
    pieces = jax.ShapeDtypeStruct((count, rows // count, D), BF16)
    return pl.pallas_call(
        setup_body,
        out_shape=[
            pieces,
            pieces,
            jax.ShapeDtypeStruct((1, rows), jnp.int32),
            jax.ShapeDtypeStruct((SEQS + 6,), jnp.int32),
        ]
        + [jax.ShapeDtypeStruct(shape, F32) for shape in SMALL_SHAPES],
        in_specs=[smem] + [vmem] * (3 + len(smalls)),
        out_specs=[vmem] * 3 + [smem] + [vmem] * 4,
        scratch_shapes=[pltpu.VMEM((128, 128), F32)],
        compiler_params=pltpu.CompilerParams(vmem_limit_bytes=VMEM_LIMIT),
        name="setup",
    )(lengths, deal, hidden, teacher, *smalls)


N_SMALL = 4


def gather_body(count, spans, fused, *refs):
    n = len(spans)
    inputs, refs = refs[: n + 4 + N_SMALL], refs[n + 4 + N_SMALL :]
    x_ref, t_ref = inputs[:2]
    shards = list(inputs[2 : 2 + n])
    own_small = list(inputs[2 + n : 2 + n + N_SMALL])
    bounds, kb_ref = inputs[2 + n + N_SMALL :]
    target_ref = refs[0]
    fulls = list(refs[1 : 1 + n])
    vec_ref, small_ref, fb_ref, kw_ref = refs[1 + n : 5 + n]
    refs = refs[5 + n :]
    if fused:
        out_hbm, conv_outs, refs = refs[:3], refs[3:10], refs[10:]
        out_ref, held_out, conv_scratch, project_sem, refs = refs[0], refs[1:4], refs[4:10], refs[10], refs[11:]
    else:
        out_ref, refs = refs[0], refs[1:]
    all_small = refs[:N_SMALL]
    local_sem, w_send, w_recv, pad_send, pad_recv = refs[N_SMALL : N_SMALL + 5]
    sems = refs[N_SMALL + 5 :]
    p = Place(count)
    k = lax.axis_index("wt")
    side = lax.rem(k, 2)
    core_mate = {"wt": k + 1 - 2 * side}
    far = lax.rem(k + 2, 4)
    far_mate = {"wt": far}

    def span(i, ref, index):
        if i >= n:
            return ref.at[index]
        axis, size = spans[i]
        window = pl.ds(pl.multiple_of(index * size, size), size)
        return ref.at[window] if axis == 0 else ref.at[:, window]

    shards += own_small
    fulls += all_small
    total = n + N_SMALL
    order = list(range(n, total)) + list(range(n))

    greet(p.others() + [(k >= 0, core_mate), (k >= 0, far_mate)])
    quarter, eighth = count // 4, count // 8
    cuts = [0, quarter, p.valid - quarter, p.valid - eighth, p.valid]
    parts = []
    for i, kind in enumerate((LinePart, LinePart, PairPart, PairPart)):
        first, end = cuts[i], cuts[i + 1]
        parts.append(
            kind(
                p,
                PieceNeeds(p, first, end - 1),
                x_ref.at[first:end],
                lambda j, first=first, end=end: out_ref.at[first:end, j],
                sems[2 * i],
                sems[2 * i + 1],
            )
        )
    low, high, *pairs = parts
    lines = [high, low]
    for part in pairs:
        part.across()
    for part in lines:
        part.start()
    for part in pairs:
        part.along()
    for i in order:
        held = span(i, fulls[i], k)
        remote(shards[i], held, w_send.at[0, i], w_recv.at[0, i], far_mate).start()
        remote(shards[i], held, w_send.at[1, i], w_recv.at[1, i], core_mate).start()

    def pad_copy(there):
        return remote(
            x_ref.at[p.valid :],
            out_ref.at[p.valid :, p.me],
            pad_send.at[there - p.valid],
            pad_recv.at[p.me],
            {"ctx": p.me * 0 + there},
        )

    def pads():
        for there in range(p.valid, count):

            @pl.when(p.me != there)
            def _(there=there):
                pad_copy(there).start()

    own_copy = pltpu.make_async_copy(x_ref, out_ref.at[:, p.me], local_sem.at[total])
    keeps = [
        pltpu.make_async_copy(shards[i], span(i, fulls[i], k), local_sem.at[i]) for i in range(total)
    ]
    for keep in [own_copy] + keeps:
        keep.start()
    swap = Swap(p, t_ref, target_ref, sems[8], sems[9])

    def relay(i):
        held = span(i, fulls[i], far)
        remote(held, held, w_send.at[2, i], w_recv.at[0, i], core_mate).wait_recv()
        remote(held, held, w_send.at[2, i], w_recv.at[2, i], core_mate).start()

    def whole(i):
        keeps[i].wait()
        held = span(i, fulls[i], k)
        remote(shards[i], held, w_send.at[1, i], w_recv.at[1, i], core_mate).wait_recv()
        remote(held, held, w_send.at[2, i], w_recv.at[2, i], core_mate).wait_recv()

    def spread(ref, step, shape):
        row = lax.broadcasted_iota(jnp.int32, shape, 0)
        column = lax.broadcasted_iota(jnp.int32, shape, 1)
        value = 0.0
        for index in range(4):
            move = jnp.where((column == row + step * index) & (row < step), 1.0, 0.0).astype(BF16)
            value += dot(ref[index].astype(BF16), move)
        return value

    def smalls():
        for i in range(n, total):
            whole(i)
        vec_ref[...] = spread(all_small[0], D // 4, (D // 4, D))
        small_ref[...] = spread(all_small[1], A // 4, (128, A))
        for index in range(4):
            fb_ref[index : index + 1, :] = all_small[2][index, 0:1, :]
            kw_ref[A // 4 * index : A // 4 * index + A // 4, :] = all_small[3][index].astype(BF16)

    def project_rows(x, blocks, sources):
        lead = out_ref[blocks, sources].shape[:-1]
        w_ref = fulls[0]
        query = (dot(x, w_ref[:, :A]) + small_ref[0:1, :]).astype(BF16).astype(F32)
        keys = dot(x, w_ref[:, A : 2 * A])
        values = dot(x, w_ref[:, 2 * A : 3 * A]) + small_ref[1:2, :]
        for value, held in zip((query * (HD**-0.5), keys, values), held_out):
            held[blocks, sources] = value.astype(BF16).reshape(lead + (A,))

    def project_copies(source):
        return [
            pltpu.make_async_copy(
                held_out[i].at[: p.valid, source], out_hbm[i].at[: p.valid, source], project_sem.at[i, source]
            )
            for i in range(3)
        ]

    def project_source(source):
        blocks = slice(0, p.valid)
        project_rows(out_ref[blocks, source].reshape(-1, D), blocks, source)
        for copy in project_copies(source):
            copy.start()

    def pad_copies():
        return [
            pltpu.make_async_copy(held_out[i].at[p.valid :], out_hbm[i].at[p.valid :], project_sem.at[i, 0])
            for i in range(3)
        ]

    def wait_pads():
        for shift in range(1, count):
            source = lax.rem(p.me + shift, count)
            held = out_ref.at[p.valid :, source]
            remote(held, held, pad_send.at[0], pad_recv.at[source], p.mate).wait_recv()

    near_count = 2 * p.length - 1

    def candidate(i):
        mates = lax.div(i, near_count)
        i = i - mates * near_count
        s = lax.div(i + 1, 2)
        odd = lax.rem(i, 2)
        line = p.line + (2 * odd - 1) * s
        source = jnp.where(mates == 1, p.mate_index, p.me) + (2 * odd - 1) * 2 * s

        @pl.when((line >= 0) & (line < p.length) & (p.me < p.valid))
        def _():
            for part in lines:

                @pl.when((mates == 1) & part.needs.at(p.me, source))
                def _(part=part):
                    theirs = part.slot(source)
                    at = (2 + odd, s)
                    part.copy(theirs, source, at, at, p.mate).wait_recv()

            project_source(source)

    def first_candidates(i, _):
        candidate(jnp.where(i < near_count - 2, i, near_count))
        return 0

    def last_candidates(i, _):
        candidate(jnp.where(i < 2, near_count - 2 + i, near_count - 1 + i))
        return 0

    for part in pairs:
        part.middle()
    for s in range(1, p.length - 1):
        for part in lines + pairs:
            part.step(s)
        if s == 1:
            for i in order[: N_SMALL + 1]:
                relay(i)
    swap.start()
    pads()
    smalls()
    whole(0)
    if fused:
        own_copy.wait()
        lax.fori_loop(0, near_count - 1, first_candidates, 0)
    for part in lines + pairs:
        part.step(p.length - 1)
    for i in order[N_SMALL + 1 :]:
        relay(i)
    if fused:
        lax.fori_loop(0, near_count + 1, last_candidates, 0)

        @pl.when(p.me >= p.valid)
        def _():
            wait_pads()
            blocks = slice(p.valid, count)
            project_rows(out_ref[blocks].reshape(-1, D), blocks, slice(0, count))
            for copy in pad_copies():
                copy.start()

        piece = x_ref.shape[1]
        conv_out, ext_ref, cv_ref = conv_outs[:3]
        before = jnp.maximum(p.me - 1, 0)
        after = jnp.minimum(p.me + 1, count - 1)
        ext_ref[0:RIM, :] = out_ref[before, count - 1, piece - RIM :, :]
        for j in range(count):
            ext_ref[RIM + piece * j : RIM + piece * j + piece, :] = out_ref[p.me, j]
        ext_ref[RIM + piece * count :, :] = out_ref[after, 0, :RIM, :]
        whole(1)
        conv_core(
            bounds, count * count * piece, fulls[0], fulls[1], kw_ref, kb_ref, vec_ref, small_ref,
            *conv_outs, *conv_scratch,
        )

        @pl.when(p.me < p.valid)
        def _():
            for source in range(count):
                for copy in project_copies(source):
                    copy.wait()

        @pl.when(p.me >= p.valid)
        def _():
            for copy in pad_copies():
                copy.wait()

    else:
        own_copy.wait()
        whole(1)

        @pl.when(p.me >= p.valid)
        def _():
            wait_pads()

    for i in range(2, n):
        whole(i)
    for i in range(total):
        held = span(i, fulls[i], k)
        remote(shards[i], held, w_send.at[0, i], w_recv.at[0, i], far_mate).wait_send()
        remote(shards[i], held, w_send.at[1, i], w_recv.at[1, i], core_mate).wait_send()
        remote(held, held, w_send.at[2, i], w_recv.at[2, i], core_mate).wait_send()
    for part in pairs:
        part.finish()
    for part in lines:
        part.finish(taken=fused)
    for there in range(p.valid, count):

        @pl.when(p.me != there)
        def _(there=there):
            pad_copy(there).wait_send()

    swap.finish()


def gather_inputs(bounds, pieces, targets, shards, axes, smalls, kern_bias, ctx_count, fused):
    length = ctx_count // 2
    rows = pieces.shape[0] * pieces.shape[1]
    fulls, spans = [], []
    for shard, axis in zip(shards, axes):
        shape = list(shard.shape)
        spans.append((axis, shape[axis]))
        shape[axis] *= 4
        fulls.append(jax.ShapeDtypeStruct(tuple(shape), shard.dtype))
    n = len(shards)
    total = n + N_SMALL
    vmem = pl.BlockSpec(memory_space=pltpu.VMEM)
    hbm = pl.BlockSpec(memory_space=pl.ANY)
    natural = (ctx_count,) + pieces.shape
    heads = (ctx_count,) + pieces.shape[:-1] + (A,)
    outs = (
        [jax.ShapeDtypeStruct(targets.shape, targets.dtype)]
        + fulls
        + [
            jax.ShapeDtypeStruct((16, D), F32),
            jax.ShapeDtypeStruct((8, A), F32),
            jax.ShapeDtypeStruct((4, D), F32),
            jax.ShapeDtypeStruct((A, 128), BF16),
        ]
    )
    specs = [hbm] + [vmem] * 2 + [hbm] * (n - 2) + [vmem] * 4
    scratch = []
    if fused:
        conv_outs, conv_scratch = conv_shapes(rows)
        outs += [jax.ShapeDtypeStruct(heads, BF16)] * 3 + conv_outs
        specs += [hbm] * 3 + [vmem] * 7
        scratch += [pltpu.VMEM(natural, BF16)] + [pltpu.VMEM(heads, BF16)] * 3 + conv_scratch
        scratch += [pltpu.SemaphoreType.DMA((3, ctx_count))]
    else:
        outs.append(jax.ShapeDtypeStruct(natural, BF16))
        specs.append(hbm)
    return pl.pallas_call(
        functools.partial(gather_body, ctx_count, spans, fused),
        out_shape=outs,
        in_specs=[vmem] * (2 + n + len(smalls)) + [pl.BlockSpec(memory_space=pltpu.SMEM), vmem],
        out_specs=specs,
        scratch_shapes=scratch
        + [pltpu.VMEM((4,) + shape, F32) for shape in SMALL_SHAPES]
        + [
            pltpu.SemaphoreType.DMA((total + 1,)),
            pltpu.SemaphoreType.DMA((3, total)),
            pltpu.SemaphoreType.DMA((3, total)),
            pltpu.SemaphoreType.DMA((ctx_count // 8,)),
            pltpu.SemaphoreType.DMA((ctx_count,)),
        ]
        + part_sems(length) * 4
        + swap_sems(ctx_count),
        compiler_params=pltpu.CompilerParams(
            collective_id=0, has_side_effects=True, vmem_limit_bytes=VMEM_LIMIT
        ),
        name="gather_inputs",
    )(pieces, targets, *shards, *smalls, bounds, kern_bias)


class Sum:
    def __init__(self, bits, chunks, packed, bufs, out, send, recv, mine=None):
        self.bits, self.chunks, self.packed, self.bufs, self.out = bits, chunks, packed, bufs, out
        self.mine = mine
        self.send, self.recv = send, recv
        self.stages = 2 + bits
        self.last = self.stages + bits
        k = lax.axis_index("wt")
        me = lax.axis_index("ctx")
        self.core = lax.rem(k, 2)
        self.far = lax.div(k, 2)
        self.bit = [lax.rem(lax.div(me, 1 << b), 2) for b in range(bits)]
        self.targets = [{"wt": k + 1 - 2 * self.core}, {"wt": lax.rem(k + 2, 4)}]
        for b in range(bits):
            self.targets.append({"ctx": me + (1 << b) * (1 - 2 * self.bit[b])})

    def source(self, stage, c, kept):
        whole = slice(None)

        def pick(value):
            return value if kept else 1 - value

        if stage == 0 and kept and self.mine is not None:
            return self.mine.at[(whole,) * (self.bits + 1) + (c,)]
        if stage == 0:
            return self.packed.at[(whole, pick(self.core)) + (whole,) * self.bits + (c,)]
        if stage == 1:
            return self.bufs[0].at[c, pick(self.far)]
        b = stage - 2
        return self.bufs[stage - 1].at[(c,) + (whole,) * (self.bits - b - 1) + (pick(self.bit[b]),)]

    def spread(self, b, c, other):
        index = [self.bit[j] for j in range(b, -1, -1)]
        if other:
            index[0] = 1 - index[0]
        return self.out.at[(slice(None),) * (self.bits - 1 - b) + tuple(index) + (c,)]

    def place_own(self, c, value):
        self.out[tuple(self.bit[j] for j in range(self.bits - 1, -1, -1)) + (c,)] = value

    def copy(self, stage, c):
        if stage < self.stages:
            src, dst, target = self.source(stage, c, False), self.bufs[stage].at[c], self.targets[stage]
        else:
            b = self.bits - 1 - (stage - self.stages)
            src, dst, target = self.spread(b, c, False), self.spread(b, c, False), self.targets[2 + b]
        return remote(src, dst, self.send.at[stage, c], self.recv.at[stage, c], target)

    def start(self, stage, c):
        self.copy(stage, c).start()

    def take(self, stage, c):
        if stage >= self.stages:
            b = self.bits - 1 - (stage - self.stages)
            held = self.spread(b, c, True)
            remote(
                held, held, self.send.at[stage, c], self.recv.at[stage, c], self.targets[2 + b]
            ).wait_recv()
            return
        self.copy(stage, c).wait_recv()
        mine, sums = self.source(stage, c, True), self.bufs[stage].at[c]
        lead = sums.shape[:-2]
        total = 1
        for size in lead:
            total *= size

        def one(at, _):
            index, rest = [], at
            for size in reversed(lead):
                index.append(lax.rem(rest, size))
                rest = lax.div(rest, size)
            index = tuple(reversed(index))
            value = mine[index].astype(F32) + sums[index].astype(F32)
            sums[index] = value.astype(BF16)
            return 0

        if lead:
            lax.fori_loop(0, total, one, 0)
        else:
            sums[...] = (mine[...].astype(F32) + sums[...].astype(F32)).astype(BF16)

    def sent(self, stage, c):
        self.copy(stage, c).wait_send()

    def open(self):
        for c in range(min(4, self.chunks)):
            self.start(0, c)

    def across(self, first, end):
        for c in range(first, min(end, self.chunks)):
            self.take(0, c)
            self.start(1, c)
            if c + 4 < self.chunks:
                self.start(0, c + 4)


def sum_shapes(ctx_count, rows, size):
    bits = ctx_count.bit_length() - 1
    piece = min(size, rows // ctx_count)
    chunks = rows // ctx_count // piece
    twos = (2,) * bits
    bufs = [
        pltpu.VMEM((chunks, 2) + twos + (piece, D), BF16),
        pltpu.VMEM((chunks,) + twos + (piece, D), BF16),
    ]
    for b in range(bits):
        bufs.append(pltpu.VMEM((chunks,) + twos[b + 1 :] + (piece, D), BF16))
    tail = (chunks, piece, D)
    return bits, chunks, (2, 2) + twos + tail, twos + tail, bufs


def seg_of(position, bounds):
    seg = jnp.zeros(position.shape, jnp.int32)
    for i in range(SEQS):
        seg = seg + jnp.where(position >= bounds[i], 1, 0)
    return seg


def reach(bounds, first, last, group_rows):
    begin, end = jnp.int32(0), jnp.int32(group_rows)
    for i in range(SEQS):
        begin = jnp.where(bounds[i] <= first, bounds[i], begin)
    for i in reversed(range(SEQS)):
        end = jnp.where(bounds[i] > last, bounds[i], end)
    return begin, end


def half_masks(rows):
    lane = lax.broadcasted_iota(jnp.int32, (rows, 128), 1)
    low = jnp.where(lane < HD, 1.0, 0.0).astype(BF16)
    return low, (1.0 - low.astype(F32)).astype(BF16)


def dot_last(left, right):
    return lax.dot_general(left, right, (((1,), (1,)), ((), ())), preferred_element_type=F32)


def attend_body(tq, tk, bounds, q_ref, k_ref, v_ref, out_ref, lse_ref, m_ref, acc_ref):
    rows, group_rows = out_ref.shape[0], k_ref.shape[0]
    base = pl.multiple_of(bounds[SEQS], tq)
    q_masks, k_masks = half_masks(tq), half_masks(tk)
    lane = lax.broadcasted_iota(jnp.int32, (tq, 128), 1)
    low = lane < HD

    def tile(qi, _):
        q0 = pl.multiple_of(qi * tq, tq)
        first = pl.multiple_of(base + q0, tq)
        begin, end = reach(bounds, first, first + tq - 1, group_rows)
        q_seg = seg_of(first + lax.broadcasted_iota(jnp.int32, (tq, 1), 0), bounds)
        m_ref[...] = jnp.full(m_ref.shape, MASKED, F32)
        acc_ref[...] = jnp.zeros(acc_ref.shape, F32)

        def step(kt, _):
            k0 = pl.multiple_of(kt * tk, tk)
            k_seg = seg_of(k0 + lax.broadcasted_iota(jnp.int32, (1, tk), 1), bounds)
            bias = jnp.where(q_seg == k_seg, 0.0, MASKED)
            for pair in range(H // 2):
                cols = slice(128 * pair, 128 * pair + 128)
                q_pair = q_ref[pl.ds(first, tq), cols]
                k_pair = k_ref[pl.ds(k0, tk), cols]
                v_pair = v_ref[pl.ds(k0, tk), cols]
                for side in range(2):
                    head = 2 * pair + side
                    scores = dot_last(q_pair * q_masks[side], k_pair) + bias
                    old = m_ref[head]
                    new = jnp.maximum(old, jnp.max(scores, axis=1, keepdims=True))
                    weights = jnp.exp(scores - jnp.tile(new, (1, tk // 128)))
                    v_ones = v_pair * k_masks[side] + k_masks[1 - side]
                    acc_ref[head] = acc_ref[head] * jnp.exp(old - new) + jnp.dot(
                        weights.astype(BF16), v_ones, preferred_element_type=F32
                    )
                    m_ref[head] = new
            return 0

        lax.fori_loop(lax.div(begin, tk), lax.div(end + tk - 1, tk), step, 0)
        lse = jnp.zeros((tq, 128), F32)
        for pair in range(H // 2):
            left, right = acc_ref[2 * pair], acc_ref[2 * pair + 1]
            crossed = jnp.where(low, right, left)
            total = pltpu.roll(crossed, HD, 1)
            out_ref[pl.ds(q0, tq), 128 * pair : 128 * pair + 128] = jnp.where(low, left, right) / total
            lse = jnp.where(lane == 2 * pair, m_ref[2 * pair] + jnp.log(total), lse)
            lse = jnp.where(lane == 2 * pair + 1, m_ref[2 * pair + 1] + jnp.log(crossed), lse)
        lse_ref[pl.ds(q0, tq), :] = lse
        return 0

    lax.fori_loop(0, rows // tq, tile, 0)


def attend(bounds, query, keys, values, rows):
    tq, tk = rows, rows // 2
    return pl.pallas_call(
        functools.partial(attend_body, tq, tk),
        out_shape=[
            jax.ShapeDtypeStruct((rows, A), F32),
            jax.ShapeDtypeStruct((rows, 128), F32),
        ],
        in_specs=[pl.BlockSpec(memory_space=pltpu.SMEM)]
        + [pl.BlockSpec(memory_space=pltpu.VMEM)] * 3,
        out_specs=[pl.BlockSpec(memory_space=pltpu.VMEM)] * 2,
        scratch_shapes=[pltpu.VMEM((H, tq, 128), F32), pltpu.VMEM((H, tq, 128), F32)],
        compiler_params=pltpu.CompilerParams(vmem_limit_bytes=VMEM_LIMIT),
        name="attend",
    )(bounds, query, keys, values)


def query_grads_body(tq, tk, bounds, q_ref, g_ref, stat_ref, k_ref, v_ref, out_ref, rep_ref):
    rows, group_rows = out_ref.shape[0], k_ref.shape[0]
    base = pl.multiple_of(bounds[SEQS], tq)
    q_masks, k_masks = half_masks(tq), half_masks(tk)

    def tile(qi, _):
        q0 = pl.multiple_of(qi * tq, tq)
        first = pl.multiple_of(base + q0, tq)
        begin, end = reach(bounds, first, first + tq - 1, group_rows)
        q_seg = seg_of(first + lax.broadcasted_iota(jnp.int32, (tq, 1), 0), bounds)
        stat = stat_ref[pl.ds(q0, tq), :]
        for head in range(H):
            rep_ref[head] = jnp.broadcast_to(stat[:, head : head + 1], (tq, 128))
            rep_ref[H + head] = jnp.broadcast_to(stat[:, 8 + head : 9 + head], (tq, 128))
        out_ref[pl.ds(q0, tq), :] = jnp.zeros((tq, A), F32)

        def step(kt, _):
            k0 = pl.multiple_of(kt * tk, tk)
            k_seg = seg_of(k0 + lax.broadcasted_iota(jnp.int32, (1, tk), 1), bounds)
            bias = jnp.where(q_seg == k_seg, 0.0, MASKED)
            for pair in range(H // 2):
                cols = slice(128 * pair, 128 * pair + 128)
                q_pair = q_ref[pl.ds(first, tq), cols]
                g_pair = g_ref[pl.ds(q0, tq), cols]
                k_pair = k_ref[pl.ds(k0, tk), cols]
                v_pair = v_ref[pl.ds(k0, tk), cols]
                total = jnp.zeros((tq, 128), F32)
                for side in range(2):
                    head = 2 * pair + side
                    scores = dot_last(q_pair * q_masks[side], k_pair) + bias
                    prob = jnp.exp(scores - jnp.tile(rep_ref[head], (1, tk // 128)))
                    back = dot_last(g_pair * q_masks[side], v_pair)
                    back = prob * (back - jnp.tile(rep_ref[H + head], (1, tk // 128)))
                    total = total + jnp.dot(
                        back.astype(BF16), k_pair * k_masks[side], preferred_element_type=F32
                    )
                out_ref[pl.ds(q0, tq), cols] += total
            return 0

        lax.fori_loop(lax.div(begin, tk), lax.div(end + tk - 1, tk), step, 0)
        return 0

    lax.fori_loop(0, rows // tq, tile, 0)


def query_grads(bounds, query, grads, stats, keys, values):
    rows = grads.shape[0]
    tq, tk = rows, rows // 2
    return pl.pallas_call(
        functools.partial(query_grads_body, tq, tk),
        out_shape=jax.ShapeDtypeStruct((rows, A), F32),
        in_specs=[pl.BlockSpec(memory_space=pltpu.SMEM)]
        + [pl.BlockSpec(memory_space=pltpu.VMEM)] * 5,
        out_specs=pl.BlockSpec(memory_space=pltpu.VMEM),
        scratch_shapes=[pltpu.VMEM((2 * H, tq, 128), F32)],
        compiler_params=pltpu.CompilerParams(vmem_limit_bytes=VMEM_LIMIT),
        name="query_grads",
    )(bounds, query, grads, stats, keys, values)


def key_grads_body(
    tk, bounds, k_all, v_all, q_ref, g_ref, stat_ref, dk_ref, dv_ref, k_ref, v_ref, sem
):
    rows, group_rows = dk_ref.shape[0], q_ref.shape[0]
    own = pl.ds(pl.multiple_of(bounds[SEQS], rows), rows)
    for copy in fetch([k_all.at[own], v_all.at[own]], [k_ref, v_ref], sem):
        copy.wait()
    tq = stat_ref.shape[2]
    base = pl.multiple_of(bounds[SEQS], tk)
    q_masks, k_masks = half_masks(tq), half_masks(tk)

    def tile(ki, _):
        k0 = pl.multiple_of(ki * tk, tk)
        first = pl.multiple_of(base + k0, tk)
        begin, end = reach(bounds, first, first + tk - 1, group_rows)
        k_seg = seg_of(first + lax.broadcasted_iota(jnp.int32, (tk, 1), 0), bounds)
        dk_ref[pl.ds(k0, tk), :] = jnp.zeros((tk, A), F32)
        dv_ref[pl.ds(k0, tk), :] = jnp.zeros((tk, A), F32)

        def step(qt, _):
            q0 = pl.multiple_of(qt * tq, tq)
            q_seg = seg_of(q0 + lax.broadcasted_iota(jnp.int32, (1, tq), 1), bounds)
            bias = jnp.where(k_seg == q_seg, 0.0, MASKED)
            for pair in range(H // 2):
                cols = slice(128 * pair, 128 * pair + 128)
                q_pair = q_ref[pl.ds(q0, tq), cols]
                g_pair = g_ref[pl.ds(q0, tq), cols]
                k_pair = k_ref[pl.ds(k0, tk), cols]
                v_pair = v_ref[pl.ds(k0, tk), cols]
                key_sum = jnp.zeros((tk, 128), F32)
                value_sum = jnp.zeros((tk, 128), F32)
                for side in range(2):
                    head = 2 * pair + side
                    scores = dot_last(k_pair * k_masks[side], q_pair) + bias
                    prob = jnp.exp(scores - stat_ref[qt, head : head + 1, :])
                    value_sum = value_sum + jnp.dot(
                        prob.astype(BF16), g_pair * q_masks[side], preferred_element_type=F32
                    )
                    back = dot_last(v_pair * k_masks[side], g_pair)
                    back = prob * (back - stat_ref[qt, 8 + head : 9 + head, :])
                    key_sum = key_sum + jnp.dot(
                        back.astype(BF16), q_pair * q_masks[side], preferred_element_type=F32
                    )
                dk_ref[pl.ds(k0, tk), cols] += key_sum
                dv_ref[pl.ds(k0, tk), cols] += value_sum
            return 0

        lax.fori_loop(lax.div(begin, tq), lax.div(end + tq - 1, tq), step, 0)
        return 0

    lax.fori_loop(0, rows // tk, tile, 0)


def key_grads(bounds, keys, values, queries, grads, stats):
    rows = stats.shape[2]
    tk = rows
    return pl.pallas_call(
        functools.partial(key_grads_body, tk),
        out_shape=[jax.ShapeDtypeStruct((rows, A), F32)] * 2,
        in_specs=[pl.BlockSpec(memory_space=pltpu.SMEM)]
        + [pl.BlockSpec(memory_space=pl.ANY)] * 2
        + [pl.BlockSpec(memory_space=pltpu.VMEM)] * 3,
        out_specs=[pl.BlockSpec(memory_space=pltpu.VMEM)] * 2,
        scratch_shapes=[pltpu.VMEM((rows, A), BF16)] * 2 + [pltpu.SemaphoreType.DMA((2,))],
        compiler_params=pltpu.CompilerParams(vmem_limit_bytes=VMEM_LIMIT),
        name="key_grads",
    )(bounds, keys, values, queries, grads, stats)


def norm_back(grad_rows, normed, inverse, gain):
    scaled = grad_rows * gain
    return inverse * (
        scaled
        - jnp.mean(scaled, axis=1, keepdims=True)
        - normed * jnp.mean(scaled * normed, axis=1, keepdims=True)
    )


def dot_first(left, right):
    return lax.dot_general(left, right, (((0,), (0,)), ((), ())), preferred_element_type=F32)


def project_body(bounds, x_ref, w_ref, b_ref, q_ref, k_ref, v_ref):
    index = pl.program_id(0)

    @pl.when((index >= bounds[SEQS + 1]) & (index <= bounds[SEQS + 2]))
    def _():
        x = x_ref[...]
        query = (dot(x, w_ref[:, :A]) + b_ref[0:1, :]).astype(BF16).astype(F32)
        q_ref[...] = (query * (HD**-0.5)).astype(BF16)
        k_ref[...] = dot(x, w_ref[:, A : 2 * A]).astype(BF16)
        v_ref[...] = (dot(x, w_ref[:, 2 * A : 3 * A]) + b_ref[1:2, :]).astype(BF16)


def project(bounds, natural, w_in, smalls, rows):
    group_rows = natural.shape[0]

    def block(index, bounds):
        return (jnp.clip(index, bounds[SEQS + 1], bounds[SEQS + 2]), 0)

    def fixed(index, bounds):
        return (0, 0)

    return pl.pallas_call(
        project_body,
        out_shape=[jax.ShapeDtypeStruct((group_rows, A), BF16)] * 3,
        grid_spec=pltpu.PrefetchScalarGridSpec(
            num_scalar_prefetch=1,
            grid=(group_rows // rows,),
            in_specs=[
                pl.BlockSpec((rows, D), block),
                pl.BlockSpec((D, 3 * A), fixed),
                pl.BlockSpec((8, A), fixed),
            ],
            out_specs=[pl.BlockSpec((rows, A), block)] * 3,
        ),
        compiler_params=pltpu.CompilerParams(vmem_limit_bytes=VMEM_LIMIT),
        name="project",
    )(bounds, natural, w_in, smalls)


def tap_lanes(tap):
    row = lax.broadcasted_iota(jnp.int32, (128, A), 0)
    column = lax.broadcasted_iota(jnp.int32, (128, A), 1)
    return jnp.where(row == lax.div(column, HD) * KW + tap, 1.0, 0.0).astype(BF16)


def tap_pick(tap):
    row = lax.broadcasted_iota(jnp.int32, (A, 128), 0)
    column = lax.broadcasted_iota(jnp.int32, (A, 128), 1)
    first = row == lax.div(row, HD) * HD
    return jnp.where(first & (column == lax.div(row, HD) * KW + tap), 1.0, 0.0).astype(BF16)


def tap_weights(kw_ref, kb_ref, wide_ref, bias_ref):
    bias_ref[:, 0:128] = jnp.zeros((8, 128), F32)
    bias_ref[0:1, 0 : H * KW] = kb_ref[...].astype(F32)
    bias = bias_ref[:, 0:128].astype(BF16)
    for tap in range(KW):
        lanes = tap_lanes(tap)
        cols = slice(A * tap, A * tap + A)
        wide_ref[:, cols] = dot(kw_ref[...], lanes).astype(BF16)
        bias_ref[:, cols] = dot(bias, lanes)


def tap_near(bounds, group_rows, seg_ref, near_ref):
    span = near_ref.shape[1]
    start = lax.axis_index("ctx") * (span - RIM)
    position = start - RIM + lax.broadcasted_iota(jnp.int32, seg_ref.shape, 0)
    inside = (position >= 0) & (position < group_rows)
    seg_ref[...] = jnp.where(inside, seg_of(position, bounds), -1)
    seg = seg_ref[RIM // 2 : RIM // 2 + span, :]
    for tap in range(KW):
        shift = RIM // 2 - KW // 2 + tap
        near_ref[tap] = jnp.where((seg_ref[shift : shift + span, :] == seg) & (seg >= 0), 1.0, 0.0)


def tap_softmax(logits, bias_ref):
    parts = [logits[:, A * tap : A * tap + A] + bias_ref[0:1, A * tap : A * tap + A] for tap in range(KW)]
    largest = functools.reduce(jnp.maximum, parts)
    parts = [jnp.exp(part - largest) for part in parts]
    total = 1.0 / functools.reduce(jnp.add, parts)
    return [part * total for part in parts]


def wide3(value):
    return jnp.tile(value, (1, 3))


def conv_body(
    bounds, natural, w_ref, pw_ref, kw_ref, kb_ref, vec_ref, small_ref,
    out_ref, ext_ref, cv_ref, kc_ref, q_ref, cq_ref, sp_ref,
    extf_ref, seg_ref, near_ref, wide_ref, bias_ref, full_ref, sem,
):
    rows, group_rows = out_ref.shape[0], natural.shape[0]
    start = bounds[SEQS]
    copies = [
        pltpu.make_async_copy(
            natural.at[pl.ds(pl.multiple_of(jnp.maximum(start - RIM, 0), RIM), RIM)],
            ext_ref.at[0:RIM],
            sem.at[0],
        ),
        pltpu.make_async_copy(
            natural.at[pl.ds(pl.multiple_of(start, RIM), rows)], ext_ref.at[RIM : RIM + rows], sem.at[1]
        ),
        pltpu.make_async_copy(
            natural.at[pl.ds(pl.multiple_of(jnp.minimum(start + rows, group_rows - RIM), RIM), RIM)],
            ext_ref.at[RIM + rows : 2 * RIM + rows],
            sem.at[2],
        ),
    ]
    for copy in copies:
        copy.start()
    for copy in copies:
        copy.wait()
    conv_core(
        bounds, group_rows, w_ref, pw_ref, kw_ref, kb_ref, vec_ref, small_ref,
        out_ref, ext_ref, cv_ref, kc_ref, q_ref, cq_ref, sp_ref,
        extf_ref, seg_ref, near_ref, wide_ref, bias_ref, full_ref,
    )


def conv_core(
    bounds, group_rows, w_ref, pw_ref, kw_ref, kb_ref, vec_ref, small_ref,
    out_ref, ext_ref, cv_ref, kc_ref, q_ref, cq_ref, sp_ref,
    extf_ref, seg_ref, near_ref, wide_ref, bias_ref, full_ref,
):
    rows = out_ref.shape[0]
    span = rows + RIM
    tap_weights(kw_ref, kb_ref, wide_ref, bias_ref)
    tap_near(bounds, group_rows, seg_ref, near_ref)
    count = group_rows // rows
    place = lax.axis_index("ctx")
    padded = count - count // 8

    @pl.when((place == 0) | (place == padded))
    def _():
        ext_ref[0:RIM, :] = jnp.zeros((RIM, D), BF16)

    @pl.when((place == padded - 1) | (place == count - 1))
    def _():
        ext_ref[RIM + rows :, :] = jnp.zeros((RIM, D), BF16)

    ext = ext_ref[...]
    extf_ref[...] = ext.astype(F32)
    cv_ref[...] = dot(ext, w_ref[:, 3 * A :]) + small_ref[2:3, :]
    q_ref[...] = (dot(ext, w_ref[:, :A]) + small_ref[0:1, :]).astype(BF16).astype(F32)
    tile = span // 3

    def spread_tile(i, _):
        t0 = pl.multiple_of(tile * i, 16)
        here = pl.ds(t0, tile)

        def column(c, _):
            cols = pl.ds(pl.multiple_of(128 * c, 128), 128)
            window = extf_ref[pl.ds(t0, tile + RIM), cols]
            total = 0.0
            for tap in range(KW):
                shift = RIM // 2 - KW // 2 + tap
                total += vec_ref[tap : tap + 1, cols] * near_ref[tap, here, :] * window[shift : shift + tile]
            sp_ref[here, cols] = total.astype(BF16)
            return 0

        return lax.fori_loop(0, 6, column, 0)

    lax.fori_loop(0, 3, spread_tile, 0)
    kc_ref[...] = dot(sp_ref[...], pw_ref[...]) + small_ref[3:4, :]
    cq_ref[...] = (kc_ref[...] * q_ref[RIM // 2 : RIM // 2 + span, :]).astype(BF16)

    def mix_tile(i, _):
        t0 = pl.multiple_of(tile * i, 16)
        here = pl.ds(t0, tile)
        kernel = tap_softmax(dot(cq_ref[here, :], wide_ref[...]), bias_ref)
        window = cv_ref[pl.ds(t0, tile + RIM), :]
        total = 0.0
        for tap in range(KW):
            shift = RIM // 2 - KW // 2 + tap
            total += kernel[tap] * wide3(near_ref[tap, here, :]) * window[shift : shift + tile]
        full_ref[here, :] = total
        return 0

    lax.fori_loop(0, 3, mix_tile, 0)
    out_ref[...] = full_ref[RIM // 2 : RIM // 2 + rows, :].astype(BF16)


def conv_shapes(rows):
    span, wide = rows + RIM, rows + 2 * RIM
    outs = [
        jax.ShapeDtypeStruct((rows, A), BF16),
        jax.ShapeDtypeStruct((wide, D), BF16),
        jax.ShapeDtypeStruct((wide, A), F32),
        jax.ShapeDtypeStruct((span, A), F32),
        jax.ShapeDtypeStruct((wide, A), F32),
        jax.ShapeDtypeStruct((span, A), BF16),
        jax.ShapeDtypeStruct((span, D), BF16),
    ]
    scratch = [
        pltpu.VMEM((wide, D), F32),
        pltpu.VMEM((wide, 128), jnp.int32),
        pltpu.VMEM((KW, span, 128), F32),
        pltpu.VMEM((A, KW * A), BF16),
        pltpu.VMEM((8, KW * A), F32),
        pltpu.VMEM((span, A), F32),
    ]
    return outs, scratch


def convolve(bounds, natural, w_in, pw, kw, kb, vectors, smalls, rows):
    outs, scratch = conv_shapes(rows)
    vmem = pl.BlockSpec(memory_space=pltpu.VMEM)
    return pl.pallas_call(
        conv_body,
        out_shape=outs,
        in_specs=[pl.BlockSpec(memory_space=pltpu.SMEM), pl.BlockSpec(memory_space=pl.ANY)] + [vmem] * 6,
        out_specs=[vmem] * 7,
        scratch_shapes=scratch + [pltpu.SemaphoreType.DMA((3,))],
        compiler_params=pltpu.CompilerParams(vmem_limit_bytes=VMEM_LIMIT),
        name="convolve",
    )(bounds, natural, w_in, pw, kw, kb, vectors, smalls)


def norm_rows(x, gain, bias):
    centered = x - jnp.mean(x, axis=1, keepdims=True)
    inverse = lax.rsqrt(jnp.mean(centered * centered, axis=1, keepdims=True) + NORM_EPS)
    normed = centered * inverse
    return normed * gain + bias, normed, inverse


ROW_OUT_B, ROW_GAIN1, ROW_BIAS1, ROW_FFN_B, ROW_GAIN2, ROW_BIAS2 = range(KW, KW + 6)
FI_ROWS, FO_ROWS, OW_ROWS = 384, 384, 192
FIRST_PACK = 1024
SECOND_PACK = 512


def layer_body(
    bounds, attn_ref, lse_ref, conv_ref, ext_ref, tgt_ref, wo_ref, fi_ref, fo_ref, vec_ref, fb_ref,
    out_ref, gfirst_ref, gctx_ref, stat_ref, statt_ref, sums_ref, fbs_ref, pack_ref,
    ctx_s, low_s, act_s, slope_s, gfl_s, gpre_s, gproj_s,
):
    rows = out_ref.shape[0]
    tm = slope_s.shape[0]
    chunk = D
    wide = FF // NG
    part = D // NG
    row_of = lax.broadcasted_iota(jnp.int32, (A, 128), 0)
    column_of = lax.broadcasted_iota(jnp.int32, (A, 128), 1)
    head_pick = jnp.where(column_of == 8 + lax.div(row_of, HD), 1.0, 0.0).astype(BF16)
    sums_ref[...] = jnp.zeros(sums_ref.shape, F32)
    fbs_ref[...] = jnp.zeros(fbs_ref.shape, F32)

    def vec(row):
        return vec_ref[row : row + 1, :]

    def add_sum(row, value):
        sums_ref[row : row + 1, :] += jnp.sum(value, axis=0, keepdims=True)

    def tile(index, _):
        r0 = pl.multiple_of(index * tm, tm)
        here = pl.ds(r0, tm)
        attn = attn_ref[here, :]
        ctx_s[here, :A] = attn.astype(BF16)
        ctx_s[here, A:] = conv_ref[here, :]
        tokens = ext_ref[pl.ds(pl.multiple_of(r0 + RIM, RIM), tm), :].astype(F32)
        first = tokens + dot(ctx_s[here, :], wo_ref[...]) + vec(ROW_OUT_B)
        after, normed_one, inverse_one = norm_rows(first, vec(ROW_GAIN1), vec(ROW_BIAS1))
        low_s[here, :] = after.astype(BF16)
        results = []
        for g in range(NG):
            low = low_s[here, part * g : part * g + part]
            total = 0.0
            for c in range(wide // chunk):
                span = slice(chunk * c, chunk * c + chunk)
                whole = slice(wide * g + chunk * c, wide * g + chunk * c + chunk)
                pre = dot(low, fi_ref[g, :, span]) + fb_ref[2 * g + c : 2 * g + c + 1, :]
                phi = 0.5 * (1.0 + lax.erf(pre * ROOT_HALF))
                act = (pre * phi).astype(BF16)
                act_s[here, whole] = act
                slope_s[:, whole] = phi + pre * DENSITY_NORM * jnp.exp(-0.5 * pre * pre)
                total += dot(act, fo_ref[g, span, :])
            results.append(total)
        second = after + jnp.concatenate(results, axis=1) + vec(ROW_FFN_B)
        result, normed_two, inverse_two = norm_rows(second, vec(ROW_GAIN2), vec(ROW_BIAS2))
        out_ref[here, :] = result.astype(BF16)
        seg = seg_of(bounds[SEQS] + r0 + lax.broadcasted_iota(jnp.int32, (tm, 1), 0), bounds)
        error = jnp.where(seg < SEQS, result - tgt_ref[here, :].astype(F32), 0.0)
        add_sum(6, error * error)
        add_sum(4, error * normed_two)
        add_sum(5, error)
        grad_second = norm_back(error, normed_two, inverse_two, vec(ROW_GAIN2))
        gfl = grad_second.astype(BF16)
        gfl_s[here, :] = gfl
        add_sum(3, gfl.astype(F32))
        grads = []
        for g in range(NG):
            total = 0.0
            for c in range(wide // chunk):
                span = slice(chunk * c, chunk * c + chunk)
                whole = slice(wide * g + chunk * c, wide * g + chunk * c + chunk)
                gact = dot_last(gfl_s[here, part * g : part * g + part], fo_ref[g, span, :])
                gpre = (gact * slope_s[:, whole]).astype(BF16)
                gpre_s[here, whole] = gpre
                fbs_ref[2 * g + c : 2 * g + c + 1, :] += jnp.sum(gpre.astype(F32), axis=0, keepdims=True)
                total += dot_last(gpre, fi_ref[g, :, span])
            grads.append(total)
        grad_after = jnp.concatenate(grads, axis=1) + grad_second
        add_sum(1, grad_after * normed_one)
        add_sum(2, grad_after)
        grad_first = norm_back(grad_after, normed_one, inverse_one, vec(ROW_GAIN1))
        gfirst_ref[here, :] = grad_first
        gproj = grad_first.astype(BF16)
        gproj_s[here, :] = gproj
        add_sum(0, gproj.astype(F32))
        gctx = dot_last(gproj, wo_ref[...]).astype(BF16)
        gctx_ref[here, :] = gctx
        product = gctx[:, :A].astype(F32) * attn
        high = product.astype(BF16)
        rest = (product - high.astype(F32)).astype(BF16)
        stat = lse_ref[here, :] + dot(high, head_pick) + dot(rest, head_pick)
        stat_ref[here, :] = stat
        return 0

    lax.fori_loop(0, rows // tm, tile, 0)
    statt_ref[...] = stat_ref[...].T[:16]
    for g in range(NG):
        for half in range(2):
            whole = slice(wide * g + D * half, wide * g + D * half + D)
            grad = dot_first(low_s[:, part * g : part * g + part], gpre_s[:, whole]).astype(BF16)
            r0 = 96 * (2 * g + half)
            for k in range(4):
                pack_ref[k, r0 : r0 + 96, :] = grad[96 * k : 96 * k + 96]
        for k in range(4):
            grad = dot_first(
                act_s[:, wide * g + A * k : wide * g + A * k + A], gfl_s[:, part * g : part * g + part]
            )
            pack_ref[k, FI_ROWS : FI_ROWS + FO_ROWS, part * g : part * g + part] = grad.astype(BF16)
    grad = dot_first(ctx_s[...], gproj_s[...]).astype(BF16)
    r0 = FI_ROWS + FO_ROWS
    for k in range(4):
        pack_ref[k, r0 : r0 + OW_ROWS, :] = grad[OW_ROWS * k : OW_ROWS * k + OW_ROWS]
        pack_ref[k, r0 + OW_ROWS :, :] = jnp.zeros((FIRST_PACK - r0 - OW_ROWS, D), BF16)


def layer(bounds, attn, lse, conv, ext, target, wo, fi, fo, vectors, fb):
    rows = attn.shape[0]
    tm = min(256, rows)
    vmem = pl.BlockSpec(memory_space=pltpu.VMEM)
    return pl.pallas_call(
        layer_body,
        out_shape=[
            jax.ShapeDtypeStruct((rows, D), BF16),
            jax.ShapeDtypeStruct((rows, D), F32),
            jax.ShapeDtypeStruct((rows, D), BF16),
            jax.ShapeDtypeStruct((rows, 128), F32),
            jax.ShapeDtypeStruct((16, rows), F32),
            jax.ShapeDtypeStruct((8, D), F32),
            jax.ShapeDtypeStruct((4, D), F32),
            jax.ShapeDtypeStruct((4, FIRST_PACK, D), BF16),
        ],
        in_specs=[pl.BlockSpec(memory_space=pltpu.SMEM)] + [vmem] * 10,
        out_specs=[vmem] * 8,
        scratch_shapes=[
            pltpu.VMEM((rows, D), BF16),
            pltpu.VMEM((rows, D), BF16),
            pltpu.VMEM((rows, FF), BF16),
            pltpu.VMEM((tm, FF), F32),
            pltpu.VMEM((rows, D), BF16),
            pltpu.VMEM((rows, FF), BF16),
            pltpu.VMEM((rows, D), BF16),
        ],
        compiler_params=pltpu.CompilerParams(vmem_limit_bytes=VMEM_LIMIT),
        name="layer",
    )(bounds, attn, lse, conv, ext, target, wo, fi, fo, vectors, fb)


TAIL_ROWS = 128


def fetch(sources, targets, sem):
    copies = [
        pltpu.make_async_copy(src, dst, sem.at[i]) for i, (src, dst) in enumerate(zip(sources, targets))
    ]
    for copy in copies:
        copy.start()
    return copies


LATE = 7


def middle_body(
    count, sums, *refs, group_rows, fused
):
    bits, chunks = sums
    (
        bounds, g_ref, stat_ref, res_ref, pack_ref, late0, late1, late2, late3, late4, late5, late6, kw_ref, kb_ref, vec_ref,
        *outs,
    ) = refs
    late = [late0, late1, late2, late3, late4, late5, late6]
    if fused:
        col_ref, query_all, key_all, value_all, dq_ref, *outs = outs
    (
        out_ref, all_ref, dealt_ref, own_ref, gq_ref, gcv_ref, gtc_ref, tail_ref, sums_ref, bsum_ref,
        edge_ref, extf_ref, seg_ref, near_ref, wide_ref, bias_ref, gc_ref, pc_ref, glc_ref, gsp_ref,
        *rest,
    ) = outs
    if fused:
        q_s, k_s, v_s, rep_s, head_sem, *rest = rest
    early_refs, rest = rest[:LATE], rest[LATE:]
    ext_ref, cv_ref, kc_ref, q_ref, cq_ref, sp_ref, pw_ref = early_refs
    mine_ref, late_sem, mine_sem, *rest = rest
    bufs, rest = rest[: 2 + bits], rest[2 + bits :]
    sum_send, sum_recv, local_sem, edge_send, edge_recv, *sems = rest
    p = Place(count)
    core = lax.rem(lax.axis_index("wt"), 2)
    mine_copy = pltpu.make_async_copy(pack_ref.at[:, core], mine_ref, mine_sem)
    mine_copy.start()
    loads = fetch(late, early_refs, late_sem)
    rows = g_ref.shape[0]
    if fused:
        own_rows = pl.ds(pl.multiple_of(p.me * rows, rows), rows)
        loads += fetch([query_all.at[own_rows], key_all, value_all], [q_s, k_s, v_s], head_sem)
    span = rows + RIM
    rim = RIM // 2
    place = p.me
    total = Sum(bits, chunks, pack_ref, bufs, None, sum_send, sum_recv, mine_ref)
    early = rows - 3 * rows // 8
    low = {"ctx": lax.rem(p.me + count - 1, count)}
    high = {"ctx": lax.rem(p.me + 1, count)}
    has_low, has_high = p.me > 0, p.me < count - 1
    greet(p.others() + [(p.me >= 0, target) for target in total.targets[:2]])
    needs = BlockNeeds(p)
    pair = PairPart(p, needs, g_ref.at[early:, :A], lambda j: out_ref.at[j, early:], sems[0], sems[1])
    line = LinePart(p, needs, g_ref.at[:early, :A], lambda j: out_ref.at[j, :early], sems[2], sems[3])
    stats = LinePart(p, needs, stat_ref, lambda j: all_ref.at[j], sems[4], sems[5])
    swap = Swap(p, res_ref, dealt_ref, sems[6], sems[7])

    def to_low():
        return remote(g_ref.at[:RIM, A:], edge_ref.at[1], edge_send.at[0], edge_recv.at[1], low)

    def to_high():
        return remote(g_ref.at[rows - RIM :, A:], edge_ref.at[0], edge_send.at[1], edge_recv.at[0], high)

    def advance(t):
        for c in range(chunks):
            stage = t - c
            if 1 <= stage <= total.stages:
                total.take(stage - 1, c)
                if stage < total.stages:
                    total.start(stage, c)
                else:
                    own_ref[c] = bufs[stage - 1][c]

    @pl.when(has_low)
    def _():
        to_low().start()

    @pl.when(has_high)
    def _():
        to_high().start()

    total.open()
    parts = [stats, line, pair]
    stats.start()
    pair.across()
    line.start()
    pair.along()
    keeps = [
        pltpu.make_async_copy(g_ref.at[:, :A], out_ref.at[p.me], local_sem.at[0]),
        pltpu.make_async_copy(stat_ref, all_ref.at[p.me], local_sem.at[1]),
    ]
    for keep in keeps:
        keep.start()
    mine_copy.wait()
    advance(1)
    tap_weights(kw_ref, kb_ref, wide_ref, bias_ref)
    pair.middle()
    for load in loads:
        load.wait()
    tap_near(bounds, group_rows, seg_ref, near_ref)
    extf_ref[...] = ext_ref[...].astype(F32)

    @pl.when(has_low)
    def _():
        to_low().wait_send()
        to_high().wait_recv()

    @pl.when(has_high)
    def _():
        to_high().wait_send()
        to_low().wait_recv()

    gc_ref[0:rim, :] = jnp.where(place > 0, edge_ref[0].astype(F32)[RIM - rim :], 0.0)
    gc_ref[rim : rim + rows, :] = g_ref[:, A:].astype(F32)
    gc_ref[rim + rows :, :] = jnp.where(place < count - 1, edge_ref[1].astype(F32)[:rim], 0.0)
    blocks = jnp.where(
        lax.div(lax.broadcasted_iota(jnp.int32, (128, 128), 0), HD)
        == lax.div(lax.broadcasted_iota(jnp.int32, (128, 128), 1), HD),
        1.0,
        0.0,
    ).astype(BF16)
    tile = span // 3
    tk = rows // 2
    first_tile = jnp.maximum(p.me - p.window, 0) * 2
    end_tile = jnp.where(p.me < p.valid, jnp.minimum(p.me + p.window + 1, p.valid), 0) * 2

    def query_tile(n):
        k0 = pl.multiple_of((first_tile + n) * tk, tk)
        keys_here = pl.ds(k0, tk)
        q_masks, k_masks = half_masks(rows), half_masks(tk)
        q_seg = seg_of(p.me * rows + lax.broadcasted_iota(jnp.int32, (rows, 1), 0), bounds)
        k_seg = seg_of(k0 + lax.broadcasted_iota(jnp.int32, (1, tk), 1), bounds)
        bias = jnp.where(q_seg == k_seg, 0.0, MASKED)
        for pair_at in range(H // 2):
            cols = slice(128 * pair_at, 128 * pair_at + 128)
            q_pair, g_pair = q_s[:, cols], g_ref[:, cols]
            k_pair, v_pair = k_s[keys_here, cols], v_s[keys_here, cols]
            sofar = jnp.zeros((rows, 128), F32)
            for side in range(2):
                head = 2 * pair_at + side
                scores = dot_last(q_pair * q_masks[side], k_pair) + bias
                prob = jnp.exp(scores - jnp.tile(rep_s[head], (1, tk // 128)))
                back = dot_last(g_pair * q_masks[side], v_pair)
                back = prob * (back - jnp.tile(rep_s[H + head], (1, tk // 128)))
                sofar = sofar + dot(back.astype(BF16), k_pair * k_masks[side])
            dq_ref[:, cols] += sofar

    if fused:
        dq_ref[...] = jnp.zeros(dq_ref.shape, F32)
        for head in range(H):
            rep_s[head] = jnp.broadcast_to(col_ref[:, head : head + 1], (rows, 128))
            rep_s[H + head] = jnp.broadcast_to(col_ref[:, 8 + head : 9 + head], (rows, 128))

    def tap_tile(i):
        t0 = pl.multiple_of(tile * i, 16)
        here = pl.ds(t0, tile)
        kernel = tap_softmax(dot(cq_ref[here, :], wide_ref[...]), bias_ref)
        window = cv_ref[pl.ds(t0, tile + RIM), :]
        grad = gc_ref[here, :]
        inner = []
        mean = 0.0
        for tap in range(KW):
            shift = rim - KW // 2 + tap
            near = wide3(near_ref[tap, here, :])
            product = (grad * window[shift : shift + tile]).astype(BF16)
            terms = jnp.concatenate(
                [dot(product[:, 128 * c : 128 * c + 128], blocks) for c in range(3)], axis=1
            )
            terms = terms * near
            inner.append(terms)
            mean += kernel[tap] * terms
            pc_ref[tap, here, :] = kernel[tap] * near * grad
        picked = 0.0
        for tap in range(KW):
            logit = (kernel[tap] * (inner[tap] - mean)).astype(BF16)
            picked += dot(logit, tap_pick(tap))
        glc_ref[here, :] = picked.astype(BF16)

    def weights_back():
        back = dot_last(glc_ref[...], kw_ref[...])
        query = q_ref[rim : rim + span, :]
        row = lax.broadcasted_iota(jnp.int32, (span, 1), 0)
        own = (row >= rim) & (row < rim + rows)
        grad_kc = (back * query).astype(BF16)
        gsp_ref[...] = dot_last(grad_kc, pw_ref[...])
        gq_ref[...] = (back * kc_ref[...])[rim : rim + rows]
        own_kc = jnp.where(own, grad_kc.astype(F32), 0.0)
        own_logits = jnp.where(own, glc_ref[...].astype(F32), 0.0)
        grad_pw = dot_first(sp_ref[...], own_kc.astype(BF16)).astype(BF16)
        grad_kern = dot_first(cq_ref[...], own_logits.astype(BF16)).astype(BF16)
        for k in range(4):
            for half in range(2):
                r0 = 192 * k + 96 * half
                tail_ref[k, 0:96, A * half : A * half + A] = grad_pw[r0 : r0 + 96]
            for m in range(6):
                r0 = 96 * k + 16 * m
                tail_ref[k, 96:112, 128 * m : 128 * m + 128] = grad_kern[r0 : r0 + 16]
            tail_ref[k, 112:, :] = jnp.zeros((TAIL_ROWS - 112, D), BF16)
        bsum_ref[...] = jnp.zeros(bsum_ref.shape, F32)
        bsum_ref[0:1, :] = jnp.sum(own_kc, axis=0, keepdims=True)
        bsum_ref[1:2, 0:128] = jnp.sum(own_logits, axis=0, keepdims=True)
        sums_ref[...] = jnp.zeros(sums_ref.shape, F32)

    step = 128

    def back_tile(i, _):
        s0 = pl.multiple_of(step * i, step)
        here = pl.ds(s0, step)
        inner = pl.ds(pl.multiple_of(s0 + rim, 8), step)

        def column(c, _):
            cols = pl.ds(pl.multiple_of(128 * c, 128), 128)
            grads = gsp_ref[inner, cols]
            tokens = extf_ref[pl.ds(pl.multiple_of(s0 + rim, 8), step + RIM), cols]
            spread = gsp_ref[pl.ds(s0, step + RIM), cols]
            sofar = 0.0
            for tap in range(KW):
                shift = rim - KW // 2 + tap
                value = near_ref[tap, inner, :] * grads * tokens[shift : shift + step]
                sums_ref[tap : tap + 1, cols] += jnp.sum(value, axis=0, keepdims=True)
                shift = rim + KW // 2 - tap
                moved = near_ref[tap, pl.ds(s0, step + RIM), :] * spread
                sofar += vec_ref[tap : tap + 1, cols] * moved[shift : shift + step]
            gtc_ref[here, cols] = sofar
            return 0

        def narrow(c, _):
            cols = pl.ds(pl.multiple_of(128 * c, 128), 128)
            sofar = 0.0
            for tap in range(KW):
                shift = rim + KW // 2 - tap
                sofar += pc_ref[tap, pl.ds(s0, step + RIM), cols][shift : shift + step]
            gcv_ref[here, cols] = sofar.astype(BF16)
            return 0

        lax.fori_loop(0, 6, column, 0)
        lax.fori_loop(0, 3, narrow, 0)

        return 0

    tap_rounds, back_tiles = 3, rows // step
    rounds = max(tap_rounds + 1 + back_tiles // 2, 7, p.valid if fused else 0)

    def round_of(n, _):
        if fused:

            def one(i, _):
                query_tile(i)
                return 0

            lax.fori_loop(2 * n, jnp.minimum(2 * n + 2, end_tile - first_tile), one, 0)

        @pl.when(n < tap_rounds)
        def _():
            tap_tile(n)

        @pl.when(n == tap_rounds)
        def _():
            weights_back()

        @pl.when((n > tap_rounds) & (n <= tap_rounds + back_tiles // 2))
        def _():
            lax.fori_loop(2 * (n - tap_rounds - 1), 2 * (n - tap_rounds), back_tile, 0)

        for s in range(1, 7):

            @pl.when(n == s - 1)
            def _(s=s):
                if s < min(3, p.length):
                    for part in parts:
                        part.step(s)
                if s == 3:
                    for far in range(3, p.length):
                        for part in parts:
                            part.step(far)
                    swap.start()
                advance(s + 1)

        return 0

    lax.fori_loop(0, rounds, round_of, 0)
    for t in range(8, chunks + total.stages):
        advance(t)
    for keep in keeps:
        keep.wait()
    for part in parts:
        part.finish()
    swap.finish()
    for stage in range(total.stages):
        for c in range(chunks):
            total.sent(stage, c)


def middle(bounds, group_rows, ctx_count, heads, grads, stats, results, pack, *args):
    length = ctx_count // 2
    rows = grads.shape[0]
    span, wide = rows + RIM, rows + 2 * RIM
    bits, chunks, packed_shape, out_shape, bufs = sum_shapes(ctx_count, pack.shape[1], 32)
    vmem = pl.BlockSpec(memory_space=pltpu.VMEM)
    hbm = pl.BlockSpec(memory_space=pl.ANY)
    return pl.pallas_call(
        functools.partial(middle_body, ctx_count, (bits, chunks), group_rows=group_rows, fused=bool(heads)),
        out_shape=([jax.ShapeDtypeStruct((rows, A), F32)] if heads else [])
        + [
            jax.ShapeDtypeStruct((ctx_count, rows, A), grads.dtype),
            jax.ShapeDtypeStruct((ctx_count,) + stats.shape, stats.dtype),
            jax.ShapeDtypeStruct(results.shape, results.dtype),
            jax.ShapeDtypeStruct(out_shape[-3:], BF16),
            jax.ShapeDtypeStruct((rows, A), F32),
            jax.ShapeDtypeStruct((rows, A), BF16),
            jax.ShapeDtypeStruct((rows, D), F32),
            jax.ShapeDtypeStruct((4, TAIL_ROWS, D), BF16),
            jax.ShapeDtypeStruct((16, D), F32),
            jax.ShapeDtypeStruct((8, A), F32),
        ],
        in_specs=[pl.BlockSpec(memory_space=pltpu.SMEM)]
        + [vmem] * 3
        + [hbm] * (1 + LATE)
        + [vmem] * (len(args) - LATE)
        + ([vmem] + [hbm] * 3 if heads else []),
        out_specs=([vmem] if heads else []) + [hbm] * 3 + [vmem] * 7,
        scratch_shapes=[
            pltpu.VMEM((2, RIM, A), BF16),
            pltpu.VMEM((wide, D), F32),
            pltpu.VMEM((wide, 128), jnp.int32),
            pltpu.VMEM((KW, span, 128), F32),
            pltpu.VMEM((A, KW * A), BF16),
            pltpu.VMEM((8, KW * A), F32),
            pltpu.VMEM((span, A), F32),
            pltpu.VMEM((KW, span, A), F32),
            pltpu.VMEM((span, 128), BF16),
            pltpu.VMEM((span, D), F32),
        ]
        + (
            [
                pltpu.VMEM((rows, A), BF16),
                pltpu.VMEM((group_rows, A), BF16),
                pltpu.VMEM((group_rows, A), BF16),
                pltpu.VMEM((2 * H, rows, 128), F32),
                pltpu.SemaphoreType.DMA((3,)),
            ]
            if heads
            else []
        )
        + [pltpu.VMEM(item.shape, item.dtype) for item in args[:LATE]]
        + [
            pltpu.VMEM(packed_shape[1:], BF16),
            pltpu.SemaphoreType.DMA((LATE,)),
            pltpu.SemaphoreType.DMA,
        ]
        + bufs
        + [
            pltpu.SemaphoreType.DMA((2 + bits, chunks)),
            pltpu.SemaphoreType.DMA((2 + bits, chunks)),
            pltpu.SemaphoreType.DMA((2,)),
            pltpu.SemaphoreType.DMA((2,)),
            pltpu.SemaphoreType.DMA((2,)),
        ]
        + part_sems(length) * 3
        + swap_sems(ctx_count),
        compiler_params=pltpu.CompilerParams(
            collective_id=1, has_side_effects=True, vmem_limit_bytes=VMEM_LIMIT
        ),
        name="middle",
    )(bounds, grads, stats, results, pack.reshape(packed_shape), *args, *heads)


def ending_body(count, sums, *refs):
    bits, second_chunks = sums
    (
        dq_ref, dk_ref, dv_ref, gq_ref, gcv_ref, late0, late1, late2, ext_ref, tail_ref, own_ref,
        tap_ref, bsum_ref, layer_ref, ffn_ref,
        first_ref, second_ref, sum_ref, dealt_ref,
        gm_ref, gtok_ref, pack_ref, f_bufs, gtc_ref, gfirst_ref, w_ref, late_sem, *rest,
    ) = refs
    loads = fetch([late0, late1, late2], [gtc_ref, gfirst_ref, w_ref], late_sem)
    bufs, rest = rest[: 2 + bits], rest[2 + bits :]
    first_send, first_recv, second_send, second_recv, f_send, f_recv, keep_sem, swap_send, swap_recv = rest
    p = Place(count)
    rows = gm_ref.shape[0]
    piece = pack_ref.shape[-2]
    first = LinePart(p, AllNeeds(p), own_ref, lambda j: first_ref.at[j], first_send, first_recv)
    second = Sum(bits, second_chunks, pack_ref, bufs, second_ref, second_send, second_recv)
    swap = Swap(p, gtok_ref, dealt_ref, swap_send, swap_recv)
    stages, last = second.stages, second.last
    greet(p.others() + [(p.me >= 0, target) for target in second.targets[:2]])
    first.start()
    keep = pltpu.make_async_copy(own_ref, first_ref.at[p.me], keep_sem)
    keep.start()

    def store(k, r0, value):
        for at in range(0, value.shape[0], piece):
            row = (r0 + at) // piece
            index = []
            rest, c = row // second_chunks, row % second_chunks
            for b in range(bits):
                index.insert(0, rest % 2)
                rest //= 2
            pack_ref[(k // 2, k % 2) + tuple(index) + (c,)] = value[at : at + piece]

    gm_ref[:, :A] = (dq_ref[...] * (HD**-0.5) + gq_ref[...]).astype(BF16)
    gm_ref[:, A : 2 * A] = dk_ref[...].astype(BF16)
    gm_ref[:, 2 * A : 3 * A] = dv_ref[...].astype(BF16)
    gm_ref[:, 3 * A :] = gcv_ref[...]
    for half in range(2):
        grad = dot_first(ext_ref[RIM : RIM + rows, :], gm_ref[:, D * half : D * half + D]).astype(BF16)
        for k in range(4):
            store(k, 192 * half, grad[192 * k : 192 * k + 192])
    for k in range(4):
        store(k, 384, tail_ref[k])
    second.open()
    first.step(1)
    second.across(0, second_chunks)
    f_bufs[0, 0] = jnp.zeros(f_bufs.shape[2:], F32)
    f_bufs[0, 0, 0:KW, :] = tap_ref[0:KW, :]
    f_bufs[0, 0, KW : KW + 7, :] = layer_ref[0:7, :]
    f_bufs[0, 0, 16:20, :] = ffn_ref[...]
    f_bufs[0, 0, 20:21, :A] = jnp.sum(gm_ref[:, :A].astype(F32), axis=0, keepdims=True)
    f_bufs[0, 0, 20:21, A:] = jnp.sum(gm_ref[:, 2 * A : 3 * A].astype(F32), axis=0, keepdims=True)
    f_bufs[0, 0, 21:22, :A] = jnp.sum(gm_ref[:, 3 * A :].astype(F32), axis=0, keepdims=True)
    f_bufs[0, 0, 21:22, A:] = bsum_ref[0:1, :]
    f_bufs[0, 0, 22:23, :A] = bsum_ref[1:2, :]

    def f_copy(stage):
        return remote(
            f_bufs.at[0, stage], f_bufs.at[1, stage], f_send.at[stage], f_recv.at[stage], second.targets[stage]
        )

    f_copy(0).start()
    def advance(t):
        for c in reversed(range(second_chunks)):
            stage = t - c + 1
            if not 2 <= stage <= last:
                continue
            second.take(stage - 1, c)
            if stage == stages:
                second.place_own(c, bufs[stage - 1][c])
            if stage < last:
                second.start(stage, c)
        if t <= stages:
            f_copy(t - 1).wait_recv()
            value = f_bufs[0, t - 1] + f_bufs[1, t - 1]
            if t < stages:
                f_bufs[0, t] = value
                f_copy(t).start()
            else:
                sum_ref[...] = value

    for load in loads:
        load.wait()
    grad = dot_last(gm_ref[...], w_ref[...]) + gfirst_ref[...] + gtc_ref[...]
    size = rows // count
    for j in range(count):
        gtok_ref[j] = grad[size * j : size * j + size].astype(BF16)
    for s in range(2, p.length):
        first.step(s)
        if s == 2:
            advance(1)
    swap.start()
    for t in range(2, second_chunks + last - 1):
        advance(t)
    first.finish()
    keep.wait()
    for stage in range(last):
        for c in range(second_chunks):
            second.sent(stage, c)
    for stage in range(stages):
        f_copy(stage).wait_send()
    swap.finish()


def ending(ctx_count, *args):
    rows = args[0].shape[0]
    bits, second_chunks, packed_shape, second_shape, bufs = sum_shapes(ctx_count, SECOND_PACK, 16)
    vmem = pl.BlockSpec(memory_space=pltpu.VMEM)
    pieces = (ctx_count, rows // ctx_count, D)
    first, second, totals, moved = pl.pallas_call(
        functools.partial(ending_body, ctx_count, (bits, second_chunks)),
        out_shape=[
            jax.ShapeDtypeStruct((ctx_count, FIRST_PACK // ctx_count, D), BF16),
            jax.ShapeDtypeStruct(second_shape, BF16),
            jax.ShapeDtypeStruct((24, D), F32),
            jax.ShapeDtypeStruct(pieces, BF16),
        ],
        in_specs=[vmem] * 5 + [pl.BlockSpec(memory_space=pl.ANY)] * 3 + [vmem] * (len(args) - 8),
        out_specs=[vmem] * 4,
        scratch_shapes=[
            pltpu.VMEM((rows, 4 * A), BF16),
            pltpu.VMEM(pieces, BF16),
            pltpu.VMEM(packed_shape, BF16),
            pltpu.VMEM((2, 2 + bits, 24, D), F32),
        ]
        + [pltpu.VMEM(item.shape, item.dtype) for item in args[5:8]]
        + [pltpu.SemaphoreType.DMA((3,))]
        + bufs
        + part_sems(ctx_count // 2)
        + [
            pltpu.SemaphoreType.DMA((2 + 2 * bits, second_chunks)),
            pltpu.SemaphoreType.DMA((2 + 2 * bits, second_chunks)),
            pltpu.SemaphoreType.DMA((2 + bits,)),
            pltpu.SemaphoreType.DMA((2 + bits,)),
            pltpu.SemaphoreType.DMA,
        ]
        + swap_sems(ctx_count),
        compiler_params=pltpu.CompilerParams(
            collective_id=2, has_side_effects=True, vmem_limit_bytes=VMEM_LIMIT
        ),
        name="ending",
    )(*args)
    return first.reshape(-1, D), second.reshape(-1, D), totals, moved.reshape(rows, D)


def finish_body(
    place, arrange_ref, out_in, tok_in, first_ref, second_ref, sum_ref,
    out_ref, tok_ref, w_ref, b_ref, dw_ref, pw_ref, pb_ref, kern_ref, ow_ref, fi_ref, fb_ref, fo_ref,
    loss_ref, kb_ref, v0_ref, v1_ref, v2_ref, v3_ref, v4_ref, v5_ref, kern_s,
):
    rows = out_ref.shape[0]
    slot = lax.broadcasted_iota(jnp.int32, (rows, rows), 0)
    sort = jnp.where(slot == arrange_ref[...], 1.0, 0.0).astype(BF16)
    out_ref[...] = dot_first(sort, out_in[...]).astype(BF16)
    tok_ref[...] = dot_first(sort, tok_in[...])
    for half in range(2):
        w_ref[:, D * half : D * half + D] = second_ref[192 * half : 192 * half + 192, :].astype(F32)
        pw_ref[96 * half : 96 * half + 96, :] = second_ref[384:480, A * half : A * half + A].astype(F32)
    for m in range(6):
        kern_s[16 * m : 16 * m + 16, :] = second_ref[480:496, 128 * m : 128 * m + 128].astype(F32)
    kern_s[A // 4 :, :] = jnp.zeros((128 - A // 4, 128), F32)
    kern_ref[...] = kern_s[...].T[: H * KW, : A // 4]
    for g in range(NG):
        for half in range(2):
            r0 = 96 * (2 * g + half)
            fi_ref[g, :, D * half : D * half + D] = first_ref[r0 : r0 + 96, :].astype(F32)
        fo_ref[g] = first_ref[384:768, A * g : A * g + A].astype(F32)
    ow_ref[...] = first_ref[768:960, :].astype(F32)
    total = jnp.sum(sum_ref[15:16, :], axis=1, keepdims=True)
    loss_ref[...] = total / (place[SEQS + 5].astype(F32) * D)
    kb_ref[...] = sum_ref[22:23, 0 : H * KW].reshape(H * KW)
    for k in range(4):

        @pl.when(place[SEQS + 4] == k)
        def _(k=k):
            cols = slice(D // 4 * k, D // 4 * k + D // 4)
            dw_ref[...] = sum_ref[0:KW, cols]
            for i, v_ref in enumerate((v0_ref, v1_ref, v2_ref, v3_ref, v4_ref, v5_ref)):
                v_ref[...] = sum_ref[KW + i : KW + i + 1, cols].reshape(D // 4)
            fb_ref[...] = sum_ref[16 + k : 17 + k, :].reshape(D)
            part = slice(A // 4 * k, A // 4 * k + A // 4)
            second = slice(A + A // 4 * k, A + A // 4 * k + A // 4)
            b_ref[0:1, :] = sum_ref[20:21, part]
            b_ref[1:2, :] = sum_ref[20:21, second]
            b_ref[2:3, :] = sum_ref[21:22, part]
            pb_ref[...] = sum_ref[21:22, second].reshape(A // 4)


def finish(place, arrange, *args):
    rows = args[0].shape[0]
    vmem = pl.BlockSpec(memory_space=pltpu.VMEM)
    shapes = [
        (rows, D), (D // 4, 4 * A), (3, A // 4), (KW, D // 4), (D // 4, A), (A // 4,), (H * KW, A // 4),
        (D // 4, D), (NG, A // 4, FF // NG), (D,), (NG, A, A), (1, 1), (H * KW,),
    ] + [(D // 4,)] * 6
    return pl.pallas_call(
        finish_body,
        out_shape=[jax.ShapeDtypeStruct((rows, D), BF16)] + [jax.ShapeDtypeStruct(shape, F32) for shape in shapes],
        in_specs=[pl.BlockSpec(memory_space=pltpu.SMEM)] + [vmem] * (len(args) + 1),
        out_specs=[vmem] * 20,
        scratch_shapes=[pltpu.VMEM((128, 128), F32)],
        compiler_params=pltpu.CompilerParams(vmem_limit_bytes=VMEM_LIMIT),
        name="finish",
    )(place, arrange, *args)


def local(
    hidden,
    teacher,
    lengths,
    deal,
    w_in,
    b_in,
    dw_kernel,
    pw_weight,
    pw_bias,
    kern_weight,
    kern_bias,
    out_weight,
    out_bias,
    norm1_gain,
    norm1_bias,
    ffn_in,
    ffn_in_bias,
    ffn_out,
    ffn_out_bias,
    norm2_gain,
    norm2_bias,
):
    rows = hidden.shape[1]
    ctx_count = lax.axis_size("ctx")
    group_rows = rows * ctx_count
    piece_rows = rows // ctx_count
    sorted_hidden, sorted_teacher, arrange, bounds, *smalls = setup(
        lengths, deal, hidden[0], teacher[0],
        [
            dw_kernel, out_bias, norm1_gain, norm1_bias, ffn_out_bias, norm2_gain, norm2_bias, ffn_in_bias,
            b_in, pw_bias, kern_weight.T,
        ],
        ctx_count,
    )
    pieces_shape = (ctx_count, piece_rows, D)
    kern_b = kern_bias[None]
    fused = group_rows <= 4096
    target, full_w_in, full_pw, full_out_w, full_ffn_in, full_ffn_out, vectors, smalls, ffn_in_b, full_kern, *rest = (
        gather_inputs(
            bounds,
            sorted_hidden,
            sorted_teacher,
            (w_in, pw_weight, out_weight, ffn_in, ffn_out),
            (0, 0, 0, 1, 1),
            smalls,
            kern_b,
            ctx_count,
            fused,
        )
    )
    target = target.reshape(rows, D)
    if fused:
        all_q8, all_keys, all_values = (item.reshape(group_rows, A) for item in rest[:3])
        conv_parts = rest[3:]
    else:
        natural = rest[0].reshape(group_rows, D)
        all_q8, all_keys, all_values = project(bounds, natural, full_w_in, smalls, rows)
        conv_parts = convolve(
            bounds, natural, full_w_in, full_pw, full_kern, kern_b, vectors, smalls, rows
        )
    conv_out, extended, conv_value, key_conv, query_ext, conv_query, spread = conv_parts
    attn_out, lse = attend(bounds, all_q8, all_keys, all_values, rows)
    result, grad_first, grad_context, stats, stats_t, layer_sums, ffn_in_sums, first_pack = layer(
        bounds, attn_out, lse, conv_out, extended, target,
        full_out_w, full_ffn_in, full_ffn_out, vectors, ffn_in_b,
    )
    heads = (stats, all_q8, all_keys, all_values) if fused else ()
    (
        *own_grad, all_grads, all_stats, output, first_own, grad_query_conv, grad_cov, grad_tokens_conv, tail, tap_sums,
        bias_sums,
    ) = middle(
        bounds, group_rows, ctx_count, heads, grad_context, stats_t, result.reshape(pieces_shape), first_pack,
        extended, conv_value, key_conv, query_ext, conv_query, spread, full_pw, full_kern, kern_b, vectors,
    )
    if fused:
        grad_query = own_grad[0]
    else:
        grad_query = query_grads(bounds, all_q8, grad_context, stats, all_keys, all_values)
    grad_keys, grad_values = key_grads(
        bounds, all_keys, all_values, all_q8, all_grads.reshape(group_rows, A), all_stats
    )
    first, second, totals, moved = ending(
        ctx_count, grad_query, grad_keys, grad_values, grad_query_conv, grad_cov, grad_tokens_conv, grad_first,
        full_w_in, extended, tail, first_own.reshape(-1, D), tap_sums, bias_sums, layer_sums, ffn_in_sums,
    )
    (
        dealt_out, dealt_grad, g_w_in, g_b_in, g_dw, g_pw, g_pw_b, g_kern, g_out, g_ffn_in, g_ffn_in_b,
        g_ffn_out, loss, g_kern_b, *g_vec,
    ) = finish(
        bounds, arrange,
        output.reshape(rows, D), moved, first, second, totals,
    )
    return (
        dealt_out[None],
        loss[0, 0],
        dealt_grad[None],
        g_w_in,
        g_b_in,
        g_dw,
        g_pw,
        g_pw_b,
        g_kern.T,
        g_kern_b,
        g_out,
        g_vec[0],
        g_vec[1],
        g_vec[2],
        g_ffn_in,
        g_ffn_in_b,
        g_ffn_out,
        g_vec[3],
        g_vec[4],
        g_vec[5],
    )


def solution(mesh):
    return jax.shard_map(
        local,
        mesh=mesh,
        in_specs=(
            P("wt", "ctx", None),
            P("wt", "ctx", None),
            P(),
            P("wt", None),
            P("wt", None),
            P(None, "wt"),
            P(None, "wt"),
            P("wt", None),
            P("wt"),
            P("wt", None),
            P(),
            P("wt", None),
            P("wt"),
            P("wt"),
            P("wt"),
            P(None, "wt", None),
            P("wt"),
            P(None, "wt", None),
            P("wt"),
            P("wt"),
            P("wt"),
        ),
        out_specs=(
            P("wt", "ctx", None),
            P(),
            P("wt", "ctx", None),
            P("wt", None),
            P(None, "wt"),
            P(None, "wt"),
            P("wt", None),
            P("wt"),
            P("wt", None),
            P(),
            P("wt", None),
            P("wt"),
            P("wt"),
            P("wt"),
            P(None, "wt", None),
            P("wt"),
            P(None, "wt", None),
            P("wt"),
            P("wt"),
            P("wt"),
        ),
        check_vma=False,
    )
```

```python
import functools

import jax
import jax.numpy as jnp
from jax import lax
from jax.experimental import pallas as pl
from jax.experimental.pallas import tpu as pltpu
from jax.sharding import PartitionSpec as P

D = 768
H = 6
HD = 64
FF = 3072
NG = 2
KW = 9
SEQS = 6
A = 384

NORM_EPS = 1e-12
MASKED = -1e30
ROOT_HALF = 0.7071067811865476
DENSITY_NORM = 0.3989422804014327
RIM = 16
MESH = pl.DeviceIdType.MESH
BF16 = jnp.bfloat16
F32 = jnp.float32
VMEM_LIMIT = 60 * 1024 * 1024


def remote(src, dst, send, recv, target):
    return pltpu.make_async_remote_copy(
        src_ref=src,
        dst_ref=dst,
        send_sem=send,
        recv_sem=recv,
        device_id=target,
        device_id_type=MESH,
    )


def greet(peers):
    barrier = pltpu.get_barrier_semaphore()
    total = 0
    for there, target in peers:

        @pl.when(there)
        def _(target=target):
            pl.semaphore_signal(barrier, inc=1, device_id=target, device_id_type=MESH)

        total = total + jnp.where(there, 1, 0)
    pl.semaphore_wait(barrier, total)


class Place:
    def __init__(self, count):
        self.count = count
        self.length = count // 2
        self.valid = count - count // 8
        self.window = count // 2
        self.me = lax.axis_index("ctx")
        self.line = lax.div(self.me, 2)
        self.side = lax.rem(self.me, 2)
        self.mate_index = self.me + 1 - 2 * self.side
        self.mate = {"ctx": self.mate_index}
        self.up = {"ctx": lax.rem(self.me + 2, count)}
        self.down = {"ctx": lax.rem(self.me + count - 2, count)}
        self.has_up = self.line < self.length - 1
        self.has_down = self.line > 0

    def others(self):
        return [
            (self.me >= 0, {"ctx": lax.rem(self.me + shift, self.count)}) for shift in range(1, self.count)
        ]


class PieceNeeds:
    def __init__(self, place, first, last):
        self.place, self.first, self.last = place, first, last

    def at(self, index, source):
        p = self.place
        return (
            (index < p.valid)
            & (self.first <= index + p.window)
            & (self.last >= index - p.window)
        )

    def above(self, line, source):
        p = self.place
        return (2 * line < p.valid) & (self.last >= 2 * line - p.window)

    def below(self, line, source):
        return self.first <= 2 * line + 1 + self.place.window

    def sent(self, source):
        return source >= 0


class BlockNeeds:
    def __init__(self, place):
        self.place = place

    def at(self, index, source):
        p = self.place
        near = (index <= source + p.window) & (index >= source - p.window)
        return near & (index < p.valid) & (source < p.valid)

    def above(self, line, source):
        p = self.place
        return (2 * line < p.valid) & (2 * line <= source + p.window) & (source < p.valid)

    def below(self, line, source):
        p = self.place
        return (2 * line + 1 >= source - p.window) & (source < p.valid)

    def sent(self, source):
        return source < self.place.valid


class AllNeeds:
    def __init__(self, place):
        self.place = place

    def at(self, index, source):
        return source * 0 == 0

    def above(self, line, source):
        return source * 0 == 0

    def below(self, line, source):
        return source * 0 == 0

    def sent(self, source):
        return source * 0 == 0


class Part:
    def __init__(self, place, needs, own, slot, send, recv):
        self.place, self.needs, self.own, self.slot = place, needs, own, slot
        self.send, self.recv = send, recv

    def copy(self, src, source, send, recv, target):
        return remote(src, self.slot(source), self.send.at[send], self.recv.at[recv], target)

    def go_up(self, source):
        p = self.place
        return p.has_up & self.needs.above(p.line + 1, source)

    def go_down(self, source):
        p = self.place
        return p.has_down & self.needs.below(p.line - 1, source)

    def from_below(self, s, source):
        p = self.place
        return (p.line - s >= 0) & self.needs.above(p.line, source)

    def from_above(self, s, source):
        p = self.place
        return (p.line + s < p.length) & self.needs.below(p.line, source)


class LinePart(Part):
    def start(self):
        p = self.place

        @pl.when(self.needs.at(p.mate_index, p.me))
        def _():
            self.copy(self.own, p.me, (2, 0), (2, 0), p.mate).start()

        @pl.when(self.go_up(p.me))
        def _():
            self.copy(self.own, p.me, (0, 0), (0, 1), p.up).start()

        @pl.when(self.go_down(p.me))
        def _():
            self.copy(self.own, p.me, (1, 0), (1, 1), p.down).start()

    def step(self, s):
        p = self.place
        for row, source, there, go, target in (
            (0, p.me - 2 * s, self.from_below, self.go_up, p.up),
            (1, p.me + 2 * s, self.from_above, self.go_down, p.down),
        ):

            @pl.when(there(s, source))
            def _(row=row, source=source, go=go, target=target):
                held = self.slot(source)
                self.copy(held, source, (2 + row, s), (row, s), p.mate).wait_recv()

                @pl.when(go(source))
                def _():
                    self.copy(held, source, (row, s), (row, s + 1), target).start()

                @pl.when(self.needs.at(p.mate_index, source))
                def _():
                    self.copy(held, source, (2 + row, s), (2 + row, s), p.mate).start()

    def finish(self, taken=False):
        p = self.place
        for s in range(p.length):
            for row, source, exists, go, target in (
                (0, p.me - 2 * s, p.line - s >= 0, self.go_up, p.up),
                (1, p.me + 2 * s, p.line + s < p.length, self.go_down, p.down),
            ):
                held = self.slot(source)
                mates = source + 1 - 2 * p.side
                if s > 0 or row == 0:

                    @pl.when(exists & self.needs.at(p.me, mates) & (not taken))
                    def _(row=row, s=s, mates=mates):
                        theirs = self.slot(mates)
                        self.copy(theirs, mates, (2 + row, s), (2 + row, s), p.mate).wait_recv()

                    @pl.when(exists & self.needs.at(p.mate_index, source))
                    def _(row=row, s=s, held=held, source=source):
                        self.copy(held, source, (2 + row, s), (2 + row, s), p.mate).wait_send()

                @pl.when(exists & go(source) & ((s == 0) | self.arrived(row, source)))
                def _(row=row, s=s, held=held, source=source, target=target):
                    self.copy(held, source, (row, s), (row, s + 1), target).wait_send()

    def arrived(self, row, source):
        p = self.place
        return self.needs.above(p.line, source) if row == 0 else self.needs.below(p.line, source)


class PairPart(Part):
    def across(self):
        p = self.place

        @pl.when(self.needs.sent(p.me))
        def _():
            self.copy(self.own, p.me, (4, 0), (4, 0), p.mate).start()

    def along(self):
        p = self.place

        @pl.when(self.go_up(p.me))
        def _():
            self.copy(self.own, p.me, (0, 0), (0, 1), p.up).start()

        @pl.when(self.go_down(p.me))
        def _():
            self.copy(self.own, p.me, (1, 0), (1, 1), p.down).start()

    def middle(self):
        p = self.place
        source = p.mate_index
        held = self.slot(source)

        @pl.when(self.needs.sent(source))
        def _():
            self.copy(held, source, (4, 0), (4, 0), p.mate).wait_recv()

        @pl.when(self.go_up(source))
        def _():
            self.copy(held, source, (2, 0), (2, 1), p.up).start()

        @pl.when(self.go_down(source))
        def _():
            self.copy(held, source, (3, 0), (3, 1), p.down).start()

    def step(self, s):
        p = self.place
        for base, column in ((0, p.me), (2, p.mate_index)):
            for row, source, there, go, target in (
                (0, column - 2 * s, self.from_below, self.go_up, p.up),
                (1, column + 2 * s, self.from_above, self.go_down, p.down),
            ):

                @pl.when(there(s, source))
                def _(row=row + base, source=source, go=go, target=target):
                    held = self.slot(source)
                    self.copy(held, source, (row, s), (row, s), p.mate).wait_recv()

                    @pl.when(go(source))
                    def _():
                        self.copy(held, source, (row, s), (row, s + 1), target).start()

    def finish(self):
        p = self.place

        @pl.when(self.needs.sent(p.me))
        def _():
            self.copy(self.own, p.me, (4, 0), (4, 0), p.mate).wait_send()

        for s in range(p.length):
            for base, column in ((0, p.me), (2, p.mate_index)):
                for row, source, there, go, target in (
                    (0, column - 2 * s, self.from_below, self.go_up, p.up),
                    (1, column + 2 * s, self.from_above, self.go_down, p.down),
                ):
                    passed = there(s, source) if s > 0 else p.me >= 0

                    @pl.when(passed & go(source))
                    def _(row=row + base, s=s, source=source, target=target):
                        held = self.slot(source)
                        self.copy(held, source, (row, s), (row, s + 1), target).wait_send()


class Swap:
    def __init__(self, place, src, dst, send, recv):
        self.place, self.src, self.dst, self.send, self.recv = place, src, dst, send, recv

    def copy(self, shift):
        p = self.place
        there = lax.rem(p.me + shift, p.count)
        return remote(
            self.src.at[there], self.dst.at[p.me], self.send.at[shift], self.recv.at[shift], {"ctx": there}
        )

    def keep(self):
        p = self.place
        return pltpu.make_async_copy(self.src.at[p.me], self.dst.at[p.me], self.send.at[0])

    def start(self):
        for shift in range(1, self.place.count):
            self.copy(shift).start()
        self.keep().start()

    def finish(self):
        p = self.place
        self.keep().wait()
        for shift in range(1, p.count):
            self.copy(shift).wait_send()
            source = lax.rem(p.me + p.count - shift, p.count)
            held = self.dst.at[source]
            remote(held, held, self.send.at[shift], self.recv.at[shift], p.mate).wait_recv()


def part_sems(length):
    return [
        pltpu.SemaphoreType.DMA((5, length + 1)),
        pltpu.SemaphoreType.DMA((5, length + 1)),
    ]


def swap_sems(count):
    return [pltpu.SemaphoreType.DMA((count,)), pltpu.SemaphoreType.DMA((count,))]


def dot(left, right):
    return jnp.dot(left, right, preferred_element_type=F32)


def setup_body(
    lengths, deal_ref, x_ref, t_ref, dw_ref, *refs
):
    rows_in, refs = refs[:6], refs[6:]
    fb_in, b_in, pb_in, kern_in = refs[:4]
    sx_ref, st_ref, arrange_ref, bounds, wide, narrow, ffn, kern, kern_s = refs[4:]
    count, piece = sx_ref.shape[:2]
    rows = count * piece
    group = lax.axis_index("wt")
    place = lax.axis_index("ctx")
    start = place * rows
    end = jnp.int32(0)
    total = jnp.int32(0)
    first, last = jnp.int32(0), jnp.int32(rows * count)
    ends = []
    for i in range(SEQS):
        end = end + lengths[group, i]
        ends.append(end)
        bounds[i] = end
        for g in range(4):
            total = total + lengths[g, i]
    for i in range(SEQS):
        first = jnp.where(ends[i] <= start, ends[i], first)
    for i in reversed(range(SEQS)):
        last = jnp.where(ends[i] >= start + rows, ends[i], last)
    bounds[SEQS] = start
    bounds[SEQS + 1] = lax.div(first, rows)
    bounds[SEQS + 2] = lax.div(last - 1, rows)
    bounds[SEQS + 3] = place
    bounds[SEQS + 4] = group
    bounds[SEQS + 5] = total
    slots = deal_ref[0:1, pl.ds(pl.multiple_of(start, 128), rows)]
    block = lax.div(slots, rows)
    arrange = block * piece + (slots - block * rows) - place * piece
    arrange_ref[...] = arrange
    sort = jnp.where(lax.broadcasted_iota(jnp.int32, (rows, rows), 0) == arrange, 1.0, 0.0).astype(BF16)
    for src, dst in ((x_ref, sx_ref), (t_ref, st_ref)):
        moved = dot(sort, src[...]).astype(BF16)
        for j in range(count):
            dst[j] = moved[piece * j : piece * j + piece]
    wide[...] = jnp.zeros(wide.shape, F32)
    wide[0:KW, :] = dw_ref[...].astype(F32)
    for i, row in enumerate(rows_in):
        wide[KW + i : KW + i + 1, :] = row[...].astype(F32).reshape(1, D // 4)
    narrow[...] = jnp.zeros(narrow.shape, F32)
    narrow[0:3, : A // 4] = b_in[...].astype(F32)
    narrow[3:4, : A // 4] = pb_in[...].astype(F32).reshape(1, A // 4)
    ffn[...] = jnp.zeros(ffn.shape, F32)
    ffn[0:1, :] = fb_in[...].astype(F32).reshape(1, D)
    kern_s[...] = jnp.zeros(kern_s.shape, F32)
    kern_s[: H * KW, : A // 4] = kern_in[...].astype(F32)
    kern[...] = kern_s[...].T[: A // 4]


SMALL_SHAPES = [(16, D // 4), (8, 128), (8, D), (A // 4, 128)]


def setup(lengths, deal, hidden, teacher, smalls, count):
    rows = hidden.shape[0]
    vmem = pl.BlockSpec(memory_space=pltpu.VMEM)
    smem = pl.BlockSpec(memory_space=pltpu.SMEM)
    pieces = jax.ShapeDtypeStruct((count, rows // count, D), BF16)
    return pl.pallas_call(
        setup_body,
        out_shape=[
            pieces,
            pieces,
            jax.ShapeDtypeStruct((1, rows), jnp.int32),
            jax.ShapeDtypeStruct((SEQS + 6,), jnp.int32),
        ]
        + [jax.ShapeDtypeStruct(shape, F32) for shape in SMALL_SHAPES],
        in_specs=[smem] + [vmem] * (3 + len(smalls)),
        out_specs=[vmem] * 3 + [smem] + [vmem] * 4,
        scratch_shapes=[pltpu.VMEM((128, 128), F32)],
        compiler_params=pltpu.CompilerParams(vmem_limit_bytes=VMEM_LIMIT),
        name="setup",
    )(lengths, deal, hidden, teacher, *smalls)


N_SMALL = 4


def gather_body(count, spans, fused, *refs):
    n = len(spans)
    inputs, refs = refs[: n + 4 + N_SMALL], refs[n + 4 + N_SMALL :]
    x_ref, t_ref = inputs[:2]
    shards = list(inputs[2 : 2 + n])
    own_small = list(inputs[2 + n : 2 + n + N_SMALL])
    bounds, kb_ref = inputs[2 + n + N_SMALL :]
    target_ref = refs[0]
    fulls = list(refs[1 : 1 + n])
    vec_ref, small_ref, fb_ref, kw_ref = refs[1 + n : 5 + n]
    refs = refs[5 + n :]
    if fused:
        out_hbm, conv_outs, refs = refs[:3], refs[3:10], refs[10:]
        out_ref, held_out, conv_scratch, project_sem, refs = refs[0], refs[1:4], refs[4:10], refs[10], refs[11:]
    else:
        out_ref, refs = refs[0], refs[1:]
    all_small = refs[:N_SMALL]
    local_sem, w_send, w_recv, pad_send, pad_recv = refs[N_SMALL : N_SMALL + 5]
    sems = refs[N_SMALL + 5 :]
    p = Place(count)
    k = lax.axis_index("wt")
    side = lax.rem(k, 2)
    core_mate = {"wt": k + 1 - 2 * side}
    far = lax.rem(k + 2, 4)
    far_mate = {"wt": far}

    def span(i, ref, index):
        if i >= n:
            return ref.at[index]
        axis, size = spans[i]
        window = pl.ds(pl.multiple_of(index * size, size), size)
        return ref.at[window] if axis == 0 else ref.at[:, window]

    shards += own_small
    fulls += all_small
    total = n + N_SMALL
    order = list(range(n, total)) + list(range(n))

    greet(p.others() + [(k >= 0, core_mate), (k >= 0, far_mate)])
    quarter, eighth = count // 4, count // 8
    cuts = [0, quarter, p.valid - quarter, p.valid - eighth, p.valid]
    parts = []
    for i, kind in enumerate((LinePart, LinePart, PairPart, PairPart)):
        first, end = cuts[i], cuts[i + 1]
        parts.append(
            kind(
                p,
                PieceNeeds(p, first, end - 1),
                x_ref.at[first:end],
                lambda j, first=first, end=end: out_ref.at[first:end, j],
                sems[2 * i],
                sems[2 * i + 1],
            )
        )
    low, high, *pairs = parts
    lines = [high, low]
    for part in pairs:
        part.across()
    for part in lines:
        part.start()
    for part in pairs:
        part.along()
    for i in order:
        held = span(i, fulls[i], k)
        remote(shards[i], held, w_send.at[0, i], w_recv.at[0, i], far_mate).start()
        remote(shards[i], held, w_send.at[1, i], w_recv.at[1, i], core_mate).start()

    def pad_copy(there):
        return remote(
            x_ref.at[p.valid :],
            out_ref.at[p.valid :, p.me],
            pad_send.at[there - p.valid],
            pad_recv.at[p.me],
            {"ctx": p.me * 0 + there},
        )

    def pads():
        for there in range(p.valid, count):

            @pl.when(p.me != there)
            def _(there=there):
                pad_copy(there).start()

    own_copy = pltpu.make_async_copy(x_ref, out_ref.at[:, p.me], local_sem.at[total])
    keeps = [
        pltpu.make_async_copy(shards[i], span(i, fulls[i], k), local_sem.at[i]) for i in range(total)
    ]
    for keep in [own_copy] + keeps:
        keep.start()
    swap = Swap(p, t_ref, target_ref, sems[8], sems[9])

    def relay(i):
        held = span(i, fulls[i], far)
        remote(held, held, w_send.at[2, i], w_recv.at[0, i], core_mate).wait_recv()
        remote(held, held, w_send.at[2, i], w_recv.at[2, i], core_mate).start()

    def whole(i):
        keeps[i].wait()
        held = span(i, fulls[i], k)
        remote(shards[i], held, w_send.at[1, i], w_recv.at[1, i], core_mate).wait_recv()
        remote(held, held, w_send.at[2, i], w_recv.at[2, i], core_mate).wait_recv()

    def spread(ref, step, shape):
        row = lax.broadcasted_iota(jnp.int32, shape, 0)
        column = lax.broadcasted_iota(jnp.int32, shape, 1)
        value = 0.0
        for index in range(4):
            move = jnp.where((column == row + step * index) & (row < step), 1.0, 0.0).astype(BF16)
            value += dot(ref[index].astype(BF16), move)
        return value

    def smalls():
        for i in range(n, total):
            whole(i)
        vec_ref[...] = spread(all_small[0], D // 4, (D // 4, D))
        small_ref[...] = spread(all_small[1], A // 4, (128, A))
        for index in range(4):
            fb_ref[index : index + 1, :] = all_small[2][index, 0:1, :]
            kw_ref[A // 4 * index : A // 4 * index + A // 4, :] = all_small[3][index].astype(BF16)

    def project_rows(x, blocks, sources):
        lead = out_ref[blocks, sources].shape[:-1]
        w_ref = fulls[0]
        query = (dot(x, w_ref[:, :A]) + small_ref[0:1, :]).astype(BF16).astype(F32)
        keys = dot(x, w_ref[:, A : 2 * A])
        values = dot(x, w_ref[:, 2 * A : 3 * A]) + small_ref[1:2, :]
        for value, held in zip((query * (HD**-0.5), keys, values), held_out):
            held[blocks, sources] = value.astype(BF16).reshape(lead + (A,))

    def project_copies(source):
        return [
            pltpu.make_async_copy(
                held_out[i].at[: p.valid, source], out_hbm[i].at[: p.valid, source], project_sem.at[i, source]
            )
            for i in range(3)
        ]

    def project_source(source):
        blocks = slice(0, p.valid)
        project_rows(out_ref[blocks, source].reshape(-1, D), blocks, source)
        for copy in project_copies(source):
            copy.start()

    def pad_copies():
        return [
            pltpu.make_async_copy(held_out[i].at[p.valid :], out_hbm[i].at[p.valid :], project_sem.at[i, 0])
            for i in range(3)
        ]

    def wait_pads():
        for shift in range(1, count):
            source = lax.rem(p.me + shift, count)
            held = out_ref.at[p.valid :, source]
            remote(held, held, pad_send.at[0], pad_recv.at[source], p.mate).wait_recv()

    near_count = 2 * p.length - 1

    def candidate(i):
        mates = lax.div(i, near_count)
        i = i - mates * near_count
        s = lax.div(i + 1, 2)
        odd = lax.rem(i, 2)
        line = p.line + (2 * odd - 1) * s
        source = jnp.where(mates == 1, p.mate_index, p.me) + (2 * odd - 1) * 2 * s

        @pl.when((line >= 0) & (line < p.length) & (p.me < p.valid))
        def _():
            for part in lines:

                @pl.when((mates == 1) & part.needs.at(p.me, source))
                def _(part=part):
                    theirs = part.slot(source)
                    at = (2 + odd, s)
                    part.copy(theirs, source, at, at, p.mate).wait_recv()

            project_source(source)

    def first_candidates(i, _):
        candidate(jnp.where(i < near_count - 2, i, near_count))
        return 0

    def last_candidates(i, _):
        candidate(jnp.where(i < 2, near_count - 2 + i, near_count - 1 + i))
        return 0

    for part in pairs:
        part.middle()
    for s in range(1, p.length - 1):
        for part in lines + pairs:
            part.step(s)
        if s == 1:
            for i in order[: N_SMALL + 1]:
                relay(i)
    swap.start()
    pads()
    smalls()
    whole(0)
    if fused:
        own_copy.wait()
        lax.fori_loop(0, near_count - 1, first_candidates, 0)
    for part in lines + pairs:
        part.step(p.length - 1)
    for i in order[N_SMALL + 1 :]:
        relay(i)
    if fused:
        lax.fori_loop(0, near_count + 1, last_candidates, 0)

        @pl.when(p.me >= p.valid)
        def _():
            wait_pads()
            blocks = slice(p.valid, count)
            project_rows(out_ref[blocks].reshape(-1, D), blocks, slice(0, count))
            for copy in pad_copies():
                copy.start()

        piece = x_ref.shape[1]
        conv_out, ext_ref, cv_ref = conv_outs[:3]
        before = jnp.maximum(p.me - 1, 0)
        after = jnp.minimum(p.me + 1, count - 1)
        ext_ref[0:RIM, :] = out_ref[before, count - 1, piece - RIM :, :]
        for j in range(count):
            ext_ref[RIM + piece * j : RIM + piece * j + piece, :] = out_ref[p.me, j]
        ext_ref[RIM + piece * count :, :] = out_ref[after, 0, :RIM, :]
        whole(1)
        conv_core(
            bounds, count * count * piece, fulls[0], fulls[1], kw_ref, kb_ref, vec_ref, small_ref,
            *conv_outs, *conv_scratch,
        )

        @pl.when(p.me < p.valid)
        def _():
            for source in range(count):
                for copy in project_copies(source):
                    copy.wait()

        @pl.when(p.me >= p.valid)
        def _():
            for copy in pad_copies():
                copy.wait()

    else:
        own_copy.wait()
        whole(1)

        @pl.when(p.me >= p.valid)
        def _():
            wait_pads()

    for i in range(2, n):
        whole(i)
    for i in range(total):
        held = span(i, fulls[i], k)
        remote(shards[i], held, w_send.at[0, i], w_recv.at[0, i], far_mate).wait_send()
        remote(shards[i], held, w_send.at[1, i], w_recv.at[1, i], core_mate).wait_send()
        remote(held, held, w_send.at[2, i], w_recv.at[2, i], core_mate).wait_send()
    for part in pairs:
        part.finish()
    for part in lines:
        part.finish(taken=fused)
    for there in range(p.valid, count):

        @pl.when(p.me != there)
        def _(there=there):
            pad_copy(there).wait_send()

    swap.finish()


def gather_inputs(bounds, pieces, targets, shards, axes, smalls, kern_bias, ctx_count, fused):
    length = ctx_count // 2
    rows = pieces.shape[0] * pieces.shape[1]
    fulls, spans = [], []
    for shard, axis in zip(shards, axes):
        shape = list(shard.shape)
        spans.append((axis, shape[axis]))
        shape[axis] *= 4
        fulls.append(jax.ShapeDtypeStruct(tuple(shape), shard.dtype))
    n = len(shards)
    total = n + N_SMALL
    vmem = pl.BlockSpec(memory_space=pltpu.VMEM)
    hbm = pl.BlockSpec(memory_space=pl.ANY)
    natural = (ctx_count,) + pieces.shape
    heads = (ctx_count,) + pieces.shape[:-1] + (A,)
    outs = (
        [jax.ShapeDtypeStruct(targets.shape, targets.dtype)]
        + fulls
        + [
            jax.ShapeDtypeStruct((16, D), F32),
            jax.ShapeDtypeStruct((8, A), F32),
            jax.ShapeDtypeStruct((4, D), F32),
            jax.ShapeDtypeStruct((A, 128), BF16),
        ]
    )
    specs = [hbm] + [vmem] * 2 + [hbm] * (n - 2) + [vmem] * 4
    scratch = []
    if fused:
        conv_outs, conv_scratch = conv_shapes(rows)
        outs += [jax.ShapeDtypeStruct(heads, BF16)] * 3 + conv_outs
        specs += [hbm] * 3 + [vmem] * 7
        scratch += [pltpu.VMEM(natural, BF16)] + [pltpu.VMEM(heads, BF16)] * 3 + conv_scratch
        scratch += [pltpu.SemaphoreType.DMA((3, ctx_count))]
    else:
        outs.append(jax.ShapeDtypeStruct(natural, BF16))
        specs.append(hbm)
    return pl.pallas_call(
        functools.partial(gather_body, ctx_count, spans, fused),
        out_shape=outs,
        in_specs=[vmem] * (2 + n + len(smalls)) + [pl.BlockSpec(memory_space=pltpu.SMEM), vmem],
        out_specs=specs,
        scratch_shapes=scratch
        + [pltpu.VMEM((4,) + shape, F32) for shape in SMALL_SHAPES]
        + [
            pltpu.SemaphoreType.DMA((total + 1,)),
            pltpu.SemaphoreType.DMA((3, total)),
            pltpu.SemaphoreType.DMA((3, total)),
            pltpu.SemaphoreType.DMA((ctx_count // 8,)),
            pltpu.SemaphoreType.DMA((ctx_count,)),
        ]
        + part_sems(length) * 4
        + swap_sems(ctx_count),
        compiler_params=pltpu.CompilerParams(
            collective_id=0, has_side_effects=True, vmem_limit_bytes=VMEM_LIMIT
        ),
        name="gather_inputs",
    )(pieces, targets, *shards, *smalls, bounds, kern_bias)


class Sum:
    def __init__(self, bits, chunks, packed, bufs, out, send, recv, mine=None):
        self.bits, self.chunks, self.packed, self.bufs, self.out = bits, chunks, packed, bufs, out
        self.mine = mine
        self.send, self.recv = send, recv
        self.stages = 2 + bits
        self.last = self.stages + bits
        k = lax.axis_index("wt")
        me = lax.axis_index("ctx")
        self.core = lax.rem(k, 2)
        self.far = lax.div(k, 2)
        self.bit = [lax.rem(lax.div(me, 1 << b), 2) for b in range(bits)]
        self.targets = [{"wt": k + 1 - 2 * self.core}, {"wt": lax.rem(k + 2, 4)}]
        for b in range(bits):
            self.targets.append({"ctx": me + (1 << b) * (1 - 2 * self.bit[b])})

    def source(self, stage, c, kept):
        whole = slice(None)

        def pick(value):
            return value if kept else 1 - value

        if stage == 0 and kept and self.mine is not None:
            return self.mine.at[(whole,) * (self.bits + 1) + (c,)]
        if stage == 0:
            return self.packed.at[(whole, pick(self.core)) + (whole,) * self.bits + (c,)]
        if stage == 1:
            return self.bufs[0].at[c, pick(self.far)]
        b = stage - 2
        return self.bufs[stage - 1].at[(c,) + (whole,) * (self.bits - b - 1) + (pick(self.bit[b]),)]

    def spread(self, b, c, other):
        index = [self.bit[j] for j in range(b, -1, -1)]
        if other:
            index[0] = 1 - index[0]
        return self.out.at[(slice(None),) * (self.bits - 1 - b) + tuple(index) + (c,)]

    def place_own(self, c, value):
        self.out[tuple(self.bit[j] for j in range(self.bits - 1, -1, -1)) + (c,)] = value

    def copy(self, stage, c):
        if stage < self.stages:
            src, dst, target = self.source(stage, c, False), self.bufs[stage].at[c], self.targets[stage]
        else:
            b = self.bits - 1 - (stage - self.stages)
            src, dst, target = self.spread(b, c, False), self.spread(b, c, False), self.targets[2 + b]
        return remote(src, dst, self.send.at[stage, c], self.recv.at[stage, c], target)

    def start(self, stage, c):
        self.copy(stage, c).start()

    def take(self, stage, c):
        if stage >= self.stages:
            b = self.bits - 1 - (stage - self.stages)
            held = self.spread(b, c, True)
            remote(
                held, held, self.send.at[stage, c], self.recv.at[stage, c], self.targets[2 + b]
            ).wait_recv()
            return
        self.copy(stage, c).wait_recv()
        mine, sums = self.source(stage, c, True), self.bufs[stage].at[c]
        lead = sums.shape[:-2]
        total = 1
        for size in lead:
            total *= size

        def one(at, _):
            index, rest = [], at
            for size in reversed(lead):
                index.append(lax.rem(rest, size))
                rest = lax.div(rest, size)
            index = tuple(reversed(index))
            value = mine[index].astype(F32) + sums[index].astype(F32)
            sums[index] = value.astype(BF16)
            return 0

        if lead:
            lax.fori_loop(0, total, one, 0)
        else:
            sums[...] = (mine[...].astype(F32) + sums[...].astype(F32)).astype(BF16)

    def sent(self, stage, c):
        self.copy(stage, c).wait_send()

    def open(self):
        for c in range(min(4, self.chunks)):
            self.start(0, c)

    def across(self, first, end):
        for c in range(first, min(end, self.chunks)):
            self.take(0, c)
            self.start(1, c)
            if c + 4 < self.chunks:
                self.start(0, c + 4)


def sum_shapes(ctx_count, rows, size):
    bits = ctx_count.bit_length() - 1
    piece = min(size, rows // ctx_count)
    chunks = rows // ctx_count // piece
    twos = (2,) * bits
    bufs = [
        pltpu.VMEM((chunks, 2) + twos + (piece, D), BF16),
        pltpu.VMEM((chunks,) + twos + (piece, D), BF16),
    ]
    for b in range(bits):
        bufs.append(pltpu.VMEM((chunks,) + twos[b + 1 :] + (piece, D), BF16))
    tail = (chunks, piece, D)
    return bits, chunks, (2, 2) + twos + tail, twos + tail, bufs


def seg_of(position, bounds):
    seg = jnp.zeros(position.shape, jnp.int32)
    for i in range(SEQS):
        seg = seg + jnp.where(position >= bounds[i], 1, 0)
    return seg


def reach(bounds, first, last, group_rows):
    begin, end = jnp.int32(0), jnp.int32(group_rows)
    for i in range(SEQS):
        begin = jnp.where(bounds[i] <= first, bounds[i], begin)
    for i in reversed(range(SEQS)):
        end = jnp.where(bounds[i] > last, bounds[i], end)
    return begin, end


def half_masks(rows):
    lane = lax.broadcasted_iota(jnp.int32, (rows, 128), 1)
    low = jnp.where(lane < HD, 1.0, 0.0).astype(BF16)
    return low, (1.0 - low.astype(F32)).astype(BF16)


def dot_last(left, right):
    return lax.dot_general(left, right, (((1,), (1,)), ((), ())), preferred_element_type=F32)


def attend_body(tq, tk, bounds, q_ref, k_ref, v_ref, out_ref, lse_ref, m_ref, acc_ref):
    rows, group_rows = out_ref.shape[0], k_ref.shape[0]
    base = pl.multiple_of(bounds[SEQS], tq)
    q_masks, k_masks = half_masks(tq), half_masks(tk)
    lane = lax.broadcasted_iota(jnp.int32, (tq, 128), 1)
    low = lane < HD

    def tile(qi, _):
        q0 = pl.multiple_of(qi * tq, tq)
        first = pl.multiple_of(base + q0, tq)
        begin, end = reach(bounds, first, first + tq - 1, group_rows)
        q_seg = seg_of(first + lax.broadcasted_iota(jnp.int32, (tq, 1), 0), bounds)
        m_ref[...] = jnp.full(m_ref.shape, MASKED, F32)
        acc_ref[...] = jnp.zeros(acc_ref.shape, F32)

        def step(kt, _):
            k0 = pl.multiple_of(kt * tk, tk)
            k_seg = seg_of(k0 + lax.broadcasted_iota(jnp.int32, (1, tk), 1), bounds)
            bias = jnp.where(q_seg == k_seg, 0.0, MASKED)
            for pair in range(H // 2):
                cols = slice(128 * pair, 128 * pair + 128)
                q_pair = q_ref[pl.ds(first, tq), cols]
                k_pair = k_ref[pl.ds(k0, tk), cols]
                v_pair = v_ref[pl.ds(k0, tk), cols]
                for side in range(2):
                    head = 2 * pair + side
                    scores = dot_last(q_pair * q_masks[side], k_pair) + bias
                    old = m_ref[head]
                    new = jnp.maximum(old, jnp.max(scores, axis=1, keepdims=True))
                    weights = jnp.exp(scores - jnp.tile(new, (1, tk // 128)))
                    v_ones = v_pair * k_masks[side] + k_masks[1 - side]
                    acc_ref[head] = acc_ref[head] * jnp.exp(old - new) + jnp.dot(
                        weights.astype(BF16), v_ones, preferred_element_type=F32
                    )
                    m_ref[head] = new
            return 0

        lax.fori_loop(lax.div(begin, tk), lax.div(end + tk - 1, tk), step, 0)
        lse = jnp.zeros((tq, 128), F32)
        for pair in range(H // 2):
            left, right = acc_ref[2 * pair], acc_ref[2 * pair + 1]
            crossed = jnp.where(low, right, left)
            total = pltpu.roll(crossed, HD, 1)
            out_ref[pl.ds(q0, tq), 128 * pair : 128 * pair + 128] = jnp.where(low, left, right) / total
            lse = jnp.where(lane == 2 * pair, m_ref[2 * pair] + jnp.log(total), lse)
            lse = jnp.where(lane == 2 * pair + 1, m_ref[2 * pair + 1] + jnp.log(crossed), lse)
        lse_ref[pl.ds(q0, tq), :] = lse
        return 0

    lax.fori_loop(0, rows // tq, tile, 0)


def attend(bounds, query, keys, values, rows):
    tq, tk = rows, rows // 2
    return pl.pallas_call(
        functools.partial(attend_body, tq, tk),
        out_shape=[
            jax.ShapeDtypeStruct((rows, A), F32),
            jax.ShapeDtypeStruct((rows, 128), F32),
        ],
        in_specs=[pl.BlockSpec(memory_space=pltpu.SMEM)]
        + [pl.BlockSpec(memory_space=pltpu.VMEM)] * 3,
        out_specs=[pl.BlockSpec(memory_space=pltpu.VMEM)] * 2,
        scratch_shapes=[pltpu.VMEM((H, tq, 128), F32), pltpu.VMEM((H, tq, 128), F32)],
        compiler_params=pltpu.CompilerParams(vmem_limit_bytes=VMEM_LIMIT),
        name="attend",
    )(bounds, query, keys, values)


def query_grads_body(tq, tk, bounds, q_ref, g_ref, stat_ref, k_ref, v_ref, out_ref, rep_ref):
    rows, group_rows = out_ref.shape[0], k_ref.shape[0]
    base = pl.multiple_of(bounds[SEQS], tq)
    q_masks, k_masks = half_masks(tq), half_masks(tk)

    def tile(qi, _):
        q0 = pl.multiple_of(qi * tq, tq)
        first = pl.multiple_of(base + q0, tq)
        begin, end = reach(bounds, first, first + tq - 1, group_rows)
        q_seg = seg_of(first + lax.broadcasted_iota(jnp.int32, (tq, 1), 0), bounds)
        stat = stat_ref[pl.ds(q0, tq), :]
        for head in range(H):
            rep_ref[head] = jnp.broadcast_to(stat[:, head : head + 1], (tq, 128))
            rep_ref[H + head] = jnp.broadcast_to(stat[:, 8 + head : 9 + head], (tq, 128))
        out_ref[pl.ds(q0, tq), :] = jnp.zeros((tq, A), F32)

        def step(kt, _):
            k0 = pl.multiple_of(kt * tk, tk)
            k_seg = seg_of(k0 + lax.broadcasted_iota(jnp.int32, (1, tk), 1), bounds)
            bias = jnp.where(q_seg == k_seg, 0.0, MASKED)
            for pair in range(H // 2):
                cols = slice(128 * pair, 128 * pair + 128)
                q_pair = q_ref[pl.ds(first, tq), cols]
                g_pair = g_ref[pl.ds(q0, tq), cols]
                k_pair = k_ref[pl.ds(k0, tk), cols]
                v_pair = v_ref[pl.ds(k0, tk), cols]
                total = jnp.zeros((tq, 128), F32)
                for side in range(2):
                    head = 2 * pair + side
                    scores = dot_last(q_pair * q_masks[side], k_pair) + bias
                    prob = jnp.exp(scores - jnp.tile(rep_ref[head], (1, tk // 128)))
                    back = dot_last(g_pair * q_masks[side], v_pair)
                    back = prob * (back - jnp.tile(rep_ref[H + head], (1, tk // 128)))
                    total = total + jnp.dot(
                        back.astype(BF16), k_pair * k_masks[side], preferred_element_type=F32
                    )
                out_ref[pl.ds(q0, tq), cols] += total
            return 0

        lax.fori_loop(lax.div(begin, tk), lax.div(end + tk - 1, tk), step, 0)
        return 0

    lax.fori_loop(0, rows // tq, tile, 0)


def query_grads(bounds, query, grads, stats, keys, values):
    rows = grads.shape[0]
    tq, tk = rows, rows // 2
    return pl.pallas_call(
        functools.partial(query_grads_body, tq, tk),
        out_shape=jax.ShapeDtypeStruct((rows, A), F32),
        in_specs=[pl.BlockSpec(memory_space=pltpu.SMEM)]
        + [pl.BlockSpec(memory_space=pltpu.VMEM)] * 5,
        out_specs=pl.BlockSpec(memory_space=pltpu.VMEM),
        scratch_shapes=[pltpu.VMEM((2 * H, tq, 128), F32)],
        compiler_params=pltpu.CompilerParams(vmem_limit_bytes=VMEM_LIMIT),
        name="query_grads",
    )(bounds, query, grads, stats, keys, values)


def key_grads_body(
    tk, bounds, k_all, v_all, q_ref, g_ref, stat_ref, dk_ref, dv_ref, k_ref, v_ref, sem
):
    rows, group_rows = dk_ref.shape[0], q_ref.shape[0]
    own = pl.ds(pl.multiple_of(bounds[SEQS], rows), rows)
    for copy in fetch([k_all.at[own], v_all.at[own]], [k_ref, v_ref], sem):
        copy.wait()
    tq = stat_ref.shape[2]
    base = pl.multiple_of(bounds[SEQS], tk)
    q_masks, k_masks = half_masks(tq), half_masks(tk)

    def tile(ki, _):
        k0 = pl.multiple_of(ki * tk, tk)
        first = pl.multiple_of(base + k0, tk)
        begin, end = reach(bounds, first, first + tk - 1, group_rows)
        k_seg = seg_of(first + lax.broadcasted_iota(jnp.int32, (tk, 1), 0), bounds)
        dk_ref[pl.ds(k0, tk), :] = jnp.zeros((tk, A), F32)
        dv_ref[pl.ds(k0, tk), :] = jnp.zeros((tk, A), F32)

        def step(qt, _):
            q0 = pl.multiple_of(qt * tq, tq)
            q_seg = seg_of(q0 + lax.broadcasted_iota(jnp.int32, (1, tq), 1), bounds)
            bias = jnp.where(k_seg == q_seg, 0.0, MASKED)
            for pair in range(H // 2):
                cols = slice(128 * pair, 128 * pair + 128)
                q_pair = q_ref[pl.ds(q0, tq), cols]
                g_pair = g_ref[pl.ds(q0, tq), cols]
                k_pair = k_ref[pl.ds(k0, tk), cols]
                v_pair = v_ref[pl.ds(k0, tk), cols]
                key_sum = jnp.zeros((tk, 128), F32)
                value_sum = jnp.zeros((tk, 128), F32)
                for side in range(2):
                    head = 2 * pair + side
                    scores = dot_last(k_pair * k_masks[side], q_pair) + bias
                    prob = jnp.exp(scores - stat_ref[qt, head : head + 1, :])
                    value_sum = value_sum + jnp.dot(
                        prob.astype(BF16), g_pair * q_masks[side], preferred_element_type=F32
                    )
                    back = dot_last(v_pair * k_masks[side], g_pair)
                    back = prob * (back - stat_ref[qt, 8 + head : 9 + head, :])
                    key_sum = key_sum + jnp.dot(
                        back.astype(BF16), q_pair * q_masks[side], preferred_element_type=F32
                    )
                dk_ref[pl.ds(k0, tk), cols] += key_sum
                dv_ref[pl.ds(k0, tk), cols] += value_sum
            return 0

        lax.fori_loop(lax.div(begin, tq), lax.div(end + tq - 1, tq), step, 0)
        return 0

    lax.fori_loop(0, rows // tk, tile, 0)


def key_grads(bounds, keys, values, queries, grads, stats):
    rows = stats.shape[2]
    tk = rows
    return pl.pallas_call(
        functools.partial(key_grads_body, tk),
        out_shape=[jax.ShapeDtypeStruct((rows, A), F32)] * 2,
        in_specs=[pl.BlockSpec(memory_space=pltpu.SMEM)]
        + [pl.BlockSpec(memory_space=pl.ANY)] * 2
        + [pl.BlockSpec(memory_space=pltpu.VMEM)] * 3,
        out_specs=[pl.BlockSpec(memory_space=pltpu.VMEM)] * 2,
        scratch_shapes=[pltpu.VMEM((rows, A), BF16)] * 2 + [pltpu.SemaphoreType.DMA((2,))],
        compiler_params=pltpu.CompilerParams(vmem_limit_bytes=VMEM_LIMIT),
        name="key_grads",
    )(bounds, keys, values, queries, grads, stats)


def norm_back(grad_rows, normed, inverse, gain):
    scaled = grad_rows * gain
    return inverse * (
        scaled
        - jnp.mean(scaled, axis=1, keepdims=True)
        - normed * jnp.mean(scaled * normed, axis=1, keepdims=True)
    )


def dot_first(left, right):
    return lax.dot_general(left, right, (((0,), (0,)), ((), ())), preferred_element_type=F32)


def project_body(bounds, x_ref, w_ref, b_ref, q_ref, k_ref, v_ref):
    index = pl.program_id(0)

    @pl.when((index >= bounds[SEQS + 1]) & (index <= bounds[SEQS + 2]))
    def _():
        x = x_ref[...]
        query = (dot(x, w_ref[:, :A]) + b_ref[0:1, :]).astype(BF16).astype(F32)
        q_ref[...] = (query * (HD**-0.5)).astype(BF16)
        k_ref[...] = dot(x, w_ref[:, A : 2 * A]).astype(BF16)
        v_ref[...] = (dot(x, w_ref[:, 2 * A : 3 * A]) + b_ref[1:2, :]).astype(BF16)


def project(bounds, natural, w_in, smalls, rows):
    group_rows = natural.shape[0]

    def block(index, bounds):
        return (jnp.clip(index, bounds[SEQS + 1], bounds[SEQS + 2]), 0)

    def fixed(index, bounds):
        return (0, 0)

    return pl.pallas_call(
        project_body,
        out_shape=[jax.ShapeDtypeStruct((group_rows, A), BF16)] * 3,
        grid_spec=pltpu.PrefetchScalarGridSpec(
            num_scalar_prefetch=1,
            grid=(group_rows // rows,),
            in_specs=[
                pl.BlockSpec((rows, D), block),
                pl.BlockSpec((D, 3 * A), fixed),
                pl.BlockSpec((8, A), fixed),
            ],
            out_specs=[pl.BlockSpec((rows, A), block)] * 3,
        ),
        compiler_params=pltpu.CompilerParams(vmem_limit_bytes=VMEM_LIMIT),
        name="project",
    )(bounds, natural, w_in, smalls)


def tap_lanes(tap):
    row = lax.broadcasted_iota(jnp.int32, (128, A), 0)
    column = lax.broadcasted_iota(jnp.int32, (128, A), 1)
    return jnp.where(row == lax.div(column, HD) * KW + tap, 1.0, 0.0).astype(BF16)


def tap_pick(tap):
    row = lax.broadcasted_iota(jnp.int32, (A, 128), 0)
    column = lax.broadcasted_iota(jnp.int32, (A, 128), 1)
    first = row == lax.div(row, HD) * HD
    return jnp.where(first & (column == lax.div(row, HD) * KW + tap), 1.0, 0.0).astype(BF16)


def tap_weights(kw_ref, kb_ref, wide_ref, bias_ref):
    bias_ref[:, 0:128] = jnp.zeros((8, 128), F32)
    bias_ref[0:1, 0 : H * KW] = kb_ref[...].astype(F32)
    bias = bias_ref[:, 0:128].astype(BF16)
    for tap in range(KW):
        lanes = tap_lanes(tap)
        cols = slice(A * tap, A * tap + A)
        wide_ref[:, cols] = dot(kw_ref[...], lanes).astype(BF16)
        bias_ref[:, cols] = dot(bias, lanes)


def tap_near(bounds, group_rows, seg_ref, near_ref):
    span = near_ref.shape[1]
    start = lax.axis_index("ctx") * (span - RIM)
    position = start - RIM + lax.broadcasted_iota(jnp.int32, seg_ref.shape, 0)
    inside = (position >= 0) & (position < group_rows)
    seg_ref[...] = jnp.where(inside, seg_of(position, bounds), -1)
    seg = seg_ref[RIM // 2 : RIM // 2 + span, :]
    for tap in range(KW):
        shift = RIM // 2 - KW // 2 + tap
        near_ref[tap] = jnp.where((seg_ref[shift : shift + span, :] == seg) & (seg >= 0), 1.0, 0.0)


def tap_softmax(logits, bias_ref):
    parts = [logits[:, A * tap : A * tap + A] + bias_ref[0:1, A * tap : A * tap + A] for tap in range(KW)]
    largest = functools.reduce(jnp.maximum, parts)
    parts = [jnp.exp(part - largest) for part in parts]
    total = 1.0 / functools.reduce(jnp.add, parts)
    return [part * total for part in parts]


def wide3(value):
    return jnp.tile(value, (1, 3))


def conv_body(
    bounds, natural, w_ref, pw_ref, kw_ref, kb_ref, vec_ref, small_ref,
    out_ref, ext_ref, cv_ref, kc_ref, q_ref, cq_ref, sp_ref,
    extf_ref, seg_ref, near_ref, wide_ref, bias_ref, full_ref, sem,
):
    rows, group_rows = out_ref.shape[0], natural.shape[0]
    start = bounds[SEQS]
    copies = [
        pltpu.make_async_copy(
            natural.at[pl.ds(pl.multiple_of(jnp.maximum(start - RIM, 0), RIM), RIM)],
            ext_ref.at[0:RIM],
            sem.at[0],
        ),
        pltpu.make_async_copy(
            natural.at[pl.ds(pl.multiple_of(start, RIM), rows)], ext_ref.at[RIM : RIM + rows], sem.at[1]
        ),
        pltpu.make_async_copy(
            natural.at[pl.ds(pl.multiple_of(jnp.minimum(start + rows, group_rows - RIM), RIM), RIM)],
            ext_ref.at[RIM + rows : 2 * RIM + rows],
            sem.at[2],
        ),
    ]
    for copy in copies:
        copy.start()
    for copy in copies:
        copy.wait()
    conv_core(
        bounds, group_rows, w_ref, pw_ref, kw_ref, kb_ref, vec_ref, small_ref,
        out_ref, ext_ref, cv_ref, kc_ref, q_ref, cq_ref, sp_ref,
        extf_ref, seg_ref, near_ref, wide_ref, bias_ref, full_ref,
    )


def conv_core(
    bounds, group_rows, w_ref, pw_ref, kw_ref, kb_ref, vec_ref, small_ref,
    out_ref, ext_ref, cv_ref, kc_ref, q_ref, cq_ref, sp_ref,
    extf_ref, seg_ref, near_ref, wide_ref, bias_ref, full_ref,
):
    rows = out_ref.shape[0]
    span = rows + RIM
    tap_weights(kw_ref, kb_ref, wide_ref, bias_ref)
    tap_near(bounds, group_rows, seg_ref, near_ref)
    count = group_rows // rows
    place = lax.axis_index("ctx")
    padded = count - count // 8

    @pl.when((place == 0) | (place == padded))
    def _():
        ext_ref[0:RIM, :] = jnp.zeros((RIM, D), BF16)

    @pl.when((place == padded - 1) | (place == count - 1))
    def _():
        ext_ref[RIM + rows :, :] = jnp.zeros((RIM, D), BF16)

    ext = ext_ref[...]
    extf_ref[...] = ext.astype(F32)
    cv_ref[...] = dot(ext, w_ref[:, 3 * A :]) + small_ref[2:3, :]
    q_ref[...] = (dot(ext, w_ref[:, :A]) + small_ref[0:1, :]).astype(BF16).astype(F32)
    tile = span // 3

    def spread_tile(i, _):
        t0 = pl.multiple_of(tile * i, 16)
        here = pl.ds(t0, tile)

        def column(c, _):
            cols = pl.ds(pl.multiple_of(128 * c, 128), 128)
            window = extf_ref[pl.ds(t0, tile + RIM), cols]
            total = 0.0
            for tap in range(KW):
                shift = RIM // 2 - KW // 2 + tap
                total += vec_ref[tap : tap + 1, cols] * near_ref[tap, here, :] * window[shift : shift + tile]
            sp_ref[here, cols] = total.astype(BF16)
            return 0

        return lax.fori_loop(0, 6, column, 0)

    lax.fori_loop(0, 3, spread_tile, 0)
    kc_ref[...] = dot(sp_ref[...], pw_ref[...]) + small_ref[3:4, :]
    cq_ref[...] = (kc_ref[...] * q_ref[RIM // 2 : RIM // 2 + span, :]).astype(BF16)

    def mix_tile(i, _):
        t0 = pl.multiple_of(tile * i, 16)
        here = pl.ds(t0, tile)
        kernel = tap_softmax(dot(cq_ref[here, :], wide_ref[...]), bias_ref)
        window = cv_ref[pl.ds(t0, tile + RIM), :]
        total = 0.0
        for tap in range(KW):
            shift = RIM // 2 - KW // 2 + tap
            total += kernel[tap] * wide3(near_ref[tap, here, :]) * window[shift : shift + tile]
        full_ref[here, :] = total
        return 0

    lax.fori_loop(0, 3, mix_tile, 0)
    out_ref[...] = full_ref[RIM // 2 : RIM // 2 + rows, :].astype(BF16)


def conv_shapes(rows):
    span, wide = rows + RIM, rows + 2 * RIM
    outs = [
        jax.ShapeDtypeStruct((rows, A), BF16),
        jax.ShapeDtypeStruct((wide, D), BF16),
        jax.ShapeDtypeStruct((wide, A), F32),
        jax.ShapeDtypeStruct((span, A), F32),
        jax.ShapeDtypeStruct((wide, A), F32),
        jax.ShapeDtypeStruct((span, A), BF16),
        jax.ShapeDtypeStruct((span, D), BF16),
    ]
    scratch = [
        pltpu.VMEM((wide, D), F32),
        pltpu.VMEM((wide, 128), jnp.int32),
        pltpu.VMEM((KW, span, 128), F32),
        pltpu.VMEM((A, KW * A), BF16),
        pltpu.VMEM((8, KW * A), F32),
        pltpu.VMEM((span, A), F32),
    ]
    return outs, scratch


def convolve(bounds, natural, w_in, pw, kw, kb, vectors, smalls, rows):
    outs, scratch = conv_shapes(rows)
    vmem = pl.BlockSpec(memory_space=pltpu.VMEM)
    return pl.pallas_call(
        conv_body,
        out_shape=outs,
        in_specs=[pl.BlockSpec(memory_space=pltpu.SMEM), pl.BlockSpec(memory_space=pl.ANY)] + [vmem] * 6,
        out_specs=[vmem] * 7,
        scratch_shapes=scratch + [pltpu.SemaphoreType.DMA((3,))],
        compiler_params=pltpu.CompilerParams(vmem_limit_bytes=VMEM_LIMIT),
        name="convolve",
    )(bounds, natural, w_in, pw, kw, kb, vectors, smalls)


def norm_rows(x, gain, bias):
    centered = x - jnp.mean(x, axis=1, keepdims=True)
    inverse = lax.rsqrt(jnp.mean(centered * centered, axis=1, keepdims=True) + NORM_EPS)
    normed = centered * inverse
    return normed * gain + bias, normed, inverse


ROW_OUT_B, ROW_GAIN1, ROW_BIAS1, ROW_FFN_B, ROW_GAIN2, ROW_BIAS2 = range(KW, KW + 6)
FI_ROWS, FO_ROWS, OW_ROWS = 384, 384, 192
FIRST_PACK = 1024
SECOND_PACK = 512


def layer_body(
    bounds, attn_ref, lse_ref, conv_ref, ext_ref, tgt_ref, wo_ref, fi_ref, fo_ref, vec_ref, fb_ref,
    out_ref, gfirst_ref, gctx_ref, stat_ref, statt_ref, sums_ref, fbs_ref, pack_ref,
    ctx_s, low_s, act_s, slope_s, gfl_s, gpre_s, gproj_s,
):
    rows = out_ref.shape[0]
    tm = slope_s.shape[0]
    chunk = D
    wide = FF // NG
    part = D // NG
    row_of = lax.broadcasted_iota(jnp.int32, (A, 128), 0)
    column_of = lax.broadcasted_iota(jnp.int32, (A, 128), 1)
    head_pick = jnp.where(column_of == 8 + lax.div(row_of, HD), 1.0, 0.0).astype(BF16)
    sums_ref[...] = jnp.zeros(sums_ref.shape, F32)
    fbs_ref[...] = jnp.zeros(fbs_ref.shape, F32)

    def vec(row):
        return vec_ref[row : row + 1, :]

    def add_sum(row, value):
        sums_ref[row : row + 1, :] += jnp.sum(value, axis=0, keepdims=True)

    def tile(index, _):
        r0 = pl.multiple_of(index * tm, tm)
        here = pl.ds(r0, tm)
        attn = attn_ref[here, :]
        ctx_s[here, :A] = attn.astype(BF16)
        ctx_s[here, A:] = conv_ref[here, :]
        tokens = ext_ref[pl.ds(pl.multiple_of(r0 + RIM, RIM), tm), :].astype(F32)
        first = tokens + dot(ctx_s[here, :], wo_ref[...]) + vec(ROW_OUT_B)
        after, normed_one, inverse_one = norm_rows(first, vec(ROW_GAIN1), vec(ROW_BIAS1))
        low_s[here, :] = after.astype(BF16)
        results = []
        for g in range(NG):
            low = low_s[here, part * g : part * g + part]
            total = 0.0
            for c in range(wide // chunk):
                span = slice(chunk * c, chunk * c + chunk)
                whole = slice(wide * g + chunk * c, wide * g + chunk * c + chunk)
                pre = dot(low, fi_ref[g, :, span]) + fb_ref[2 * g + c : 2 * g + c + 1, :]
                phi = 0.5 * (1.0 + lax.erf(pre * ROOT_HALF))
                act = (pre * phi).astype(BF16)
                act_s[here, whole] = act
                slope_s[:, whole] = phi + pre * DENSITY_NORM * jnp.exp(-0.5 * pre * pre)
                total += dot(act, fo_ref[g, span, :])
            results.append(total)
        second = after + jnp.concatenate(results, axis=1) + vec(ROW_FFN_B)
        result, normed_two, inverse_two = norm_rows(second, vec(ROW_GAIN2), vec(ROW_BIAS2))
        out_ref[here, :] = result.astype(BF16)
        seg = seg_of(bounds[SEQS] + r0 + lax.broadcasted_iota(jnp.int32, (tm, 1), 0), bounds)
        error = jnp.where(seg < SEQS, result - tgt_ref[here, :].astype(F32), 0.0)
        add_sum(6, error * error)
        add_sum(4, error * normed_two)
        add_sum(5, error)
        grad_second = norm_back(error, normed_two, inverse_two, vec(ROW_GAIN2))
        gfl = grad_second.astype(BF16)
        gfl_s[here, :] = gfl
        add_sum(3, gfl.astype(F32))
        grads = []
        for g in range(NG):
            total = 0.0
            for c in range(wide // chunk):
                span = slice(chunk * c, chunk * c + chunk)
                whole = slice(wide * g + chunk * c, wide * g + chunk * c + chunk)
                gact = dot_last(gfl_s[here, part * g : part * g + part], fo_ref[g, span, :])
                gpre = (gact * slope_s[:, whole]).astype(BF16)
                gpre_s[here, whole] = gpre
                fbs_ref[2 * g + c : 2 * g + c + 1, :] += jnp.sum(gpre.astype(F32), axis=0, keepdims=True)
                total += dot_last(gpre, fi_ref[g, :, span])
            grads.append(total)
        grad_after = jnp.concatenate(grads, axis=1) + grad_second
        add_sum(1, grad_after * normed_one)
        add_sum(2, grad_after)
        grad_first = norm_back(grad_after, normed_one, inverse_one, vec(ROW_GAIN1))
        gfirst_ref[here, :] = grad_first
        gproj = grad_first.astype(BF16)
        gproj_s[here, :] = gproj
        add_sum(0, gproj.astype(F32))
        gctx = dot_last(gproj, wo_ref[...]).astype(BF16)
        gctx_ref[here, :] = gctx
        product = gctx[:, :A].astype(F32) * attn
        high = product.astype(BF16)
        rest = (product - high.astype(F32)).astype(BF16)
        stat = lse_ref[here, :] + dot(high, head_pick) + dot(rest, head_pick)
        stat_ref[here, :] = stat
        return 0

    lax.fori_loop(0, rows // tm, tile, 0)
    statt_ref[...] = stat_ref[...].T[:16]
    for g in range(NG):
        for half in range(2):
            whole = slice(wide * g + D * half, wide * g + D * half + D)
            grad = dot_first(low_s[:, part * g : part * g + part], gpre_s[:, whole]).astype(BF16)
            r0 = 96 * (2 * g + half)
            for k in range(4):
                pack_ref[k, r0 : r0 + 96, :] = grad[96 * k : 96 * k + 96]
        for k in range(4):
            grad = dot_first(
                act_s[:, wide * g + A * k : wide * g + A * k + A], gfl_s[:, part * g : part * g + part]
            )
            pack_ref[k, FI_ROWS : FI_ROWS + FO_ROWS, part * g : part * g + part] = grad.astype(BF16)
    grad = dot_first(ctx_s[...], gproj_s[...]).astype(BF16)
    r0 = FI_ROWS + FO_ROWS
    for k in range(4):
        pack_ref[k, r0 : r0 + OW_ROWS, :] = grad[OW_ROWS * k : OW_ROWS * k + OW_ROWS]
        pack_ref[k, r0 + OW_ROWS :, :] = jnp.zeros((FIRST_PACK - r0 - OW_ROWS, D), BF16)


def layer(bounds, attn, lse, conv, ext, target, wo, fi, fo, vectors, fb):
    rows = attn.shape[0]
    tm = min(256, rows)
    vmem = pl.BlockSpec(memory_space=pltpu.VMEM)
    return pl.pallas_call(
        layer_body,
        out_shape=[
            jax.ShapeDtypeStruct((rows, D), BF16),
            jax.ShapeDtypeStruct((rows, D), F32),
            jax.ShapeDtypeStruct((rows, D), BF16),
            jax.ShapeDtypeStruct((rows, 128), F32),
            jax.ShapeDtypeStruct((16, rows), F32),
            jax.ShapeDtypeStruct((8, D), F32),
            jax.ShapeDtypeStruct((4, D), F32),
            jax.ShapeDtypeStruct((4, FIRST_PACK, D), BF16),
        ],
        in_specs=[pl.BlockSpec(memory_space=pltpu.SMEM)] + [vmem] * 10,
        out_specs=[vmem] * 8,
        scratch_shapes=[
            pltpu.VMEM((rows, D), BF16),
            pltpu.VMEM((rows, D), BF16),
            pltpu.VMEM((rows, FF), BF16),
            pltpu.VMEM((tm, FF), F32),
            pltpu.VMEM((rows, D), BF16),
            pltpu.VMEM((rows, FF), BF16),
            pltpu.VMEM((rows, D), BF16),
        ],
        compiler_params=pltpu.CompilerParams(vmem_limit_bytes=VMEM_LIMIT),
        name="layer",
    )(bounds, attn, lse, conv, ext, target, wo, fi, fo, vectors, fb)


TAIL_ROWS = 128


def fetch(sources, targets, sem):
    copies = [
        pltpu.make_async_copy(src, dst, sem.at[i]) for i, (src, dst) in enumerate(zip(sources, targets))
    ]
    for copy in copies:
        copy.start()
    return copies


LATE = 7


def middle_body(
    count, sums, *refs, group_rows, fused
):
    bits, chunks = sums
    (
        bounds, g_ref, stat_ref, res_ref, pack_ref, late0, late1, late2, late3, late4, late5, late6, kw_ref, kb_ref, vec_ref,
        *outs,
    ) = refs
    late = [late0, late1, late2, late3, late4, late5, late6]
    if fused:
        col_ref, query_all, key_all, value_all, dq_ref, *outs = outs
    (
        out_ref, all_ref, dealt_ref, own_ref, gq_ref, gcv_ref, gtc_ref, tail_ref, sums_ref, bsum_ref,
        edge_ref, extf_ref, seg_ref, near_ref, wide_ref, bias_ref, gc_ref, pc_ref, glc_ref, gsp_ref,
        *rest,
    ) = outs
    if fused:
        q_s, k_s, v_s, rep_s, head_sem, *rest = rest
    early_refs, rest = rest[:LATE], rest[LATE:]
    ext_ref, cv_ref, kc_ref, q_ref, cq_ref, sp_ref, pw_ref = early_refs
    mine_ref, late_sem, mine_sem, *rest = rest
    bufs, rest = rest[: 2 + bits], rest[2 + bits :]
    sum_send, sum_recv, local_sem, edge_send, edge_recv, *sems = rest
    p = Place(count)
    core = lax.rem(lax.axis_index("wt"), 2)
    mine_copy = pltpu.make_async_copy(pack_ref.at[:, core], mine_ref, mine_sem)
    mine_copy.start()
    loads = fetch(late, early_refs, late_sem)
    rows = g_ref.shape[0]
    if fused:
        own_rows = pl.ds(pl.multiple_of(p.me * rows, rows), rows)
        loads += fetch([query_all.at[own_rows], key_all, value_all], [q_s, k_s, v_s], head_sem)
    span = rows + RIM
    rim = RIM // 2
    place = p.me
    total = Sum(bits, chunks, pack_ref, bufs, None, sum_send, sum_recv, mine_ref)
    early = rows - 3 * rows // 8
    low = {"ctx": lax.rem(p.me + count - 1, count)}
    high = {"ctx": lax.rem(p.me + 1, count)}
    has_low, has_high = p.me > 0, p.me < count - 1
    greet(p.others() + [(p.me >= 0, target) for target in total.targets[:2]])
    needs = BlockNeeds(p)
    pair = PairPart(p, needs, g_ref.at[early:, :A], lambda j: out_ref.at[j, early:], sems[0], sems[1])
    line = LinePart(p, needs, g_ref.at[:early, :A], lambda j: out_ref.at[j, :early], sems[2], sems[3])
    stats = LinePart(p, needs, stat_ref, lambda j: all_ref.at[j], sems[4], sems[5])
    swap = Swap(p, res_ref, dealt_ref, sems[6], sems[7])

    def to_low():
        return remote(g_ref.at[:RIM, A:], edge_ref.at[1], edge_send.at[0], edge_recv.at[1], low)

    def to_high():
        return remote(g_ref.at[rows - RIM :, A:], edge_ref.at[0], edge_send.at[1], edge_recv.at[0], high)

    def advance(t):
        for c in range(chunks):
            stage = t - c
            if 1 <= stage <= total.stages:
                total.take(stage - 1, c)
                if stage < total.stages:
                    total.start(stage, c)
                else:
                    own_ref[c] = bufs[stage - 1][c]

    @pl.when(has_low)
    def _():
        to_low().start()

    @pl.when(has_high)
    def _():
        to_high().start()

    total.open()
    parts = [stats, line, pair]
    stats.start()
    pair.across()
    line.start()
    pair.along()
    keeps = [
        pltpu.make_async_copy(g_ref.at[:, :A], out_ref.at[p.me], local_sem.at[0]),
        pltpu.make_async_copy(stat_ref, all_ref.at[p.me], local_sem.at[1]),
    ]
    for keep in keeps:
        keep.start()
    mine_copy.wait()
    advance(1)
    tap_weights(kw_ref, kb_ref, wide_ref, bias_ref)
    pair.middle()
    for load in loads:
        load.wait()
    tap_near(bounds, group_rows, seg_ref, near_ref)
    extf_ref[...] = ext_ref[...].astype(F32)

    @pl.when(has_low)
    def _():
        to_low().wait_send()
        to_high().wait_recv()

    @pl.when(has_high)
    def _():
        to_high().wait_send()
        to_low().wait_recv()

    gc_ref[0:rim, :] = jnp.where(place > 0, edge_ref[0].astype(F32)[RIM - rim :], 0.0)
    gc_ref[rim : rim + rows, :] = g_ref[:, A:].astype(F32)
    gc_ref[rim + rows :, :] = jnp.where(place < count - 1, edge_ref[1].astype(F32)[:rim], 0.0)
    blocks = jnp.where(
        lax.div(lax.broadcasted_iota(jnp.int32, (128, 128), 0), HD)
        == lax.div(lax.broadcasted_iota(jnp.int32, (128, 128), 1), HD),
        1.0,
        0.0,
    ).astype(BF16)
    tile = span // 3
    tk = rows // 2
    first_tile = jnp.maximum(p.me - p.window, 0) * 2
    end_tile = jnp.where(p.me < p.valid, jnp.minimum(p.me + p.window + 1, p.valid), 0) * 2

    def query_tile(n):
        k0 = pl.multiple_of((first_tile + n) * tk, tk)
        keys_here = pl.ds(k0, tk)
        q_masks, k_masks = half_masks(rows), half_masks(tk)
        q_seg = seg_of(p.me * rows + lax.broadcasted_iota(jnp.int32, (rows, 1), 0), bounds)
        k_seg = seg_of(k0 + lax.broadcasted_iota(jnp.int32, (1, tk), 1), bounds)
        bias = jnp.where(q_seg == k_seg, 0.0, MASKED)
        for pair_at in range(H // 2):
            cols = slice(128 * pair_at, 128 * pair_at + 128)
            q_pair, g_pair = q_s[:, cols], g_ref[:, cols]
            k_pair, v_pair = k_s[keys_here, cols], v_s[keys_here, cols]
            sofar = jnp.zeros((rows, 128), F32)
            for side in range(2):
                head = 2 * pair_at + side
                scores = dot_last(q_pair * q_masks[side], k_pair) + bias
                prob = jnp.exp(scores - jnp.tile(rep_s[head], (1, tk // 128)))
                back = dot_last(g_pair * q_masks[side], v_pair)
                back = prob * (back - jnp.tile(rep_s[H + head], (1, tk // 128)))
                sofar = sofar + dot(back.astype(BF16), k_pair * k_masks[side])
            dq_ref[:, cols] += sofar

    if fused:
        dq_ref[...] = jnp.zeros(dq_ref.shape, F32)
        for head in range(H):
            rep_s[head] = jnp.broadcast_to(col_ref[:, head : head + 1], (rows, 128))
            rep_s[H + head] = jnp.broadcast_to(col_ref[:, 8 + head : 9 + head], (rows, 128))

    def tap_tile(i):
        t0 = pl.multiple_of(tile * i, 16)
        here = pl.ds(t0, tile)
        kernel = tap_softmax(dot(cq_ref[here, :], wide_ref[...]), bias_ref)
        window = cv_ref[pl.ds(t0, tile + RIM), :]
        grad = gc_ref[here, :]
        inner = []
        mean = 0.0
        for tap in range(KW):
            shift = rim - KW // 2 + tap
            near = wide3(near_ref[tap, here, :])
            product = (grad * window[shift : shift + tile]).astype(BF16)
            terms = jnp.concatenate(
                [dot(product[:, 128 * c : 128 * c + 128], blocks) for c in range(3)], axis=1
            )
            terms = terms * near
            inner.append(terms)
            mean += kernel[tap] * terms
            pc_ref[tap, here, :] = kernel[tap] * near * grad
        picked = 0.0
        for tap in range(KW):
            logit = (kernel[tap] * (inner[tap] - mean)).astype(BF16)
            picked += dot(logit, tap_pick(tap))
        glc_ref[here, :] = picked.astype(BF16)

    def weights_back():
        back = dot_last(glc_ref[...], kw_ref[...])
        query = q_ref[rim : rim + span, :]
        row = lax.broadcasted_iota(jnp.int32, (span, 1), 0)
        own = (row >= rim) & (row < rim + rows)
        grad_kc = (back * query).astype(BF16)
        gsp_ref[...] = dot_last(grad_kc, pw_ref[...])
        gq_ref[...] = (back * kc_ref[...])[rim : rim + rows]
        own_kc = jnp.where(own, grad_kc.astype(F32), 0.0)
        own_logits = jnp.where(own, glc_ref[...].astype(F32), 0.0)
        grad_pw = dot_first(sp_ref[...], own_kc.astype(BF16)).astype(BF16)
        grad_kern = dot_first(cq_ref[...], own_logits.astype(BF16)).astype(BF16)
        for k in range(4):
            for half in range(2):
                r0 = 192 * k + 96 * half
                tail_ref[k, 0:96, A * half : A * half + A] = grad_pw[r0 : r0 + 96]
            for m in range(6):
                r0 = 96 * k + 16 * m
                tail_ref[k, 96:112, 128 * m : 128 * m + 128] = grad_kern[r0 : r0 + 16]
            tail_ref[k, 112:, :] = jnp.zeros((TAIL_ROWS - 112, D), BF16)
        bsum_ref[...] = jnp.zeros(bsum_ref.shape, F32)
        bsum_ref[0:1, :] = jnp.sum(own_kc, axis=0, keepdims=True)
        bsum_ref[1:2, 0:128] = jnp.sum(own_logits, axis=0, keepdims=True)
        sums_ref[...] = jnp.zeros(sums_ref.shape, F32)

    step = 128

    def back_tile(i, _):
        s0 = pl.multiple_of(step * i, step)
        here = pl.ds(s0, step)
        inner = pl.ds(pl.multiple_of(s0 + rim, 8), step)

        def column(c, _):
            cols = pl.ds(pl.multiple_of(128 * c, 128), 128)
            grads = gsp_ref[inner, cols]
            tokens = extf_ref[pl.ds(pl.multiple_of(s0 + rim, 8), step + RIM), cols]
            spread = gsp_ref[pl.ds(s0, step + RIM), cols]
            sofar = 0.0
            for tap in range(KW):
                shift = rim - KW // 2 + tap
                value = near_ref[tap, inner, :] * grads * tokens[shift : shift + step]
                sums_ref[tap : tap + 1, cols] += jnp.sum(value, axis=0, keepdims=True)
                shift = rim + KW // 2 - tap
                moved = near_ref[tap, pl.ds(s0, step + RIM), :] * spread
                sofar += vec_ref[tap : tap + 1, cols] * moved[shift : shift + step]
            gtc_ref[here, cols] = sofar
            return 0

        def narrow(c, _):
            cols = pl.ds(pl.multiple_of(128 * c, 128), 128)
            sofar = 0.0
            for tap in range(KW):
                shift = rim + KW // 2 - tap
                sofar += pc_ref[tap, pl.ds(s0, step + RIM), cols][shift : shift + step]
            gcv_ref[here, cols] = sofar.astype(BF16)
            return 0

        lax.fori_loop(0, 6, column, 0)
        lax.fori_loop(0, 3, narrow, 0)

        return 0

    tap_rounds, back_tiles = 3, rows // step
    rounds = max(tap_rounds + 1 + back_tiles // 2, 7, p.valid if fused else 0)

    def round_of(n, _):
        for s in range(1, 7):

            @pl.when(n == s - 1)
            def _(s=s):
                if s < min(3, p.length):
                    for part in parts:
                        part.step(s)
                if s == 3:
                    for far in range(3, p.length):
                        for part in parts:
                            part.step(far)
                    swap.start()
                advance(s + 1)

        if fused:

            def one(i, _):
                query_tile(i)
                return 0

            lax.fori_loop(2 * n, jnp.minimum(2 * n + 2, end_tile - first_tile), one, 0)

        @pl.when(n < tap_rounds)
        def _():
            tap_tile(n)

        @pl.when(n == tap_rounds)
        def _():
            weights_back()

        @pl.when((n > tap_rounds) & (n <= tap_rounds + back_tiles // 2))
        def _():
            lax.fori_loop(2 * (n - tap_rounds - 1), 2 * (n - tap_rounds), back_tile, 0)

        return 0

    lax.fori_loop(0, rounds, round_of, 0)
    for t in range(8, chunks + total.stages):
        advance(t)
    for keep in keeps:
        keep.wait()
    for part in parts:
        part.finish()
    swap.finish()
    for stage in range(total.stages):
        for c in range(chunks):
            total.sent(stage, c)


def middle(bounds, group_rows, ctx_count, heads, grads, stats, results, pack, *args):
    length = ctx_count // 2
    rows = grads.shape[0]
    span, wide = rows + RIM, rows + 2 * RIM
    bits, chunks, packed_shape, out_shape, bufs = sum_shapes(ctx_count, pack.shape[1], 32)
    vmem = pl.BlockSpec(memory_space=pltpu.VMEM)
    hbm = pl.BlockSpec(memory_space=pl.ANY)
    return pl.pallas_call(
        functools.partial(middle_body, ctx_count, (bits, chunks), group_rows=group_rows, fused=bool(heads)),
        out_shape=([jax.ShapeDtypeStruct((rows, A), F32)] if heads else [])
        + [
            jax.ShapeDtypeStruct((ctx_count, rows, A), grads.dtype),
            jax.ShapeDtypeStruct((ctx_count,) + stats.shape, stats.dtype),
            jax.ShapeDtypeStruct(results.shape, results.dtype),
            jax.ShapeDtypeStruct(out_shape[-3:], BF16),
            jax.ShapeDtypeStruct((rows, A), F32),
            jax.ShapeDtypeStruct((rows, A), BF16),
            jax.ShapeDtypeStruct((rows, D), F32),
            jax.ShapeDtypeStruct((4, TAIL_ROWS, D), BF16),
            jax.ShapeDtypeStruct((16, D), F32),
            jax.ShapeDtypeStruct((8, A), F32),
        ],
        in_specs=[pl.BlockSpec(memory_space=pltpu.SMEM)]
        + [vmem] * 3
        + [hbm] * (1 + LATE)
        + [vmem] * (len(args) - LATE)
        + ([vmem] + [hbm] * 3 if heads else []),
        out_specs=([vmem] if heads else []) + [hbm] * 3 + [vmem] * 7,
        scratch_shapes=[
            pltpu.VMEM((2, RIM, A), BF16),
            pltpu.VMEM((wide, D), F32),
            pltpu.VMEM((wide, 128), jnp.int32),
            pltpu.VMEM((KW, span, 128), F32),
            pltpu.VMEM((A, KW * A), BF16),
            pltpu.VMEM((8, KW * A), F32),
            pltpu.VMEM((span, A), F32),
            pltpu.VMEM((KW, span, A), F32),
            pltpu.VMEM((span, 128), BF16),
            pltpu.VMEM((span, D), F32),
        ]
        + (
            [
                pltpu.VMEM((rows, A), BF16),
                pltpu.VMEM((group_rows, A), BF16),
                pltpu.VMEM((group_rows, A), BF16),
                pltpu.VMEM((2 * H, rows, 128), F32),
                pltpu.SemaphoreType.DMA((3,)),
            ]
            if heads
            else []
        )
        + [pltpu.VMEM(item.shape, item.dtype) for item in args[:LATE]]
        + [
            pltpu.VMEM(packed_shape[1:], BF16),
            pltpu.SemaphoreType.DMA((LATE,)),
            pltpu.SemaphoreType.DMA,
        ]
        + bufs
        + [
            pltpu.SemaphoreType.DMA((2 + bits, chunks)),
            pltpu.SemaphoreType.DMA((2 + bits, chunks)),
            pltpu.SemaphoreType.DMA((2,)),
            pltpu.SemaphoreType.DMA((2,)),
            pltpu.SemaphoreType.DMA((2,)),
        ]
        + part_sems(length) * 3
        + swap_sems(ctx_count),
        compiler_params=pltpu.CompilerParams(
            collective_id=1, has_side_effects=True, vmem_limit_bytes=VMEM_LIMIT
        ),
        name="middle",
    )(bounds, grads, stats, results, pack.reshape(packed_shape), *args, *heads)


def ending_body(count, sums, *refs):
    bits, second_chunks = sums
    (
        dq_ref, dk_ref, dv_ref, gq_ref, gcv_ref, late0, late1, late2, ext_ref, tail_ref, own_ref,
        tap_ref, bsum_ref, layer_ref, ffn_ref,
        first_ref, second_ref, sum_ref, dealt_ref,
        gm_ref, gtok_ref, pack_ref, f_bufs, gtc_ref, gfirst_ref, w_ref, late_sem, *rest,
    ) = refs
    loads = fetch([late0, late1, late2], [gtc_ref, gfirst_ref, w_ref], late_sem)
    bufs, rest = rest[: 2 + bits], rest[2 + bits :]
    first_send, first_recv, second_send, second_recv, f_send, f_recv, keep_sem, swap_send, swap_recv = rest
    p = Place(count)
    rows = gm_ref.shape[0]
    piece = pack_ref.shape[-2]
    first = LinePart(p, AllNeeds(p), own_ref, lambda j: first_ref.at[j], first_send, first_recv)
    second = Sum(bits, second_chunks, pack_ref, bufs, second_ref, second_send, second_recv)
    swap = Swap(p, gtok_ref, dealt_ref, swap_send, swap_recv)
    stages, last = second.stages, second.last
    greet(p.others() + [(p.me >= 0, target) for target in second.targets[:2]])
    first.start()
    keep = pltpu.make_async_copy(own_ref, first_ref.at[p.me], keep_sem)
    keep.start()

    def store(k, r0, value):
        for at in range(0, value.shape[0], piece):
            row = (r0 + at) // piece
            index = []
            rest, c = row // second_chunks, row % second_chunks
            for b in range(bits):
                index.insert(0, rest % 2)
                rest //= 2
            pack_ref[(k // 2, k % 2) + tuple(index) + (c,)] = value[at : at + piece]

    gm_ref[:, :A] = (dq_ref[...] * (HD**-0.5) + gq_ref[...]).astype(BF16)
    gm_ref[:, A : 2 * A] = dk_ref[...].astype(BF16)
    gm_ref[:, 2 * A : 3 * A] = dv_ref[...].astype(BF16)
    gm_ref[:, 3 * A :] = gcv_ref[...]
    for half in range(2):
        grad = dot_first(ext_ref[RIM : RIM + rows, :], gm_ref[:, D * half : D * half + D]).astype(BF16)
        for k in range(4):
            store(k, 192 * half, grad[192 * k : 192 * k + 192])
    for k in range(4):
        store(k, 384, tail_ref[k])
    second.open()
    first.step(1)
    second.across(0, second_chunks)
    f_bufs[0, 0] = jnp.zeros(f_bufs.shape[2:], F32)
    f_bufs[0, 0, 0:KW, :] = tap_ref[0:KW, :]
    f_bufs[0, 0, KW : KW + 7, :] = layer_ref[0:7, :]
    f_bufs[0, 0, 16:20, :] = ffn_ref[...]
    f_bufs[0, 0, 20:21, :A] = jnp.sum(gm_ref[:, :A].astype(F32), axis=0, keepdims=True)
    f_bufs[0, 0, 20:21, A:] = jnp.sum(gm_ref[:, 2 * A : 3 * A].astype(F32), axis=0, keepdims=True)
    f_bufs[0, 0, 21:22, :A] = jnp.sum(gm_ref[:, 3 * A :].astype(F32), axis=0, keepdims=True)
    f_bufs[0, 0, 21:22, A:] = bsum_ref[0:1, :]
    f_bufs[0, 0, 22:23, :A] = bsum_ref[1:2, :]

    def f_copy(stage):
        return remote(
            f_bufs.at[0, stage], f_bufs.at[1, stage], f_send.at[stage], f_recv.at[stage], second.targets[stage]
        )

    f_copy(0).start()
    def advance(t):
        for c in reversed(range(second_chunks)):
            stage = t - c + 1
            if not 2 <= stage <= last:
                continue
            second.take(stage - 1, c)
            if stage == stages:
                second.place_own(c, bufs[stage - 1][c])
            if stage < last:
                second.start(stage, c)
        if t <= stages:
            f_copy(t - 1).wait_recv()
            value = f_bufs[0, t - 1] + f_bufs[1, t - 1]
            if t < stages:
                f_bufs[0, t] = value
                f_copy(t).start()
            else:
                sum_ref[...] = value

    for load in loads:
        load.wait()
    grad = dot_last(gm_ref[...], w_ref[...]) + gfirst_ref[...] + gtc_ref[...]
    size = rows // count
    for j in range(count):
        gtok_ref[j] = grad[size * j : size * j + size].astype(BF16)
    for s in range(2, p.length):
        first.step(s)
        if s == 2:
            advance(1)
    swap.start()
    for t in range(2, second_chunks + last - 1):
        advance(t)
    first.finish()
    keep.wait()
    for stage in range(last):
        for c in range(second_chunks):
            second.sent(stage, c)
    for stage in range(stages):
        f_copy(stage).wait_send()
    swap.finish()


def ending(ctx_count, *args):
    rows = args[0].shape[0]
    bits, second_chunks, packed_shape, second_shape, bufs = sum_shapes(ctx_count, SECOND_PACK, 16)
    vmem = pl.BlockSpec(memory_space=pltpu.VMEM)
    pieces = (ctx_count, rows // ctx_count, D)
    first, second, totals, moved = pl.pallas_call(
        functools.partial(ending_body, ctx_count, (bits, second_chunks)),
        out_shape=[
            jax.ShapeDtypeStruct((ctx_count, FIRST_PACK // ctx_count, D), BF16),
            jax.ShapeDtypeStruct(second_shape, BF16),
            jax.ShapeDtypeStruct((24, D), F32),
            jax.ShapeDtypeStruct(pieces, BF16),
        ],
        in_specs=[vmem] * 5 + [pl.BlockSpec(memory_space=pl.ANY)] * 3 + [vmem] * (len(args) - 8),
        out_specs=[vmem] * 4,
        scratch_shapes=[
            pltpu.VMEM((rows, 4 * A), BF16),
            pltpu.VMEM(pieces, BF16),
            pltpu.VMEM(packed_shape, BF16),
            pltpu.VMEM((2, 2 + bits, 24, D), F32),
        ]
        + [pltpu.VMEM(item.shape, item.dtype) for item in args[5:8]]
        + [pltpu.SemaphoreType.DMA((3,))]
        + bufs
        + part_sems(ctx_count // 2)
        + [
            pltpu.SemaphoreType.DMA((2 + 2 * bits, second_chunks)),
            pltpu.SemaphoreType.DMA((2 + 2 * bits, second_chunks)),
            pltpu.SemaphoreType.DMA((2 + bits,)),
            pltpu.SemaphoreType.DMA((2 + bits,)),
            pltpu.SemaphoreType.DMA,
        ]
        + swap_sems(ctx_count),
        compiler_params=pltpu.CompilerParams(
            collective_id=2, has_side_effects=True, vmem_limit_bytes=VMEM_LIMIT
        ),
        name="ending",
    )(*args)
    return first.reshape(-1, D), second.reshape(-1, D), totals, moved.reshape(rows, D)


def finish_body(
    place, arrange_ref, out_in, tok_in, first_ref, second_ref, sum_ref,
    out_ref, tok_ref, w_ref, b_ref, dw_ref, pw_ref, pb_ref, kern_ref, ow_ref, fi_ref, fb_ref, fo_ref,
    loss_ref, kb_ref, v0_ref, v1_ref, v2_ref, v3_ref, v4_ref, v5_ref, kern_s,
):
    rows = out_ref.shape[0]
    slot = lax.broadcasted_iota(jnp.int32, (rows, rows), 0)
    sort = jnp.where(slot == arrange_ref[...], 1.0, 0.0).astype(BF16)
    out_ref[...] = dot_first(sort, out_in[...]).astype(BF16)
    tok_ref[...] = dot_first(sort, tok_in[...])
    for half in range(2):
        w_ref[:, D * half : D * half + D] = second_ref[192 * half : 192 * half + 192, :].astype(F32)
        pw_ref[96 * half : 96 * half + 96, :] = second_ref[384:480, A * half : A * half + A].astype(F32)
    for m in range(6):
        kern_s[16 * m : 16 * m + 16, :] = second_ref[480:496, 128 * m : 128 * m + 128].astype(F32)
    kern_s[A // 4 :, :] = jnp.zeros((128 - A // 4, 128), F32)
    kern_ref[...] = kern_s[...].T[: H * KW, : A // 4]
    for g in range(NG):
        for half in range(2):
            r0 = 96 * (2 * g + half)
            fi_ref[g, :, D * half : D * half + D] = first_ref[r0 : r0 + 96, :].astype(F32)
        fo_ref[g] = first_ref[384:768, A * g : A * g + A].astype(F32)
    ow_ref[...] = first_ref[768:960, :].astype(F32)
    total = jnp.sum(sum_ref[15:16, :], axis=1, keepdims=True)
    loss_ref[...] = total / (place[SEQS + 5].astype(F32) * D)
    kb_ref[...] = sum_ref[22:23, 0 : H * KW].reshape(H * KW)
    for k in range(4):

        @pl.when(place[SEQS + 4] == k)
        def _(k=k):
            cols = slice(D // 4 * k, D // 4 * k + D // 4)
            dw_ref[...] = sum_ref[0:KW, cols]
            for i, v_ref in enumerate((v0_ref, v1_ref, v2_ref, v3_ref, v4_ref, v5_ref)):
                v_ref[...] = sum_ref[KW + i : KW + i + 1, cols].reshape(D // 4)
            fb_ref[...] = sum_ref[16 + k : 17 + k, :].reshape(D)
            part = slice(A // 4 * k, A // 4 * k + A // 4)
            second = slice(A + A // 4 * k, A + A // 4 * k + A // 4)
            b_ref[0:1, :] = sum_ref[20:21, part]
            b_ref[1:2, :] = sum_ref[20:21, second]
            b_ref[2:3, :] = sum_ref[21:22, part]
            pb_ref[...] = sum_ref[21:22, second].reshape(A // 4)


def finish(place, arrange, *args):
    rows = args[0].shape[0]
    vmem = pl.BlockSpec(memory_space=pltpu.VMEM)
    shapes = [
        (rows, D), (D // 4, 4 * A), (3, A // 4), (KW, D // 4), (D // 4, A), (A // 4,), (H * KW, A // 4),
        (D // 4, D), (NG, A // 4, FF // NG), (D,), (NG, A, A), (1, 1), (H * KW,),
    ] + [(D // 4,)] * 6
    return pl.pallas_call(
        finish_body,
        out_shape=[jax.ShapeDtypeStruct((rows, D), BF16)] + [jax.ShapeDtypeStruct(shape, F32) for shape in shapes],
        in_specs=[pl.BlockSpec(memory_space=pltpu.SMEM)] + [vmem] * (len(args) + 1),
        out_specs=[vmem] * 20,
        scratch_shapes=[pltpu.VMEM((128, 128), F32)],
        compiler_params=pltpu.CompilerParams(vmem_limit_bytes=VMEM_LIMIT),
        name="finish",
    )(place, arrange, *args)


def local(
    hidden,
    teacher,
    lengths,
    deal,
    w_in,
    b_in,
    dw_kernel,
    pw_weight,
    pw_bias,
    kern_weight,
    kern_bias,
    out_weight,
    out_bias,
    norm1_gain,
    norm1_bias,
    ffn_in,
    ffn_in_bias,
    ffn_out,
    ffn_out_bias,
    norm2_gain,
    norm2_bias,
):
    rows = hidden.shape[1]
    ctx_count = lax.axis_size("ctx")
    group_rows = rows * ctx_count
    piece_rows = rows // ctx_count
    sorted_hidden, sorted_teacher, arrange, bounds, *smalls = setup(
        lengths, deal, hidden[0], teacher[0],
        [
            dw_kernel, out_bias, norm1_gain, norm1_bias, ffn_out_bias, norm2_gain, norm2_bias, ffn_in_bias,
            b_in, pw_bias, kern_weight.T,
        ],
        ctx_count,
    )
    pieces_shape = (ctx_count, piece_rows, D)
    kern_b = kern_bias[None]
    fused = group_rows <= 4096
    target, full_w_in, full_pw, full_out_w, full_ffn_in, full_ffn_out, vectors, smalls, ffn_in_b, full_kern, *rest = (
        gather_inputs(
            bounds,
            sorted_hidden,
            sorted_teacher,
            (w_in, pw_weight, out_weight, ffn_in, ffn_out),
            (0, 0, 0, 1, 1),
            smalls,
            kern_b,
            ctx_count,
            fused,
        )
    )
    target = target.reshape(rows, D)
    if fused:
        all_q8, all_keys, all_values = (item.reshape(group_rows, A) for item in rest[:3])
        conv_parts = rest[3:]
    else:
        natural = rest[0].reshape(group_rows, D)
        all_q8, all_keys, all_values = project(bounds, natural, full_w_in, smalls, rows)
        conv_parts = convolve(
            bounds, natural, full_w_in, full_pw, full_kern, kern_b, vectors, smalls, rows
        )
    conv_out, extended, conv_value, key_conv, query_ext, conv_query, spread = conv_parts
    attn_out, lse = attend(bounds, all_q8, all_keys, all_values, rows)
    result, grad_first, grad_context, stats, stats_t, layer_sums, ffn_in_sums, first_pack = layer(
        bounds, attn_out, lse, conv_out, extended, target,
        full_out_w, full_ffn_in, full_ffn_out, vectors, ffn_in_b,
    )
    heads = (stats, all_q8, all_keys, all_values) if fused else ()
    (
        *own_grad, all_grads, all_stats, output, first_own, grad_query_conv, grad_cov, grad_tokens_conv, tail, tap_sums,
        bias_sums,
    ) = middle(
        bounds, group_rows, ctx_count, heads, grad_context, stats_t, result.reshape(pieces_shape), first_pack,
        extended, conv_value, key_conv, query_ext, conv_query, spread, full_pw, full_kern, kern_b, vectors,
    )
    if fused:
        grad_query = own_grad[0]
    else:
        grad_query = query_grads(bounds, all_q8, grad_context, stats, all_keys, all_values)
    grad_keys, grad_values = key_grads(
        bounds, all_keys, all_values, all_q8, all_grads.reshape(group_rows, A), all_stats
    )
    first, second, totals, moved = ending(
        ctx_count, grad_query, grad_keys, grad_values, grad_query_conv, grad_cov, grad_tokens_conv, grad_first,
        full_w_in, extended, tail, first_own.reshape(-1, D), tap_sums, bias_sums, layer_sums, ffn_in_sums,
    )
    (
        dealt_out, dealt_grad, g_w_in, g_b_in, g_dw, g_pw, g_pw_b, g_kern, g_out, g_ffn_in, g_ffn_in_b,
        g_ffn_out, loss, g_kern_b, *g_vec,
    ) = finish(
        bounds, arrange,
        output.reshape(rows, D), moved, first, second, totals,
    )
    return (
        dealt_out[None],
        loss[0, 0],
        dealt_grad[None],
        g_w_in,
        g_b_in,
        g_dw,
        g_pw,
        g_pw_b,
        g_kern.T,
        g_kern_b,
        g_out,
        g_vec[0],
        g_vec[1],
        g_vec[2],
        g_ffn_in,
        g_ffn_in_b,
        g_ffn_out,
        g_vec[3],
        g_vec[4],
        g_vec[5],
    )


def solution(mesh):
    return jax.shard_map(
        local,
        mesh=mesh,
        in_specs=(
            P("wt", "ctx", None),
            P("wt", "ctx", None),
            P(),
            P("wt", None),
            P("wt", None),
            P(None, "wt"),
            P(None, "wt"),
            P("wt", None),
            P("wt"),
            P("wt", None),
            P(),
            P("wt", None),
            P("wt"),
            P("wt"),
            P("wt"),
            P(None, "wt", None),
            P("wt"),
            P(None, "wt", None),
            P("wt"),
            P("wt"),
            P("wt"),
        ),
        out_specs=(
            P("wt", "ctx", None),
            P(),
            P("wt", "ctx", None),
            P("wt", None),
            P(None, "wt"),
            P(None, "wt"),
            P("wt", None),
            P("wt"),
            P("wt", None),
            P(),
            P("wt", None),
            P("wt"),
            P("wt"),
            P("wt"),
            P(None, "wt", None),
            P("wt"),
            P(None, "wt", None),
            P("wt"),
            P("wt"),
            P("wt"),
        ),
        check_vma=False,
    )
```
